32 devices in a mesh: rep: 4 (over y, x), shard: 8 (over z, core).
Axes of the slice: x: 2, y: 2, z: 4, core: 2. Of those that a mesh axis runs over, the one named last changes fastest.
Arguments:
- tokens: bfloat16 [12288, 768], P(('rep', 'shard')), may hold values from -6 to 6
- routes: int32 [12288], P(('rep', 'shard')), may hold values from 0 to 7, as said below
- slot_ids: int32 [12288], P(('rep', 'shard')), may hold values from 0 to 95, as said below
- w_query: bfloat16 [768, 768], P('shard'), may hold values from -0.21875 to 0.21875
- w_key: bfloat16 [768, 768], P('shard'), may hold values from -0.21875 to 0.21875
- w_value: bfloat16 [768, 768], P('shard'), may hold values from -0.21875 to 0.21875
- w_output: bfloat16 [768, 768], P('shard'), may hold values from -3 to 3
- w_router: bfloat16 [768, 8], P('shard'), may hold values from -0.15625 to 0.15625
- norm_attn: bfloat16 [768], P('shard'), may hold values from 0.5 to 1.5
- norm_moe: bfloat16 [768], P('shard'), may hold values from 0.5 to 1.5
- rel_table: bfloat16 [32, 12], P('shard'), may hold values from -4 to 4
- w_in: bfloat16 [8, 768, 3072], P('shard'), may hold values from -0.21875 to 0.21875
- w_out: bfloat16 [8, 3072, 768], P('shard'), may hold values from -2.390625 to 2.390625
- cotangent: bfloat16 [12288, 768], P(('rep', 'shard')), may hold values from -6 to 6
Outputs:
- mixed: bfloat16 [12288, 768], P(('rep', 'shard'))
- grad_tokens: float32 [12288, 768], P(('rep', 'shard'))
- grad_w_query: float32 [768, 768], P('shard')
- grad_w_key: float32 [768, 768], P('shard')
- grad_w_value: float32 [768, 768], P('shard')
- grad_w_output: float32 [768, 768], P('shard')
- grad_w_router: float32 [768, 8], P('shard')
- grad_norm_attn: float32 [768], P('shard')
- grad_norm_moe: float32 [768], P('shard')
- grad_rel_table: float32 [32, 12], P('shard')
- grad_w_in: float32 [8, 768, 3072], P('shard', 'rep')
- grad_w_out: float32 [8, 3072, 768], P('shard', 'rep')
The draws below stay inside these ranges and needn't reach their ends.
Inputs may be any that keep to these rules, and one draw needn't show every extreme that they name: `routes`: in each device's block of 384 tokens no expert is named more than 96 times; in every group one expert, drawn from the seed, is named exactly 96 times in each of the group's blocks. `slot_ids`: within a block, tokens with the same route have different slots.
All inputs are finite; a program needn't handle non-finite values.
Results may differ from the reference program's by a relative error of at most 0.024.
Values may be sent and summed in bfloat16 or wider, within the bound.
A program may use at most 256 MiB of HBM per device.

```python
import jax
import jax.numpy as jnp
from jax import lax

D = 768
HEADS = 12
HD = 64
FF = 3072
BUCKETS = 32
PR_DEV = 128
CT_DEV = 256
TOK_DEV = 384
EXPERTS = 8
CAP = 96
PROMPT = 1024
TOKENS = 12288
N_REP = 4
N_SHARD = 8


def route_cells(key):
    block_count = N_REP * N_SHARD
    cell_count = EXPERTS * CAP
    hot_experts = jax.random.randint(jax.random.fold_in(key, 7), (N_REP,), 0, EXPERTS)

    def one_block(block_id):
        block_key = jax.random.fold_in(key, 1000 + block_id)
        order_key, place_key = jax.random.split(block_key)
        shuffled = jax.random.permutation(order_key, cell_count).astype(jnp.int32)
        hot_expert = hot_experts[block_id // N_SHARD]
        colder = (shuffled // CAP != hot_expert).astype(jnp.int32)
        ranked = shuffled[jnp.argsort(colder, stable=True)]
        chosen = ranked[:TOK_DEV]
        return chosen[jax.random.permutation(place_key, TOK_DEV)]
    cells = jax.vmap(one_block)(jnp.arange(block_count, dtype=jnp.int32))
    return cells.reshape(-1).astype(jnp.int32)


def draw_routes(key, part):
    return (route_cells(key) // CAP).astype(jnp.int32)


def draw_slot_ids(key, part):
    return (route_cells(key) % CAP).astype(jnp.int32)


def block_scale(own_key, extent, cuts, smallest, high):
    level, own = 1.0, jax.random.fold_in(own_key, 6)
    for position, shards_of in cuts:
        draws = jnp.exp(jax.random.uniform(jax.random.fold_in(own, position), (shards_of,), jnp.float32, smallest / len(cuts), high / len(cuts)))
        level = level * jnp.repeat(draws, extent[position] // shards_of).reshape([-1 if axis == position else 1 for axis in range(len(extent))])
    return level


def gaussian(own_key, shape, width, most, pieces=(), held_as=jnp.bfloat16):
    gain = block_scale(own_key, shape, pieces, -0.22, 0.18) if pieces else 1.0
    entries = jax.random.normal(own_key, shape, jnp.float32) * width * gain
    return jnp.minimum(jnp.maximum(entries, -most), most).astype(held_as)


def setup_inputs(seed: int = 0) -> dict:
    keys = jax.random.split(jax.random.key(seed), 15)
    return {
        "tokens": gaussian(keys[0], (TOKENS, D), 1.0, 6.0, ((0, 32),)),
        "routes": draw_routes(jax.random.fold_in(keys[14], 71), 0),
        "slot_ids": draw_slot_ids(jax.random.fold_in(keys[14], 71), 0),
        "w_query": gaussian(keys[3], (D, D), D ** -0.5, 0.21875, ((0, 8),)),
        "w_key": gaussian(keys[4], (D, D), D ** -0.5, 0.21875, ((0, 8),)),
        "w_value": gaussian(keys[5], (D, D), D ** -0.5, 0.21875, ((0, 8),)),
        "w_output": gaussian(keys[6], (D, D), 0.5, 3.0, ((0, 8),)),
        "w_router": gaussian(keys[7], (D, EXPERTS), (2 * D) ** -0.5, 0.15625, ((0, 8),)),
        "norm_attn": jnp.clip(1.0 + 0.1 * jax.random.normal(keys[8], (D,), jnp.float32), 0.5, 1.5).astype(jnp.bfloat16),
        "norm_moe": jnp.clip(1.0 + 0.1 * jax.random.normal(keys[9], (D,), jnp.float32), 0.5, 1.5).astype(jnp.bfloat16),
        "rel_table": gaussian(keys[10], (BUCKETS, HEADS), 1.0, 4.0, ((0, 8),)),
        "w_in": gaussian(keys[11], (EXPERTS, D, FF), D ** -0.5, 0.21875, ((0, 8),)),
        "w_out": gaussian(keys[12], (EXPERTS, FF, D), 0.4, 2.390625, ((0, 8),)),
        "cotangent": gaussian(keys[13], (TOKENS, D), 1.0, 6.0, ((0, 32),)),
    }


@jax.custom_vjp
def low(v):
    return lax.optimization_barrier(v.astype(jnp.bfloat16)).astype(jnp.float32)

@jax.custom_vjp
def low_back(v):
    return v

def low_keep(v):
    return (low(v), None)

def low_pass(kept, grad):
    return (grad,)

def back_keep(v):
    return (v, None)

def back_low(kept, grad):
    return (low(grad),)
low.defvjp(low_keep, low_pass)
low_back.defvjp(back_keep, back_low)
bucket_edges = (12, 16, 23, 32, 46, 64, 91)
norm_epsilon = 1e-06
masked_score = -1e+30
highest = lax.Precision.HIGHEST

def bucket_of(distance):
    magnitude = jnp.abs(distance)
    far_steps = jnp.zeros_like(magnitude)
    for edge_value in bucket_edges:
        far_steps = far_steps + (magnitude >= edge_value).astype(jnp.int32)
    exact_span = BUCKETS // 4
    within = jnp.where(magnitude < exact_span, magnitude, exact_span + far_steps)
    return (jnp.where(distance > 0, BUCKETS // 2, 0) + within).astype(jnp.int32)

def norm_apply(values, gain_row):
    return values * lax.rsqrt(lax.optimization_barrier(jnp.mean(values * values, axis=-1, keepdims=True)) + norm_epsilon) * gain_row

def matmul_high(left, right):
    return jnp.dot(left, right, precision=highest, preferred_element_type=jnp.float32)

def token_layout(shard_ids, row_ids):
    in_prompt = row_ids < PR_DEV
    positions = jnp.where(in_prompt, shard_ids * PR_DEV + row_ids, PROMPT + shard_ids % 2 * CT_DEV + row_ids - PR_DEV)
    cont_ids = jnp.where(in_prompt, -1, shard_ids // 2)
    return (positions.astype(jnp.int32), cont_ids.astype(jnp.int32))

def group_attention(queries, keys_all, values_all, table):
    shard_ids = jnp.repeat(jnp.arange(N_SHARD, dtype=jnp.int32), TOK_DEV)
    row_ids = jnp.tile(jnp.arange(TOK_DEV, dtype=jnp.int32), N_SHARD)
    positions, cont_ids = token_layout(shard_ids, row_ids)
    key_cont = jnp.where(row_ids < PR_DEV, -2, cont_ids).astype(jnp.int32)
    table_heads = table.T

    def attend_rows(query_rows, query_pos, query_cont):
        raw_scores = low_back(jnp.einsum('qhd,khd->hqk', query_rows, keys_all, precision=highest))
        buckets = bucket_of(positions[None, :] - query_pos[:, None])
        scores = raw_scores * HD ** (-0.5) + jnp.take(table_heads, buckets, axis=1)
        visible = (key_cont[None, :] == -2) | (key_cont[None, :] == query_cont[:, None]) & (positions[None, :] <= query_pos[:, None])
        scores = jnp.where(visible[None], scores, masked_score)
        weights = low(jax.nn.softmax(scores, axis=-1))
        return jnp.einsum('hqk,khd->qhd', weights, values_all, precision=highest)
    checked = jax.checkpoint(attend_rows)

    def one_block(item_set):
        return checked(item_set[0], item_set[1], item_set[2])
    stacked = (queries.reshape(N_SHARD, TOK_DEV, HEADS, HD), positions.reshape(N_SHARD, TOK_DEV), cont_ids.reshape(N_SHARD, TOK_DEV))
    return lax.map(one_block, stacked)

def expert_rows(rows_in, first_weight, second_weight):
    pre_act = low_back(matmul_high(rows_in, first_weight))
    hidden = low(jax.nn.gelu(pre_act, approximate=True))
    return low_back(low(matmul_high(hidden, second_weight)))

def to_single(values):
    return values.astype(jnp.float32)

def reference(tokens, routes, slot_ids, w_query, w_key, w_value, w_output, w_router, norm_attn, norm_moe, rel_table, w_in, w_out, cotangent):
    block_ids = jnp.arange(N_REP * N_SHARD, dtype=jnp.int32)[:, None]
    dispatch = ((block_ids * EXPERTS + routes.reshape(-1, TOK_DEV)) * CAP + slot_ids.reshape(-1, TOK_DEV)).reshape(-1).astype(jnp.int32)
    route_match = routes[:, None] == jnp.arange(EXPERTS, dtype=jnp.int32)[None, :]

    def forward_all(resid_in, query_w, key_w, value_w, output_w, router_w, gain_attn, gain_moe, table, first_w, second_w):
        normed = low(norm_apply(resid_in, gain_attn))
        queries = low_back(low(matmul_high(normed, query_w)))
        keys_tok = low_back(low(matmul_high(normed, key_w)))
        values_tok = low_back(low(matmul_high(normed, value_w)))
        group_shape = (N_REP, N_SHARD * TOK_DEV, HEADS, HD)

        def one_group(item_set):
            return group_attention(item_set[0], item_set[1], item_set[2], table)
        attended = lax.map(one_group, (queries.reshape(group_shape), keys_tok.reshape(group_shape), values_tok.reshape(group_shape)))
        attn_low = low_back(low(attended.reshape(-1, D)))
        resid_mid = resid_in + low_back(matmul_high(attn_low, output_w))
        mid_low = low(norm_apply(resid_mid, gain_moe))
        router_probs = jax.nn.softmax(matmul_high(mid_low, router_w), axis=-1)
        gate_value = lax.optimization_barrier(jnp.sum(jnp.where(route_match, router_probs, 0.0), axis=-1))
        sent = low_back(mid_low)
        buffer = jnp.zeros((N_REP * N_SHARD * EXPERTS * CAP, D), jnp.float32).at[dispatch].set(sent)
        buffer = buffer.reshape(N_REP, N_SHARD, EXPERTS, CAP, D).transpose(2, 0, 1, 3, 4).reshape(EXPERTS, N_REP * N_SHARD * CAP, D)
        checked = jax.checkpoint(expert_rows)

        def one_expert(item_set):
            return checked(item_set[0], item_set[1], item_set[2])
        expert_res = lax.map(one_expert, (buffer, first_w, second_w))
        returned = expert_res.reshape(EXPERTS, N_REP, N_SHARD, CAP, D).transpose(1, 2, 0, 3, 4).reshape(-1, D)
        return resid_mid + gate_value[:, None] * returned[dispatch]
    result, pull = jax.vjp(forward_all, to_single(tokens), to_single(w_query), to_single(w_key), to_single(w_value), to_single(w_output), to_single(w_router), to_single(norm_attn), to_single(norm_moe), to_single(rel_table), to_single(w_in), to_single(w_out))
    grads = pull(to_single(cotangent))
    return (result.astype(jnp.bfloat16), grads[0], grads[1], grads[2], grads[3], grads[4], grads[5], grads[6], grads[7], grads[8], grads[9], grads[10])
```

```python
import jax
import jax.numpy as jnp
import numpy as np
from jax import lax
from jax.experimental import pallas as pl
from jax.experimental.pallas import tpu as pltpu
from jax.sharding import PartitionSpec as P

PR_DEV = 128


bucket_edges = (12, 16, 23, 32, 46, 64, 91)
norm_epsilon = 1e-06
masked_score = -1e30


def norm_apply(values, gain_row):
    return (
        values
        * lax.rsqrt(jnp.mean(values * values, axis=-1, keepdims=True) + norm_epsilon)
        * gain_row
    )


def gelu_tanh(values):
    return jax.nn.gelu(values, approximate=True)


TILE = 128
SPAN = 2 * TILE
far_before, far_after, causal_tile, hidden_tile, tile_kinds = 3, 4, 5, 6, 7
vmem_cap = 60 * 1024 * 1024


def nt(left, right):
    return lax.dot_general(
        left, right, (((1,), (1,)), ((), ())), preferred_element_type=jnp.float32
    )


def nn(left, right):
    return jnp.dot(left, right, preferred_element_type=jnp.float32)


def fill_tiles(tiles_ref, rev_row, low, high):
    spread = jnp.broadcast_to(rev_row, (TILE, 4 * TILE))
    rolled = pltpu.roll(spread, 0, 1, stride=1, stride_axis=0)
    keys = lax.broadcasted_iota(jnp.int32, (TILE, TILE), 0)
    rows = lax.broadcasted_iota(jnp.int32, (TILE, TILE), 1)
    tiles_ref[0] = rolled[:, TILE : 2 * TILE]
    tiles_ref[1] = rolled[:, :TILE]
    tiles_ref[2] = rolled[:, 3 * TILE :]
    tiles_ref[far_before] = jnp.broadcast_to(low, (TILE, TILE))
    tiles_ref[far_after] = jnp.broadcast_to(high, (TILE, TILE))
    tiles_ref[causal_tile] = jnp.where(keys <= rows, rolled[:, :TILE], masked_score)
    tiles_ref[hidden_tile] = jnp.full((TILE, TILE), masked_score, jnp.float32)


def prompt_tile(block, chunk, shard_id, block_count):
    if chunk == 0:
        gap = block - shard_id
        far = jnp.where(gap < 0, far_before, far_after)
        return jnp.where(jnp.abs(gap) <= 1, gap + 1, far)
    if chunk == 1 and block == block_count - 1:
        return jnp.where(shard_id % 2 == 0, 0, far_before)
    return far_before


def local_tile(block, chunk, shard_id):
    if block >= 2:
        return ((causal_tile, 0), (hidden_tile, causal_tile))[block - 2][chunk]
    kind = 0 if (block, chunk) == (1, 0) else far_before
    return jnp.where(shard_id % 2 == 1, kind, hidden_tile)


def prompt_grid(part, shard_id, block_count):
    return [
        [prompt_tile(2 * part + half, chunk, shard_id, block_count) for chunk in range(3)]
        for half in range(2)
    ]


def local_grid(part, shard_id):
    return [[local_tile(2 * part + half, chunk, shard_id) for chunk in range(2)] for half in range(2)]


def with_bias(scores, tiles_ref, grid):
    return jnp.concatenate(
        [
            jnp.concatenate(
                [
                    scores[i * TILE : (i + 1) * TILE, j * TILE : (j + 1) * TILE] + tiles_ref[kind]
                    for j, kind in enumerate(row)
                ],
                axis=1,
            )
            for i, row in enumerate(grid)
        ],
        axis=0,
    )


def fold8(values):
    return values.reshape(values.shape[0] // 8, 8, values.shape[1])


def head_mask(rows, side):
    lanes = lax.broadcasted_iota(jnp.int32, (rows, TILE), 1)
    return (lanes < TILE // 2) if side == 0 else (lanes >= TILE // 2)


def attn_forward_kernel(
    rev_ref, q_ref, k_ref, v_ref, out_ref, lse_ref,
    tiles, vt, sp, sl, ot,
):
    shard_id = lax.axis_index("shard")
    rows = q_ref.shape[0]
    prompt_rows = TILE
    blocks = k_ref.shape[0] // TILE - 4
    half = TILE // 2

    @pl.loop(0, q_ref.shape[1] // TILE)
    def pair_loop(pair):
        cols = pl.ds(pl.multiple_of(pair * TILE, TILE), TILE)
        vt[...] = v_ref[:, cols].T
        q_pair = q_ref[:, cols] * jnp.asarray(0.125, q_ref.dtype)
        for side in range(2):
            head = pair * 2 + side
            rev_row = rev_ref[pl.ds(head, 1), :]
            fill_tiles(tiles, rev_row, rev_row[:, 4 * TILE // 2 - 1 : 4 * TILE // 2], rev_row[:, 4 * TILE // 2 : 4 * TILE // 2 + 1])
            q_head = jnp.where(head_mask(rows, side), q_pair, jnp.zeros_like(q_pair))
            top = jnp.full((8, rows), masked_score, jnp.float32)
            for part in range(blocks // 2):
                keys = slice(part * SPAN, (part + 1) * SPAN)
                scores = with_bias(nt(k_ref[keys, cols], q_head), tiles, prompt_grid(part, shard_id, blocks))
                sp[keys, :] = scores
                top = jnp.maximum(top, jnp.max(fold8(scores), axis=0))
            top_local = top[:, prompt_rows:]
            for part in range(2):
                keys = slice(part * SPAN, (part + 1) * SPAN)
                held = slice((blocks // 2 + part) * SPAN, (blocks // 2 + part + 1) * SPAN)
                scores = with_bias(nt(k_ref[held, cols], q_head[prompt_rows:]), tiles, local_grid(part, shard_id))
                sl[keys, :] = scores
                top_local = jnp.maximum(top_local, jnp.max(fold8(scores), axis=0))
            top = jnp.max(jnp.concatenate([top[:, :prompt_rows], top_local], axis=1), axis=0, keepdims=True)
            total = jnp.zeros((8, rows), jnp.float32)
            summed = jnp.zeros((half, rows), jnp.float32)
            heads = slice(side * half, (side + 1) * half)
            for part in range(blocks // 2):
                keys = slice(part * SPAN, (part + 1) * SPAN)
                weights = jnp.exp(sp[keys, :] - top)
                total = total + jnp.sum(fold8(weights), axis=0)
                summed = summed + nn(vt[heads, keys], weights.astype(jnp.bfloat16))
            top_c = top[:, prompt_rows:]
            total_c = total[:, prompt_rows:]
            summed_c = summed[:, prompt_rows:]
            for part in range(2):
                keys = slice(part * SPAN, (part + 1) * SPAN)
                held = slice((blocks // 2 + part) * SPAN, (blocks // 2 + part + 1) * SPAN)
                weights = jnp.exp(sl[keys, :] - top_c)
                total_c = total_c + jnp.sum(fold8(weights), axis=0)
                summed_c = summed_c + nn(vt[heads, held], weights.astype(jnp.bfloat16))
            total = jnp.sum(jnp.concatenate([total[:, :prompt_rows], total_c], axis=1), axis=0, keepdims=True)
            summed = jnp.concatenate([summed[:, :prompt_rows], summed_c], axis=1)
            ot[heads, :] = summed / total
            lse_ref[pl.ds(head, 1), :] = top + jnp.log(total)
        out_ref[:, cols] = ot[...].T


def attn_forward(rev, queries, keys, values):
    rows, width = queries.shape
    head_rows = rev.shape[0]
    spec = pl.BlockSpec(memory_space=pltpu.VMEM)
    return pl.pallas_call(
        attn_forward_kernel,
        out_shape=(
            jax.ShapeDtypeStruct((rows, width), jnp.float32),
            jax.ShapeDtypeStruct((head_rows, rows), jnp.float32),
        ),
        in_specs=[spec] * 4,
        out_specs=(spec, spec),
        scratch_shapes=[
            pltpu.VMEM((tile_kinds, TILE, TILE), jnp.float32),
            pltpu.VMEM((TILE, keys.shape[0]), jnp.bfloat16),
            pltpu.VMEM((keys.shape[0] - 2 * SPAN, rows), jnp.float32),
            pltpu.VMEM((2 * SPAN, rows - TILE), jnp.float32),
            pltpu.VMEM((TILE, rows), jnp.float32),
        ],
        compiler_params=pltpu.CompilerParams(vmem_limit_bytes=vmem_cap),
        cost_estimate=pl.CostEstimate(flops=20_000_000_000, bytes_accessed=12_000_000, transcendentals=8_000_000),
        name="attn_forward",
    )(rev, queries, keys, values)


def attn_backward_kernel(
    rev_ref, hot_ref, q_ref, k_ref, v_ref, g_ref, o_ref, lse_ref,
    dq_ref, dk_ref, dv_ref, table_ref,
    tiles, sums, diag, kt, dqt, far_sums, dk_sum, dv_sum,
):
    shard_id = lax.axis_index("shard")
    rows = q_ref.shape[0]
    prompt_rows = TILE
    blocks = k_ref.shape[0] // TILE - 4
    half = TILE // 2
    diag[...] = jnp.zeros_like(diag)
    far_sums[...] = jnp.zeros_like(far_sums)
    tile_rows = lax.broadcasted_iota(jnp.int32, (TILE, TILE), 0)
    tile_cols = lax.broadcasted_iota(jnp.int32, (TILE, TILE), 1)
    flip = (tile_rows + tile_cols == TILE - 1).astype(jnp.float32)

    @pl.loop(0, q_ref.shape[1] // TILE)
    def pair_loop(pair):
        cols = pl.ds(pl.multiple_of(pair * TILE, TILE), TILE)
        kt[...] = k_ref[:, cols].T
        q_pair = q_ref[:, cols] * jnp.asarray(0.125, q_ref.dtype)
        g_pair = g_ref[:, cols]
        delta_t = (g_pair.astype(jnp.float32) * o_ref[:, cols]).T
        for side in range(2):
            head = pair * 2 + side
            heads = slice(side * half, (side + 1) * half)
            rev_row = rev_ref[pl.ds(head, 1), :]
            fill_tiles(tiles, rev_row, rev_row[:, 4 * TILE // 2 - 1 : 4 * TILE // 2], rev_row[:, 4 * TILE // 2 : 4 * TILE // 2 + 1])
            sums[...] = jnp.zeros_like(sums)
            mask = head_mask(rows, side)
            q_head = jnp.where(mask, q_pair, jnp.zeros_like(q_pair))
            g_head = jnp.where(mask, g_pair, jnp.zeros_like(g_pair))
            delta = jnp.sum(delta_t[heads, :], axis=0, keepdims=True)
            log_total = lse_ref[pl.ds(head, 1), :]

            def block_grads(part, first, grid):
                keys = slice(part * SPAN, (part + 1) * SPAN)
                q_rows, g_rows = q_head[first:], g_head[first:]
                scores = with_bias(nt(k_ref[keys, cols], q_rows), tiles, grid)
                weights = jnp.exp(scores - log_total[:, first:])
                grad_weights = nt(v_ref[keys, cols], g_rows)
                grad_scores = weights * (grad_weights - delta[:, first:])
                for i, row in enumerate(grid):
                    for j, kind in enumerate(row):
                        sums[kind] += grad_scores[i * TILE : (i + 1) * TILE, j * TILE : (j + 1) * TILE]
                raw = grad_scores.astype(jnp.bfloat16)
                dk = nn(raw, q_rows)
                dv = nn(weights.astype(jnp.bfloat16), g_rows)
                if side == 0:
                    dk_sum[keys, :] = dk
                    dv_sum[keys, :] = dv
                else:
                    dk_ref[keys, cols] = (dk_sum[keys, :] + dk).astype(dk_ref.dtype)
                    dv_ref[keys, cols] = (dv_sum[keys, :] + dv).astype(dv_ref.dtype)
                return nn(kt[heads, keys], raw)

            dq = jnp.zeros((half, rows), jnp.float32)
            for part in range(blocks // 2):
                dq = dq + block_grads(part, 0, prompt_grid(part, shard_id, blocks))
            dq_c = dq[:, prompt_rows:]
            for part in range(2):
                dq_c = dq_c + block_grads(blocks // 2 + part, prompt_rows, local_grid(part, shard_id))
            dqt[heads, :] = jnp.concatenate([dq[:, :prompt_rows], dq_c], axis=1)
            near = jnp.concatenate(
                [sums[1] + sums[causal_tile], sums[0], jnp.zeros((TILE, TILE), jnp.float32), sums[2]], axis=1
            )
            flipped = jnp.dot(flip, near, precision=lax.Precision.HIGHEST, preferred_element_type=jnp.float32)
            rolled = pltpu.roll(flipped, 3 * TILE + 1, 1, stride=1, stride_axis=0)
            diag[pl.ds(head, 1), :] = jnp.sum(rolled, axis=0, keepdims=True)
            far_sums[pl.ds(head, 1), :] = jnp.concatenate(
                [jnp.sum(sums[far_before], axis=0, keepdims=True), jnp.sum(sums[far_after], axis=0, keepdims=True)], axis=1
            )
        dq_ref[:, cols] = (dqt[...].T * 0.125).astype(dq_ref.dtype)

    by_bucket = jnp.dot(diag[...], hot_ref[...], precision=lax.Precision.HIGHEST, preferred_element_type=jnp.float32)
    lanes = lax.broadcasted_iota(jnp.int32, by_bucket.shape, 1)
    before = jnp.sum(far_sums[:, :TILE], axis=1, keepdims=True)
    after = jnp.sum(far_sums[:, TILE:], axis=1, keepdims=True)
    table_ref[...] = by_bucket + jnp.where(lanes == 15, before, 0.0) + jnp.where(lanes == 31, after, 0.0)


def attn_backward(rev, hot, queries, keys, values, grad_heads, attended, lse):
    rows, width = queries.shape
    head_rows = rev.shape[0]
    spec = pl.BlockSpec(memory_space=pltpu.VMEM)
    return pl.pallas_call(
        attn_backward_kernel,
        out_shape=(
            jax.ShapeDtypeStruct((rows, width), jnp.bfloat16),
            jax.ShapeDtypeStruct(keys.shape, jnp.bfloat16),
            jax.ShapeDtypeStruct(values.shape, jnp.bfloat16),
            jax.ShapeDtypeStruct((head_rows, hot.shape[1]), jnp.float32),
        ),
        in_specs=[spec] * 8,
        out_specs=(spec,) * 4,
        scratch_shapes=[
            pltpu.VMEM((tile_kinds, TILE, TILE), jnp.float32),
            pltpu.VMEM((tile_kinds, TILE, TILE), jnp.float32),
            pltpu.VMEM((head_rows, 4 * TILE), jnp.float32),
            pltpu.VMEM((TILE, keys.shape[0]), jnp.bfloat16),
            pltpu.VMEM((TILE, rows), jnp.float32),
            pltpu.VMEM((head_rows, 2 * TILE), jnp.float32),
            pltpu.VMEM((keys.shape[0], TILE), jnp.float32),
            pltpu.VMEM((keys.shape[0], TILE), jnp.float32),
        ],
        compiler_params=pltpu.CompilerParams(vmem_limit_bytes=vmem_cap),
        cost_estimate=pl.CostEstimate(flops=40_000_000_000, bytes_accessed=24_000_000, transcendentals=8_000_000),
        name="attn_backward",
    )(rev, hot, queries, keys, values, grad_heads, attended, lse)


def distance_buckets(bucket_count):
    steps = np.arange(4 * TILE)
    gap = -np.where(steps < 2 * TILE, steps, steps - 4 * TILE)
    size = np.abs(gap)
    far = sum((size >= edge).astype(np.int64) for edge in bucket_edges)
    exact = bucket_count // 4
    return np.where(gap > 0, bucket_count // 2, 0) + np.where(size < exact, size, exact + far)


QUARTERS = 4
mesh_ids = pl.DeviceIdType.MESH


def places():
    rep, shard = lax.axis_index("rep"), lax.axis_index("shard")
    return rep, shard // 2, shard % 2, lax.axis_size("shard") // 2, rep % QUARTERS


def peer_lists():
    rep, chip, core, chips, quarter = places()
    along = [(rep, (chip + k) % chips * 2 + core) for k in range(1, chips)]
    across = [(rep - quarter + (quarter + j) % QUARTERS, chip * 2 + core) for j in range(1, QUARTERS)]
    twin = (rep, chip * 2 + 1 - core)
    return along, across, twin


def greet(devices):
    barrier = pltpu.get_barrier_semaphore()
    for device in devices:
        pl.semaphore_signal(barrier, inc=1, device_id=device, device_id_type=mesh_ids)
    pl.semaphore_wait(barrier, len(devices))


def send(source, target, sems, device):
    return pltpu.make_async_remote_copy(
        src_ref=source, dst_ref=target, send_sem=sems[0], recv_sem=sems[1],
        device_id=device, device_id_type=mesh_ids,
    )


def gather_kernel(
    w_ref, tok_ref, small_ref, wg_ref, tg_ref, near_ref, sg_ref,
    wz_s, wz_r, tz_s, tz_r, sz_s, sz_r, wr_s, wr_r, wt_s, wt_r, et_s, et_r, loc,
):
    rep, chip, core, chips, quarter = places()
    along, across, twin = peer_lists()
    prompt = tok_ref.at[pl.ds(0, PR_DEV)]
    rest = tok_ref.at[pl.ds(PR_DEV, tok_ref.shape[0] - PR_DEV)]
    own = [
        pltpu.make_async_copy(w_ref, wg_ref.at[:, chip, core], loc.at[0]),
        pltpu.make_async_copy(prompt, tg_ref.at[chip, core], loc.at[1]),
        pltpu.make_async_copy(small_ref, sg_ref.at[chip, core], loc.at[2]),
    ]
    for copy in own:
        copy.start()
    greet(along + across + [twin])
    w_out, t_out, s_out = [], [], []
    for k, device in enumerate(along):
        w_out.append(send(w_ref.at[:, quarter], wg_ref.at[:, chip, core, quarter], (wz_s.at[k], wz_r.at[k]), device))
        s_out.append(send(small_ref, sg_ref.at[chip, core], (sz_s.at[k], sz_r.at[k]), device))
        t_out.append(send(prompt, tg_ref.at[chip, core], (tz_s.at[k], tz_r.at[k]), device))
    for copy in w_out + s_out + t_out:
        copy.start()
    near = send(rest, near_ref, (et_s.at[0], et_r.at[0]), twin)
    near.start()
    for copy in own:
        copy.wait()
    row_out = [send(wg_ref.at[:, chip, core], wg_ref.at[:, chip, core], (wt_s.at[0], wt_r.at[0]), twin)]
    row_out[0].start()
    r_out = []
    for k in range(1, chips):
        source = (chip + chips - k) % chips
        piece = wg_ref.at[:, source, core, quarter]
        send(piece, piece, (wz_s.at[k - 1], wz_r.at[k - 1]), twin).wait_recv()
        for j, device in enumerate(across):
            r_out.append(send(piece, piece, (wr_s.at[k - 1, j], wr_r.at[k - 1, j]), device))
            r_out[-1].start()
    for k in range(1, chips):
        source = (chip + chips - k) % chips
        for j in range(1, QUARTERS):
            piece = wg_ref.at[:, source, core, (quarter + QUARTERS - j) % QUARTERS]
            send(piece, piece, (wr_s.at[k - 1, j - 1], wr_r.at[k - 1, j - 1]), twin).wait_recv()
        row = wg_ref.at[:, source, core]
        row_out.append(send(row, row, (wt_s.at[k], wt_r.at[k]), twin))
        row_out[-1].start()
    for k in range(1, chips):
        source = (chip + chips - k) % chips
        send(prompt, tg_ref.at[source, core], (tz_s.at[k - 1], tz_r.at[k - 1]), twin).wait_recv()
        send(small_ref, sg_ref.at[source, core], (sz_s.at[k - 1], sz_r.at[k - 1]), twin).wait_recv()
    ends = [
        send(tg_ref.at[:, core], tg_ref.at[:, core], (et_s.at[1], et_r.at[1]), twin),
        send(sg_ref.at[:, core], sg_ref.at[:, core], (et_s.at[2], et_r.at[2]), twin),
    ]
    for copy in ends:
        copy.start()
    near.wait_recv()
    for k in range(chips):
        source = (chip + chips - k) % chips
        row = wg_ref.at[:, source, 1 - core]
        send(row, row, (wt_s.at[k], wt_r.at[k]), twin).wait_recv()
    send(tg_ref.at[:, core], tg_ref.at[:, 1 - core], (et_s.at[1], et_r.at[1]), twin).wait_recv()
    send(sg_ref.at[:, core], sg_ref.at[:, 1 - core], (et_s.at[2], et_r.at[2]), twin).wait_recv()
    for copy in w_out + s_out + t_out + r_out + row_out + ends + [near]:
        copy.wait_send()


def gather_all(weights, tokens, small):
    chips = lax.axis_size("shard") // 2
    width = tokens.shape[1]
    pairs = pltpu.SemaphoreType.DMA
    anywhere = pl.BlockSpec(memory_space=pl.ANY)
    count = chips - 1
    return pl.pallas_call(
        gather_kernel,
        out_shape=(
            jax.ShapeDtypeStruct((weights.shape[0], chips, 2) + weights.shape[1:], weights.dtype),
            jax.ShapeDtypeStruct((chips, 2, PR_DEV, width), tokens.dtype),
            jax.ShapeDtypeStruct((tokens.shape[0] - PR_DEV, width), tokens.dtype),
            jax.ShapeDtypeStruct((chips, 2) + small.shape, small.dtype),
        ),
        in_specs=[anywhere] * 3,
        out_specs=(anywhere,) * 4,
        scratch_shapes=[
            pairs((count,)), pairs((count,)), pairs((count,)), pairs((count,)), pairs((count,)), pairs((count,)),
            pairs((count, 3)), pairs((count, 3)), pairs((chips,)), pairs((chips,)), pairs((3,)), pairs((3,)),
            pairs((3,)),
        ],
        compiler_params=pltpu.CompilerParams(collective_id=0, has_side_effects=True),
        cost_estimate=pl.CostEstimate(flops=0, bytes_accessed=100_000_000, transcendentals=0),
        name="gather_all",
    )(weights, tokens, small)


def reduce_kernel(
    d_ref, p_ref, e_ref, out_ref, po_ref, eo_ref,
    half, summed, third, thirds, fourth, fourths, last, gathered, p_half, p_sum, p_in,
    ds_s, ds_r, ps_s, ps_r, dr_s, dr_r, dh_s, dh_r, dz_s, dz_r, pz_s, pz_r, da_s, da_r,
):
    rep, chip, core, chips, quarter = places()
    along, across, twin = peer_lists()
    classes = lax.axis_size("rep") // QUARTERS
    above = [
        ((rep // QUARTERS + k) % classes * QUARTERS + quarter, chip * 2 + core) for k in range(1, classes)
    ]
    greet(along + across + above + [twin])
    single = jnp.float32
    first = [
        send(p_ref.at[:, 1 - core], p_half, (ps_s.at[0], ps_r.at[0]), twin),
        send(e_ref, eo_ref, (ps_s.at[1], ps_r.at[1]), twin),
    ] + [
        send(d_ref.at[k, 1 - core], half.at[k], (ds_s.at[k], ds_r.at[k]), twin) for k in range(chips)
    ]
    for copy in first:
        copy.start()
    pending = list(first)
    first[0].wait_recv()
    for k in range(chips):
        p_sum[k] = (p_ref[k, core].astype(single) + p_half[k].astype(single)).astype(p_sum.dtype)
    for k, device in enumerate(along):
        copy = send(p_sum.at[(chip + k + 1) % chips], p_in.at[k], (pz_s.at[k], pz_r.at[k]), device)
        copy.start()
        pending.append(copy)
    for k in range(chips):
        first[2 + k].wait_recv()
        for t in range(QUARTERS):
            summed[t, k] = (d_ref[k, core, t].astype(single) + half[k, t].astype(single)).astype(summed.dtype)
    for j, device in enumerate(across):
        copy = send(summed.at[(quarter + j + 1) % QUARTERS], third.at[j], (dr_s.at[j], dr_r.at[j]), device)
        copy.start()
        pending.append(copy)
    for j in range(QUARTERS - 1):
        send(third.at[j], third.at[j], (dr_s.at[j], dr_r.at[j]), twin).wait_recv()
    for k in range(chips):
        total = summed[quarter, k].astype(single)
        for j in range(QUARTERS - 1):
            total = total + third[j, k].astype(single)
        thirds[k] = total.astype(thirds.dtype)
    if classes > 1:
        for j, device in enumerate(above):
            copy = send(thirds, fourth.at[j], (dh_s.at[j], dh_r.at[j]), device)
            copy.start()
            pending.append(copy)
        for j in range(classes - 1):
            send(thirds, fourth.at[j], (dh_s.at[j], dh_r.at[j]), twin).wait_recv()
        for k in range(chips):
            total = thirds[k].astype(single)
            for j in range(classes - 1):
                total = total + fourth[j, k].astype(single)
            fourths[k] = total.astype(fourths.dtype)
    else:
        fourths = thirds
    for k, device in enumerate(along):
        copy = send(fourths.at[(chip + k + 1) % chips], last.at[k], (dz_s.at[k], dz_r.at[k]), device)
        copy.start()
        pending.append(copy)
    for k in range(chips - 1):
        send(p_in.at[k], p_in.at[k], (pz_s.at[k], pz_r.at[k]), twin).wait_recv()
    total = p_sum[chip].astype(single)
    for k in range(chips - 1):
        total = total + p_in[k].astype(single)
    po_ref[...] = total
    for k in range(chips - 1):
        send(last.at[k], last.at[k], (dz_s.at[k], dz_r.at[k]), twin).wait_recv()
    total = fourths[chip].astype(single)
    for k in range(chips - 1):
        total = total + last[k].astype(single)
    gathered[quarter] = total.astype(gathered.dtype)
    for j, device in enumerate(across):
        copy = send(gathered.at[quarter], gathered.at[quarter], (da_s.at[j], da_r.at[j]), device)
        copy.start()
        pending.append(copy)
    for j in range(QUARTERS - 1):
        piece = gathered.at[(quarter + QUARTERS - j - 1) % QUARTERS]
        send(piece, piece, (da_s.at[j], da_r.at[j]), twin).wait_recv()
    out_ref[...] = gathered[...].astype(single)
    first[1].wait_recv()
    for copy in pending:
        copy.wait_send()


def reduce_all(dense, prompt_part, near_part):
    chips = lax.axis_size("shard") // 2
    classes = lax.axis_size("rep") // QUARTERS
    piece = dense.shape[3:]
    low = jnp.bfloat16
    pairs = pltpu.SemaphoreType.DMA
    spec = pl.BlockSpec(memory_space=pltpu.VMEM)
    count = chips - 1
    return pl.pallas_call(
        reduce_kernel,
        out_shape=(
            jax.ShapeDtypeStruct((QUARTERS,) + piece, jnp.float32),
            jax.ShapeDtypeStruct(prompt_part.shape[2:], jnp.float32),
            jax.ShapeDtypeStruct(near_part.shape, low),
        ),
        in_specs=[spec] * 3,
        out_specs=(spec,) * 3,
        scratch_shapes=[
            pltpu.VMEM((chips, QUARTERS) + piece, low),
            pltpu.VMEM((QUARTERS, chips) + piece, low),
            pltpu.VMEM((QUARTERS - 1, chips) + piece, low),
            pltpu.VMEM((chips,) + piece, low),
            pltpu.VMEM((max(classes - 1, 1), chips if classes > 1 else 1) + piece, low),
            pltpu.VMEM((chips if classes > 1 else 1,) + piece, low),
            pltpu.VMEM((count,) + piece, low),
            pltpu.VMEM((QUARTERS,) + piece, low),
            pltpu.VMEM((chips,) + prompt_part.shape[2:], low),
            pltpu.VMEM((chips,) + prompt_part.shape[2:], low),
            pltpu.VMEM((count,) + prompt_part.shape[2:], low),
            pairs((chips,)), pairs((chips,)), pairs((2,)), pairs((2,)), pairs((3,)), pairs((3,)),
            pairs((max(classes - 1, 1),)), pairs((max(classes - 1, 1),)),
            pairs((count,)), pairs((count,)), pairs((count,)), pairs((count,)), pairs((3,)), pairs((3,)),
        ],
        compiler_params=pltpu.CompilerParams(collective_id=1, has_side_effects=True, vmem_limit_bytes=vmem_cap),
        cost_estimate=pl.CostEstimate(flops=0, bytes_accessed=200_000_000, transcendentals=0),
        name="reduce_all",
    )(dense, prompt_part, near_part)


def local(
    tokens,
    routes,
    slot_ids,
    w_query,
    w_key,
    w_value,
    w_output,
    w_router,
    norm_attn,
    norm_moe,
    rel_table,
    w_in,
    w_out,
    cotangent,
):
    shard_count = lax.axis_size("shard")
    token_rows, model_width = tokens.shape
    cont_rows = token_rows - PR_DEV
    prompt_len = PR_DEV * shard_count
    low, single = jnp.bfloat16, jnp.float32
    weight_rows, expert_count = w_router.shape
    table_rows, head_count = rel_table.shape
    bucket_count = table_rows * shard_count
    capacity = 2 * token_rows // expert_count

    weights = jnp.stack([w_query, w_key, w_value, w_output]).reshape(4, QUARTERS, -1, model_width)
    small = jnp.concatenate(
        [w_router, norm_attn[:, None], norm_moe[:, None],
         jnp.pad(rel_table, ((0, weight_rows - table_rows), (0, 0)))], axis=1
    )
    small = jnp.pad(small, ((0, 0), (0, TILE - small.shape[1])))
    weights, prompt_tok, near_tok, small = gather_all(weights, tokens, small)
    query_full, key_full, value_full, output_full = (
        weights[i].reshape(model_width, model_width) for i in range(4)
    )
    small = small.reshape(model_width, TILE)
    router_full = small[:, :expert_count]
    gain_attn = small[:, expert_count].astype(single)
    gain_moe = small[:, expert_count + 1].astype(single)
    table_full = small.reshape(shard_count, weight_rows, TILE)[
        :, :table_rows, expert_count + 2 : expert_count + 2 + head_count
    ].reshape(bucket_count, head_count)

    buckets = distance_buckets(bucket_count)
    hot = (buckets[:, None] == np.arange(TILE)[None]).astype(np.float32)
    rev = jnp.dot(
        jnp.pad(table_full.T, ((0, 16 - head_count), (0, 0))),
        jnp.asarray(hot[:, :bucket_count].T, low),
        preferred_element_type=single,
    )
    resid_in = tokens.astype(single)

    def scaled(values):
        return values * lax.rsqrt(jnp.mean(values * values, axis=-1, keepdims=True) + norm_epsilon)

    every_tok = jnp.concatenate(
        [prompt_tok.reshape(prompt_len, model_width), near_tok, tokens[PR_DEV:]]
    ).astype(single)
    normed_all = (scaled(every_tok) * gain_attn).astype(low)
    normed_own, norm_pull_in = jax.vjp(norm_apply, resid_in, gain_attn)
    normed_own = normed_own.astype(low)
    queries = jnp.dot(normed_own, query_full, preferred_element_type=single).astype(low)
    keys = jnp.dot(normed_all, key_full, preferred_element_type=single).astype(low)
    values = jnp.dot(normed_all, value_full, preferred_element_type=single).astype(low)
    attended, lse = attn_forward(rev, queries, keys, values)
    attn_low = attended.astype(low)
    resid_mid = resid_in + jnp.dot(attn_low, output_full, preferred_element_type=single)
    normed_mid, norm_pull_mid = jax.vjp(norm_apply, resid_mid, gain_moe)
    mid_low = normed_mid.astype(low)
    router_probs = jax.nn.softmax(
        jnp.dot(mid_low, router_full, preferred_element_type=single), axis=-1
    )
    route_match = routes[:, None] == jnp.arange(expert_count, dtype=jnp.int32)[None, :]
    gate_value = jnp.sum(jnp.where(route_match, router_probs, 0.0), axis=-1)
    dispatch = routes * capacity + slot_ids
    slots = jnp.arange(expert_count * capacity, dtype=jnp.int32)
    place = (slots[:, None] == dispatch[None, :]).astype(low)

    def to_experts(rows):
        buffer = jnp.dot(place, rows, preferred_element_type=single).astype(low)
        return lax.all_to_all(
            buffer.reshape(expert_count, capacity, model_width),
            "shard", split_axis=0, concat_axis=0, tiled=True,
        ).reshape(-1, model_width)

    def from_experts(rows):
        back = lax.all_to_all(
            rows.reshape(expert_count, capacity, model_width),
            "shard", split_axis=0, concat_axis=0, tiled=True,
        ).reshape(-1, model_width)
        return lax.dot_general(place, back, (((0,), (0,)), ((), ())), preferred_element_type=single)

    grad_final = cotangent.astype(single)
    rows_in = to_experts(mid_low)
    grad_rows = to_experts((gate_value[:, None] * grad_final).astype(low))
    pre_act = jnp.dot(rows_in, w_in[0], preferred_element_type=single)
    hidden_single, gelu_pull = jax.vjp(gelu_tanh, pre_act)
    hidden = hidden_single.astype(low)
    expert_single = from_experts(
        jnp.dot(hidden, w_out[0], preferred_element_type=single).astype(low)
    )
    mixed = (resid_mid + gate_value[:, None] * expert_single).astype(low)
    grad_gate = jnp.sum(grad_final * expert_single, axis=-1)
    grad_hidden = jnp.einsum("sd,fd->sf", grad_rows, w_out[0], preferred_element_type=single)
    grad_pre = gelu_pull(grad_hidden)[0].astype(low)
    grad_slot = from_experts(
        jnp.einsum("sf,df->sd", grad_pre, w_in[0], preferred_element_type=single).astype(low)
    )
    grad_w_out = jnp.einsum("sf,sd->fd", hidden, grad_rows, preferred_element_type=single)
    grad_w_in = jnp.einsum("sd,sf->df", rows_in, grad_pre, preferred_element_type=single)
    grad_w_in, grad_w_out = grad_w_in[None].astype(low), grad_w_out[None].astype(low)

    grad_logits = (gate_value * grad_gate)[:, None] * (route_match.astype(single) - router_probs)
    grad_router = jnp.dot(
        mid_low.astype(single).T, grad_logits, precision=lax.Precision.HIGHEST
    )
    grad_mid = grad_slot + jnp.dot(
        grad_logits, router_full.astype(single).T, precision=lax.Precision.HIGHEST
    )
    grad_resid_part, grad_gain_moe = norm_pull_mid(grad_mid)
    grad_resid = grad_final + grad_resid_part
    grad_attn = grad_resid.astype(low)
    grad_heads = jnp.einsum(
        "te,de->td", grad_attn, output_full, preferred_element_type=single
    ).astype(low)
    grad_heads, grad_w_in, grad_w_out = lax.optimization_barrier((grad_heads, grad_w_in, grad_w_out))
    expert_in_grad = lax.psum_scatter(grad_w_in, "rep", scatter_dimension=1, tiled=True).astype(single)
    expert_out_grad = lax.psum_scatter(grad_w_out, "rep", scatter_dimension=1, tiled=True).astype(single)
    grad_queries, grad_keys, grad_values, grad_table = attn_backward(
        rev, jnp.asarray(hot), queries, keys, values, grad_heads, attended, lse
    )
    outer = lambda left, right: jnp.einsum("td,te->de", left, right, preferred_element_type=single)
    back = lambda left, right: jnp.einsum("te,de->td", left, right, preferred_element_type=single)
    grad_all = back(grad_keys, key_full) + back(grad_values, value_full)
    grad_own = back(grad_queries, query_full)
    grad_gain_attn = jnp.sum(grad_all * scaled(every_tok), axis=0) + jnp.sum(
        grad_own * scaled(resid_in), axis=0
    )
    table_small = jnp.pad(
        grad_table[:head_count, :bucket_count].T.reshape(shard_count, table_rows, head_count),
        ((0, 0), (0, weight_rows - table_rows), (0, 0)),
    ).reshape(model_width, head_count)
    small_grads = jnp.concatenate(
        [grad_router, grad_gain_attn[:, None], grad_gain_moe[:, None], table_small], axis=1
    )
    small_grads = jnp.pad(small_grads, ((0, 0), (0, TILE - small_grads.shape[1])))
    dense = jnp.concatenate(
        [
            outer(normed_own, grad_queries), outer(normed_all, grad_keys),
            outer(normed_all, grad_values), outer(attn_low, grad_attn), small_grads,
        ],
        axis=1,
    ).astype(low)
    chips = shard_count // 2
    dense, prompt_sum, near_grad = reduce_all(
        dense.reshape(chips, 2, QUARTERS, weight_rows // QUARTERS, -1),
        grad_all[:prompt_len].astype(low).reshape(chips, 2, PR_DEV, model_width),
        grad_all[prompt_len : prompt_len + cont_rows].astype(low),
    )
    grad_normed = grad_own + jnp.concatenate(
        [prompt_sum, grad_all[prompt_len + cont_rows :] + near_grad.astype(single)]
    )
    grad_tokens = grad_resid + norm_pull_in(grad_normed)[0]
    dense = dense.reshape(weight_rows, -1)
    parts = [dense[:, i * model_width : (i + 1) * model_width] for i in range(4)]
    tail = dense[:, 4 * model_width :]
    return (
        mixed,
        grad_tokens,
        *parts,
        tail[:, :expert_count],
        tail[:, expert_count],
        tail[:, expert_count + 1],
        tail[:table_rows, expert_count + 2 : expert_count + 2 + head_count],
        expert_in_grad,
        expert_out_grad,
    )


def solution(mesh):
    return jax.shard_map(
        local,
        mesh=mesh,
        in_specs=(
            P(("rep", "shard"), None),
            P(("rep", "shard")),
            P(("rep", "shard")),
            P("shard", None),
            P("shard", None),
            P("shard", None),
            P("shard", None),
            P("shard", None),
            P("shard"),
            P("shard"),
            P("shard", None),
            P("shard", None, None),
            P("shard", None, None),
            P(("rep", "shard"), None),
        ),
        out_specs=(
            P(("rep", "shard"), None),
            P(("rep", "shard"), None),
            P("shard", None),
            P("shard", None),
            P("shard", None),
            P("shard", None),
            P("shard", None),
            P("shard"),
            P("shard"),
            P("shard", None),
            P("shard", "rep", None),
            P("shard", "rep", None),
        ),
        check_vma=False,
    )
```

```python
import jax
import jax.numpy as jnp
import numpy as np
from jax import lax
from jax.experimental import pallas as pl
from jax.experimental.pallas import tpu as pltpu
from jax.sharding import PartitionSpec as P

PR_DEV = 128
TILE = 128
SPAN = 2 * TILE
QUARTERS = 4
far_before, far_after, causal_tile, hidden_tile, tile_kinds = 3, 4, 5, 6, 7
vmem_cap = 60 * 1024 * 1024
mesh_ids = pl.DeviceIdType.MESH
bucket_edges = (12, 16, 23, 32, 46, 64, 91)
norm_epsilon = 1e-06
masked_score = -1e30
low, single = jnp.bfloat16, jnp.float32
in_vmem = pl.BlockSpec(memory_space=pltpu.VMEM)
anywhere = pl.BlockSpec(memory_space=pl.ANY)


def inverse_rms(values):
    return lax.rsqrt(jnp.mean(values * values, axis=-1, keepdims=True) + norm_epsilon)


def norm_pull(grad, values, gain):
    scale = inverse_rms(values)
    pulled = grad * gain
    mean = jnp.mean(pulled * values, axis=-1, keepdims=True)
    return scale * pulled - values * (scale * scale * scale * mean)


def nt(left, right):
    return lax.dot_general(left, right, (((1,), (1,)), ((), ())), preferred_element_type=single)


def tn(left, right):
    return lax.dot_general(left, right, (((0,), (0,)), ((), ())), preferred_element_type=single)


def nn(left, right):
    return jnp.dot(left, right, preferred_element_type=single)


def thirds_of(values):
    first = values.astype(low)
    rest = values - first.astype(single)
    second = rest.astype(low)
    return first, second, (rest - second.astype(single)).astype(low)


def fill_tiles(tiles_ref, rev_row, low, high):
    spread = jnp.broadcast_to(rev_row, (TILE, 4 * TILE))
    rolled = pltpu.roll(spread, 0, 1, stride=1, stride_axis=0)
    keys = lax.broadcasted_iota(jnp.int32, (TILE, TILE), 0)
    rows = lax.broadcasted_iota(jnp.int32, (TILE, TILE), 1)
    tiles_ref[0] = rolled[:, TILE : 2 * TILE]
    tiles_ref[1] = rolled[:, :TILE]
    tiles_ref[2] = rolled[:, 3 * TILE :]
    tiles_ref[far_before] = jnp.broadcast_to(low, (TILE, TILE))
    tiles_ref[far_after] = jnp.broadcast_to(high, (TILE, TILE))
    tiles_ref[causal_tile] = jnp.where(keys <= rows, rolled[:, :TILE], masked_score)
    tiles_ref[hidden_tile] = jnp.full((TILE, TILE), masked_score, jnp.float32)


def prompt_tile(block, chunk, shard_id, block_count):
    if chunk == 0:
        gap = block - shard_id
        far = jnp.where(gap < 0, far_before, far_after)
        return jnp.where(jnp.abs(gap) <= 1, gap + 1, far)
    if chunk == 1 and block == block_count - 1:
        return jnp.where(shard_id % 2 == 0, 0, far_before)
    return far_before


def local_tile(block, chunk, shard_id):
    if block >= 2:
        return ((causal_tile, 0), (hidden_tile, causal_tile))[block - 2][chunk]
    kind = 0 if (block, chunk) == (1, 0) else far_before
    return jnp.where(shard_id % 2 == 1, kind, hidden_tile)


def prompt_grid(part, shard_id, block_count):
    return [
        [prompt_tile(2 * part + half, chunk, shard_id, block_count) for chunk in range(3)]
        for half in range(2)
    ]


def local_grid(part, shard_id):
    return [[local_tile(2 * part + half, chunk, shard_id) for chunk in range(2)] for half in range(2)]


def with_bias(scores, tiles_ref, grid):
    return jnp.concatenate(
        [
            jnp.concatenate(
                [
                    scores[i * TILE : (i + 1) * TILE, j * TILE : (j + 1) * TILE] + tiles_ref[kind]
                    for j, kind in enumerate(row)
                ],
                axis=1,
            )
            for i, row in enumerate(grid)
        ],
        axis=0,
    )


def fold8(values):
    return values.reshape(values.shape[0] // 8, 8, values.shape[1])


def head_mask(rows, side):
    lanes = lax.broadcasted_iota(jnp.int32, (rows, TILE), 1)
    return (lanes < TILE // 2) if side == 0 else (lanes >= TILE // 2)


def distance_buckets(bucket_count):
    steps = np.arange(4 * TILE)
    gap = -np.where(steps < 2 * TILE, steps, steps - 4 * TILE)
    size = np.abs(gap)
    far = sum((size >= edge).astype(np.int64) for edge in bucket_edges)
    exact = bucket_count // 4
    return np.where(gap > 0, bucket_count // 2, 0) + np.where(size < exact, size, exact + far)


def front_kernel(
    every_ref, tok_ref, w_ref, small_ref, bucket_ref, route_ref, row_ref, cot_ref,
    n_ref, q_ref, k_ref, v_ref, o_ref, lse_ref, rev_ref, mid_ref, gate_ref, gain_ref, x_ref, gin_ref,
    tiles, vt, sp, sl, ot, gbuf, gs, gr, loc,
):
    shard_id = lax.axis_index("shard")
    shards = lax.axis_size("shard")
    rows, width = tok_ref.shape
    experts = shards
    blocks = every_ref.shape[0] // TILE - 4
    half = TILE // 2
    heads_held = rev_ref.shape[0]

    rep = lax.axis_index("rep")
    others = [(rep, (shard_id + k) % shards) for k in range(1, shards)]
    slots = lax.broadcasted_iota(jnp.int32, (x_ref.shape[0], rows), 0)
    place = (slots == row_ref[0:1, :]).astype(low)
    gbuf[...] = nn(place, cot_ref[...]).astype(low).reshape(gbuf.shape)
    greet(others)
    mine = pltpu.make_async_copy(gbuf.at[shard_id], gin_ref.at[shard_id], loc)
    mine.start()
    sent = [
        send(gbuf.at[device[1]], gin_ref.at[shard_id], (gs.at[k], gr.at[k]), device)
        for k, device in enumerate(others)
    ]
    for copy in sent:
        copy.start()

    small_t = small_ref[...].astype(single).T
    gain_attn = small_t[experts : experts + 1]
    gain_moe = small_t[experts + 1 : experts + 2]
    gain_ref[...] = jnp.concatenate([gain_attn, gain_moe, jnp.zeros((6, width), single)], axis=0)
    shard_rows = width // shards
    table_rows = 2 * TILE // 8 // shards
    owner = lax.broadcasted_iota(jnp.int32, (shards, shard_rows, 4 * TILE), 0)
    offset = lax.broadcasted_iota(jnp.int32, (shards, shard_rows, 4 * TILE), 1)
    held = jnp.where(offset < table_rows, owner * table_rows + offset, -1).reshape(width, 4 * TILE)
    hot = (held == bucket_ref[0:1, :]).astype(low)
    table_t = small_t[experts + 2 : experts + 2 + heads_held].astype(low)
    rev_ref[...] = nn(table_t, hot)

    @pl.loop(0, every_ref.shape[0] // SPAN)
    def project(part):
        span = pl.ds(pl.multiple_of(part * SPAN, SPAN), SPAN)
        values = every_ref[span, :].astype(single)
        normed = (values * inverse_rms(values) * gain_attn).astype(low)
        n_ref[span, :] = normed
        k_ref[span, :] = nn(normed, w_ref[1]).astype(low)
        v_ref[span, :] = nn(normed, w_ref[2]).astype(low)

    own = pl.ds(pl.multiple_of(shard_id * TILE, TILE), TILE)
    normed = jnp.concatenate([n_ref[own, :], n_ref[(blocks + 2) * TILE :, :]], axis=0)
    q_ref[...] = (nn(normed, w_ref[0]).astype(low) * jnp.asarray(0.125, low)).astype(low)

    @pl.loop(0, width // TILE)
    def pair_loop(pair):
        cols = pl.ds(pl.multiple_of(pair * TILE, TILE), TILE)
        vt[...] = v_ref[:, cols].T
        q_pair = q_ref[:, cols]
        for side in range(2):
            head = pair * 2 + side
            rev_row = rev_ref[pl.ds(head, 1), :]
            fill_tiles(tiles, rev_row, rev_row[:, SPAN - 1 : SPAN], rev_row[:, SPAN : SPAN + 1])
            q_head = jnp.where(head_mask(rows, side), q_pair, jnp.zeros_like(q_pair))
            top = jnp.full((8, rows), masked_score, single)
            for part in range(blocks // 2):
                keys = slice(part * SPAN, (part + 1) * SPAN)
                scores = with_bias(nt(k_ref[keys, cols], q_head), tiles, prompt_grid(part, shard_id, blocks))
                sp[keys, :] = scores
                top = jnp.maximum(top, jnp.max(fold8(scores), axis=0))
            top_local = top[:, PR_DEV:]
            for part in range(2):
                keys = slice(part * SPAN, (part + 1) * SPAN)
                held = slice((blocks // 2 + part) * SPAN, (blocks // 2 + part + 1) * SPAN)
                scores = with_bias(nt(k_ref[held, cols], q_head[PR_DEV:]), tiles, local_grid(part, shard_id))
                sl[keys, :] = scores
                top_local = jnp.maximum(top_local, jnp.max(fold8(scores), axis=0))
            top = jnp.max(jnp.concatenate([top[:, :PR_DEV], top_local], axis=1), axis=0, keepdims=True)
            total = jnp.zeros((8, rows), single)
            summed = jnp.zeros((half, rows), single)
            heads = slice(side * half, (side + 1) * half)
            for part in range(blocks // 2):
                keys = slice(part * SPAN, (part + 1) * SPAN)
                weights = jnp.exp(sp[keys, :] - top)
                total = total + jnp.sum(fold8(weights), axis=0)
                summed = summed + nn(vt[heads, keys], weights.astype(low))
            top_c = top[:, PR_DEV:]
            total_c = total[:, PR_DEV:]
            summed_c = summed[:, PR_DEV:]
            for part in range(2):
                keys = slice(part * SPAN, (part + 1) * SPAN)
                held = slice((blocks // 2 + part) * SPAN, (blocks // 2 + part + 1) * SPAN)
                weights = jnp.exp(sl[keys, :] - top_c)
                total_c = total_c + jnp.sum(fold8(weights), axis=0)
                summed_c = summed_c + nn(vt[heads, held], weights.astype(low))
            total = jnp.sum(jnp.concatenate([total[:, :PR_DEV], total_c], axis=1), axis=0, keepdims=True)
            summed = jnp.concatenate([summed[:, :PR_DEV], summed_c], axis=1)
            ot[heads, :] = summed / total
            lse_ref[pl.ds(head, 1), :] = top + jnp.log(total)
        o_ref[:, cols] = ot[...].T

    resid_mid = tok_ref[...].astype(single) + nn(o_ref[...].astype(low), w_ref[3])
    mid_ref[...] = resid_mid
    mid_low = (resid_mid * inverse_rms(resid_mid) * gain_moe).astype(low)
    probs = router_softmax(mid_low, small_ref[...], experts)
    lanes = lax.broadcasted_iota(jnp.int32, probs.shape, 1)
    gate = jnp.sum(jnp.where(lanes == route_ref[...], probs, 0.0), axis=1, keepdims=True)
    gate_ref[...] = jnp.broadcast_to(gate, gate_ref.shape)
    x_ref[...] = nn(place, mid_low).astype(low)
    mine.wait()
    for k in range(shards - 1):
        piece = gin_ref.at[(shard_id + shards - k - 1) % shards]
        send(piece, piece, (gs.at[k], gr.at[k]), others[0]).wait_recv()
    for copy in sent:
        copy.wait_send()


def router_softmax(rows_low, small, experts):
    logits = nn(rows_low, small)
    lanes = lax.broadcasted_iota(jnp.int32, logits.shape, 1)
    logits = jnp.where(lanes < experts, logits, masked_score)
    powers = jnp.exp(logits - jnp.max(logits, axis=1, keepdims=True))
    return powers / jnp.sum(powers, axis=1, keepdims=True)


def front(every_tok, tokens, weights, small, bucket_row, route_col, row_slots, cotangent, slot_count):
    rows, width = tokens.shape
    keys = every_tok.shape[0]
    shards = lax.axis_size("shard")
    shape = jax.ShapeDtypeStruct
    return pl.pallas_call(
        front_kernel,
        out_shape=(
            shape((keys, width), low), shape((rows, width), low), shape((keys, width), low),
            shape((keys, width), low), shape((rows, width), single), shape((16, rows), single),
            shape((16, 4 * TILE), single), shape((rows, width), single), shape((rows, TILE), single),
            shape((8, width), single), shape((slot_count, width), low),
            shape((shards, slot_count // shards, width), low),
        ),
        in_specs=[in_vmem] * 8,
        out_specs=(in_vmem,) * 11 + (anywhere,),
        scratch_shapes=[
            pltpu.VMEM((tile_kinds, TILE, TILE), single),
            pltpu.VMEM((TILE, keys), low),
            pltpu.VMEM((keys - 2 * SPAN, rows), single),
            pltpu.VMEM((2 * SPAN, rows - TILE), single),
            pltpu.VMEM((TILE, rows), single),
            pltpu.VMEM((shards, slot_count // shards, width), low),
            pltpu.SemaphoreType.DMA((shards - 1,)), pltpu.SemaphoreType.DMA((shards - 1,)), pltpu.SemaphoreType.DMA,
        ],
        compiler_params=pltpu.CompilerParams(collective_id=2, has_side_effects=True, vmem_limit_bytes=vmem_cap),
        cost_estimate=pl.CostEstimate(flops=30_000_000_000, bytes_accessed=20_000_000, transcendentals=8_000_000),
        name="front",
    )(every_tok, tokens, weights, small, bucket_row, route_col, row_slots, cotangent)


def moe_kernel(
    x_ref, g_ref, small_ref, w_in_ref, w_out_ref,
    back_ref, out_ref, gwin_ref, gwout_ref, rg_ref,
    w_in, w_out, xin, gm, gg, hid, gpre, acc, gacc, logit_grads, x_t, gwin, gwout,
    xs, xr, ms, mr, ws, ls, os_in, os_out,
):
    rep, chip, core, chips, quarter = places()
    experts = chips * 2
    here = chip * 2 + core
    pair_rows = acc.shape[0]
    cap = pair_rows // 2
    hidden = w_in_ref.shape[1]
    block = 512
    loads = [
        pltpu.make_async_copy(w_in_ref, w_in, ws.at[0]),
        pltpu.make_async_copy(w_out_ref, w_out, ws.at[1]),
    ]
    for copy in loads:
        copy.start()
    twin = (rep, chip * 2 + 1 - core)
    targets = [
        (k, side, (rep, (chip + k) % chips * 2 + side)) for k in range(1, chips) for side in range(2)
    ]
    greet([twin] + [device for _, _, device in targets])
    sent = [send(x_ref.at[chip, 1 - core], xin.at[chip, core], (xs.at[0, 0], xr.at[0, core]), twin)]
    for k, side, device in targets:
        sent.append(
            send(x_ref.at[(chip + k) % chips, side], xin.at[chip, core], (xs.at[k, side], xr.at[k, core]), device)
        )
    for copy in sent:
        copy.start()
    xin[chip, core] = x_ref[chip, core]
    for copy in loads:
        copy.wait()

    def arrived(k, source, side):
        piece = xin.at[source, side]
        send(piece, piece, (xs.at[0, 0], xr.at[k, side]), twin).wait_recv()

    @pl.loop(0, chips)
    def chunk(k):
        source = (chip + chips - k) % chips

        @pl.when(k == 0)
        def _():
            arrived(0, chip, 1 - core)

        @pl.when(k > 0)
        def _():
            for side in range(2):
                arrived(k, source, side)

        rows = xin[source].reshape(pair_rows, xin.shape[3])
        grads = g_ref[source].reshape(pair_rows, xin.shape[3])
        probs = router_softmax(rows, small_ref[...], experts)
        lanes = lax.broadcasted_iota(jnp.int32, probs.shape, 1)
        gate = jnp.sum(jnp.where(lanes == here, probs, 0.0), axis=1, keepdims=True)
        gated = (gate * grads.astype(single)).astype(low)
        span = pl.ds(pl.multiple_of(source * pair_rows, pair_rows), pair_rows)
        gg[span, :] = gated
        acc[...] = jnp.zeros_like(acc)
        gacc[...] = jnp.zeros_like(gacc)

        @pl.loop(0, hidden // block)
        def strip(part):
            cols = pl.ds(pl.multiple_of(part * block, block), block)
            pre = nn(rows, w_in[:, cols])
            grad_hidden = nt(gated, w_out[cols, :])
            square = pre * pre
            wave = jnp.tanh(0.7978845608028654 * pre * (1.0 + 0.044715 * square))
            left = 0.5 + 0.5 * wave
            active = (pre * left).astype(low)
            slope = left + (0.5 * pre) * (1.0 - wave * wave) * (
                0.7978845608028654 + 0.10703222440890037 * square
            )
            grad_pre = (grad_hidden * slope).astype(low)
            hid[span, cols] = active
            gpre[span, cols] = grad_pre
            acc[...] += nn(active, w_out[cols, :])
            gacc[...] += nt(grad_pre, w_in[:, cols])

        out = acc[...].astype(low)
        out_ref[source] = out.reshape(out_ref.shape[1:])
        grad_gate = jnp.sum(grads.astype(single) * out.astype(single), axis=1, keepdims=True)
        chosen = jnp.where(lanes == here, 1.0, 0.0)
        grad_logits = jnp.where(lanes < experts, gate * grad_gate * (chosen - probs), 0.0)
        logit_grads[span, :] = grad_logits
        router = small_ref[...]
        total = gacc[...] + sum(nt(part, router) for part in thirds_of(grad_logits))
        gm[source] = total.astype(low).reshape(gm.shape[1:])

        def reply(side, slot):
            return send(
                gm.at[source, side], back_ref.at[chip, core], (ms.at[k, slot], mr.at[k, core]), (rep, source * 2 + side)
            )

        @pl.when(k == 0)
        def _():
            reply(1 - core, 0).start()
            pltpu.make_async_copy(gm.at[chip, core], back_ref.at[chip, core], ls).start()

        @pl.when(k > 0)
        def _():
            for side in range(2):
                reply(side, side).start()

    every = xin[...].reshape(gg.shape)
    x_t[...] = every.T
    writes = []
    for part in range(hidden // block):
        cols = slice(part * block, (part + 1) * block)
        gwin[:, cols] = nn(x_t[...], gpre[:, cols]).astype(low)
        writes.append(pltpu.make_async_copy(gwin.at[:, cols], gwin_ref.at[:, cols], os_in.at[part]))
        writes[-1].start()
        gwout[cols, :] = tn(hid[:, cols], gg[...]).astype(low)
        writes.append(pltpu.make_async_copy(gwout.at[cols], gwout_ref.at[cols], os_out.at[part]))
        writes[-1].start()
    rg_ref[...] = sum(nn(x_t[...], part) for part in thirds_of(logit_grads[...]))
    pltpu.make_async_copy(gm.at[chip, core], back_ref.at[chip, core], ls).wait()

    def replied(k, source, side):
        piece = back_ref.at[source, side]
        send(piece, piece, (ms.at[0, 0], mr.at[k, side]), twin).wait_recv()

    replied(0, chip, 1 - core)
    for k in range(1, chips):
        for side in range(2):
            replied(k, (chip + k) % chips, side)
    for copy in sent:
        copy.wait_send()
    for copy in writes:
        copy.wait()
    send(gm.at[chip, 0], back_ref.at[chip, core], (ms.at[0, 0], mr.at[0, 0]), twin).wait_send()
    for k in range(1, chips):
        for side in range(2):
            send(gm.at[chip, 0], back_ref.at[chip, core], (ms.at[k, side], mr.at[0, 0]), twin).wait_send()


def moe(rows_out, grad_in, small, w_in, w_out):
    chips, _, cap, width = rows_out.shape
    slots = chips * 2 * cap
    hidden = w_in.shape[1]
    shape = jax.ShapeDtypeStruct
    pairs = pltpu.SemaphoreType.DMA
    strips = hidden // 512
    return pl.pallas_call(
        moe_kernel,
        out_shape=(
            shape(rows_out.shape, low), shape(rows_out.shape, low), shape((width, hidden), low),
            shape((hidden, width), low), shape((width, TILE), single),
        ),
        in_specs=[in_vmem] * 3 + [anywhere] * 2,
        out_specs=(anywhere, in_vmem, anywhere, anywhere, in_vmem),
        scratch_shapes=[
            pltpu.VMEM((width, hidden), low), pltpu.VMEM((hidden, width), low),
            pltpu.VMEM(rows_out.shape, low), pltpu.VMEM(rows_out.shape, low), pltpu.VMEM((slots, width), low),
            pltpu.VMEM((slots, hidden), low), pltpu.VMEM((slots, hidden), low),
            pltpu.VMEM((2 * cap, width), single), pltpu.VMEM((2 * cap, width), single), pltpu.VMEM((slots, TILE), single),
            pltpu.VMEM((width, slots), low), pltpu.VMEM((width, hidden), low), pltpu.VMEM((hidden, width), low),
            pairs((chips, 2)), pairs((chips, 2)), pairs((chips, 2)), pairs((chips, 2)), pairs((2,)), pairs,
            pairs((strips,)), pairs((strips,)),
        ],
        compiler_params=pltpu.CompilerParams(collective_id=3, has_side_effects=True, vmem_limit_bytes=vmem_cap),
        cost_estimate=pl.CostEstimate(flops=40_000_000_000, bytes_accessed=40_000_000, transcendentals=3_000_000),
        name="moe",
    )(rows_out, grad_in, small, w_in, w_out)


def back_kernel(
    back_ref, col_ref, mid_ref, cot_ref, gain_ref, every_ref, w_ref, n_ref, q_ref, k_ref, v_ref, o_ref,
    lse_ref, rev_ref, bucket_ref, rg_ref,
    dense_ref, p_ref, e_ref, own_ref, gres_ref,
    tiles, sums, diag, kt, dqt, far_sums, dk_sum, dv_sum, g_ref, dq_ref, dk_ref, dv_ref, attn_gain,
):
    shard_id = lax.axis_index("shard")
    shards = lax.axis_size("shard")
    rows, width = mid_ref.shape
    blocks = k_ref.shape[0] // TILE - 4
    half = TILE // 2
    experts = shards
    heads_held = rev_ref.shape[0]
    diag[...] = jnp.zeros_like(diag)
    far_sums[...] = jnp.zeros_like(far_sums)
    tile_rows = lax.broadcasted_iota(jnp.int32, (TILE, TILE), 0)
    tile_cols = lax.broadcasted_iota(jnp.int32, (TILE, TILE), 1)
    flip = (tile_rows + tile_cols == TILE - 1).astype(single)

    slots = lax.broadcasted_iota(jnp.int32, (rows, back_ref.shape[0]), 1)
    grad_mid = nn((slots == col_ref[...]).astype(low), back_ref[...])
    resid_mid = mid_ref[...]
    grad_gain_moe = jnp.sum(grad_mid * resid_mid * inverse_rms(resid_mid), axis=0, keepdims=True)
    grad_resid = cot_ref[...].astype(single) + norm_pull(grad_mid, resid_mid, gain_ref[1:2, :])
    gres_ref[...] = grad_resid
    grad_attn = grad_resid.astype(low)
    g_ref[...] = nt(grad_attn, w_ref[3]).astype(low)
    dense_ref[:, 3 * width : 4 * width] = tn(o_ref[...].astype(low), grad_attn).astype(low)

    @pl.loop(0, width // TILE)
    def pair_loop(pair):
        cols = pl.ds(pl.multiple_of(pair * TILE, TILE), TILE)
        kt[...] = k_ref[:, cols].T
        q_pair = q_ref[:, cols]
        g_pair = g_ref[:, cols]
        delta_t = (g_pair.astype(single) * o_ref[:, cols]).T
        for side in range(2):
            head = pair * 2 + side
            heads = slice(side * half, (side + 1) * half)
            rev_row = rev_ref[pl.ds(head, 1), :]
            fill_tiles(tiles, rev_row, rev_row[:, SPAN - 1 : SPAN], rev_row[:, SPAN : SPAN + 1])
            sums[...] = jnp.zeros_like(sums)
            mask = head_mask(rows, side)
            q_head = jnp.where(mask, q_pair, jnp.zeros_like(q_pair))
            g_head = jnp.where(mask, g_pair, jnp.zeros_like(g_pair))
            delta = jnp.sum(delta_t[heads, :], axis=0, keepdims=True)
            log_total = lse_ref[pl.ds(head, 1), :]

            def block_grads(part, first, grid):
                keys = slice(part * SPAN, (part + 1) * SPAN)
                q_rows, g_rows = q_head[first:], g_head[first:]
                scores = with_bias(nt(k_ref[keys, cols], q_rows), tiles, grid)
                weights = jnp.exp(scores - log_total[:, first:])
                grad_weights = nt(v_ref[keys, cols], g_rows)
                grad_scores = weights * (grad_weights - delta[:, first:])
                for i, row in enumerate(grid):
                    for j, kind in enumerate(row):
                        sums[kind] += grad_scores[i * TILE : (i + 1) * TILE, j * TILE : (j + 1) * TILE]
                raw = grad_scores.astype(low)
                dk = nn(raw, q_rows)
                dv = nn(weights.astype(low), g_rows)
                if side == 0:
                    dk_sum[keys, :] = dk
                    dv_sum[keys, :] = dv
                else:
                    dk_ref[keys, cols] = (dk_sum[keys, :] + dk).astype(low)
                    dv_ref[keys, cols] = (dv_sum[keys, :] + dv).astype(low)
                return nn(kt[heads, keys], raw)

            dq = jnp.zeros((half, rows), single)
            for part in range(blocks // 2):
                dq = dq + block_grads(part, 0, prompt_grid(part, shard_id, blocks))
            dq_c = dq[:, PR_DEV:]
            for part in range(2):
                dq_c = dq_c + block_grads(blocks // 2 + part, PR_DEV, local_grid(part, shard_id))
            dqt[heads, :] = jnp.concatenate([dq[:, :PR_DEV], dq_c], axis=1)
            near = jnp.concatenate(
                [sums[1] + sums[causal_tile], sums[0], jnp.zeros((TILE, TILE), single), sums[2]], axis=1
            )
            flipped = jnp.dot(flip, near, precision=lax.Precision.HIGHEST, preferred_element_type=single)
            rolled = pltpu.roll(flipped, 3 * TILE + 1, 1, stride=1, stride_axis=0)
            diag[pl.ds(head, 1), :] = jnp.sum(rolled, axis=0, keepdims=True)
            far_sums[pl.ds(head, 1), :] = jnp.concatenate(
                [jnp.sum(sums[far_before], axis=0, keepdims=True), jnp.sum(sums[far_after], axis=0, keepdims=True)],
                axis=1,
            )
        dq_ref[:, cols] = (dqt[...].T * 0.125).astype(low)

    lanes = lax.broadcasted_iota(jnp.int32, (heads_held, 4 * TILE), 1)
    before = jnp.sum(far_sums[:, :TILE], axis=1, keepdims=True)
    after = jnp.sum(far_sums[:, TILE:], axis=1, keepdims=True)
    by_gap = diag[...] + jnp.where(lanes == SPAN - 1, before, 0.0) + jnp.where(lanes == SPAN, after, 0.0)
    shard_rows = width // shards
    table_rows = 2 * TILE // 8 // shards
    owner = lax.broadcasted_iota(jnp.int32, (shards, shard_rows, 4 * TILE), 0)
    offset = lax.broadcasted_iota(jnp.int32, (shards, shard_rows, 4 * TILE), 1)
    held = jnp.where(offset < table_rows, owner * table_rows + offset, -1).reshape(width, 4 * TILE)
    hot = (held == bucket_ref[0:1, :]).astype(low)
    grad_table = sum(nt(part, hot) for part in thirds_of(by_gap))

    attn_gain[...] = jnp.zeros_like(attn_gain)
    own = pl.ds(pl.multiple_of(shard_id * TILE, TILE), TILE)
    tail = slice((blocks + 2) * TILE, (blocks + 4) * TILE)
    normed = jnp.concatenate([n_ref[own, :], n_ref[tail, :]], axis=0)
    dense_ref[:, :width] = tn(normed, dq_ref[...]).astype(low)
    grad_own = nt(dq_ref[...], w_ref[0])
    values = jnp.concatenate([every_ref[own, :], every_ref[tail, :]], axis=0).astype(single)
    attn_gain[...] += jnp.sum(fold8(grad_own * (values * inverse_rms(values))), axis=0)
    own_ref[...] = grad_own

    def pull_rows(part):
        span = pl.ds(pl.multiple_of(part * SPAN, SPAN), SPAN)
        values = every_ref[span, :].astype(single)
        grads = nt(dk_ref[span, :], w_ref[1]) + nt(dv_ref[span, :], w_ref[2])
        attn_gain[...] += jnp.sum(fold8(grads * (values * inverse_rms(values))), axis=0)
        return grads

    @pl.loop(0, blocks // 2)
    def pull_prompt(part):
        p_ref[pl.ds(pl.multiple_of(part * SPAN, SPAN), SPAN), :] = pull_rows(part).astype(low)

    e_ref[...] = pull_rows(blocks // 2).astype(low)
    own_ref[PR_DEV:, :] += pull_rows(blocks // 2 + 1)

    @pl.loop(0, width // SPAN)
    def outer(part):
        cols = pl.ds(pl.multiple_of(part * SPAN, SPAN), SPAN)
        k_cols = pl.ds(pl.multiple_of(width + part * SPAN, SPAN), SPAN)
        v_cols = pl.ds(pl.multiple_of(2 * width + part * SPAN, SPAN), SPAN)
        dense_ref[:, k_cols] = tn(n_ref[...], dk_ref[:, cols]).astype(low)
        dense_ref[:, v_cols] = tn(n_ref[...], dv_ref[:, cols]).astype(low)

    small_t = jnp.concatenate(
        [
            jnp.zeros((experts, width), single), jnp.sum(attn_gain[...], axis=0, keepdims=True), grad_gain_moe,
            grad_table, jnp.zeros((TILE - experts - 2 - heads_held, width), single),
        ],
        axis=0,
    )
    dense_ref[:, 4 * width :] = (small_t.T + rg_ref[...]).astype(low)


def back(returned, col_slots, mid, cotangent, gains, every_tok, weights, kept, bucket_row, router_grads):
    rows, width = mid.shape
    normed, queries, keys, values, attended, lse, rev = kept
    count = keys.shape[0]
    shape = jax.ShapeDtypeStruct
    args = (
        returned, col_slots, mid, cotangent, gains, every_tok, weights, normed, queries, keys, values, attended,
        lse, rev, bucket_row, router_grads,
    )
    return pl.pallas_call(
        back_kernel,
        out_shape=(
            shape((width, 4 * width + TILE), low), shape((count - 2 * SPAN, width), low), shape((SPAN, width), low),
            shape((rows, width), single), shape((rows, width), single),
        ),
        in_specs=[in_vmem] * len(args),
        out_specs=(in_vmem,) * 5,
        scratch_shapes=[
            pltpu.VMEM((tile_kinds, TILE, TILE), single), pltpu.VMEM((tile_kinds, TILE, TILE), single),
            pltpu.VMEM((16, 4 * TILE), single), pltpu.VMEM((TILE, count), low), pltpu.VMEM((TILE, rows), single),
            pltpu.VMEM((16, 2 * TILE), single), pltpu.VMEM((count, TILE), single), pltpu.VMEM((count, TILE), single),
            pltpu.VMEM((rows, width), low), pltpu.VMEM((rows, width), low), pltpu.VMEM((count, width), low),
            pltpu.VMEM((count, width), low), pltpu.VMEM((8, width), single),
        ],
        compiler_params=pltpu.CompilerParams(vmem_limit_bytes=vmem_cap),
        cost_estimate=pl.CostEstimate(flops=60_000_000_000, bytes_accessed=40_000_000, transcendentals=8_000_000),
        name="back",
    )(*args)


def places():
    rep, shard = lax.axis_index("rep"), lax.axis_index("shard")
    return rep, shard // 2, shard % 2, lax.axis_size("shard") // 2, rep % QUARTERS


def peer_lists():
    rep, chip, core, chips, quarter = places()
    along = [(rep, (chip + k) % chips * 2 + core) for k in range(1, chips)]
    across = [(rep - quarter + (quarter + j) % QUARTERS, chip * 2 + core) for j in range(1, QUARTERS)]
    twin = (rep, chip * 2 + 1 - core)
    return along, across, twin


def greet(devices):
    barrier = pltpu.get_barrier_semaphore()
    for device in devices:
        pl.semaphore_signal(barrier, inc=1, device_id=device, device_id_type=mesh_ids)
    pl.semaphore_wait(barrier, len(devices))


def send(source, target, sems, device):
    return pltpu.make_async_remote_copy(
        src_ref=source, dst_ref=target, send_sem=sems[0], recv_sem=sems[1],
        device_id=device, device_id_type=mesh_ids,
    )


def gather_kernel(
    w_ref, tok_ref, small_ref, wg_ref, tg_ref, sg_ref,
    wz_s, wz_r, tz_s, tz_r, sz_s, sz_r, wr_s, wr_r, wt_s, wt_r, tt_s, tt_r, et_s, et_r, loc,
):
    rep, chip, core, chips, quarter = places()
    along, across, twin = peer_lists()
    rest_rows = tok_ref.shape[0] - PR_DEV
    prompt_len = chips * 2 * PR_DEV
    prompt = tok_ref.at[pl.ds(0, PR_DEV)]
    rest = tok_ref.at[pl.ds(PR_DEV, rest_rows)]
    near_rows = tg_ref.at[pl.ds(prompt_len, rest_rows)]

    def tok_rows(source, side):
        return tg_ref.at[pl.ds(pl.multiple_of((source * 2 + side) * PR_DEV, PR_DEV), PR_DEV)]

    mine = tok_rows(chip, core)
    own = [
        pltpu.make_async_copy(w_ref, wg_ref.at[:, chip, core], loc.at[0]),
        pltpu.make_async_copy(prompt, mine, loc.at[1]),
        pltpu.make_async_copy(small_ref, sg_ref.at[chip, core], loc.at[2]),
        pltpu.make_async_copy(rest, tg_ref.at[pl.ds(prompt_len + rest_rows, rest_rows)], loc.at[3]),
    ]
    for copy in own:
        copy.start()
    greet(along + across + [twin])
    started = []

    def go(copy):
        copy.start()
        started.append(copy)

    for k, device in enumerate(along):
        go(send(w_ref.at[:, quarter], wg_ref.at[:, chip, core, quarter], (wz_s.at[k], wz_r.at[k]), device))
        go(send(small_ref, sg_ref.at[chip, core], (sz_s.at[k], sz_r.at[k]), device))
    go(send(rest, near_rows, (et_s.at[0], et_r.at[0]), twin))
    go(send(prompt, mine, (tt_s.at[0], tt_r.at[0]), twin))
    go(send(w_ref, wg_ref.at[:, chip, core], (wt_s.at[0], wt_r.at[0]), twin))
    for k in range(1, chips):
        source = (chip + chips - k) % chips
        piece = wg_ref.at[:, source, core, quarter]
        send(piece, piece, (wz_s.at[k - 1], wz_r.at[k - 1]), twin).wait_recv()
        for j, device in enumerate(across):
            go(send(piece, piece, (wr_s.at[k - 1, j], wr_r.at[k - 1, j]), device))
        go(send(prompt, mine, (tz_s.at[k - 1], tz_r.at[k - 1]), along[k - 1]))
    for k in range(1, chips):
        source = (chip + chips - k) % chips
        for j in range(1, QUARTERS):
            piece = wg_ref.at[:, source, core, (quarter + QUARTERS - j) % QUARTERS]
            send(piece, piece, (wr_s.at[k - 1, j - 1], wr_r.at[k - 1, j - 1]), twin).wait_recv()
        row = wg_ref.at[:, source, core]
        go(send(row, row, (wt_s.at[k], wt_r.at[k]), twin))
        theirs = tok_rows(source, core)
        send(theirs, theirs, (tz_s.at[k - 1], tz_r.at[k - 1]), twin).wait_recv()
        go(send(theirs, theirs, (tt_s.at[k], tt_r.at[k]), twin))
        send(small_ref, sg_ref.at[source, core], (sz_s.at[k - 1], sz_r.at[k - 1]), twin).wait_recv()
    for copy in own:
        copy.wait()
    go(send(sg_ref.at[:, core], sg_ref.at[:, core], (et_s.at[1], et_r.at[1]), twin))
    send(rest, near_rows, (et_s.at[0], et_r.at[0]), twin).wait_recv()
    for k in range(chips):
        source = (chip + chips - k) % chips
        row = wg_ref.at[:, source, 1 - core]
        send(row, row, (wt_s.at[k], wt_r.at[k]), twin).wait_recv()
        theirs = tok_rows(source, 1 - core)
        send(theirs, theirs, (tt_s.at[k], tt_r.at[k]), twin).wait_recv()
    send(sg_ref.at[:, core], sg_ref.at[:, 1 - core], (et_s.at[1], et_r.at[1]), twin).wait_recv()
    for copy in started:
        copy.wait_send()


def gather_all(weights, tokens, small):
    chips = lax.axis_size("shard") // 2
    width = tokens.shape[1]
    pairs = pltpu.SemaphoreType.DMA
    count = chips - 1
    return pl.pallas_call(
        gather_kernel,
        out_shape=(
            jax.ShapeDtypeStruct((weights.shape[0], chips, 2) + weights.shape[1:], weights.dtype),
            jax.ShapeDtypeStruct((2 * chips * PR_DEV + 2 * (tokens.shape[0] - PR_DEV), width), tokens.dtype),
            jax.ShapeDtypeStruct((chips, 2) + small.shape, small.dtype),
        ),
        in_specs=[anywhere] * 3,
        out_specs=(anywhere,) * 3,
        scratch_shapes=[
            pairs((count,)), pairs((count,)), pairs((count,)), pairs((count,)), pairs((count,)), pairs((count,)),
            pairs((count, 3)), pairs((count, 3)), pairs((chips,)), pairs((chips,)), pairs((chips,)), pairs((chips,)),
            pairs((2,)), pairs((2,)), pairs((4,)),
        ],
        compiler_params=pltpu.CompilerParams(collective_id=0, has_side_effects=True),
        cost_estimate=pl.CostEstimate(flops=0, bytes_accessed=100_000_000, transcendentals=0),
        name="gather_all",
    )(weights, tokens, small)


def reduce_kernel(
    d_ref, p_ref, e_ref, out_ref, po_ref, eo_ref,
    half, summed, third, thirds, fourth, fourths, last, gathered, p_half, p_sum, p_in,
    ds_s, ds_r, ps_s, ps_r, dr_s, dr_r, dh_s, dh_r, dz_s, dz_r, pz_s, pz_r, da_s, da_r,
):
    rep, chip, core, chips, quarter = places()
    along, across, twin = peer_lists()
    classes = lax.axis_size("rep") // QUARTERS
    above = [
        ((rep // QUARTERS + k) % classes * QUARTERS + quarter, chip * 2 + core) for k in range(1, classes)
    ]
    greet(along + across + above + [twin])
    first = [
        send(p_ref.at[:, 1 - core], p_half, (ps_s.at[0], ps_r.at[0]), twin),
        send(e_ref, eo_ref, (ps_s.at[1], ps_r.at[1]), twin),
    ] + [
        send(d_ref.at[k, 1 - core], half.at[k], (ds_s.at[k], ds_r.at[k]), twin) for k in range(chips)
    ]
    for copy in first:
        copy.start()
    pending = list(first)
    first[0].wait_recv()
    for k in range(chips):
        p_sum[k] = (p_ref[k, core].astype(single) + p_half[k].astype(single)).astype(p_sum.dtype)
    for k, device in enumerate(along):
        copy = send(p_sum.at[(chip + k + 1) % chips], p_in.at[k], (pz_s.at[k], pz_r.at[k]), device)
        copy.start()
        pending.append(copy)
    for k in range(chips):
        first[2 + k].wait_recv()
        for t in range(QUARTERS):
            summed[t, k] = (d_ref[k, core, t].astype(single) + half[k, t].astype(single)).astype(summed.dtype)
    for j, device in enumerate(across):
        copy = send(summed.at[(quarter + j + 1) % QUARTERS], third.at[j], (dr_s.at[j], dr_r.at[j]), device)
        copy.start()
        pending.append(copy)
    for j in range(QUARTERS - 1):
        send(third.at[j], third.at[j], (dr_s.at[j], dr_r.at[j]), twin).wait_recv()
    for k in range(chips):
        total = summed[quarter, k].astype(single)
        for j in range(QUARTERS - 1):
            total = total + third[j, k].astype(single)
        thirds[k] = total.astype(thirds.dtype)
    if classes > 1:
        for j, device in enumerate(above):
            copy = send(thirds, fourth.at[j], (dh_s.at[j], dh_r.at[j]), device)
            copy.start()
            pending.append(copy)
        for j in range(classes - 1):
            send(thirds, fourth.at[j], (dh_s.at[j], dh_r.at[j]), twin).wait_recv()
        for k in range(chips):
            total = thirds[k].astype(single)
            for j in range(classes - 1):
                total = total + fourth[j, k].astype(single)
            fourths[k] = total.astype(fourths.dtype)
    else:
        fourths = thirds
    for k, device in enumerate(along):
        copy = send(fourths.at[(chip + k + 1) % chips], last.at[k], (dz_s.at[k], dz_r.at[k]), device)
        copy.start()
        pending.append(copy)
    for k in range(chips - 1):
        send(p_in.at[k], p_in.at[k], (pz_s.at[k], pz_r.at[k]), twin).wait_recv()
    total = p_sum[chip].astype(single)
    for k in range(chips - 1):
        total = total + p_in[k].astype(single)
    po_ref[...] = total
    for k in range(chips - 1):
        send(last.at[k], last.at[k], (dz_s.at[k], dz_r.at[k]), twin).wait_recv()
    total = fourths[chip].astype(single)
    for k in range(chips - 1):
        total = total + last[k].astype(single)
    gathered[quarter] = total.astype(gathered.dtype)
    for j, device in enumerate(across):
        copy = send(gathered.at[quarter], gathered.at[quarter], (da_s.at[j], da_r.at[j]), device)
        copy.start()
        pending.append(copy)
    for j in range(QUARTERS - 1):
        piece = gathered.at[(quarter + QUARTERS - j - 1) % QUARTERS]
        send(piece, piece, (da_s.at[j], da_r.at[j]), twin).wait_recv()
    out_ref[...] = gathered[...].astype(single)
    first[1].wait_recv()
    for copy in pending:
        copy.wait_send()


def reduce_all(dense, prompt_part, near_part):
    chips = lax.axis_size("shard") // 2
    classes = lax.axis_size("rep") // QUARTERS
    piece = dense.shape[3:]
    pairs = pltpu.SemaphoreType.DMA
    count = chips - 1
    return pl.pallas_call(
        reduce_kernel,
        out_shape=(
            jax.ShapeDtypeStruct((QUARTERS,) + piece, single),
            jax.ShapeDtypeStruct(prompt_part.shape[2:], single),
            jax.ShapeDtypeStruct(near_part.shape, low),
        ),
        in_specs=[in_vmem] * 3,
        out_specs=(in_vmem,) * 3,
        scratch_shapes=[
            pltpu.VMEM((chips, QUARTERS) + piece, low),
            pltpu.VMEM((QUARTERS, chips) + piece, low),
            pltpu.VMEM((QUARTERS - 1, chips) + piece, low),
            pltpu.VMEM((chips,) + piece, low),
            pltpu.VMEM((max(classes - 1, 1), chips if classes > 1 else 1) + piece, low),
            pltpu.VMEM((chips if classes > 1 else 1,) + piece, low),
            pltpu.VMEM((count,) + piece, low),
            pltpu.VMEM((QUARTERS,) + piece, low),
            pltpu.VMEM((chips,) + prompt_part.shape[2:], low),
            pltpu.VMEM((chips,) + prompt_part.shape[2:], low),
            pltpu.VMEM((count,) + prompt_part.shape[2:], low),
            pairs((chips,)), pairs((chips,)), pairs((2,)), pairs((2,)), pairs((3,)), pairs((3,)),
            pairs((max(classes - 1, 1),)), pairs((max(classes - 1, 1),)),
            pairs((count,)), pairs((count,)), pairs((count,)), pairs((count,)), pairs((3,)), pairs((3,)),
        ],
        compiler_params=pltpu.CompilerParams(collective_id=1, has_side_effects=True, vmem_limit_bytes=vmem_cap),
        cost_estimate=pl.CostEstimate(flops=0, bytes_accessed=200_000_000, transcendentals=0),
        name="reduce_all",
    )(dense, prompt_part, near_part)


def local(
    tokens,
    routes,
    slot_ids,
    w_query,
    w_key,
    w_value,
    w_output,
    w_router,
    norm_attn,
    norm_moe,
    rel_table,
    w_in,
    w_out,
    cotangent,
):
    shard_count = lax.axis_size("shard")
    token_rows, model_width = tokens.shape
    prompt_len = PR_DEV * shard_count
    weight_rows, expert_count = w_router.shape
    table_rows, head_count = rel_table.shape
    capacity = 2 * token_rows // expert_count
    slot_count = expert_count * capacity

    weights = jnp.stack([w_query, w_key, w_value, w_output]).reshape(4, QUARTERS, -1, model_width)
    small = jnp.concatenate(
        [w_router, norm_attn[:, None], norm_moe[:, None],
         jnp.pad(rel_table, ((0, weight_rows - table_rows), (0, 0)))], axis=1
    )
    small = jnp.pad(small, ((0, 0), (0, TILE - small.shape[1])))
    dispatch = routes * capacity + slot_ids

    weights, every_tok, small = gather_all(weights, tokens, small)
    weights = weights.reshape(4, model_width, model_width)
    small = small.reshape(model_width, TILE)
    bucket_row = jnp.asarray(np.tile(distance_buckets(table_rows * shard_count), (8, 1)), jnp.int32)
    normed, queries, keys, values, attended, lse, rev, mid, gate, gains, slots_out, grad_in = front(
        every_tok, tokens, weights, small, bucket_row, routes[:, None],
        jnp.broadcast_to(dispatch[None, :], (8, token_rows)), cotangent, slot_count,
    )
    by_chip = (shard_count // 2, 2, capacity, model_width)
    grad_back, result, grad_w_in, grad_w_out, router_grads = moe(
        slots_out.reshape(by_chip), grad_in.reshape(by_chip), small, w_in[0], w_out[0]
    )
    grad_w_in, grad_w_out = grad_w_in[None], grad_w_out[None]
    grad_back = grad_back.reshape(slot_count, model_width)
    returned = lax.all_to_all(
        result.reshape(expert_count, capacity, model_width), "shard", split_axis=0, concat_axis=0, tiled=True
    ).reshape(slot_count, model_width)
    expert_in_grad = lax.psum_scatter(grad_w_in, "rep", scatter_dimension=1, tiled=True).astype(single)
    expert_out_grad = lax.psum_scatter(grad_w_out, "rep", scatter_dimension=1, tiled=True).astype(single)
    dense, prompt_part, near_part, grad_own, grad_resid = back(
        grad_back, dispatch[:, None], mid, cotangent, gains, every_tok, weights,
        (normed, queries, keys, values, attended, lse, rev), bucket_row, router_grads,
    )
    place = (jnp.arange(slot_count, dtype=jnp.int32)[:, None] == dispatch[None, :]).astype(low)
    expert_single = lax.dot_general(
        place, returned, (((0,), (0,)), ((), ())), preferred_element_type=single
    )
    mixed = (mid + gate[:, :1] * expert_single).astype(low)
    chips = shard_count // 2
    dense, prompt_sum, near_grad = reduce_all(
        dense.reshape(chips, 2, QUARTERS, weight_rows // QUARTERS, -1),
        prompt_part.reshape(chips, 2, PR_DEV, model_width), near_part,
    )
    grad_normed = grad_own + jnp.concatenate([prompt_sum, near_grad.astype(single)])
    grad_tokens = grad_resid + norm_pull(grad_normed, tokens.astype(single), gains[0:1])
    dense = dense.reshape(weight_rows, -1)
    parts = [dense[:, i * model_width : (i + 1) * model_width] for i in range(4)]
    tail = dense[:, 4 * model_width :]
    return (
        mixed,
        grad_tokens,
        *parts,
        tail[:, :expert_count],
        tail[:, expert_count],
        tail[:, expert_count + 1],
        tail[:table_rows, expert_count + 2 : expert_count + 2 + head_count],
        expert_in_grad,
        expert_out_grad,
    )


def solution(mesh):
    return jax.shard_map(
        local,
        mesh=mesh,
        in_specs=(
            P(("rep", "shard"), None),
            P(("rep", "shard")),
            P(("rep", "shard")),
            P("shard", None),
            P("shard", None),
            P("shard", None),
            P("shard", None),
            P("shard", None),
            P("shard"),
            P("shard"),
            P("shard", None),
            P("shard", None, None),
            P("shard", None, None),
            P(("rep", "shard"), None),
        ),
        out_specs=(
            P(("rep", "shard"), None),
            P(("rep", "shard"), None),
            P("shard", None),
            P("shard", None),
            P("shard", None),
            P("shard", None),
            P("shard", None),
            P("shard"),
            P("shard"),
            P("shard", None),
            P("shard", "rep", None),
            P("shard", "rep", None),
        ),
        check_vma=False,
    )
```

```python
import jax
import jax.numpy as jnp
import numpy as np
from jax import lax
from jax.experimental import pallas as pl
from jax.experimental.pallas import tpu as pltpu
from jax.sharding import PartitionSpec as P

PR_DEV = 128
TILE = 128
SPAN = 2 * TILE
BLOCK = 1536
QUARTERS = 4
far_before, far_after, causal_tile, hidden_tile, tile_kinds = 3, 4, 5, 6, 7
vmem_cap = 60 * 1024 * 1024
mesh_ids = pl.DeviceIdType.MESH
bucket_edges = (12, 16, 23, 32, 46, 64, 91)
norm_epsilon = 1e-06
masked_score = -1e30
low, single = jnp.bfloat16, jnp.float32
in_vmem = pl.BlockSpec(memory_space=pltpu.VMEM)
anywhere = pl.BlockSpec(memory_space=pl.ANY)


def inverse_rms(values):
    return lax.rsqrt(jnp.mean(values * values, axis=-1, keepdims=True) + norm_epsilon)


def norm_pull(grad, values, gain):
    scale = inverse_rms(values)
    pulled = grad * gain
    mean = jnp.mean(pulled * values, axis=-1, keepdims=True)
    return scale * pulled - values * (scale * scale * scale * mean)


def nt(left, right):
    return lax.dot_general(left, right, (((1,), (1,)), ((), ())), preferred_element_type=single)


def tn(left, right):
    return lax.dot_general(left, right, (((0,), (0,)), ((), ())), preferred_element_type=single)


def nn(left, right):
    return jnp.dot(left, right, preferred_element_type=single)


def thirds_of(values):
    first = values.astype(low)
    rest = values - first.astype(single)
    second = rest.astype(low)
    return first, second, (rest - second.astype(single)).astype(low)


def fill_tiles(tiles_ref, rev_row, low, high):
    spread = jnp.broadcast_to(rev_row, (TILE, 4 * TILE))
    rolled = pltpu.roll(spread, 0, 1, stride=1, stride_axis=0)
    keys = lax.broadcasted_iota(jnp.int32, (TILE, TILE), 0)
    rows = lax.broadcasted_iota(jnp.int32, (TILE, TILE), 1)
    tiles_ref[0] = rolled[:, TILE : 2 * TILE]
    tiles_ref[1] = rolled[:, :TILE]
    tiles_ref[2] = rolled[:, 3 * TILE :]
    tiles_ref[far_before] = jnp.broadcast_to(low, (TILE, TILE))
    tiles_ref[far_after] = jnp.broadcast_to(high, (TILE, TILE))
    tiles_ref[causal_tile] = jnp.where(keys <= rows, rolled[:, :TILE], masked_score)
    tiles_ref[hidden_tile] = jnp.full((TILE, TILE), masked_score, jnp.float32)


def prompt_tile(block, chunk, shard_id, block_count):
    if chunk == 0:
        gap = block - shard_id
        far = jnp.where(gap < 0, far_before, far_after)
        return jnp.where(jnp.abs(gap) <= 1, gap + 1, far)
    if chunk == 1 and block == block_count - 1:
        return jnp.where(shard_id % 2 == 0, 0, far_before)
    return far_before


def local_tile(block, chunk, shard_id):
    if block >= 2:
        return ((causal_tile, 0), (hidden_tile, causal_tile))[block - 2][chunk]
    kind = 0 if (block, chunk) == (1, 0) else far_before
    return jnp.where(shard_id % 2 == 1, kind, hidden_tile)


def prompt_grid(part, shard_id, block_count):
    return [
        [prompt_tile(2 * part + half, chunk, shard_id, block_count) for chunk in range(3)]
        for half in range(2)
    ]


def local_grid(part, shard_id):
    return [[local_tile(2 * part + half, chunk, shard_id) for chunk in range(2)] for half in range(2)]


def with_bias(scores, tiles_ref, grid):
    return jnp.concatenate(
        [
            jnp.concatenate(
                [
                    scores[i * TILE : (i + 1) * TILE, j * TILE : (j + 1) * TILE] + tiles_ref[kind]
                    for j, kind in enumerate(row)
                ],
                axis=1,
            )
            for i, row in enumerate(grid)
        ],
        axis=0,
    )


def fold8(values):
    return values.reshape(values.shape[0] // 8, 8, values.shape[1])


def head_mask(rows, side):
    lanes = lax.broadcasted_iota(jnp.int32, (rows, TILE), 1)
    return (lanes < TILE // 2) if side == 0 else (lanes >= TILE // 2)


def distance_buckets(bucket_count):
    steps = np.arange(4 * TILE)
    gap = -np.where(steps < 2 * TILE, steps, steps - 4 * TILE)
    size = np.abs(gap)
    far = sum((size >= edge).astype(np.int64) for edge in bucket_edges)
    exact = bucket_count // 4
    return np.where(gap > 0, bucket_count // 2, 0) + np.where(size < exact, size, exact + far)


def front_kernel(
    every_ref, tok_ref, w_ref, small_ref, bucket_ref, route_ref, row_ref, cot_ref,
    n_ref, q_ref, k_ref, v_ref, o_ref, lse_ref, rev_ref, mid_ref, gate_ref, gain_ref, x_ref, gin_ref,
    tiles, vt, sp, sl, ot, gbuf, gs, gr, loc,
):
    shard_id = lax.axis_index("shard")
    shards = lax.axis_size("shard")
    rows, width = tok_ref.shape
    experts = shards
    blocks = every_ref.shape[0] // TILE - 4
    half = TILE // 2
    heads_held = rev_ref.shape[0]

    rep = lax.axis_index("rep")
    others = [(rep, (shard_id + k) % shards) for k in range(1, shards)]
    slots = lax.broadcasted_iota(jnp.int32, (x_ref.shape[0], rows), 0)
    place = (slots == row_ref[0:1, :]).astype(low)
    gbuf[...] = nn(place, cot_ref[...]).astype(low).reshape(gbuf.shape)
    greet(others)
    mine = pltpu.make_async_copy(gbuf.at[shard_id], gin_ref.at[shard_id], loc)
    mine.start()
    sent = [
        send(gbuf.at[device[1]], gin_ref.at[shard_id], (gs.at[k], gr.at[k]), device)
        for k, device in enumerate(others)
    ]
    for copy in sent:
        copy.start()

    small_t = small_ref[...].astype(single).T
    gain_attn = small_t[experts : experts + 1]
    gain_moe = small_t[experts + 1 : experts + 2]
    gain_ref[...] = jnp.concatenate([gain_attn, gain_moe, jnp.zeros((6, width), single)], axis=0)
    shard_rows = width // shards
    table_rows = 2 * TILE // 8 // shards
    owner = lax.broadcasted_iota(jnp.int32, (shards, shard_rows, 4 * TILE), 0)
    offset = lax.broadcasted_iota(jnp.int32, (shards, shard_rows, 4 * TILE), 1)
    held = jnp.where(offset < table_rows, owner * table_rows + offset, -1).reshape(width, 4 * TILE)
    hot = (held == bucket_ref[0:1, :]).astype(low)
    table_t = small_t[experts + 2 : experts + 2 + heads_held].astype(low)
    rev_ref[...] = nn(table_t, hot)

    @pl.loop(0, every_ref.shape[0] // SPAN)
    def project(part):
        span = pl.ds(pl.multiple_of(part * SPAN, SPAN), SPAN)
        values = every_ref[span, :].astype(single)
        normed = (values * inverse_rms(values) * gain_attn).astype(low)
        n_ref[span, :] = normed
        k_ref[span, :] = nn(normed, w_ref[1]).astype(low)
        v_ref[span, :] = nn(normed, w_ref[2]).astype(low)

    own = pl.ds(pl.multiple_of(shard_id * TILE, TILE), TILE)
    normed = jnp.concatenate([n_ref[own, :], n_ref[(blocks + 2) * TILE :, :]], axis=0)
    q_ref[...] = (nn(normed, w_ref[0]).astype(low) * jnp.asarray(0.125, low)).astype(low)

    @pl.loop(0, width // TILE)
    def pair_loop(pair):
        cols = pl.ds(pl.multiple_of(pair * TILE, TILE), TILE)
        vt[...] = v_ref[:, cols].T
        q_pair = q_ref[:, cols]
        for side in range(2):
            head = pair * 2 + side
            rev_row = rev_ref[pl.ds(head, 1), :]
            fill_tiles(tiles, rev_row, rev_row[:, SPAN - 1 : SPAN], rev_row[:, SPAN : SPAN + 1])
            q_head = jnp.where(head_mask(rows, side), q_pair, jnp.zeros_like(q_pair))
            top = jnp.full((8, rows), masked_score, single)
            for part in range(blocks // 2):
                keys = slice(part * SPAN, (part + 1) * SPAN)
                scores = with_bias(nt(k_ref[keys, cols], q_head), tiles, prompt_grid(part, shard_id, blocks))
                sp[keys, :] = scores
                top = jnp.maximum(top, jnp.max(fold8(scores), axis=0))
            top_local = top[:, PR_DEV:]
            for part in range(2):
                keys = slice(part * SPAN, (part + 1) * SPAN)
                held = slice((blocks // 2 + part) * SPAN, (blocks // 2 + part + 1) * SPAN)
                scores = with_bias(nt(k_ref[held, cols], q_head[PR_DEV:]), tiles, local_grid(part, shard_id))
                sl[keys, :] = scores
                top_local = jnp.maximum(top_local, jnp.max(fold8(scores), axis=0))
            top = jnp.max(jnp.concatenate([top[:, :PR_DEV], top_local], axis=1), axis=0, keepdims=True)
            total = jnp.zeros((8, rows), single)
            summed = jnp.zeros((half, rows), single)
            heads = slice(side * half, (side + 1) * half)
            for part in range(blocks // 2):
                keys = slice(part * SPAN, (part + 1) * SPAN)
                weights = jnp.exp(sp[keys, :] - top)
                total = total + jnp.sum(fold8(weights), axis=0)
                summed = summed + nn(vt[heads, keys], weights.astype(low))
            top_c = top[:, PR_DEV:]
            total_c = total[:, PR_DEV:]
            summed_c = summed[:, PR_DEV:]
            for part in range(2):
                keys = slice(part * SPAN, (part + 1) * SPAN)
                held = slice((blocks // 2 + part) * SPAN, (blocks // 2 + part + 1) * SPAN)
                weights = jnp.exp(sl[keys, :] - top_c)
                total_c = total_c + jnp.sum(fold8(weights), axis=0)
                summed_c = summed_c + nn(vt[heads, held], weights.astype(low))
            total = jnp.sum(jnp.concatenate([total[:, :PR_DEV], total_c], axis=1), axis=0, keepdims=True)
            summed = jnp.concatenate([summed[:, :PR_DEV], summed_c], axis=1)
            ot[heads, :] = summed / total
            lse_ref[pl.ds(head, 1), :] = top + jnp.log(total)
        o_ref[:, cols] = ot[...].T

    resid_mid = tok_ref[...].astype(single) + nn(o_ref[...].astype(low), w_ref[3])
    mid_ref[...] = resid_mid
    mid_low = (resid_mid * inverse_rms(resid_mid) * gain_moe).astype(low)
    probs = router_softmax(mid_low, small_ref[...], experts)
    lanes = lax.broadcasted_iota(jnp.int32, probs.shape, 1)
    gate = jnp.sum(jnp.where(lanes == route_ref[...], probs, 0.0), axis=1, keepdims=True)
    gate_ref[...] = jnp.broadcast_to(gate, gate_ref.shape)
    x_ref[...] = nn(place, mid_low).astype(low)
    mine.wait()
    for k in range(shards - 1):
        piece = gin_ref.at[(shard_id + shards - k - 1) % shards]
        send(piece, piece, (gs.at[k], gr.at[k]), others[0]).wait_recv()
    for copy in sent:
        copy.wait_send()


def router_softmax(rows_low, small, experts):
    logits = nn(rows_low, small)
    lanes = lax.broadcasted_iota(jnp.int32, logits.shape, 1)
    logits = jnp.where(lanes < experts, logits, masked_score)
    powers = jnp.exp(logits - jnp.max(logits, axis=1, keepdims=True))
    return powers / jnp.sum(powers, axis=1, keepdims=True)


def front(every_tok, tokens, weights, small, bucket_row, route_col, row_slots, cotangent, slot_count):
    rows, width = tokens.shape
    keys = every_tok.shape[0]
    shards = lax.axis_size("shard")
    shape = jax.ShapeDtypeStruct
    return pl.pallas_call(
        front_kernel,
        out_shape=(
            shape((keys, width), low), shape((rows, width), low), shape((keys, width), low),
            shape((keys, width), low), shape((rows, width), single), shape((16, rows), single),
            shape((16, 4 * TILE), single), shape((rows, width), single), shape((rows, TILE), single),
            shape((8, width), single), shape((slot_count, width), low),
            shape((shards, slot_count // shards, width), low),
        ),
        in_specs=[in_vmem] * 8,
        out_specs=(in_vmem,) * 11 + (anywhere,),
        scratch_shapes=[
            pltpu.VMEM((tile_kinds, TILE, TILE), single),
            pltpu.VMEM((TILE, keys), low),
            pltpu.VMEM((keys - 2 * SPAN, rows), single),
            pltpu.VMEM((2 * SPAN, rows - TILE), single),
            pltpu.VMEM((TILE, rows), single),
            pltpu.VMEM((shards, slot_count // shards, width), low),
            pltpu.SemaphoreType.DMA((shards - 1,)), pltpu.SemaphoreType.DMA((shards - 1,)), pltpu.SemaphoreType.DMA,
        ],
        compiler_params=pltpu.CompilerParams(collective_id=2, has_side_effects=True, vmem_limit_bytes=vmem_cap),
        cost_estimate=pl.CostEstimate(flops=30_000_000_000, bytes_accessed=20_000_000, transcendentals=8_000_000),
        name="front",
    )(every_tok, tokens, weights, small, bucket_row, route_col, row_slots, cotangent)


def moe_kernel(
    x_ref, g_ref, small_ref, w_in_ref, w_out_ref,
    back_ref, out_ref, gwin_ref, gwout_ref, rg_ref,
    w_in, w_out, xin, gm, gg, hid, gpre, logit_grads, x_t, gwin, gwout,
    xs, xr, ms, mr, ws, ls, os_in, os_out,
):
    rep, chip, core, chips, quarter = places()
    experts = chips * 2
    here = chip * 2 + core
    pair_rows = 2 * xin.shape[2]
    hidden = w_in_ref.shape[1]
    block = BLOCK
    loads = [
        pltpu.make_async_copy(w_in_ref, w_in, ws.at[0]),
        pltpu.make_async_copy(w_out_ref, w_out, ws.at[1]),
    ]
    for copy in loads:
        copy.start()
    twin = (rep, chip * 2 + 1 - core)
    targets = [
        (k, side, (rep, chip_across(chip, k) * 2 + side)) for k in range(1, chips) for side in range(2)
    ]
    greet([twin] + [device for _, _, device in targets])
    sent = [send(x_ref.at[chip, 1 - core], xin.at[chip, core], (xs.at[0, 0], xr.at[0, core]), twin)]
    for k, side, device in targets:
        sent.append(
            send(x_ref.at[chip_across(chip, k), side], xin.at[chip, core], (xs.at[k, side], xr.at[k, core]), device)
        )
    for copy in sent[:5]:
        copy.start()
    xin[chip, core] = x_ref[chip, core]
    for copy in loads:
        copy.wait()

    def arrived(k, source, side):
        piece = xin.at[source, side]
        send(piece, piece, (xs.at[0, 0], xr.at[k, side]), twin).wait_recv()

    @pl.loop(0, chips)
    def chunk(k):
        source = chip_across(chip, k)

        @pl.when(k == 0)
        def _():
            arrived(0, chip, 1 - core)

        @pl.when(k > 0)
        def _():
            for side in range(2):
                arrived(k, source, side)

        rows = xin[source].reshape(pair_rows, xin.shape[3])
        grads = g_ref[source].reshape(pair_rows, xin.shape[3])
        probs = router_softmax(rows, small_ref[...], experts)
        lanes = lax.broadcasted_iota(jnp.int32, probs.shape, 1)
        gate = jnp.sum(jnp.where(lanes == here, probs, 0.0), axis=1, keepdims=True)
        gated = (gate * grads.astype(single)).astype(low)
        span = pl.ds(pl.multiple_of(source * pair_rows, pair_rows), pair_rows)
        gg[span, :] = gated
        pre = nn(rows, w_in[...])
        grad_hidden = nt(gated, w_out[...])
        square = pre * pre
        wave = jnp.tanh(0.7978845608028654 * pre * (1.0 + 0.044715 * square))
        left = 0.5 + 0.5 * wave
        active = (pre * left).astype(low)
        slope = left + (0.5 * pre) * (1.0 - wave * wave) * (0.7978845608028654 + 0.10703222440890037 * square)
        grad_pre = (grad_hidden * slope).astype(low)
        hid[span, :] = active
        gpre[span, :] = grad_pre
        out = nn(active, w_out[...]).astype(low)
        out_ref[source] = out.reshape(out_ref.shape[1:])
        grad_gate = jnp.sum(grads.astype(single) * out.astype(single), axis=1, keepdims=True)
        chosen = jnp.where(lanes == here, 1.0, 0.0)
        grad_logits = jnp.where(lanes < experts, gate * grad_gate * (chosen - probs), 0.0)
        logit_grads[span, :] = grad_logits
        router = small_ref[...]
        total = nt(grad_pre, w_in[...]) + sum(nt(part, router) for part in thirds_of(grad_logits))
        gm[source] = total.astype(low).reshape(gm.shape[1:])

        def reply(side, slot):
            return send(
                gm.at[source, side], back_ref.at[chip, core], (ms.at[k, slot], mr.at[k, core]), (rep, source * 2 + side)
            )

        @pl.when(k == 0)
        def _():
            for copy in sent[5:]:
                copy.start()
            reply(1 - core, 0).start()
            pltpu.make_async_copy(gm.at[chip, core], back_ref.at[chip, core], ls).start()

        @pl.when(k > 0)
        def _():
            for side in range(2):
                reply(side, side).start()

    every = xin[...].reshape(gg.shape)
    x_t[...] = every.T
    writes = []
    for part in range(hidden // block):
        cols = slice(part * block, (part + 1) * block)
        gwin[:, cols] = nn(x_t[...], gpre[:, cols]).astype(low)
        writes.append(pltpu.make_async_copy(gwin.at[:, cols], gwin_ref.at[:, cols], os_in.at[part]))
        writes[-1].start()
        gwout[cols, :] = tn(hid[:, cols], gg[...]).astype(low)
        writes.append(pltpu.make_async_copy(gwout.at[cols], gwout_ref.at[cols], os_out.at[part]))
        writes[-1].start()
    rg_ref[...] = sum(nn(x_t[...], part) for part in thirds_of(logit_grads[...]))
    pltpu.make_async_copy(gm.at[chip, core], back_ref.at[chip, core], ls).wait()

    def replied(k, source, side):
        piece = back_ref.at[source, side]
        send(piece, piece, (ms.at[0, 0], mr.at[k, side]), twin).wait_recv()

    replied(0, chip, 1 - core)
    for k in range(1, chips):
        for side in range(2):
            replied(k, chip_across(chip, k), side)
    for copy in sent:
        copy.wait_send()
    for copy in writes:
        copy.wait()
    send(gm.at[chip, 0], back_ref.at[chip, core], (ms.at[0, 0], mr.at[0, 0]), twin).wait_send()
    for k in range(1, chips):
        for side in range(2):
            send(gm.at[chip, 0], back_ref.at[chip, core], (ms.at[k, side], mr.at[0, 0]), twin).wait_send()


def moe(rows_out, grad_in, small, w_in, w_out):
    chips, _, cap, width = rows_out.shape
    slots = chips * 2 * cap
    hidden = w_in.shape[1]
    shape = jax.ShapeDtypeStruct
    pairs = pltpu.SemaphoreType.DMA
    strips = hidden // BLOCK
    return pl.pallas_call(
        moe_kernel,
        out_shape=(
            shape(rows_out.shape, low), shape(rows_out.shape, low), shape((width, hidden), low),
            shape((hidden, width), low), shape((width, TILE), single),
        ),
        in_specs=[in_vmem] * 3 + [anywhere] * 2,
        out_specs=(anywhere, in_vmem, anywhere, anywhere, in_vmem),
        scratch_shapes=[
            pltpu.VMEM((width, hidden), low), pltpu.VMEM((hidden, width), low),
            pltpu.VMEM(rows_out.shape, low), pltpu.VMEM(rows_out.shape, low), pltpu.VMEM((slots, width), low),
            pltpu.VMEM((slots, hidden), low), pltpu.VMEM((slots, hidden), low),
            pltpu.VMEM((slots, TILE), single), pltpu.VMEM((width, slots), low), pltpu.VMEM((width, hidden), low), pltpu.VMEM((hidden, width), low),
            pairs((chips, 2)), pairs((chips, 2)), pairs((chips, 2)), pairs((chips, 2)), pairs((2,)), pairs,
            pairs((strips,)), pairs((strips,)),
        ],
        compiler_params=pltpu.CompilerParams(collective_id=3, has_side_effects=True, vmem_limit_bytes=vmem_cap),
        cost_estimate=pl.CostEstimate(flops=40_000_000_000, bytes_accessed=40_000_000, transcendentals=3_000_000),
        name="moe",
    )(rows_out, grad_in, small, w_in, w_out)


def back_kernel(
    back_ref, col_ref, mid_ref, cot_ref, gain_ref, q_ref, k_ref, v_ref, o_ref,
    lse_ref, rev_ref, bucket_ref, rg_ref, every_hbm, w_hbm, n_hbm, out_hbm, gwin_hbm, gwout_hbm,
    dense_ref, p_ref, e_ref, own_ref, gres_ref, ret_hbm, ra_hbm, rb_hbm,
    tiles, sums, diag, kt, dqt, far_sums, dk_sum, dv_sum, g_ref, dq_ref, dk_ref, dv_ref, attn_gain,
    every_ref, w_ref, n_ref, loc, xs, xr, as_, ar, bs, br,
):
    shard_id = lax.axis_index("shard")
    shards = lax.axis_size("shard")
    rows, width = mid_ref.shape
    blocks = k_ref.shape[0] // TILE - 4
    half = TILE // 2
    experts = shards
    heads_held = rev_ref.shape[0]
    rep, slow, fast, slows, fasts = rep_places()
    loads = [
        pltpu.make_async_copy(w_hbm.at[3], w_ref.at[3], loc.at[0]),
        pltpu.make_async_copy(w_hbm.at[pl.ds(0, 3)], w_ref.at[pl.ds(0, 3)], loc.at[1]),
        pltpu.make_async_copy(n_hbm, n_ref, loc.at[2]),
        pltpu.make_async_copy(every_hbm, every_ref, loc.at[3]),
        pltpu.make_async_copy(out_hbm.at[shard_id], ret_hbm.at[shard_id], loc.at[4]),
    ]
    for copy in loads:
        copy.start()
    others = [(rep, (shard_id + k) % shards) for k in range(1, shards)]
    beside = [(slow * fasts + (fast + j) % fasts, shard_id) for j in range(1, fasts)]
    beyond = [((slow + j) % slows * fasts + fast, shard_id) for j in range(1, slows)]
    greet(others + beside + beyond)
    sent = [
        send(gwin_hbm.at[:, (fast + j + 1) % fasts], ra_hbm.at[j], (as_.at[j], ar.at[j]), device)
        for j, device in enumerate(beside)
    ] + [
        send(gwout_hbm.at[(slow + j + 1) % slows], rb_hbm.at[j], (bs.at[j], br.at[j]), device)
        for j, device in enumerate(beyond)
    ] + [
        send(out_hbm.at[device[1]], ret_hbm.at[shard_id], (xs.at[k], xr.at[k]), device)
        for k, device in enumerate(others)
    ]
    for copy in sent:
        copy.start()
    diag[...] = jnp.zeros_like(diag)
    far_sums[...] = jnp.zeros_like(far_sums)
    tile_rows = lax.broadcasted_iota(jnp.int32, (TILE, TILE), 0)
    tile_cols = lax.broadcasted_iota(jnp.int32, (TILE, TILE), 1)
    flip = (tile_rows + tile_cols == TILE - 1).astype(single)

    slots = lax.broadcasted_iota(jnp.int32, (rows, back_ref.shape[0]), 1)
    grad_mid = nn((slots == col_ref[...]).astype(low), back_ref[...])
    resid_mid = mid_ref[...]
    grad_gain_moe = jnp.sum(grad_mid * resid_mid * inverse_rms(resid_mid), axis=0, keepdims=True)
    grad_resid = cot_ref[...].astype(single) + norm_pull(grad_mid, resid_mid, gain_ref[1:2, :])
    gres_ref[...] = grad_resid
    grad_attn = grad_resid.astype(low)
    loads[0].wait()
    g_ref[...] = nt(grad_attn, w_ref[3]).astype(low)
    dense_ref[:, 3 * width : 4 * width] = tn(o_ref[...].astype(low), grad_attn).astype(low)

    @pl.loop(0, width // TILE)
    def pair_loop(pair):
        cols = pl.ds(pl.multiple_of(pair * TILE, TILE), TILE)
        kt[...] = k_ref[:, cols].T
        q_pair = q_ref[:, cols]
        g_pair = g_ref[:, cols]
        delta_t = (g_pair.astype(single) * o_ref[:, cols]).T
        for side in range(2):
            head = pair * 2 + side
            heads = slice(side * half, (side + 1) * half)
            rev_row = rev_ref[pl.ds(head, 1), :]
            fill_tiles(tiles, rev_row, rev_row[:, SPAN - 1 : SPAN], rev_row[:, SPAN : SPAN + 1])
            sums[...] = jnp.zeros_like(sums)
            mask = head_mask(rows, side)
            q_head = jnp.where(mask, q_pair, jnp.zeros_like(q_pair))
            g_head = jnp.where(mask, g_pair, jnp.zeros_like(g_pair))
            delta = jnp.sum(delta_t[heads, :], axis=0, keepdims=True)
            log_total = lse_ref[pl.ds(head, 1), :]

            def block_grads(part, first, grid):
                keys = slice(part * SPAN, (part + 1) * SPAN)
                q_rows, g_rows = q_head[first:], g_head[first:]
                scores = with_bias(nt(k_ref[keys, cols], q_rows), tiles, grid)
                weights = jnp.exp(scores - log_total[:, first:])
                grad_weights = nt(v_ref[keys, cols], g_rows)
                grad_scores = weights * (grad_weights - delta[:, first:])
                for i, row in enumerate(grid):
                    for j, kind in enumerate(row):
                        sums[kind] += grad_scores[i * TILE : (i + 1) * TILE, j * TILE : (j + 1) * TILE]
                raw = grad_scores.astype(low)
                dk = nn(raw, q_rows)
                dv = nn(weights.astype(low), g_rows)
                if side == 0:
                    dk_sum[keys, :] = dk
                    dv_sum[keys, :] = dv
                else:
                    dk_ref[keys, cols] = (dk_sum[keys, :] + dk).astype(low)
                    dv_ref[keys, cols] = (dv_sum[keys, :] + dv).astype(low)
                return nn(kt[heads, keys], raw)

            dq = jnp.zeros((half, rows), single)
            for part in range(blocks // 2):
                dq = dq + block_grads(part, 0, prompt_grid(part, shard_id, blocks))
            dq_c = dq[:, PR_DEV:]
            for part in range(2):
                dq_c = dq_c + block_grads(blocks // 2 + part, PR_DEV, local_grid(part, shard_id))
            dqt[heads, :] = jnp.concatenate([dq[:, :PR_DEV], dq_c], axis=1)
            near = jnp.concatenate(
                [sums[1] + sums[causal_tile], sums[0], jnp.zeros((TILE, TILE), single), sums[2]], axis=1
            )
            flipped = jnp.dot(flip, near, precision=lax.Precision.HIGHEST, preferred_element_type=single)
            rolled = pltpu.roll(flipped, 3 * TILE + 1, 1, stride=1, stride_axis=0)
            diag[pl.ds(head, 1), :] = jnp.sum(rolled, axis=0, keepdims=True)
            far_sums[pl.ds(head, 1), :] = jnp.concatenate(
                [jnp.sum(sums[far_before], axis=0, keepdims=True), jnp.sum(sums[far_after], axis=0, keepdims=True)],
                axis=1,
            )
        dq_ref[:, cols] = (dqt[...].T * 0.125).astype(low)

    lanes = lax.broadcasted_iota(jnp.int32, (heads_held, 4 * TILE), 1)
    before = jnp.sum(far_sums[:, :TILE], axis=1, keepdims=True)
    after = jnp.sum(far_sums[:, TILE:], axis=1, keepdims=True)
    by_gap = diag[...] + jnp.where(lanes == SPAN - 1, before, 0.0) + jnp.where(lanes == SPAN, after, 0.0)
    shard_rows = width // shards
    table_rows = 2 * TILE // 8 // shards
    owner = lax.broadcasted_iota(jnp.int32, (shards, shard_rows, 4 * TILE), 0)
    offset = lax.broadcasted_iota(jnp.int32, (shards, shard_rows, 4 * TILE), 1)
    held = jnp.where(offset < table_rows, owner * table_rows + offset, -1).reshape(width, 4 * TILE)
    hot = (held == bucket_ref[0:1, :]).astype(low)
    grad_table = sum(nt(part, hot) for part in thirds_of(by_gap))

    attn_gain[...] = jnp.zeros_like(attn_gain)
    for copy in loads[1:]:
        copy.wait()
    own = pl.ds(pl.multiple_of(shard_id * TILE, TILE), TILE)
    tail = slice((blocks + 2) * TILE, (blocks + 4) * TILE)
    normed = jnp.concatenate([n_ref[own, :], n_ref[tail, :]], axis=0)
    dense_ref[:, :width] = tn(normed, dq_ref[...]).astype(low)
    grad_own = nt(dq_ref[...], w_ref[0])
    values = jnp.concatenate([every_ref[own, :], every_ref[tail, :]], axis=0).astype(single)
    attn_gain[...] += jnp.sum(fold8(grad_own * (values * inverse_rms(values))), axis=0)
    own_ref[...] = grad_own

    def pull_rows(part):
        span = pl.ds(pl.multiple_of(part * SPAN, SPAN), SPAN)
        values = every_ref[span, :].astype(single)
        grads = nt(dk_ref[span, :], w_ref[1]) + nt(dv_ref[span, :], w_ref[2])
        attn_gain[...] += jnp.sum(fold8(grads * (values * inverse_rms(values))), axis=0)
        return grads

    @pl.loop(0, blocks // 2)
    def pull_prompt(part):
        p_ref[pl.ds(pl.multiple_of(part * SPAN, SPAN), SPAN), :] = pull_rows(part).astype(low)

    e_ref[...] = pull_rows(blocks // 2).astype(low)
    own_ref[PR_DEV:, :] += pull_rows(blocks // 2 + 1)

    @pl.loop(0, width // SPAN)
    def outer(part):
        cols = pl.ds(pl.multiple_of(part * SPAN, SPAN), SPAN)
        k_cols = pl.ds(pl.multiple_of(width + part * SPAN, SPAN), SPAN)
        v_cols = pl.ds(pl.multiple_of(2 * width + part * SPAN, SPAN), SPAN)
        dense_ref[:, k_cols] = tn(n_ref[...], dk_ref[:, cols]).astype(low)
        dense_ref[:, v_cols] = tn(n_ref[...], dv_ref[:, cols]).astype(low)

    small_t = jnp.concatenate(
        [
            jnp.zeros((experts, width), single), jnp.sum(attn_gain[...], axis=0, keepdims=True), grad_gain_moe,
            grad_table, jnp.zeros((TILE - experts - 2 - heads_held, width), single),
        ],
        axis=0,
    )
    dense_ref[:, 4 * width :] = (small_t.T + rg_ref[...]).astype(low)
    for k in range(shards - 1):
        piece = ret_hbm.at[(shard_id + shards - k - 1) % shards]
        send(piece, piece, (xs.at[k], xr.at[k]), others[0]).wait_recv()
    for j in range(fasts - 1):
        send(ra_hbm.at[j], ra_hbm.at[j], (as_.at[j], ar.at[j]), others[0]).wait_recv()
    for j in range(slows - 1):
        send(rb_hbm.at[j], rb_hbm.at[j], (bs.at[j], br.at[j]), others[0]).wait_recv()
    for copy in sent:
        copy.wait_send()


def back(
    returned, col_slots, mid, cotangent, gains, every_tok, weights, kept, bucket_row, router_grads, result, gwin, gwout
):
    rows, width = mid.shape
    normed, queries, keys, values, attended, lse, rev = kept
    count = keys.shape[0]
    shards = result.shape[0]
    slows, fasts = gwin.shape[:2]
    shape = jax.ShapeDtypeStruct
    pairs = pltpu.SemaphoreType.DMA
    args = (
        returned, col_slots, mid, cotangent, gains, queries, keys, values, attended, lse, rev, bucket_row,
        router_grads, every_tok, weights, normed, result, gwin, gwout,
    )
    return pl.pallas_call(
        back_kernel,
        out_shape=(
            shape((width, 4 * width + TILE), low), shape((count - 2 * SPAN, width), low), shape((SPAN, width), low),
            shape((rows, width), single), shape((rows, width), single), shape(result.shape, low),
            shape((fasts - 1, slows) + gwin.shape[2:], low), shape((slows - 1, fasts) + gwout.shape[2:], low),
        ),
        in_specs=[in_vmem] * 13 + [anywhere] * 6,
        out_specs=(in_vmem,) * 5 + (anywhere,) * 3,
        scratch_shapes=[
            pltpu.VMEM((tile_kinds, TILE, TILE), single), pltpu.VMEM((tile_kinds, TILE, TILE), single),
            pltpu.VMEM((16, 4 * TILE), single), pltpu.VMEM((TILE, count), low), pltpu.VMEM((TILE, rows), single),
            pltpu.VMEM((16, 2 * TILE), single), pltpu.VMEM((count, TILE), single), pltpu.VMEM((count, TILE), single),
            pltpu.VMEM((rows, width), low), pltpu.VMEM((rows, width), low), pltpu.VMEM((count, width), low),
            pltpu.VMEM((count, width), low), pltpu.VMEM((8, width), single),
            pltpu.VMEM(every_tok.shape, low), pltpu.VMEM(weights.shape, low), pltpu.VMEM(normed.shape, low),
            pairs((5,)), pairs((shards - 1,)), pairs((shards - 1,)), pairs((fasts - 1,)), pairs((fasts - 1,)),
            pairs((slows - 1,)), pairs((slows - 1,)),
        ],
        compiler_params=pltpu.CompilerParams(collective_id=4, has_side_effects=True, vmem_limit_bytes=vmem_cap),
        cost_estimate=pl.CostEstimate(flops=60_000_000_000, bytes_accessed=40_000_000, transcendentals=8_000_000),
        name="back",
    )(*args)


def places():
    rep, shard = lax.axis_index("rep"), lax.axis_index("shard")
    return rep, shard // 2, shard % 2, lax.axis_size("shard") // 2, rep % QUARTERS


def peer_lists():
    rep, chip, core, chips, quarter = places()
    along = [(rep, (chip + k) % chips * 2 + core) for k in range(1, chips)]
    across = [(rep - quarter + (quarter + j) % QUARTERS, chip * 2 + core) for j in range(1, QUARTERS)]
    twin = (rep, chip * 2 + 1 - core)
    return along, across, twin


def chip_across(chip, k):
    partner, bit = 0, 1
    while bit < lax.axis_size("shard") // 2:
        partner = partner + bit * ((chip // bit + k // bit) % 2)
        bit = bit * 2
    return partner


def greet(devices):
    barrier = pltpu.get_barrier_semaphore()
    for device in devices:
        pl.semaphore_signal(barrier, inc=1, device_id=device, device_id_type=mesh_ids)
    pl.semaphore_wait(barrier, len(devices))


def send(source, target, sems, device):
    return pltpu.make_async_remote_copy(
        src_ref=source, dst_ref=target, send_sem=sems[0], recv_sem=sems[1],
        device_id=device, device_id_type=mesh_ids,
    )


def gather_kernel(
    w_ref, tok_ref, small_ref, wg_ref, tg_ref, sg_ref,
    wz_s, wz_r, tz_s, tz_r, sz_s, sz_r, wr_s, wr_r, wt_s, wt_r, tt_s, tt_r, et_s, et_r, loc,
):
    rep, chip, core, chips, quarter = places()
    along, across, twin = peer_lists()
    rest_rows = tok_ref.shape[0] - PR_DEV
    prompt_len = chips * 2 * PR_DEV
    prompt = tok_ref.at[pl.ds(0, PR_DEV)]
    rest = tok_ref.at[pl.ds(PR_DEV, rest_rows)]
    near_rows = tg_ref.at[pl.ds(prompt_len, rest_rows)]

    def tok_rows(source, side):
        return tg_ref.at[pl.ds(pl.multiple_of((source * 2 + side) * PR_DEV, PR_DEV), PR_DEV)]

    mine = tok_rows(chip, core)
    own = [
        pltpu.make_async_copy(w_ref, wg_ref.at[:, chip, core], loc.at[0]),
        pltpu.make_async_copy(prompt, mine, loc.at[1]),
        pltpu.make_async_copy(small_ref, sg_ref.at[chip, core], loc.at[2]),
        pltpu.make_async_copy(rest, tg_ref.at[pl.ds(prompt_len + rest_rows, rest_rows)], loc.at[3]),
    ]
    for copy in own:
        copy.start()
    greet(along + across + [twin])
    started = []

    def go(copy):
        copy.start()
        started.append(copy)

    for k, device in enumerate(along):
        go(send(w_ref.at[:, quarter], wg_ref.at[:, chip, core, quarter], (wz_s.at[k], wz_r.at[k]), device))
        go(send(small_ref, sg_ref.at[chip, core], (sz_s.at[k], sz_r.at[k]), device))
    go(send(rest, near_rows, (et_s.at[0], et_r.at[0]), twin))
    go(send(prompt, mine, (tt_s.at[0], tt_r.at[0]), twin))
    go(send(w_ref, wg_ref.at[:, chip, core], (wt_s.at[0], wt_r.at[0]), twin))
    for k in range(1, chips):
        source = (chip + chips - k) % chips
        piece = wg_ref.at[:, source, core, quarter]
        send(piece, piece, (wz_s.at[k - 1], wz_r.at[k - 1]), twin).wait_recv()
        for j, device in enumerate(across):
            go(send(piece, piece, (wr_s.at[k - 1, j], wr_r.at[k - 1, j]), device))
        go(send(prompt, mine, (tz_s.at[k - 1], tz_r.at[k - 1]), along[k - 1]))
    for k in range(1, chips):
        source = (chip + chips - k) % chips
        for j in range(1, QUARTERS):
            piece = wg_ref.at[:, source, core, (quarter + QUARTERS - j) % QUARTERS]
            send(piece, piece, (wr_s.at[k - 1, j - 1], wr_r.at[k - 1, j - 1]), twin).wait_recv()
        row = wg_ref.at[:, source, core]
        go(send(row, row, (wt_s.at[k], wt_r.at[k]), twin))
        theirs = tok_rows(source, core)
        send(theirs, theirs, (tz_s.at[k - 1], tz_r.at[k - 1]), twin).wait_recv()
        go(send(theirs, theirs, (tt_s.at[k], tt_r.at[k]), twin))
        send(small_ref, sg_ref.at[source, core], (sz_s.at[k - 1], sz_r.at[k - 1]), twin).wait_recv()
    for copy in own:
        copy.wait()
    go(send(sg_ref.at[:, core], sg_ref.at[:, core], (et_s.at[1], et_r.at[1]), twin))
    send(rest, near_rows, (et_s.at[0], et_r.at[0]), twin).wait_recv()
    for k in range(chips):
        source = (chip + chips - k) % chips
        row = wg_ref.at[:, source, 1 - core]
        send(row, row, (wt_s.at[k], wt_r.at[k]), twin).wait_recv()
        theirs = tok_rows(source, 1 - core)
        send(theirs, theirs, (tt_s.at[k], tt_r.at[k]), twin).wait_recv()
    send(sg_ref.at[:, core], sg_ref.at[:, 1 - core], (et_s.at[1], et_r.at[1]), twin).wait_recv()
    for copy in started:
        copy.wait_send()


def gather_all(weights, tokens, small):
    chips = lax.axis_size("shard") // 2
    width = tokens.shape[1]
    pairs = pltpu.SemaphoreType.DMA
    count = chips - 1
    return pl.pallas_call(
        gather_kernel,
        out_shape=(
            jax.ShapeDtypeStruct((weights.shape[0], chips, 2) + weights.shape[1:], weights.dtype),
            jax.ShapeDtypeStruct((2 * chips * PR_DEV + 2 * (tokens.shape[0] - PR_DEV), width), tokens.dtype),
            jax.ShapeDtypeStruct((chips, 2) + small.shape, small.dtype),
        ),
        in_specs=[anywhere] * 3,
        out_specs=(anywhere,) * 3,
        scratch_shapes=[
            pairs((count,)), pairs((count,)), pairs((count,)), pairs((count,)), pairs((count,)), pairs((count,)),
            pairs((count, 3)), pairs((count, 3)), pairs((chips,)), pairs((chips,)), pairs((chips,)), pairs((chips,)),
            pairs((2,)), pairs((2,)), pairs((4,)),
        ],
        compiler_params=pltpu.CompilerParams(collective_id=0, has_side_effects=True),
        cost_estimate=pl.CostEstimate(flops=0, bytes_accessed=100_000_000, transcendentals=0),
        name="gather_all",
    )(weights, tokens, small)


def rep_places():
    rep, reps = lax.axis_index("rep"), lax.axis_size("rep")
    fasts = QUARTERS if reps % (QUARTERS * QUARTERS) == 0 else 2
    return rep, rep // fasts, rep % fasts, reps // fasts, fasts


def reduce_kernel(
    gain_ref, col_ref, d_hbm, p_hbm, e_hbm, own_hbm, gres_hbm, tok_hbm, mid_hbm, gate_hbm, ret_hbm,
    gwin_hbm, ra_hbm, gwout_hbm, rb_hbm,
    gt_ref, mix_ref, dq_ref, dk_ref, dv_ref, do_ref, sm_ref, ka_ref, la_hbm, kb_ref, lb_hbm,
    d_own, half, hr, hz, tr, mr, cr, cz, zs, tz, last, above_in, gathered,
    p_own, p_half, p_sum, p_in, e_in, own, gres, tok, mid, gate, ret,
    a_own, a_in, a_sum, b_own, b_in, b_sum,
    loc, ps_s, ps_r, ds_s, ds_r, pz_s, pz_r, rr_s, rr_r, rz_s, rz_r, zz_s, zz_r, zr_s, zr_r, dh_s, dh_r,
    da_s, da_r, ea_s, ea_r, eb_s, eb_r,
):
    rep, chip, core, chips, quarter = places()
    along, across, twin = peer_lists()
    _, slow, fast, slows, fasts = rep_places()
    classes = lax.axis_size("rep") // QUARTERS
    here = chip * 2 + core
    beside = [(slow * fasts + (fast + j) % fasts, here) for j in range(1, fasts)]
    beyond = [((slow + j) % slows * fasts + fast, here) for j in range(1, slows)]
    above = [((rep // QUARTERS + k) % classes * QUARTERS + quarter, here) for k in range(1, classes)]
    width = gain_ref.shape[1]
    cut = hr.shape[3]
    wide = lambda ref_value: ref_value.astype(single)
    pending = []

    def load(source, target, index):
        copy = pltpu.make_async_copy(source, target, loc.at[index])
        copy.start()
        return copy

    def go(source, target, sems, device):
        copy = send(source, target, sems, device)
        copy.start()
        pending.append(copy)

    def landed(piece, sems):
        send(piece, piece, sems, twin).wait_recv()

    experts_in = [
        load(gwin_hbm.at[:, fast], a_own, 0), load(ra_hbm, a_in, 1),
        load(gwout_hbm.at[slow], b_own, 2), load(rb_hbm, b_in, 3),
    ]
    halves = [load(p_hbm.at[:, core], p_own, 4), load(d_hbm.at[:, core], d_own, 5)]
    rest = [
        load(ret_hbm, ret, 6), load(mid_hbm, mid, 7), load(gate_hbm, gate, 8), load(own_hbm, own, 9),
        load(gres_hbm, gres, 10), load(tok_hbm, tok, 11),
    ]
    greets = [twin] + along
    for device in across + beside + beyond + above:
        greets.append(device)
    greet(greets)
    go(p_hbm.at[:, 1 - core], p_half, (ps_s.at[0], ps_r.at[0]), twin)
    for k in range(chips):
        go(d_hbm.at[k, 1 - core], half.at[k], (ds_s.at[k], ds_r.at[k]), twin)
    go(e_hbm, e_in, (ps_s.at[1], ps_r.at[1]), twin)

    for copy in experts_in:
        copy.wait()
    for t in range(slows):
        total = wide(a_own[t])
        for j in range(fasts - 1):
            total = total + wide(a_in[j, t])
        a_sum[t] = total.astype(low)
    for t in range(fasts):
        total = wide(b_own[t])
        for j in range(slows - 1):
            total = total + wide(b_in[j, t])
        b_sum[t] = total.astype(low)
    for j, device in enumerate(beyond):
        go(a_sum.at[(slow + j + 1) % slows], la_hbm.at[j], (ea_s.at[j], ea_r.at[j]), device)
    for j, device in enumerate(beside):
        go(b_sum.at[(fast + j + 1) % fasts], lb_hbm.at[j], (eb_s.at[j], eb_r.at[j]), device)

    halves[0].wait()
    landed(p_half, (ps_s.at[0], ps_r.at[0]))
    for k in range(chips):
        p_sum[k] = (wide(p_own[k]) + wide(p_half[k])).astype(low)
    for k, device in enumerate(along):
        go(p_sum.at[(chip + k + 1) % chips], p_in.at[k], (pz_s.at[k], pz_r.at[k]), device)
    halves[1].wait()
    for k in range(chips):
        landed(half.at[k], (ds_s.at[k], ds_r.at[k]))
        for t in range(QUARTERS):
            total = (wide(d_own[k, t]) + wide(half[k, t])).astype(low)
            hr[t, k] = total[:, :cut]
            hz[k, t] = total[:, cut:]
    for j, device in enumerate(across):
        go(hr.at[(quarter + j + 1) % QUARTERS], tr.at[j], (rr_s.at[j], rr_r.at[j]), device)
    for k, device in enumerate(along):
        go(hz.at[(chip + k + 1) % chips], cz.at[k], (zz_s.at[k], zz_r.at[k]), device)

    for copy in rest:
        copy.wait()
    slots = lax.broadcasted_iota(jnp.int32, (tok.shape[0], ret.shape[0]), 1)
    chosen = nn((slots == col_ref[...]).astype(low), ret[...])
    mix_ref[...] = (mid[...] + gate[:, 0:1] * chosen).astype(low)
    ka_ref[...] = a_sum[slow]
    kb_ref[...] = b_sum[fast]

    for j in range(QUARTERS - 1):
        landed(tr.at[j], (rr_s.at[j], rr_r.at[j]))
    for k in range(chips):
        total = wide(hr[quarter, k])
        for j in range(QUARTERS - 1):
            total = total + wide(tr[j, k])
        mr[k] = total.astype(low)
    for k, device in enumerate(along):
        go(mr.at[(chip + k + 1) % chips], cr.at[k], (rz_s.at[k], rz_r.at[k]), device)

    for k in range(chips - 1):
        landed(p_in.at[k], (pz_s.at[k], pz_r.at[k]))
    landed(e_in, (ps_s.at[1], ps_r.at[1]))
    total = wide(p_sum[chip])
    for k in range(chips - 1):
        total = total + wide(p_in[k])
    grads = own[...] + jnp.concatenate([total, wide(e_in[...])], axis=0)
    gt_ref[...] = gres[...] + norm_pull(grads, wide(tok[...]), gain_ref[0:1, :])

    for k in range(chips - 1):
        landed(cz.at[k], (zz_s.at[k], zz_r.at[k]))
    for t in range(QUARTERS):
        total = wide(hz[chip, t])
        for k in range(chips - 1):
            total = total + wide(cz[k, t])
        zs[t] = total.astype(low)
    for j, device in enumerate(across):
        go(zs.at[(quarter + j + 1) % QUARTERS], tz.at[j], (zr_s.at[j], zr_r.at[j]), device)
    for k in range(chips - 1):
        landed(cr.at[k], (rz_s.at[k], rz_r.at[k]))
    left = wide(mr[chip])
    for k in range(chips - 1):
        left = left + wide(cr[k])
    for j in range(QUARTERS - 1):
        landed(tz.at[j], (zr_s.at[j], zr_r.at[j]))
    right = wide(zs[quarter])
    for j in range(QUARTERS - 1):
        right = right + wide(tz[j])
    last[...] = jnp.concatenate([left, right], axis=1).astype(low)
    if classes > 1:
        for j, device in enumerate(above):
            go(last, above_in.at[j], (dh_s.at[j], dh_r.at[j]), device)
        total = wide(last[...])
        for j in range(classes - 1):
            landed(above_in.at[j], (dh_s.at[j], dh_r.at[j]))
            total = total + wide(above_in[j])
        gathered[quarter] = total.astype(low)
    else:
        gathered[quarter] = last[...]
    for j, device in enumerate(across):
        go(gathered.at[quarter], gathered.at[quarter], (da_s.at[j], da_r.at[j]), device)
    for j in range(QUARTERS - 1):
        landed(gathered.at[(quarter + QUARTERS - j - 1) % QUARTERS], (da_s.at[j], da_r.at[j]))
    for i, ref in enumerate((dq_ref, dk_ref, dv_ref, do_ref)):
        ref[...] = wide(gathered[:, :, i * width : (i + 1) * width])
    sm_ref[...] = wide(gathered[:, :, 4 * width :])
    for j in range(slows - 1):
        landed(la_hbm.at[j], (ea_s.at[j], ea_r.at[j]))
    for j in range(fasts - 1):
        landed(lb_hbm.at[j], (eb_s.at[j], eb_r.at[j]))
    for copy in pending:
        copy.wait_send()


def reduce_all(gains, col_slots, dense, prompt_part, near_part, own, gres, tokens, mid, gate, returned, gwin, ra, gwout, rb):
    chips = lax.axis_size("shard") // 2
    classes = lax.axis_size("rep") // QUARTERS
    slows, fasts = gwin.shape[:2]
    rows, width = mid.shape
    lines, lanes = dense.shape[3:]
    cut = 2 * width
    shape = jax.ShapeDtypeStruct
    sem = pltpu.SemaphoreType.DMA
    vm = pltpu.VMEM
    count, others = chips - 1, QUARTERS - 1
    ours = prompt_part.shape[2:]
    extra = max(classes - 1, 1)
    args = (gains, col_slots, dense, prompt_part, near_part, own, gres, tokens, mid, gate, returned, gwin, ra, gwout, rb)
    return pl.pallas_call(
        reduce_kernel,
        out_shape=(
            shape((rows, width), single), shape((rows, width), low),
            shape((QUARTERS, lines, width), single), shape((QUARTERS, lines, width), single),
            shape((QUARTERS, lines, width), single), shape((QUARTERS, lines, width), single),
            shape((QUARTERS, lines, TILE), single),
            shape(gwin.shape[2:], low), shape((slows - 1,) + gwin.shape[2:], low),
            shape(gwout.shape[2:], low), shape((fasts - 1,) + gwout.shape[2:], low),
        ),
        in_specs=[in_vmem] * 2 + [anywhere] * 13,
        out_specs=(in_vmem,) * 8 + (anywhere, in_vmem, anywhere),
        scratch_shapes=[
            vm((chips, QUARTERS, lines, lanes), low), vm((chips, QUARTERS, lines, lanes), low),
            vm((QUARTERS, chips, lines, cut), low), vm((chips, QUARTERS, lines, lanes - cut), low),
            vm((others, chips, lines, cut), low), vm((chips, lines, cut), low), vm((count, lines, cut), low),
            vm((count, QUARTERS, lines, lanes - cut), low), vm((QUARTERS, lines, lanes - cut), low),
            vm((others, lines, lanes - cut), low), vm((lines, lanes), low), vm((extra, lines, lanes), low),
            vm((QUARTERS, lines, lanes), low),
            vm((chips,) + ours, low), vm((chips,) + ours, low), vm((chips,) + ours, low), vm((count,) + ours, low),
            vm(near_part.shape, low), vm((rows, width), single), vm((rows, width), single), vm((rows, width), low),
            vm((rows, width), single), vm(gate.shape, single), vm(returned.shape, low),
            vm((slows,) + gwin.shape[2:], low), vm(ra.shape, low), vm((slows,) + gwin.shape[2:], low),
            vm((fasts,) + gwout.shape[2:], low), vm(rb.shape, low), vm((fasts,) + gwout.shape[2:], low),
            sem((12,)), sem((2,)), sem((2,)), sem((chips,)), sem((chips,)), sem((count,)), sem((count,)),
            sem((others,)), sem((others,)), sem((count,)), sem((count,)), sem((count,)), sem((count,)),
            sem((others,)), sem((others,)), sem((extra,)), sem((extra,)), sem((others,)), sem((others,)),
            sem((slows - 1,)), sem((slows - 1,)), sem((fasts - 1,)), sem((fasts - 1,)),
        ],
        compiler_params=pltpu.CompilerParams(collective_id=1, has_side_effects=True, vmem_limit_bytes=vmem_cap),
        cost_estimate=pl.CostEstimate(flops=0, bytes_accessed=200_000_000, transcendentals=0),
        name="reduce_all",
    )(*args)


def local(
    tokens,
    routes,
    slot_ids,
    w_query,
    w_key,
    w_value,
    w_output,
    w_router,
    norm_attn,
    norm_moe,
    rel_table,
    w_in,
    w_out,
    cotangent,
):
    shard_count = lax.axis_size("shard")
    token_rows, model_width = tokens.shape
    prompt_len = PR_DEV * shard_count
    weight_rows, expert_count = w_router.shape
    table_rows, head_count = rel_table.shape
    capacity = 2 * token_rows // expert_count
    slot_count = expert_count * capacity

    weights = jnp.stack([w_query, w_key, w_value, w_output]).reshape(4, QUARTERS, -1, model_width)
    small = jnp.concatenate(
        [w_router, norm_attn[:, None], norm_moe[:, None],
         jnp.pad(rel_table, ((0, weight_rows - table_rows), (0, 0)))], axis=1
    )
    small = jnp.pad(small, ((0, 0), (0, TILE - small.shape[1])))
    dispatch = routes * capacity + slot_ids

    weights, every_tok, small = gather_all(weights, tokens, small)
    weights = weights.reshape(4, model_width, model_width)
    small = small.reshape(model_width, TILE)
    bucket_row = jnp.asarray(np.tile(distance_buckets(table_rows * shard_count), (8, 1)), jnp.int32)
    normed, queries, keys, values, attended, lse, rev, mid, gate, gains, slots_out, grad_in = front(
        every_tok, tokens, weights, small, bucket_row, routes[:, None],
        jnp.broadcast_to(dispatch[None, :], (8, token_rows)), cotangent, slot_count,
    )
    by_chip = (shard_count // 2, 2, capacity, model_width)
    grad_back, result, grad_w_in, grad_w_out, router_grads = moe(
        slots_out.reshape(by_chip), grad_in.reshape(by_chip), small, w_in[0], w_out[0]
    )
    rep_count = lax.axis_size("rep")
    slows, fasts = rep_places()[3:]
    gwin = grad_w_in.reshape(slows, fasts, model_width // rep_count, -1)
    gwout = grad_w_out.reshape(slows, fasts, -1, model_width)
    col_slots = dispatch[:, None]
    dense, prompt_part, near_part, grad_own, grad_resid, returned, ra, rb = back(
        grad_back.reshape(slot_count, model_width), col_slots, mid, cotangent, gains, every_tok, weights,
        (normed, queries, keys, values, attended, lse, rev), bucket_row, router_grads,
        result.reshape(expert_count, capacity, model_width), gwin, gwout,
    )
    chips = shard_count // 2
    grad_tokens, mixed, gq, gk, gv, go, tail, ka, la, kb, lb = reduce_all(
        gains, col_slots, dense.reshape(chips, 2, QUARTERS, weight_rows // QUARTERS, -1),
        prompt_part.reshape(chips, 2, PR_DEV, model_width), near_part, grad_own, grad_resid, tokens, mid, gate,
        returned.reshape(slot_count, model_width), gwin, ra, gwout, rb,
    )
    total = lambda held, come: (held.astype(single) + jnp.sum(come.astype(single), axis=0))[None]
    tail = tail.reshape(weight_rows, TILE)
    return (
        mixed,
        grad_tokens,
        *(part.reshape(weight_rows, model_width) for part in (gq, gk, gv, go)),
        tail[:, :expert_count],
        tail[:, expert_count],
        tail[:, expert_count + 1],
        tail[:table_rows, expert_count + 2 : expert_count + 2 + head_count],
        total(ka, la),
        total(kb, lb),
    )


def solution(mesh):
    return jax.shard_map(
        local,
        mesh=mesh,
        in_specs=(
            P(("rep", "shard"), None),
            P(("rep", "shard")),
            P(("rep", "shard")),
            P("shard", None),
            P("shard", None),
            P("shard", None),
            P("shard", None),
            P("shard", None),
            P("shard"),
            P("shard"),
            P("shard", None),
            P("shard", None, None),
            P("shard", None, None),
            P(("rep", "shard"), None),
        ),
        out_specs=(
            P(("rep", "shard"), None),
            P(("rep", "shard"), None),
            P("shard", None),
            P("shard", None),
            P("shard", None),
            P("shard", None),
            P("shard", None),
            P("shard"),
            P("shard"),
            P("shard", None),
            P("shard", "rep", None),
            P("shard", "rep", None),
        ),
        check_vma=False,
    )
```

```python
import jax
import jax.numpy as jnp
import numpy as np
from jax import lax
from jax.experimental import pallas as pl
from jax.experimental.pallas import tpu as pltpu
from jax.sharding import PartitionSpec as P

PR_DEV = 128
TILE = 128
SPAN = 2 * TILE
BLOCK = 1536
QUARTERS = 4
far_before, far_after, causal_tile, hidden_tile, tile_kinds = 3, 4, 5, 6, 7
vmem_cap = 60 * 1024 * 1024
mesh_ids = pl.DeviceIdType.MESH
bucket_edges = (12, 16, 23, 32, 46, 64, 91)
norm_epsilon = 1e-06
masked_score = -1e30
low, single = jnp.bfloat16, jnp.float32
in_vmem = pl.BlockSpec(memory_space=pltpu.VMEM)
anywhere = pl.BlockSpec(memory_space=pl.ANY)


def inverse_rms(values):
    return lax.rsqrt(jnp.mean(values * values, axis=-1, keepdims=True) + norm_epsilon)


def norm_pull(grad, values, gain):
    scale = inverse_rms(values)
    pulled = grad * gain
    mean = jnp.mean(pulled * values, axis=-1, keepdims=True)
    return scale * pulled - values * (scale * scale * scale * mean)


def nt(left, right):
    return lax.dot_general(left, right, (((1,), (1,)), ((), ())), preferred_element_type=single)


def tn(left, right):
    return lax.dot_general(left, right, (((0,), (0,)), ((), ())), preferred_element_type=single)


def nn(left, right):
    return jnp.dot(left, right, preferred_element_type=single)


def thirds_of(values):
    first = values.astype(low)
    rest = values - first.astype(single)
    second = rest.astype(low)
    return first, second, (rest - second.astype(single)).astype(low)


def fill_tiles(tiles_ref, rev_row, low, high):
    spread = jnp.broadcast_to(rev_row, (TILE, 4 * TILE))
    rolled = pltpu.roll(spread, 0, 1, stride=1, stride_axis=0)
    keys = lax.broadcasted_iota(jnp.int32, (TILE, TILE), 0)
    rows = lax.broadcasted_iota(jnp.int32, (TILE, TILE), 1)
    tiles_ref[0] = rolled[:, TILE : 2 * TILE]
    tiles_ref[1] = rolled[:, :TILE]
    tiles_ref[2] = rolled[:, 3 * TILE :]
    tiles_ref[far_before] = jnp.broadcast_to(low, (TILE, TILE))
    tiles_ref[far_after] = jnp.broadcast_to(high, (TILE, TILE))
    tiles_ref[causal_tile] = jnp.where(keys <= rows, rolled[:, :TILE], masked_score)
    tiles_ref[hidden_tile] = jnp.full((TILE, TILE), masked_score, jnp.float32)


def prompt_tile(block, chunk, shard_id, block_count):
    if chunk == 0:
        gap = block - shard_id
        far = jnp.where(gap < 0, far_before, far_after)
        return jnp.where(jnp.abs(gap) <= 1, gap + 1, far)
    if chunk == 1 and block == block_count - 1:
        return jnp.where(shard_id % 2 == 0, 0, far_before)
    return far_before


def local_tile(block, chunk, shard_id):
    if block >= 2:
        return ((causal_tile, 0), (hidden_tile, causal_tile))[block - 2][chunk]
    kind = 0 if (block, chunk) == (1, 0) else far_before
    return jnp.where(shard_id % 2 == 1, kind, hidden_tile)


def prompt_grid(part, shard_id, block_count):
    return [
        [prompt_tile(2 * part + half, chunk, shard_id, block_count) for chunk in range(3)]
        for half in range(2)
    ]


def local_grid(part, shard_id):
    return [[local_tile(2 * part + half, chunk, shard_id) for chunk in range(2)] for half in range(2)]


def with_bias(scores, tiles_ref, grid):
    return jnp.concatenate(
        [
            jnp.concatenate(
                [
                    scores[i * TILE : (i + 1) * TILE, j * TILE : (j + 1) * TILE] + tiles_ref[kind]
                    for j, kind in enumerate(row)
                ],
                axis=1,
            )
            for i, row in enumerate(grid)
        ],
        axis=0,
    )


def fold8(values):
    return values.reshape(values.shape[0] // 8, 8, values.shape[1])


def head_mask(rows, side):
    lanes = lax.broadcasted_iota(jnp.int32, (rows, TILE), 1)
    return (lanes < TILE // 2) if side == 0 else (lanes >= TILE // 2)


def distance_buckets(bucket_count):
    steps = np.arange(4 * TILE)
    gap = -np.where(steps < 2 * TILE, steps, steps - 4 * TILE)
    size = np.abs(gap)
    far = sum((size >= edge).astype(np.int64) for edge in bucket_edges)
    exact = bucket_count // 4
    return np.where(gap > 0, bucket_count // 2, 0) + np.where(size < exact, size, exact + far)


def front_kernel(
    ints_ref, bucket_ref, cot_ref, wq_hbm, wk_hbm, wv_hbm, wo_hbm, tok_hbm, little_hbm,
    n_ref, q_ref, k_ref, v_ref, o_ref, lse_ref, rev_ref, mid_ref, gate_ref, col_ref, gain_ref, x_ref, gin_hbm,
    w_hbm, every_hbm, small_hbm,
    tiles, vt, sp, sl, ot, gbuf, w_ref, every_ref, small_ref, tok_ref, shard_w, little,
    gs, gr, loc, wz_s, wz_r, tz_s, tz_r, sz_s, sz_r, wr_s, wr_r, wt_s, wt_r, tt_s, tt_r, st_s, st_r, et_s, et_r,
):
    rep, chip, core, chips, quarter = places()
    along, across, twin = peer_lists()
    shards = chips * 2
    shard_id = chip * 2 + core
    rows, width = tok_ref.shape
    experts = shards
    blocks = every_ref.shape[0] // TILE - 4
    half = TILE // 2
    heads_held = rev_ref.shape[0]
    lines = shard_w.shape[1]
    rest_rows = rows - PR_DEV
    prompt_len = blocks * TILE
    others = [(rep, (shard_id + k) % shards) for k in range(1, shards)]

    def w_rows(source, side):
        return pl.ds(pl.multiple_of((source * 2 + side) * lines, lines), lines)

    def t_rows(source, side):
        return every_ref.at[pl.ds(pl.multiple_of((source * 2 + side) * PR_DEV, PR_DEV), PR_DEV)]

    loads = [
        pltpu.make_async_copy(source, shard_w.at[i], loc.at[i])
        for i, source in enumerate((wq_hbm, wk_hbm, wv_hbm, wo_hbm))
    ] + [pltpu.make_async_copy(tok_hbm, tok_ref, loc.at[4]), pltpu.make_async_copy(little_hbm, little, loc.at[5])]
    for copy in loads:
        copy.start()
    greeted = [twin] + along
    for device in across + [(rep, (chip + k) % chips * 2 + 1 - core) for k in range(1, chips)]:
        greeted.append(device)
    greet(greeted)
    started = []

    def go(source, target, sems, device):
        copy = send(source, target, sems, device)
        copy.start()
        started.append(copy)

    def landed(piece, sems):
        send(piece, piece, sems, twin).wait_recv()

    for copy in loads:
        copy.wait()
    mine = w_rows(chip, core)
    prompt, rest = tok_ref.at[pl.ds(0, PR_DEV)], tok_ref.at[pl.ds(PR_DEV, rest_rows)]
    for k, device in enumerate(along):
        go(shard_w.at[quarter], w_ref.at[quarter, mine], (wz_s.at[k], wz_r.at[k]), device)
        go(little, small_ref.at[mine], (sz_s.at[k], sz_r.at[k]), device)
    go(little, small_ref.at[mine], (st_s.at[0], st_r.at[0]), twin)
    go(rest, every_ref.at[pl.ds(prompt_len, rest_rows)], (et_s.at[0], et_r.at[0]), twin)
    go(prompt, t_rows(chip, core), (tt_s.at[0], tt_r.at[0]), twin)
    go(shard_w, w_ref.at[:, mine], (wt_s.at[0], wt_r.at[0]), twin)
    w_ref[:, mine, :] = shard_w[...]
    small_ref[mine, :] = little[...]
    every_ref[pl.ds(pl.multiple_of(shard_id * PR_DEV, PR_DEV), PR_DEV), :] = tok_ref[:PR_DEV, :]
    every_ref[prompt_len + rest_rows :, :] = tok_ref[PR_DEV:, :]
    ints = ints_ref[...].astype(single).T
    route_col = ints[:, 0:1].astype(jnp.int32)
    col_ref[...] = jnp.broadcast_to(ints[:, 1:2].astype(jnp.int32), col_ref.shape)
    slots = lax.broadcasted_iota(jnp.int32, (x_ref.shape[0], rows), 0)
    place = (slots == ints_ref[1:2, :]).astype(low)
    gbuf[...] = nn(place, cot_ref[...]).astype(low).reshape(gbuf.shape)
    own_g = pltpu.make_async_copy(gbuf.at[shard_id], gin_hbm.at[shard_id], loc.at[6])
    own_g.start()

    for k in range(1, chips):
        source = (chip + chips - k) % chips
        piece = w_ref.at[quarter, w_rows(source, core)]
        landed(piece, (wz_s.at[k - 1], wz_r.at[k - 1]))
        for j, device in enumerate(across):
            go(piece, piece, (wr_s.at[k - 1, j], wr_r.at[k - 1, j]), device)
        go(prompt, t_rows(chip, core), (tz_s.at[k - 1], tz_r.at[k - 1]), along[k - 1])
    for k in range(1, chips):
        source = (chip + chips - k) % chips
        piece = small_ref.at[w_rows(source, core)]
        landed(piece, (sz_s.at[k - 1], sz_r.at[k - 1]))
        go(piece, piece, (st_s.at[k], st_r.at[k]), twin)
    for k in range(1, chips):
        source = (chip + chips - k) % chips
        piece = t_rows(source, core)
        landed(piece, (tz_s.at[k - 1], tz_r.at[k - 1]))
        go(piece, piece, (tt_s.at[k], tt_r.at[k]), twin)
    for k, device in enumerate(others):
        go(gbuf.at[device[1]], gin_hbm.at[shard_id], (gs.at[k], gr.at[k]), device)
    for k in range(chips):
        source = (chip + chips - k) % chips
        landed(small_ref.at[w_rows(source, 1 - core)], (st_s.at[k], st_r.at[k]))
    writes = [pltpu.make_async_copy(small_ref, small_hbm, loc.at[7])]
    writes[0].start()

    small_t = small_ref[...].astype(single).T
    gain_attn = small_t[experts : experts + 1]
    gain_moe = small_t[experts + 1 : experts + 2]
    gain_ref[...] = jnp.concatenate([gain_attn, gain_moe, jnp.zeros((6, width), single)], axis=0)
    shard_rows = width // shards
    table_rows = 2 * TILE // 8 // shards
    owner = lax.broadcasted_iota(jnp.int32, (shards, shard_rows, 4 * TILE), 0)
    offset = lax.broadcasted_iota(jnp.int32, (shards, shard_rows, 4 * TILE), 1)
    held = jnp.where(offset < table_rows, owner * table_rows + offset, -1).reshape(width, 4 * TILE)
    hot = (held == bucket_ref[0:1, :]).astype(low)
    table_t = small_t[experts + 2 : experts + 2 + heads_held].astype(low)
    rev_ref[...] = nn(table_t, hot)

    for k in range(chips):
        source = (chip + chips - k) % chips
        landed(t_rows(source, 1 - core), (tt_s.at[k], tt_r.at[k]))
    landed(every_ref.at[pl.ds(prompt_len, rest_rows)], (et_s.at[0], et_r.at[0]))
    writes.append(pltpu.make_async_copy(every_ref, every_hbm, loc.at[8]))
    writes[-1].start()

    @pl.loop(0, every_ref.shape[0] // SPAN)
    def scale(part):
        span = pl.ds(pl.multiple_of(part * SPAN, SPAN), SPAN)
        values = every_ref[span, :].astype(single)
        n_ref[span, :] = (values * inverse_rms(values) * gain_attn).astype(low)

    for k in range(1, chips):
        source = (chip + chips - k) % chips
        for j in range(1, QUARTERS):
            piece = w_ref.at[(quarter + QUARTERS - j) % QUARTERS, w_rows(source, core)]
            landed(piece, (wr_s.at[k - 1, j - 1], wr_r.at[k - 1, j - 1]))
        piece = w_ref.at[:, w_rows(source, core)]
        go(piece, piece, (wt_s.at[k], wt_r.at[k]), twin)
    for k in range(chips):
        source = (chip + chips - k) % chips
        landed(w_ref.at[:, w_rows(source, 1 - core)], (wt_s.at[k], wt_r.at[k]))
    writes.append(pltpu.make_async_copy(w_ref, w_hbm, loc.at[9]))
    writes[-1].start()

    @pl.loop(0, every_ref.shape[0] // (2 * SPAN))
    def project(part):
        span = pl.ds(pl.multiple_of(part * 2 * SPAN, 2 * SPAN), 2 * SPAN)
        k_ref[span, :] = nn(n_ref[span, :], w_ref[1]).astype(low)
        v_ref[span, :] = nn(n_ref[span, :], w_ref[2]).astype(low)

    own = pl.ds(pl.multiple_of(shard_id * TILE, TILE), TILE)
    normed = jnp.concatenate([n_ref[own, :], n_ref[(blocks + 2) * TILE :, :]], axis=0)
    q_ref[...] = (nn(normed, w_ref[0]).astype(low) * jnp.asarray(0.125, low)).astype(low)

    @pl.loop(0, width // TILE)
    def pair_loop(pair):
        cols = pl.ds(pl.multiple_of(pair * TILE, TILE), TILE)
        vt[...] = v_ref[:, cols].T
        q_pair = q_ref[:, cols]
        for side in range(2):
            head = pair * 2 + side
            rev_row = rev_ref[pl.ds(head, 1), :]
            fill_tiles(tiles, rev_row, rev_row[:, SPAN - 1 : SPAN], rev_row[:, SPAN : SPAN + 1])
            q_head = jnp.where(head_mask(rows, side), q_pair, jnp.zeros_like(q_pair))
            top = jnp.full((8, rows), masked_score, single)
            for part in range(blocks // 2):
                keys = slice(part * SPAN, (part + 1) * SPAN)
                scores = with_bias(nt(k_ref[keys, cols], q_head), tiles, prompt_grid(part, shard_id, blocks))
                sp[keys, :] = scores
                top = jnp.maximum(top, jnp.max(fold8(scores), axis=0))
            top_local = top[:, PR_DEV:]
            for part in range(2):
                keys = slice(part * SPAN, (part + 1) * SPAN)
                held = slice((blocks // 2 + part) * SPAN, (blocks // 2 + part + 1) * SPAN)
                scores = with_bias(nt(k_ref[held, cols], q_head[PR_DEV:]), tiles, local_grid(part, shard_id))
                sl[keys, :] = scores
                top_local = jnp.maximum(top_local, jnp.max(fold8(scores), axis=0))
            top = jnp.max(jnp.concatenate([top[:, :PR_DEV], top_local], axis=1), axis=0, keepdims=True)
            total = jnp.zeros((8, rows), single)
            summed = jnp.zeros((half, rows), single)
            heads = slice(side * half, (side + 1) * half)
            for part in range(blocks // 2):
                keys = slice(part * SPAN, (part + 1) * SPAN)
                weights = jnp.exp(sp[keys, :] - top)
                total = total + jnp.sum(fold8(weights), axis=0)
                summed = summed + nn(vt[heads, keys], weights.astype(low))
            top_c = top[:, PR_DEV:]
            total_c = total[:, PR_DEV:]
            summed_c = summed[:, PR_DEV:]
            for part in range(2):
                keys = slice(part * SPAN, (part + 1) * SPAN)
                held = slice((blocks // 2 + part) * SPAN, (blocks // 2 + part + 1) * SPAN)
                weights = jnp.exp(sl[keys, :] - top_c)
                total_c = total_c + jnp.sum(fold8(weights), axis=0)
                summed_c = summed_c + nn(vt[heads, held], weights.astype(low))
            total = jnp.sum(jnp.concatenate([total[:, :PR_DEV], total_c], axis=1), axis=0, keepdims=True)
            summed = jnp.concatenate([summed[:, :PR_DEV], summed_c], axis=1)
            ot[heads, :] = summed / total
            lse_ref[pl.ds(head, 1), :] = top + jnp.log(total)
        o_ref[:, cols] = ot[...].T

    resid_mid = tok_ref[...].astype(single) + nn(o_ref[...].astype(low), w_ref[3])
    mid_ref[...] = resid_mid
    mid_low = (resid_mid * inverse_rms(resid_mid) * gain_moe).astype(low)
    probs = router_softmax(mid_low, small_ref[...], experts)
    lanes = lax.broadcasted_iota(jnp.int32, probs.shape, 1)
    gate = jnp.sum(jnp.where(lanes == route_col, probs, 0.0), axis=1, keepdims=True)
    gate_ref[...] = jnp.broadcast_to(gate, gate_ref.shape)
    x_ref[...] = nn(place, mid_low).astype(low)
    own_g.wait()
    for k in range(shards - 1):
        landed(gin_hbm.at[(shard_id + shards - k - 1) % shards], (gs.at[k], gr.at[k]))
    for copy in writes:
        copy.wait()
    for copy in started:
        copy.wait_send()


def router_softmax(rows_low, small, experts):
    logits = nn(rows_low, small)
    lanes = lax.broadcasted_iota(jnp.int32, logits.shape, 1)
    logits = jnp.where(lanes < experts, logits, masked_score)
    powers = jnp.exp(logits - jnp.max(logits, axis=1, keepdims=True))
    return powers / jnp.sum(powers, axis=1, keepdims=True)


def front(ints, bucket_row, cotangent, weights, tokens, small, slot_count):
    rows, width = tokens.shape
    shards = lax.axis_size("shard")
    chips, count = shards // 2, shards // 2 - 1
    keys = shards * PR_DEV + 2 * (rows - PR_DEV)
    lines = small.shape[0]
    shape = jax.ShapeDtypeStruct
    sem = pltpu.SemaphoreType.DMA
    vm = pltpu.VMEM
    return pl.pallas_call(
        front_kernel,
        out_shape=(
            shape((keys, width), low), shape((rows, width), low), shape((keys, width), low),
            shape((keys, width), low), shape((rows, width), single), shape((16, rows), single),
            shape((16, 4 * TILE), single), shape((rows, width), single), shape((rows, TILE), single),
            shape((rows, TILE), jnp.int32), shape((8, width), single), shape((slot_count, width), low),
            shape((shards, slot_count // shards, width), low), shape((4, width, width), low),
            shape((keys, width), low), shape((width, TILE), low),
        ),
        in_specs=[in_vmem] * 3 + [anywhere] * 6,
        out_specs=(in_vmem,) * 12 + (anywhere,) * 4,
        scratch_shapes=[
            vm((tile_kinds, TILE, TILE), single), vm((TILE, keys), low), vm((keys - 2 * SPAN, rows), single),
            vm((2 * SPAN, rows - TILE), single), vm((TILE, rows), single),
            vm((shards, slot_count // shards, width), low), vm((4, width, width), low), vm((keys, width), low),
            vm((width, TILE), low), vm((rows, width), low), vm((4, lines, width), low), vm((lines, TILE), low),
            sem((shards - 1,)), sem((shards - 1,)), sem((10,)), sem((count,)), sem((count,)), sem((count,)),
            sem((count,)), sem((count,)), sem((count,)), sem((count, 3)), sem((count, 3)), sem((chips,)), sem((chips,)),
            sem((chips,)), sem((chips,)), sem((chips,)), sem((chips,)), sem((1,)), sem((1,)),
        ],
        compiler_params=pltpu.CompilerParams(collective_id=2, has_side_effects=True, vmem_limit_bytes=vmem_cap),
        cost_estimate=pl.CostEstimate(flops=30_000_000_000, bytes_accessed=20_000_000, transcendentals=8_000_000),
        name="front",
    )(ints, bucket_row, cotangent, *weights, tokens, small)


def moe_kernel(
    x_ref, g_ref, small_ref, w_in_ref, w_out_ref,
    back_ref, out_ref, gwin_ref, gwout_ref, rg_ref,
    w_in, w_out, xin, gm, gg, hid, gpre, logit_grads, x_t, gwin, gwout,
    xs, xr, ms, mr, ws, ls, os_in, os_out,
):
    rep, chip, core, chips, quarter = places()
    experts = chips * 2
    here = chip * 2 + core
    pair_rows = 2 * xin.shape[2]
    hidden = w_in_ref.shape[1]
    block = BLOCK
    loads = [
        pltpu.make_async_copy(w_in_ref, w_in, ws.at[0]),
        pltpu.make_async_copy(w_out_ref, w_out, ws.at[1]),
    ]
    for copy in loads:
        copy.start()
    twin = (rep, chip * 2 + 1 - core)
    targets = [
        (k, side, (rep, chip_across(chip, k) * 2 + side)) for k in range(1, chips) for side in range(2)
    ]
    greet([twin] + [device for _, _, device in targets])
    sent = [send(x_ref.at[chip, 1 - core], xin.at[chip, core], (xs.at[0, 0], xr.at[0, core]), twin)]
    for k, side, device in targets:
        sent.append(
            send(x_ref.at[chip_across(chip, k), side], xin.at[chip, core], (xs.at[k, side], xr.at[k, core]), device)
        )
    for copy in sent[:5]:
        copy.start()
    xin[chip, core] = x_ref[chip, core]
    for copy in loads:
        copy.wait()

    def arrived(k, source, side):
        piece = xin.at[source, side]
        send(piece, piece, (xs.at[0, 0], xr.at[k, side]), twin).wait_recv()

    @pl.loop(0, chips)
    def chunk(k):
        source = chip_across(chip, k)

        @pl.when(k == 0)
        def _():
            arrived(0, chip, 1 - core)

        @pl.when(k > 0)
        def _():
            for side in range(2):
                arrived(k, source, side)

        rows = xin[source].reshape(pair_rows, xin.shape[3])
        grads = g_ref[source].reshape(pair_rows, xin.shape[3])
        probs = router_softmax(rows, small_ref[...], experts)
        lanes = lax.broadcasted_iota(jnp.int32, probs.shape, 1)
        gate = jnp.sum(jnp.where(lanes == here, probs, 0.0), axis=1, keepdims=True)
        gated = (gate * grads.astype(single)).astype(low)
        span = pl.ds(pl.multiple_of(source * pair_rows, pair_rows), pair_rows)
        gg[span, :] = gated
        pre = nn(rows, w_in[...])
        grad_hidden = nt(gated, w_out[...])
        square = pre * pre
        wave = jnp.tanh(0.7978845608028654 * pre * (1.0 + 0.044715 * square))
        left = 0.5 + 0.5 * wave
        active = (pre * left).astype(low)
        slope = left + (0.5 * pre) * (1.0 - wave * wave) * (0.7978845608028654 + 0.10703222440890037 * square)
        grad_pre = (grad_hidden * slope).astype(low)
        hid[span, :] = active
        gpre[span, :] = grad_pre
        out = nn(active, w_out[...]).astype(low)
        out_ref[source] = out.reshape(out_ref.shape[1:])
        grad_gate = jnp.sum(grads.astype(single) * out.astype(single), axis=1, keepdims=True)
        chosen = jnp.where(lanes == here, 1.0, 0.0)
        grad_logits = jnp.where(lanes < experts, gate * grad_gate * (chosen - probs), 0.0)
        logit_grads[span, :] = grad_logits
        router = small_ref[...]
        total = nt(grad_pre, w_in[...]) + sum(nt(part, router) for part in thirds_of(grad_logits))
        gm[source] = total.astype(low).reshape(gm.shape[1:])

        def reply(side, slot):
            return send(
                gm.at[source, side], back_ref.at[chip, core], (ms.at[k, slot], mr.at[k, core]), (rep, source * 2 + side)
            )

        @pl.when(k == 0)
        def _():
            for copy in sent[5:]:
                copy.start()
            reply(1 - core, 0).start()
            pltpu.make_async_copy(gm.at[chip, core], back_ref.at[chip, core], ls).start()

        @pl.when(k > 0)
        def _():
            for side in range(2):
                reply(side, side).start()

    every = xin[...].reshape(gg.shape)
    x_t[...] = every.T
    writes = []
    for part in range(hidden // block):
        cols = slice(part * block, (part + 1) * block)
        gwin[:, cols] = nn(x_t[...], gpre[:, cols]).astype(low)
        writes.append(pltpu.make_async_copy(gwin.at[:, cols], gwin_ref.at[:, cols], os_in.at[part]))
        writes[-1].start()
        gwout[cols, :] = tn(hid[:, cols], gg[...]).astype(low)
        writes.append(pltpu.make_async_copy(gwout.at[cols], gwout_ref.at[cols], os_out.at[part]))
        writes[-1].start()
    rg_ref[...] = sum(nn(x_t[...], part) for part in thirds_of(logit_grads[...]))
    pltpu.make_async_copy(gm.at[chip, core], back_ref.at[chip, core], ls).wait()

    def replied(k, source, side):
        piece = back_ref.at[source, side]
        send(piece, piece, (ms.at[0, 0], mr.at[k, side]), twin).wait_recv()

    replied(0, chip, 1 - core)
    for k in range(1, chips):
        for side in range(2):
            replied(k, chip_across(chip, k), side)
    for copy in sent:
        copy.wait_send()
    for copy in writes:
        copy.wait()
    send(gm.at[chip, 0], back_ref.at[chip, core], (ms.at[0, 0], mr.at[0, 0]), twin).wait_send()
    for k in range(1, chips):
        for side in range(2):
            send(gm.at[chip, 0], back_ref.at[chip, core], (ms.at[k, side], mr.at[0, 0]), twin).wait_send()


def moe(rows_out, grad_in, small, w_in, w_out):
    chips, _, cap, width = rows_out.shape
    slots = chips * 2 * cap
    hidden = w_in.shape[1]
    shape = jax.ShapeDtypeStruct
    pairs = pltpu.SemaphoreType.DMA
    strips = hidden // BLOCK
    return pl.pallas_call(
        moe_kernel,
        out_shape=(
            shape(rows_out.shape, low), shape(rows_out.shape, low), shape((width, hidden), low),
            shape((hidden, width), low), shape((width, TILE), single),
        ),
        in_specs=[in_vmem] * 3 + [anywhere] * 2,
        out_specs=(anywhere, in_vmem, anywhere, anywhere, in_vmem),
        scratch_shapes=[
            pltpu.VMEM((width, hidden), low), pltpu.VMEM((hidden, width), low),
            pltpu.VMEM(rows_out.shape, low), pltpu.VMEM(rows_out.shape, low), pltpu.VMEM((slots, width), low),
            pltpu.VMEM((slots, hidden), low), pltpu.VMEM((slots, hidden), low),
            pltpu.VMEM((slots, TILE), single), pltpu.VMEM((width, slots), low), pltpu.VMEM((width, hidden), low), pltpu.VMEM((hidden, width), low),
            pairs((chips, 2)), pairs((chips, 2)), pairs((chips, 2)), pairs((chips, 2)), pairs((2,)), pairs,
            pairs((strips,)), pairs((strips,)),
        ],
        compiler_params=pltpu.CompilerParams(collective_id=3, has_side_effects=True, vmem_limit_bytes=vmem_cap),
        cost_estimate=pl.CostEstimate(flops=40_000_000_000, bytes_accessed=40_000_000, transcendentals=3_000_000),
        name="moe",
    )(rows_out, grad_in, small, w_in, w_out)


def back_kernel(
    back_ref, col_ref, mid_ref, cot_ref, gain_ref, q_ref, k_ref, v_ref, o_ref,
    lse_ref, rev_ref, bucket_ref, rg_ref, every_hbm, w_hbm, n_hbm, out_hbm, gwin_hbm, gwout_hbm,
    dense_ref, p_ref, e_ref, own_ref, gres_ref, zo_ref, ret_hbm, ra_hbm, rb_hbm,
    tiles, sums, diag, kt, dqt, far_sums, dk_sum, dv_sum, g_ref, dq_ref, dk_ref, dv_ref, attn_gain,
    every_ref, w_ref, n_ref, o_grad, o_half, o_sum, o_in, loc, xs, xr, as_, ar, bs, br, os_, or_, oz_s, oz_r,
):
    shard_id = lax.axis_index("shard")
    shards = lax.axis_size("shard")
    rows, width = mid_ref.shape
    blocks = k_ref.shape[0] // TILE - 4
    half = TILE // 2
    experts = shards
    heads_held = rev_ref.shape[0]
    rep, slow, fast, slows, fasts = rep_places()
    _, chip, core, chips, _ = places()
    along, _, twin = peer_lists()
    loads = [
        pltpu.make_async_copy(w_hbm.at[3], w_ref.at[3], loc.at[0]),
        pltpu.make_async_copy(w_hbm.at[pl.ds(0, 3)], w_ref.at[pl.ds(0, 3)], loc.at[1]),
        pltpu.make_async_copy(n_hbm, n_ref, loc.at[2]),
        pltpu.make_async_copy(every_hbm, every_ref, loc.at[3]),
        pltpu.make_async_copy(out_hbm.at[shard_id], ret_hbm.at[shard_id], loc.at[4]),
    ]
    for copy in loads:
        copy.start()
    others = [(rep, (shard_id + k) % shards) for k in range(1, shards)]
    beside = [(slow * fasts + (fast + j) % fasts, shard_id) for j in range(1, fasts)]
    beyond = [((slow + j) % slows * fasts + fast, shard_id) for j in range(1, slows)]
    greet(others + beside + beyond)
    sent = [
        send(gwin_hbm.at[:, (fast + j + 1) % fasts], ra_hbm.at[j], (as_.at[j], ar.at[j]), device)
        for j, device in enumerate(beside)
    ] + [
        send(gwout_hbm.at[(slow + j + 1) % slows], rb_hbm.at[j], (bs.at[j], br.at[j]), device)
        for j, device in enumerate(beyond)
    ] + [
        send(out_hbm.at[device[1]], ret_hbm.at[shard_id], (xs.at[k], xr.at[k]), device)
        for k, device in enumerate(others)
    ]
    for copy in sent:
        copy.start()
    diag[...] = jnp.zeros_like(diag)
    far_sums[...] = jnp.zeros_like(far_sums)
    tile_rows = lax.broadcasted_iota(jnp.int32, (TILE, TILE), 0)
    tile_cols = lax.broadcasted_iota(jnp.int32, (TILE, TILE), 1)
    flip = (tile_rows + tile_cols == TILE - 1).astype(single)

    slots = lax.broadcasted_iota(jnp.int32, (rows, back_ref.shape[0]), 1)
    grad_mid = nn((slots == col_ref[:, 0:1]).astype(low), back_ref[...])
    resid_mid = mid_ref[...]
    grad_gain_moe = jnp.sum(grad_mid * resid_mid * inverse_rms(resid_mid), axis=0, keepdims=True)
    grad_resid = cot_ref[...].astype(single) + norm_pull(grad_mid, resid_mid, gain_ref[1:2, :])
    gres_ref[...] = grad_resid
    grad_attn = grad_resid.astype(low)
    loads[0].wait()
    g_ref[...] = nt(grad_attn, w_ref[3]).astype(low)
    o_grad[...] = tn(o_ref[...].astype(low), grad_attn).reshape(o_grad.shape).astype(low)
    o_halves = [send(o_grad.at[2 * k + 1 - core], o_half.at[k], (os_.at[k], or_.at[k]), twin) for k in range(chips)]
    o_sends = [
        send(o_sum.at[(chip + k + 1) % chips], o_in.at[k], (oz_s.at[k], oz_r.at[k]), device)
        for k, device in enumerate(along)
    ]
    for copy in o_halves:
        copy.start()

    @pl.loop(0, width // TILE)
    def pair_loop(pair):
        cols = pl.ds(pl.multiple_of(pair * TILE, TILE), TILE)
        kt[...] = k_ref[:, cols].T
        q_pair = q_ref[:, cols]
        g_pair = g_ref[:, cols]
        delta_t = (g_pair.astype(single) * o_ref[:, cols]).T
        for side in range(2):
            head = pair * 2 + side
            heads = slice(side * half, (side + 1) * half)
            rev_row = rev_ref[pl.ds(head, 1), :]
            fill_tiles(tiles, rev_row, rev_row[:, SPAN - 1 : SPAN], rev_row[:, SPAN : SPAN + 1])
            sums[...] = jnp.zeros_like(sums)
            mask = head_mask(rows, side)
            q_head = jnp.where(mask, q_pair, jnp.zeros_like(q_pair))
            g_head = jnp.where(mask, g_pair, jnp.zeros_like(g_pair))
            delta = jnp.sum(delta_t[heads, :], axis=0, keepdims=True)
            log_total = lse_ref[pl.ds(head, 1), :]

            def block_grads(part, first, grid):
                keys = slice(part * SPAN, (part + 1) * SPAN)
                q_rows, g_rows = q_head[first:], g_head[first:]
                scores = with_bias(nt(k_ref[keys, cols], q_rows), tiles, grid)
                weights = jnp.exp(scores - log_total[:, first:])
                grad_weights = nt(v_ref[keys, cols], g_rows)
                grad_scores = weights * (grad_weights - delta[:, first:])
                for i, row in enumerate(grid):
                    for j, kind in enumerate(row):
                        sums[kind] += grad_scores[i * TILE : (i + 1) * TILE, j * TILE : (j + 1) * TILE]
                raw = grad_scores.astype(low)
                dk = nn(raw, q_rows)
                dv = nn(weights.astype(low), g_rows)
                if side == 0:
                    dk_sum[keys, :] = dk
                    dv_sum[keys, :] = dv
                else:
                    dk_ref[keys, cols] = (dk_sum[keys, :] + dk).astype(low)
                    dv_ref[keys, cols] = (dv_sum[keys, :] + dv).astype(low)
                return nn(kt[heads, keys], raw)

            dq = jnp.zeros((half, rows), single)
            for part in range(blocks // 2):
                dq = dq + block_grads(part, 0, prompt_grid(part, shard_id, blocks))
            dq_c = dq[:, PR_DEV:]
            for part in range(2):
                dq_c = dq_c + block_grads(blocks // 2 + part, PR_DEV, local_grid(part, shard_id))
            dqt[heads, :] = jnp.concatenate([dq[:, :PR_DEV], dq_c], axis=1)
            near = jnp.concatenate(
                [sums[1] + sums[causal_tile], sums[0], jnp.zeros((TILE, TILE), single), sums[2]], axis=1
            )
            flipped = jnp.dot(flip, near, precision=lax.Precision.HIGHEST, preferred_element_type=single)
            rolled = pltpu.roll(flipped, 3 * TILE + 1, 1, stride=1, stride_axis=0)
            diag[pl.ds(head, 1), :] = jnp.sum(rolled, axis=0, keepdims=True)
            far_sums[pl.ds(head, 1), :] = jnp.concatenate(
                [jnp.sum(sums[far_before], axis=0, keepdims=True), jnp.sum(sums[far_after], axis=0, keepdims=True)],
                axis=1,
            )
        dq_ref[:, cols] = (dqt[...].T * 0.125).astype(low)

        @pl.when(pair == 0)
        def _():
            for k in range(chips):
                o_halves[k].wait_recv()
                o_sum[k] = (o_grad[2 * k + core].astype(single) + o_half[k].astype(single)).astype(low)
            for copy in o_sends:
                copy.start()

    lanes = lax.broadcasted_iota(jnp.int32, (heads_held, 4 * TILE), 1)
    before = jnp.sum(far_sums[:, :TILE], axis=1, keepdims=True)
    after = jnp.sum(far_sums[:, TILE:], axis=1, keepdims=True)
    by_gap = diag[...] + jnp.where(lanes == SPAN - 1, before, 0.0) + jnp.where(lanes == SPAN, after, 0.0)
    shard_rows = width // shards
    table_rows = 2 * TILE // 8 // shards
    owner = lax.broadcasted_iota(jnp.int32, (shards, shard_rows, 4 * TILE), 0)
    offset = lax.broadcasted_iota(jnp.int32, (shards, shard_rows, 4 * TILE), 1)
    held = jnp.where(offset < table_rows, owner * table_rows + offset, -1).reshape(width, 4 * TILE)
    hot = (held == bucket_ref[0:1, :]).astype(low)
    grad_table = sum(nt(part, hot) for part in thirds_of(by_gap))

    attn_gain[...] = jnp.zeros_like(attn_gain)
    for copy in loads[1:]:
        copy.wait()
    own = pl.ds(pl.multiple_of(shard_id * TILE, TILE), TILE)
    tail = slice((blocks + 2) * TILE, (blocks + 4) * TILE)
    normed = jnp.concatenate([n_ref[own, :], n_ref[tail, :]], axis=0)
    dense_ref[:, :width] = tn(normed, dq_ref[...]).astype(low)
    grad_own = nt(dq_ref[...], w_ref[0])
    values = jnp.concatenate([every_ref[own, :], every_ref[tail, :]], axis=0).astype(single)
    attn_gain[...] += jnp.sum(fold8(grad_own * (values * inverse_rms(values))), axis=0)
    own_ref[...] = grad_own

    def pull_rows(part):
        span = pl.ds(pl.multiple_of(part * SPAN, SPAN), SPAN)
        values = every_ref[span, :].astype(single)
        grads = nt(dk_ref[span, :], w_ref[1]) + nt(dv_ref[span, :], w_ref[2])
        attn_gain[...] += jnp.sum(fold8(grads * (values * inverse_rms(values))), axis=0)
        return grads

    @pl.loop(0, blocks // 2)
    def pull_prompt(part):
        p_ref[pl.ds(pl.multiple_of(part * SPAN, SPAN), SPAN), :] = pull_rows(part).astype(low)

    e_ref[...] = pull_rows(blocks // 2).astype(low)
    own_ref[PR_DEV:, :] += pull_rows(blocks // 2 + 1)

    @pl.loop(0, width // SPAN)
    def outer(part):
        cols = pl.ds(pl.multiple_of(part * SPAN, SPAN), SPAN)
        k_cols = pl.ds(pl.multiple_of(width + part * SPAN, SPAN), SPAN)
        v_cols = pl.ds(pl.multiple_of(2 * width + part * SPAN, SPAN), SPAN)
        dense_ref[:, k_cols] = tn(n_ref[...], dk_ref[:, cols]).astype(low)
        dense_ref[:, v_cols] = tn(n_ref[...], dv_ref[:, cols]).astype(low)

    small_t = jnp.concatenate(
        [
            jnp.zeros((experts, width), single), jnp.sum(attn_gain[...], axis=0, keepdims=True), grad_gain_moe,
            grad_table, jnp.zeros((TILE - experts - 2 - heads_held, width), single),
        ],
        axis=0,
    )
    dense_ref[:, 3 * width :] = (small_t.T + rg_ref[...]).astype(low)
    o_total = o_sum[chip].astype(single)
    for k in range(chips - 1):
        o_sends[k].wait_recv()
        o_total = o_total + o_in[k].astype(single)
    zo_ref[...] = o_total.astype(low)
    for copy in o_halves + o_sends:
        copy.wait_send()
    for k in range(shards - 1):
        piece = ret_hbm.at[(shard_id + shards - k - 1) % shards]
        send(piece, piece, (xs.at[k], xr.at[k]), others[0]).wait_recv()
    for j in range(fasts - 1):
        send(ra_hbm.at[j], ra_hbm.at[j], (as_.at[j], ar.at[j]), others[0]).wait_recv()
    for j in range(slows - 1):
        send(rb_hbm.at[j], rb_hbm.at[j], (bs.at[j], br.at[j]), others[0]).wait_recv()
    for copy in sent:
        copy.wait_send()


def back(
    returned, col_slots, mid, cotangent, gains, every_tok, weights, kept, bucket_row, router_grads, result, gwin, gwout
):
    rows, width = mid.shape
    normed, queries, keys, values, attended, lse, rev = kept
    count = keys.shape[0]
    shards = result.shape[0]
    slows, fasts = gwin.shape[:2]
    chips, lines = shards // 2, width // shards
    shape = jax.ShapeDtypeStruct
    pairs = pltpu.SemaphoreType.DMA
    args = (
        returned, col_slots, mid, cotangent, gains, queries, keys, values, attended, lse, rev, bucket_row,
        router_grads, every_tok, weights, normed, result, gwin, gwout,
    )
    return pl.pallas_call(
        back_kernel,
        out_shape=(
            shape((width, 3 * width + TILE), low), shape((count - 2 * SPAN, width), low), shape((SPAN, width), low),
            shape((rows, width), single), shape((rows, width), single), shape((lines, width), low),
            shape(result.shape, low),
            shape((fasts - 1, slows) + gwin.shape[2:], low), shape((slows - 1, fasts) + gwout.shape[2:], low),
        ),
        in_specs=[in_vmem] * 13 + [anywhere] * 6,
        out_specs=(in_vmem,) * 6 + (anywhere,) * 3,
        scratch_shapes=[
            pltpu.VMEM((tile_kinds, TILE, TILE), single), pltpu.VMEM((tile_kinds, TILE, TILE), single),
            pltpu.VMEM((16, 4 * TILE), single), pltpu.VMEM((TILE, count), low), pltpu.VMEM((TILE, rows), single),
            pltpu.VMEM((16, 2 * TILE), single), pltpu.VMEM((count, TILE), single), pltpu.VMEM((count, TILE), single),
            pltpu.VMEM((rows, width), low), pltpu.VMEM((rows, width), low), pltpu.VMEM((count, width), low),
            pltpu.VMEM((count, width), low), pltpu.VMEM((8, width), single),
            pltpu.VMEM(every_tok.shape, low), pltpu.VMEM(weights.shape, low), pltpu.VMEM(normed.shape, low),
            pltpu.VMEM((shards, lines, width), low), pltpu.VMEM((chips, lines, width), low),
            pltpu.VMEM((chips, lines, width), low), pltpu.VMEM((chips - 1, lines, width), low),
            pairs((5,)), pairs((shards - 1,)), pairs((shards - 1,)), pairs((fasts - 1,)), pairs((fasts - 1,)),
            pairs((slows - 1,)), pairs((slows - 1,)), pairs((chips,)), pairs((chips,)), pairs((chips - 1,)),
            pairs((chips - 1,)),
        ],
        compiler_params=pltpu.CompilerParams(collective_id=4, has_side_effects=True, vmem_limit_bytes=vmem_cap),
        cost_estimate=pl.CostEstimate(flops=60_000_000_000, bytes_accessed=40_000_000, transcendentals=8_000_000),
        name="back",
    )(*args)


def places():
    rep, shard = lax.axis_index("rep"), lax.axis_index("shard")
    return rep, shard // 2, shard % 2, lax.axis_size("shard") // 2, rep % QUARTERS


def peer_lists():
    rep, chip, core, chips, quarter = places()
    along = [(rep, (chip + k) % chips * 2 + core) for k in range(1, chips)]
    across = [(rep - quarter + (quarter + j) % QUARTERS, chip * 2 + core) for j in range(1, QUARTERS)]
    twin = (rep, chip * 2 + 1 - core)
    return along, across, twin


def chip_across(chip, k):
    partner, bit = 0, 1
    while bit < lax.axis_size("shard") // 2:
        partner = partner + bit * ((chip // bit + k // bit) % 2)
        bit = bit * 2
    return partner


def greet(devices):
    barrier = pltpu.get_barrier_semaphore()
    for device in devices:
        pl.semaphore_signal(barrier, inc=1, device_id=device, device_id_type=mesh_ids)
    pl.semaphore_wait(barrier, len(devices))


def send(source, target, sems, device):
    return pltpu.make_async_remote_copy(
        src_ref=source, dst_ref=target, send_sem=sems[0], recv_sem=sems[1],
        device_id=device, device_id_type=mesh_ids,
    )


def rep_places():
    rep, reps = lax.axis_index("rep"), lax.axis_size("rep")
    fasts = QUARTERS if reps % (QUARTERS * QUARTERS) == 0 else 2
    return rep, rep // fasts, rep % fasts, reps // fasts, fasts


def reduce_kernel(
    gain_ref, col_ref, d_hbm, p_hbm, e_hbm, own_hbm, gres_hbm, tok_hbm, mid_hbm, gate_hbm, ret_hbm,
    gwin_hbm, ra_hbm, gwout_hbm, rb_hbm, zo_hbm,
    gt_ref, mix_ref, gathered_ref, ka_ref, la_hbm, kb_ref, lb_hbm,
    d_own, half, hr, hz, tr, mr, cr, cz, zs, tz, last, above_in, gathered,
    p_own, p_half, p_sum, p_in, e_in, own, gres, tok, mid, gate, ret,
    a_own, a_in, a_sum, b_own, b_in, b_sum, zo,
    loc, ps_s, ps_r, ds_s, ds_r, pz_s, pz_r, rr_s, rr_r, rz_s, rz_r, zz_s, zz_r, zr_s, zr_r, dh_s, dh_r,
    da_s, da_r, ea_s, ea_r, eb_s, eb_r,
):
    rep, chip, core, chips, quarter = places()
    along, across, twin = peer_lists()
    _, slow, fast, slows, fasts = rep_places()
    classes = lax.axis_size("rep") // QUARTERS
    here = chip * 2 + core
    beside = [(slow * fasts + (fast + j) % fasts, here) for j in range(1, fasts)]
    beyond = [((slow + j) % slows * fasts + fast, here) for j in range(1, slows)]
    above = [((rep // QUARTERS + k) % classes * QUARTERS + quarter, here) for k in range(1, classes)]
    width = gain_ref.shape[1]
    cut = hr.shape[3]
    wide = lambda ref_value: ref_value.astype(single)
    pending = []

    def load(source, target, index):
        copy = pltpu.make_async_copy(source, target, loc.at[index])
        copy.start()
        return copy

    def go(source, target, sems, device):
        copy = send(source, target, sems, device)
        copy.start()
        pending.append(copy)

    def landed(piece, sems):
        send(piece, piece, sems, twin).wait_recv()

    experts_in = [
        load(gwin_hbm.at[:, fast], a_own, 0), load(ra_hbm, a_in, 1),
        load(gwout_hbm.at[slow], b_own, 2), load(rb_hbm, b_in, 3),
    ]
    halves = [load(p_hbm.at[:, core], p_own, 4), load(d_hbm.at[:, core], d_own, 5)]
    rest = [
        load(ret_hbm, ret, 6), load(mid_hbm, mid, 7), load(gate_hbm, gate, 8), load(own_hbm, own, 9),
        load(gres_hbm, gres, 10), load(tok_hbm, tok, 11), load(zo_hbm, zo, 12),
    ]
    greets = [twin] + along
    for device in across + beside + beyond + above:
        greets.append(device)
    greet(greets)
    go(p_hbm.at[:, 1 - core], p_half, (ps_s.at[0], ps_r.at[0]), twin)
    for k in range(chips):
        go(d_hbm.at[k, 1 - core], half.at[k], (ds_s.at[k], ds_r.at[k]), twin)
    go(e_hbm, e_in, (ps_s.at[1], ps_r.at[1]), twin)

    for copy in experts_in:
        copy.wait()
    for t in range(slows):
        total = wide(a_own[t])
        for j in range(fasts - 1):
            total = total + wide(a_in[j, t])
        a_sum[t] = total.astype(low)
    for t in range(fasts):
        total = wide(b_own[t])
        for j in range(slows - 1):
            total = total + wide(b_in[j, t])
        b_sum[t] = total.astype(low)
    for j, device in enumerate(beyond):
        go(a_sum.at[(slow + j + 1) % slows], la_hbm.at[j], (ea_s.at[j], ea_r.at[j]), device)
    for j, device in enumerate(beside):
        go(b_sum.at[(fast + j + 1) % fasts], lb_hbm.at[j], (eb_s.at[j], eb_r.at[j]), device)

    halves[0].wait()
    landed(p_half, (ps_s.at[0], ps_r.at[0]))
    for k in range(chips):
        p_sum[k] = (wide(p_own[k]) + wide(p_half[k])).astype(low)
    for k, device in enumerate(along):
        go(p_sum.at[(chip + k + 1) % chips], p_in.at[k], (pz_s.at[k], pz_r.at[k]), device)
    halves[1].wait()
    for k in range(chips):
        landed(half.at[k], (ds_s.at[k], ds_r.at[k]))
        for t in range(QUARTERS):
            total = (wide(d_own[k, t]) + wide(half[k, t])).astype(low)
            hr[t, k] = total[:, :cut]
            hz[k, t] = total[:, cut:]
    for j, device in enumerate(across):
        go(hr.at[(quarter + j + 1) % QUARTERS], tr.at[j], (rr_s.at[j], rr_r.at[j]), device)
    for k, device in enumerate(along):
        go(hz.at[(chip + k + 1) % chips], cz.at[k], (zz_s.at[k], zz_r.at[k]), device)

    for copy in rest:
        copy.wait()
    slots = lax.broadcasted_iota(jnp.int32, (tok.shape[0], ret.shape[0]), 1)
    chosen = nn((slots == col_ref[:, 0:1]).astype(low), ret[...])
    mix_ref[...] = (mid[...] + gate[:, 0:1] * chosen).astype(low)
    ka_ref[...] = a_sum[slow]
    kb_ref[...] = b_sum[fast]

    for j in range(QUARTERS - 1):
        landed(tr.at[j], (rr_s.at[j], rr_r.at[j]))
    for k in range(chips):
        total = wide(hr[quarter, k])
        for j in range(QUARTERS - 1):
            total = total + wide(tr[j, k])
        mr[k] = total.astype(low)
    for k, device in enumerate(along):
        go(mr.at[(chip + k + 1) % chips], cr.at[k], (rz_s.at[k], rz_r.at[k]), device)

    for k in range(chips - 1):
        landed(p_in.at[k], (pz_s.at[k], pz_r.at[k]))
    landed(e_in, (ps_s.at[1], ps_r.at[1]))
    total = wide(p_sum[chip])
    for k in range(chips - 1):
        total = total + wide(p_in[k])
    grads = own[...] + jnp.concatenate([total, wide(e_in[...])], axis=0)
    gt_ref[...] = gres[...] + norm_pull(grads, wide(tok[...]), gain_ref[0:1, :])

    for k in range(chips - 1):
        landed(cz.at[k], (zz_s.at[k], zz_r.at[k]))
    for t in range(QUARTERS):
        total = wide(hz[chip, t])
        for k in range(chips - 1):
            total = total + wide(cz[k, t])
        zs[t] = jnp.concatenate([total.astype(low), zo[t]], axis=1)
    for j, device in enumerate(across):
        go(zs.at[(quarter + j + 1) % QUARTERS], tz.at[j], (zr_s.at[j], zr_r.at[j]), device)
    for k in range(chips - 1):
        landed(cr.at[k], (rz_s.at[k], rz_r.at[k]))
    left = wide(mr[chip])
    for k in range(chips - 1):
        left = left + wide(cr[k])
    for j in range(QUARTERS - 1):
        landed(tz.at[j], (zr_s.at[j], zr_r.at[j]))
    right = wide(zs[quarter])
    for j in range(QUARTERS - 1):
        right = right + wide(tz[j])
    last[...] = jnp.concatenate([left, right], axis=1).astype(low)
    if classes > 1:
        for j, device in enumerate(above):
            go(last, above_in.at[j], (dh_s.at[j], dh_r.at[j]), device)
        total = wide(last[...])
        for j in range(classes - 1):
            landed(above_in.at[j], (dh_s.at[j], dh_r.at[j]))
            total = total + wide(above_in[j])
        gathered[quarter] = total.astype(low)
    else:
        gathered[quarter] = last[...]
    for j, device in enumerate(across):
        go(gathered.at[quarter], gathered.at[quarter], (da_s.at[j], da_r.at[j]), device)
    for j in range(QUARTERS - 1):
        landed(gathered.at[(quarter + QUARTERS - j - 1) % QUARTERS], (da_s.at[j], da_r.at[j]))
    gathered_ref[...] = gathered[...]
    for j in range(slows - 1):
        landed(la_hbm.at[j], (ea_s.at[j], ea_r.at[j]))
    for j in range(fasts - 1):
        landed(lb_hbm.at[j], (eb_s.at[j], eb_r.at[j]))
    for copy in pending:
        copy.wait_send()


def reduce_all(gains, col_slots, dense, prompt_part, near_part, own, gres, tokens, mid, gate, returned, gwin, ra, gwout, rb, zo):
    chips = lax.axis_size("shard") // 2
    classes = lax.axis_size("rep") // QUARTERS
    slows, fasts = gwin.shape[:2]
    rows, width = mid.shape
    lines, lanes = dense.shape[3:]
    cut, full = 2 * width, 4 * width + TILE
    shape = jax.ShapeDtypeStruct
    sem = pltpu.SemaphoreType.DMA
    vm = pltpu.VMEM
    count, others = chips - 1, QUARTERS - 1
    ours = prompt_part.shape[2:]
    extra = max(classes - 1, 1)
    args = (gains, col_slots, dense, prompt_part, near_part, own, gres, tokens, mid, gate, returned, gwin, ra, gwout, rb, zo)
    return pl.pallas_call(
        reduce_kernel,
        out_shape=(
            shape((rows, width), single), shape((rows, width), low),
            shape((QUARTERS, lines, full), low),
            shape(gwin.shape[2:], low), shape((slows - 1,) + gwin.shape[2:], low),
            shape(gwout.shape[2:], low), shape((fasts - 1,) + gwout.shape[2:], low),
        ),
        in_specs=[in_vmem] * 2 + [anywhere] * 14,
        out_specs=(in_vmem,) * 4 + (anywhere, in_vmem, anywhere),
        scratch_shapes=[
            vm((chips, QUARTERS, lines, lanes), low), vm((chips, QUARTERS, lines, lanes), low),
            vm((QUARTERS, chips, lines, cut), low), vm((chips, QUARTERS, lines, lanes - cut), low),
            vm((others, chips, lines, cut), low), vm((chips, lines, cut), low), vm((count, lines, cut), low),
            vm((count, QUARTERS, lines, lanes - cut), low), vm((QUARTERS, lines, full - cut), low),
            vm((others, lines, full - cut), low), vm((lines, full), low), vm((extra, lines, full), low),
            vm((QUARTERS, lines, full), low),
            vm((chips,) + ours, low), vm((chips,) + ours, low), vm((chips,) + ours, low), vm((count,) + ours, low),
            vm(near_part.shape, low), vm((rows, width), single), vm((rows, width), single), vm((rows, width), low),
            vm((rows, width), single), vm(gate.shape, single), vm(returned.shape, low),
            vm((slows,) + gwin.shape[2:], low), vm(ra.shape, low), vm((slows,) + gwin.shape[2:], low),
            vm((fasts,) + gwout.shape[2:], low), vm(rb.shape, low), vm((fasts,) + gwout.shape[2:], low),
            vm(zo.shape, low), sem((13,)), sem((2,)), sem((2,)), sem((chips,)), sem((chips,)), sem((count,)), sem((count,)),
            sem((others,)), sem((others,)), sem((count,)), sem((count,)), sem((count,)), sem((count,)),
            sem((others,)), sem((others,)), sem((extra,)), sem((extra,)), sem((others,)), sem((others,)),
            sem((slows - 1,)), sem((slows - 1,)), sem((fasts - 1,)), sem((fasts - 1,)),
        ],
        compiler_params=pltpu.CompilerParams(collective_id=1, has_side_effects=True, vmem_limit_bytes=vmem_cap),
        cost_estimate=pl.CostEstimate(flops=0, bytes_accessed=200_000_000, transcendentals=0),
        name="reduce_all",
    )(*args)


def finish_kernel(ka_ref, la_ref, kb_ref, lb_ref, g_ref, small_ref, *outs):
    ea_ref, eb_ref, q_ref, k_ref, v_ref, o_ref, router_ref, attn_ref, moe_ref, table_ref = outs
    width = q_ref.shape[2]
    experts = router_ref.shape[1]
    ea_ref[...] = ka_ref[...].astype(single) + jnp.sum(la_ref[...].astype(single), axis=0)
    eb_ref[...] = kb_ref[...].astype(single) + jnp.sum(lb_ref[...].astype(single), axis=0)
    starts = (0, width, 2 * width, 3 * width + TILE)
    for start, ref in zip(starts, (q_ref, k_ref, v_ref, o_ref)):
        ref[...] = g_ref[:, :, start : start + width].astype(single)

    @pl.when(pl.program_id(0) == 0)
    def _():
        small = small_ref[...].astype(single)
        router_ref[...] = small[:, :experts]
        turned = small.T
        attn_ref[...] = turned[experts : experts + 1]
        moe_ref[...] = turned[experts + 1 : experts + 2]
        table_ref[...] = small[: table_ref.shape[0], experts + 2 : experts + 2 + table_ref.shape[1]]


def finish(ka, la, kb, lb, gathered, experts, table_rows, heads):
    shape = jax.ShapeDtypeStruct
    _, lines, full = gathered.shape
    width = kb.shape[1]
    rows = QUARTERS * lines
    small = gathered[:, :, 3 * width : 3 * width + TILE].reshape(rows, TILE)
    steps = QUARTERS
    a_cols, b_rows = ka.shape[1] // steps, kb.shape[0] // steps
    part = pl.BlockSpec((1, lines, width), lambda i: (i, 0, 0))
    once = lambda *dims: pl.BlockSpec(dims, lambda i: (0,) * len(dims))
    return pl.pallas_call(
        finish_kernel,
        grid=(steps,),
        out_shape=(
            shape(ka.shape, single), shape(kb.shape, single), *(shape((QUARTERS, lines, width), single),) * 4,
            shape((rows, experts), single), shape((1, rows), single), shape((1, rows), single),
            shape((table_rows, heads), single),
        ),
        in_specs=[
            pl.BlockSpec((ka.shape[0], a_cols), lambda i: (0, i)),
            pl.BlockSpec((la.shape[0], ka.shape[0], a_cols), lambda i: (0, 0, i)),
            pl.BlockSpec((b_rows, width), lambda i: (i, 0)),
            pl.BlockSpec((lb.shape[0], b_rows, width), lambda i: (0, i, 0)),
            pl.BlockSpec((1, lines, full), lambda i: (i, 0, 0)), once(rows, TILE),
        ],
        out_specs=(
            pl.BlockSpec((ka.shape[0], a_cols), lambda i: (0, i)), pl.BlockSpec((b_rows, width), lambda i: (i, 0)),
            part, part, part, part, once(rows, experts), once(1, rows), once(1, rows), once(table_rows, heads),
        ),
        compiler_params=pltpu.CompilerParams(vmem_limit_bytes=vmem_cap),
        cost_estimate=pl.CostEstimate(flops=0, bytes_accessed=12_000_000, transcendentals=0),
        name="finish",
    )(ka, la, kb, lb, gathered, small)


def local(
    tokens,
    routes,
    slot_ids,
    w_query,
    w_key,
    w_value,
    w_output,
    w_router,
    norm_attn,
    norm_moe,
    rel_table,
    w_in,
    w_out,
    cotangent,
):
    shard_count = lax.axis_size("shard")
    token_rows, model_width = tokens.shape
    prompt_len = PR_DEV * shard_count
    weight_rows, expert_count = w_router.shape
    table_rows, head_count = rel_table.shape
    capacity = 2 * token_rows // expert_count
    slot_count = expert_count * capacity

    small = jnp.concatenate(
        [w_router, norm_attn[:, None], norm_moe[:, None],
         jnp.pad(rel_table, ((0, weight_rows - table_rows), (0, 0)))], axis=1
    )
    small = jnp.pad(small, ((0, 0), (0, TILE - small.shape[1])))
    dispatch = routes * capacity + slot_ids

    ints = jnp.concatenate([routes[None], dispatch[None], jnp.zeros((6, token_rows), jnp.int32)])
    bucket_row = jnp.asarray(np.tile(distance_buckets(table_rows * shard_count), (8, 1)), jnp.int32)
    (
        normed, queries, keys, values, attended, lse, rev, mid, gate, col_slots, gains, slots_out, grad_in, weights,
        every_tok, small,
    ) = front(ints, bucket_row, cotangent, (w_query, w_key, w_value, w_output), tokens, small, slot_count)
    by_chip = (shard_count // 2, 2, capacity, model_width)
    grad_back, result, grad_w_in, grad_w_out, router_grads = moe(
        slots_out.reshape(by_chip), grad_in.reshape(by_chip), small, w_in[0], w_out[0]
    )
    rep_count = lax.axis_size("rep")
    slows, fasts = rep_places()[3:]
    gwin = grad_w_in.reshape(slows, fasts, model_width // rep_count, -1)
    gwout = grad_w_out.reshape(slows, fasts, -1, model_width)
    dense, prompt_part, near_part, grad_own, grad_resid, output_part, returned, ra, rb = back(
        grad_back.reshape(slot_count, model_width), col_slots, mid, cotangent, gains, every_tok, weights,
        (normed, queries, keys, values, attended, lse, rev), bucket_row, router_grads,
        result.reshape(expert_count, capacity, model_width), gwin, gwout,
    )
    chips = shard_count // 2
    lines = weight_rows // QUARTERS
    grad_tokens, mixed, gathered, ka, la, kb, lb = reduce_all(
        gains, col_slots, dense.reshape(chips, 2, QUARTERS, lines, -1),
        prompt_part.reshape(chips, 2, PR_DEV, model_width), near_part, grad_own, grad_resid, tokens, mid, gate,
        returned.reshape(slot_count, model_width), gwin, ra, gwout, rb,
        output_part.reshape(QUARTERS, lines, model_width),
    )
    in_grad, out_grad, gq, gk, gv, go, router, gain_attn, gain_moe, table = finish(
        ka, la, kb, lb, gathered, expert_count, table_rows, head_count
    )
    return (
        mixed,
        grad_tokens,
        *(part.reshape(weight_rows, model_width) for part in (gq, gk, gv, go)),
        router,
        gain_attn[0],
        gain_moe[0],
        table,
        in_grad[None],
        out_grad[None],
    )


def solution(mesh):
    return jax.shard_map(
        local,
        mesh=mesh,
        in_specs=(
            P(("rep", "shard"), None),
            P(("rep", "shard")),
            P(("rep", "shard")),
            P("shard", None),
            P("shard", None),
            P("shard", None),
            P("shard", None),
            P("shard", None),
            P("shard"),
            P("shard"),
            P("shard", None),
            P("shard", None, None),
            P("shard", None, None),
            P(("rep", "shard"), None),
        ),
        out_specs=(
            P(("rep", "shard"), None),
            P(("rep", "shard"), None),
            P("shard", None),
            P("shard", None),
            P("shard", None),
            P("shard", None),
            P("shard", None),
            P("shard"),
            P("shard"),
            P("shard", None),
            P("shard", "rep", None),
            P("shard", "rep", None),
        ),
        check_vma=False,
    )
```

```python
import jax
import jax.numpy as jnp
import numpy as np
from jax import lax
from jax.experimental import pallas as pl
from jax.experimental.pallas import tpu as pltpu
from jax.sharding import PartitionSpec as P

PR_DEV = 128
TILE = 128
SPAN = 2 * TILE
BLOCK = 1536
QUARTERS = 4
far_before, far_after, causal_tile, hidden_tile, tile_kinds = 3, 4, 5, 6, 7
vmem_cap = 60 * 1024 * 1024
mesh_ids = pl.DeviceIdType.MESH
bucket_edges = (12, 16, 23, 32, 46, 64, 91)
norm_epsilon = 1e-06
masked_score = -1e30
low, single = jnp.bfloat16, jnp.float32
in_vmem = pl.BlockSpec(memory_space=pltpu.VMEM)
anywhere = pl.BlockSpec(memory_space=pl.ANY)


def inverse_rms(values):
    return lax.rsqrt(jnp.mean(values * values, axis=-1, keepdims=True) + norm_epsilon)


def norm_pull(grad, values, gain):
    scale = inverse_rms(values)
    pulled = grad * gain
    mean = jnp.mean(pulled * values, axis=-1, keepdims=True)
    return scale * pulled - values * (scale * scale * scale * mean)


def nt(left, right):
    return lax.dot_general(left, right, (((1,), (1,)), ((), ())), preferred_element_type=single)


def tn(left, right):
    return lax.dot_general(left, right, (((0,), (0,)), ((), ())), preferred_element_type=single)


def nn(left, right):
    return jnp.dot(left, right, preferred_element_type=single)


def thirds_of(values):
    first = values.astype(low)
    rest = values - first.astype(single)
    second = rest.astype(low)
    return first, second, (rest - second.astype(single)).astype(low)


def fill_tiles(tiles_ref, rev_row, low, high):
    spread = jnp.broadcast_to(rev_row, (TILE, 4 * TILE))
    rolled = pltpu.roll(spread, 0, 1, stride=1, stride_axis=0)
    keys = lax.broadcasted_iota(jnp.int32, (TILE, TILE), 0)
    rows = lax.broadcasted_iota(jnp.int32, (TILE, TILE), 1)
    tiles_ref[0] = rolled[:, TILE : 2 * TILE]
    tiles_ref[1] = rolled[:, :TILE]
    tiles_ref[2] = rolled[:, 3 * TILE :]
    tiles_ref[far_before] = jnp.broadcast_to(low, (TILE, TILE))
    tiles_ref[far_after] = jnp.broadcast_to(high, (TILE, TILE))
    tiles_ref[causal_tile] = jnp.where(keys <= rows, rolled[:, :TILE], masked_score)
    tiles_ref[hidden_tile] = jnp.full((TILE, TILE), masked_score, jnp.float32)


def prompt_tile(block, chunk, shard_id, block_count):
    if chunk == 0:
        gap = block - shard_id
        far = jnp.where(gap < 0, far_before, far_after)
        return jnp.where(jnp.abs(gap) <= 1, gap + 1, far)
    if chunk == 1 and block == block_count - 1:
        return jnp.where(shard_id % 2 == 0, 0, far_before)
    return far_before


def local_tile(block, chunk, shard_id):
    if block >= 2:
        return ((causal_tile, 0), (hidden_tile, causal_tile))[block - 2][chunk]
    kind = 0 if (block, chunk) == (1, 0) else far_before
    return jnp.where(shard_id % 2 == 1, kind, hidden_tile)


def prompt_grid(part, shard_id, block_count):
    return [
        [prompt_tile(2 * part + half, chunk, shard_id, block_count) for chunk in range(3)]
        for half in range(2)
    ]


def local_grid(part, shard_id):
    return [[local_tile(2 * part + half, chunk, shard_id) for chunk in range(2)] for half in range(2)]


def with_bias(scores, tiles_ref, grid):
    return jnp.concatenate(
        [
            jnp.concatenate(
                [
                    scores[i * TILE : (i + 1) * TILE, j * TILE : (j + 1) * TILE] + tiles_ref[kind]
                    for j, kind in enumerate(row)
                ],
                axis=1,
            )
            for i, row in enumerate(grid)
        ],
        axis=0,
    )


def fold8(values):
    return values.reshape(values.shape[0] // 8, 8, values.shape[1])


def head_mask(rows, side):
    lanes = lax.broadcasted_iota(jnp.int32, (rows, TILE), 1)
    return (lanes < TILE // 2) if side == 0 else (lanes >= TILE // 2)


def distance_buckets(bucket_count):
    steps = np.arange(4 * TILE)
    gap = -np.where(steps < 2 * TILE, steps, steps - 4 * TILE)
    size = np.abs(gap)
    far = sum((size >= edge).astype(np.int64) for edge in bucket_edges)
    exact = bucket_count // 4
    return np.where(gap > 0, bucket_count // 2, 0) + np.where(size < exact, size, exact + far)


def front_kernel(
    ints_ref, bucket_ref, cot_ref, wq_hbm, wk_hbm, wv_hbm, wo_hbm, tok_hbm, little_hbm,
    lse_ref, rev_ref, gate_ref, col_ref, gain_ref, x_ref, gin_hbm, w_hbm, every_hbm, small_hbm,
    n_hbm, q_hbm, k_hbm, v_hbm, o_hbm, mid_hbm,
    tiles, vt, sp, sl, gbuf, w_ref, every_ref, small_ref, tok_ref, shard_w, little,
    n_ref, nt_ref, q_ref, k_ref, v_ref, ot_ref, mid_ref,
    gs, gr, loc, wz_s, wz_r, tz_s, tz_r, sz_s, sz_r, wr_s, wr_r, wt_s, wt_r, tt_s, tt_r, st_s, st_r, et_s, et_r,
):
    rep, chip, core, chips, quarter = places()
    along, across, twin = peer_lists()
    shards = chips * 2
    shard_id = chip * 2 + core
    rows, width = tok_ref.shape
    experts = shards
    blocks = every_ref.shape[0] // TILE - 4
    half = TILE // 2
    heads_held = rev_ref.shape[0]
    lines = shard_w.shape[1]
    rest_rows = rows - PR_DEV
    prompt_len = blocks * TILE
    others = [(rep, (shard_id + k) % shards) for k in range(1, shards)]

    def w_rows(source, side):
        return pl.ds(pl.multiple_of((source * 2 + side) * lines, lines), lines)

    def t_rows(source, side):
        return every_ref.at[pl.ds(pl.multiple_of((source * 2 + side) * PR_DEV, PR_DEV), PR_DEV)]

    loads = [
        pltpu.make_async_copy(source, shard_w.at[i], loc.at[i])
        for i, source in enumerate((wq_hbm, wk_hbm, wv_hbm, wo_hbm))
    ] + [pltpu.make_async_copy(tok_hbm, tok_ref, loc.at[4]), pltpu.make_async_copy(little_hbm, little, loc.at[5])]
    for copy in loads:
        copy.start()
    greeted = [twin] + along
    for device in across + [(rep, (chip + k) % chips * 2 + 1 - core) for k in range(1, chips)]:
        greeted.append(device)
    greet(greeted)
    started = []

    def go(source, target, sems, device):
        copy = send(source, target, sems, device)
        copy.start()
        started.append(copy)

    def landed(piece, sems):
        send(piece, piece, sems, twin).wait_recv()

    for copy in loads:
        copy.wait()
    mine = w_rows(chip, core)
    prompt, rest = tok_ref.at[pl.ds(0, PR_DEV)], tok_ref.at[pl.ds(PR_DEV, rest_rows)]
    for k, device in enumerate(along):
        go(shard_w.at[quarter], w_ref.at[quarter, mine], (wz_s.at[k], wz_r.at[k]), device)
        go(little, small_ref.at[mine], (sz_s.at[k], sz_r.at[k]), device)
    go(little, small_ref.at[mine], (st_s.at[0], st_r.at[0]), twin)
    go(rest, every_ref.at[pl.ds(prompt_len, rest_rows)], (et_s.at[0], et_r.at[0]), twin)
    go(prompt, t_rows(chip, core), (tt_s.at[0], tt_r.at[0]), twin)
    go(shard_w, w_ref.at[:, mine], (wt_s.at[0], wt_r.at[0]), twin)
    w_ref[:, mine, :] = shard_w[...]
    small_ref[mine, :] = little[...]
    every_ref[pl.ds(pl.multiple_of(shard_id * PR_DEV, PR_DEV), PR_DEV), :] = tok_ref[:PR_DEV, :]
    every_ref[prompt_len + rest_rows :, :] = tok_ref[PR_DEV:, :]
    ints = ints_ref[...].astype(single).T
    route_col = ints[:, 0:1].astype(jnp.int32)
    col_ref[...] = jnp.broadcast_to(ints[:, 1:2].astype(jnp.int32), col_ref.shape)
    slots = lax.broadcasted_iota(jnp.int32, (x_ref.shape[0], rows), 0)
    place = (slots == ints_ref[1:2, :]).astype(low)
    gbuf[...] = nn(place, cot_ref[...]).astype(low).reshape(gbuf.shape)
    own_g = pltpu.make_async_copy(gbuf.at[shard_id], gin_hbm.at[shard_id], loc.at[6])
    own_g.start()

    for k in range(1, chips):
        source = (chip + chips - k) % chips
        piece = w_ref.at[quarter, w_rows(source, core)]
        landed(piece, (wz_s.at[k - 1], wz_r.at[k - 1]))
        for j, device in enumerate(across):
            go(piece, piece, (wr_s.at[k - 1, j], wr_r.at[k - 1, j]), device)
        go(prompt, t_rows(chip, core), (tz_s.at[k - 1], tz_r.at[k - 1]), along[k - 1])
    for k in range(1, chips):
        source = (chip + chips - k) % chips
        piece = small_ref.at[w_rows(source, core)]
        landed(piece, (sz_s.at[k - 1], sz_r.at[k - 1]))
        go(piece, piece, (st_s.at[k], st_r.at[k]), twin)
    for k in range(1, chips):
        source = (chip + chips - k) % chips
        piece = t_rows(source, core)
        landed(piece, (tz_s.at[k - 1], tz_r.at[k - 1]))
        go(piece, piece, (tt_s.at[k], tt_r.at[k]), twin)
    for k, device in enumerate(others):
        go(gbuf.at[device[1]], gin_hbm.at[shard_id], (gs.at[k], gr.at[k]), device)
    for k in range(chips):
        source = (chip + chips - k) % chips
        landed(small_ref.at[w_rows(source, 1 - core)], (st_s.at[k], st_r.at[k]))
    writes = []

    def write(source, target):
        writes.append(pltpu.make_async_copy(source, target, loc.at[7 + len(writes)]))
        writes[-1].start()

    write(small_ref, small_hbm)

    small_t = small_ref[...].astype(single).T
    gain_attn = small_t[experts : experts + 1]
    gain_moe = small_t[experts + 1 : experts + 2]
    gain_ref[...] = jnp.concatenate([gain_attn, gain_moe, jnp.zeros((6, width), single)], axis=0)
    shard_rows = width // shards
    table_rows = 2 * TILE // 8 // shards
    owner = lax.broadcasted_iota(jnp.int32, (shards, shard_rows, 4 * TILE), 0)
    offset = lax.broadcasted_iota(jnp.int32, (shards, shard_rows, 4 * TILE), 1)
    held = jnp.where(offset < table_rows, owner * table_rows + offset, -1).reshape(width, 4 * TILE)
    hot = (held == bucket_ref[0:1, :]).astype(low)
    table_t = small_t[experts + 2 : experts + 2 + heads_held].astype(low)
    rev_ref[...] = nn(table_t, hot)

    for k in range(chips):
        source = (chip + chips - k) % chips
        landed(t_rows(source, 1 - core), (tt_s.at[k], tt_r.at[k]))
    landed(every_ref.at[pl.ds(prompt_len, rest_rows)], (et_s.at[0], et_r.at[0]))
    write(every_ref, every_hbm)

    @pl.loop(0, every_ref.shape[0] // SPAN)
    def scale(part):
        span = pl.ds(pl.multiple_of(part * SPAN, SPAN), SPAN)
        values = every_ref[span, :].astype(single)
        normed = values * inverse_rms(values) * gain_attn
        n_ref[span, :] = normed.astype(low)
        nt_ref[:, span] = normed.T.astype(low)

    write(nt_ref, n_hbm)
    for k in range(1, chips):
        source = (chip + chips - k) % chips
        for j in range(1, QUARTERS):
            piece = w_ref.at[(quarter + QUARTERS - j) % QUARTERS, w_rows(source, core)]
            landed(piece, (wr_s.at[k - 1, j - 1], wr_r.at[k - 1, j - 1]))
        piece = w_ref.at[:, w_rows(source, core)]
        go(piece, piece, (wt_s.at[k], wt_r.at[k]), twin)
    for k in range(chips):
        source = (chip + chips - k) % chips
        landed(w_ref.at[:, w_rows(source, 1 - core)], (wt_s.at[k], wt_r.at[k]))
    write(w_ref, w_hbm)

    @pl.loop(0, every_ref.shape[0] // (2 * SPAN))
    def project(part):
        span = pl.ds(pl.multiple_of(part * 2 * SPAN, 2 * SPAN), 2 * SPAN)
        k_ref[span, :] = nn(n_ref[span, :], w_ref[1]).astype(low)
        v_ref[span, :] = nn(n_ref[span, :], w_ref[2]).astype(low)

    own = pl.ds(pl.multiple_of(shard_id * TILE, TILE), TILE)
    normed = jnp.concatenate([n_ref[own, :], n_ref[(blocks + 2) * TILE :, :]], axis=0)
    q_ref[...] = (nn(normed, w_ref[0]).astype(low) * jnp.asarray(0.125, low)).astype(low)
    write(k_ref, k_hbm)
    write(v_ref, v_hbm)
    write(q_ref, q_hbm)

    @pl.loop(0, width // TILE)
    def pair_loop(pair):
        cols = pl.ds(pl.multiple_of(pair * TILE, TILE), TILE)
        vt[...] = v_ref[:, cols].T
        q_pair = q_ref[:, cols]
        for side in range(2):
            head = pair * 2 + side
            rev_row = rev_ref[pl.ds(head, 1), :]
            fill_tiles(tiles, rev_row, rev_row[:, SPAN - 1 : SPAN], rev_row[:, SPAN : SPAN + 1])
            q_head = jnp.where(head_mask(rows, side), q_pair, jnp.zeros_like(q_pair))
            top = jnp.full((8, rows), masked_score, single)
            for part in range(blocks // 2):
                keys = slice(part * SPAN, (part + 1) * SPAN)
                scores = with_bias(nt(k_ref[keys, cols], q_head), tiles, prompt_grid(part, shard_id, blocks))
                sp[keys, :] = scores
                top = jnp.maximum(top, jnp.max(fold8(scores), axis=0))
            top_local = top[:, PR_DEV:]
            for part in range(2):
                keys = slice(part * SPAN, (part + 1) * SPAN)
                held = slice((blocks // 2 + part) * SPAN, (blocks // 2 + part + 1) * SPAN)
                scores = with_bias(nt(k_ref[held, cols], q_head[PR_DEV:]), tiles, local_grid(part, shard_id))
                sl[keys, :] = scores
                top_local = jnp.maximum(top_local, jnp.max(fold8(scores), axis=0))
            top = jnp.max(jnp.concatenate([top[:, :PR_DEV], top_local], axis=1), axis=0, keepdims=True)
            total = jnp.zeros((8, rows), single)
            summed = jnp.zeros((half, rows), single)
            heads = slice(side * half, (side + 1) * half)
            for part in range(blocks // 2):
                keys = slice(part * SPAN, (part + 1) * SPAN)
                weights = jnp.exp(sp[keys, :] - top)
                total = total + jnp.sum(fold8(weights), axis=0)
                summed = summed + nn(vt[heads, keys], weights.astype(low))
            top_c = top[:, PR_DEV:]
            total_c = total[:, PR_DEV:]
            summed_c = summed[:, PR_DEV:]
            for part in range(2):
                keys = slice(part * SPAN, (part + 1) * SPAN)
                held = slice((blocks // 2 + part) * SPAN, (blocks // 2 + part + 1) * SPAN)
                weights = jnp.exp(sl[keys, :] - top_c)
                total_c = total_c + jnp.sum(fold8(weights), axis=0)
                summed_c = summed_c + nn(vt[heads, held], weights.astype(low))
            total = jnp.sum(jnp.concatenate([total[:, :PR_DEV], total_c], axis=1), axis=0, keepdims=True)
            summed = jnp.concatenate([summed[:, :PR_DEV], summed_c], axis=1)
            ot_ref[pl.ds(pl.multiple_of(head * half, half), half), :] = summed / total
            lse_ref[pl.ds(head, 1), :] = top + jnp.log(total)

    resid_mid = tok_ref[...].astype(single) + nn(ot_ref[...].T.astype(low), w_ref[3])
    mid_ref[...] = resid_mid
    write(ot_ref, o_hbm)
    write(mid_ref, mid_hbm)
    mid_low = (resid_mid * inverse_rms(resid_mid) * gain_moe).astype(low)
    probs = router_softmax(mid_low, small_ref[...], experts)
    lanes = lax.broadcasted_iota(jnp.int32, probs.shape, 1)
    gate = jnp.sum(jnp.where(lanes == route_col, probs, 0.0), axis=1, keepdims=True)
    gate_ref[...] = jnp.broadcast_to(gate, gate_ref.shape)
    x_ref[...] = nn(place, mid_low).astype(low)
    own_g.wait()
    for k in range(shards - 1):
        landed(gin_hbm.at[(shard_id + shards - k - 1) % shards], (gs.at[k], gr.at[k]))
    for copy in writes:
        copy.wait()
    for copy in started:
        copy.wait_send()


def router_softmax(rows_low, small, experts):
    logits = nn(rows_low, small)
    lanes = lax.broadcasted_iota(jnp.int32, logits.shape, 1)
    logits = jnp.where(lanes < experts, logits, masked_score)
    powers = jnp.exp(logits - jnp.max(logits, axis=1, keepdims=True))
    return powers / jnp.sum(powers, axis=1, keepdims=True)


def front(ints, bucket_row, cotangent, weights, tokens, small, slot_count):
    rows, width = tokens.shape
    shards = lax.axis_size("shard")
    chips, count = shards // 2, shards // 2 - 1
    keys = shards * PR_DEV + 2 * (rows - PR_DEV)
    lines = small.shape[0]
    shape = jax.ShapeDtypeStruct
    sem = pltpu.SemaphoreType.DMA
    vm = pltpu.VMEM
    return pl.pallas_call(
        front_kernel,
        out_shape=(
            shape((16, rows), single), shape((16, 4 * TILE), single), shape((rows, TILE), single),
            shape((rows, TILE), jnp.int32), shape((8, width), single), shape((slot_count, width), low),
            shape((shards, slot_count // shards, width), low), shape((4, width, width), low),
            shape((keys, width), low), shape((width, TILE), low),
            shape((width, keys), low), shape((rows, width), low), shape((keys, width), low),
            shape((keys, width), low), shape((width, rows), single), shape((rows, width), single),
        ),
        in_specs=[in_vmem] * 3 + [anywhere] * 6,
        out_specs=(in_vmem,) * 6 + (anywhere,) * 10,
        scratch_shapes=[
            vm((tile_kinds, TILE, TILE), single), vm((TILE, keys), low), vm((keys - 2 * SPAN, rows), single),
            vm((2 * SPAN, rows - TILE), single),
            vm((shards, slot_count // shards, width), low), vm((4, width, width), low), vm((keys, width), low),
            vm((width, TILE), low), vm((rows, width), low), vm((4, lines, width), low), vm((lines, TILE), low),
            vm((keys, width), low), vm((width, keys), low), vm((rows, width), low), vm((keys, width), low),
            vm((keys, width), low), vm((width, rows), single), vm((rows, width), single),
            sem((shards - 1,)), sem((shards - 1,)), sem((16,)), sem((count,)), sem((count,)), sem((count,)),
            sem((count,)), sem((count,)), sem((count,)), sem((count, 3)), sem((count, 3)), sem((chips,)), sem((chips,)),
            sem((chips,)), sem((chips,)), sem((chips,)), sem((chips,)), sem((1,)), sem((1,)),
        ],
        compiler_params=pltpu.CompilerParams(collective_id=2, has_side_effects=True, vmem_limit_bytes=vmem_cap),
        cost_estimate=pl.CostEstimate(flops=30_000_000_000, bytes_accessed=20_000_000, transcendentals=8_000_000),
        name="front",
    )(ints, bucket_row, cotangent, *weights, tokens, small)


def moe_kernel(
    x_ref, g_ref, small_ref, w_in_ref, w_out_ref,
    back_ref, out_ref, gwin_ref, gwout_ref, rg_ref,
    w_in, w_out, xin, gm, gg, hid, gpre, logit_grads, x_t, gwin, gwout,
    xs, xr, ms, mr, ws, ls, os_in, os_out,
):
    rep, chip, core, chips, quarter = places()
    experts = chips * 2
    here = chip * 2 + core
    pair_rows = 2 * xin.shape[2]
    hidden = w_in_ref.shape[1]
    block = BLOCK
    loads = [
        pltpu.make_async_copy(w_in_ref, w_in, ws.at[0]),
        pltpu.make_async_copy(w_out_ref, w_out, ws.at[1]),
    ]
    for copy in loads:
        copy.start()
    twin = (rep, chip * 2 + 1 - core)
    targets = [
        (k, side, (rep, chip_across(chip, k) * 2 + side)) for k in range(1, chips) for side in range(2)
    ]
    greet([twin] + [device for _, _, device in targets])
    sent = [send(x_ref.at[chip, 1 - core], xin.at[chip, core], (xs.at[0, 0], xr.at[0, core]), twin)]
    for k, side, device in targets:
        sent.append(
            send(x_ref.at[chip_across(chip, k), side], xin.at[chip, core], (xs.at[k, side], xr.at[k, core]), device)
        )
    for copy in sent[:5]:
        copy.start()
    xin[chip, core] = x_ref[chip, core]
    for copy in loads:
        copy.wait()

    def arrived(k, source, side):
        piece = xin.at[source, side]
        send(piece, piece, (xs.at[0, 0], xr.at[k, side]), twin).wait_recv()

    @pl.loop(0, chips)
    def chunk(k):
        source = chip_across(chip, k)

        @pl.when(k == 0)
        def _():
            arrived(0, chip, 1 - core)

        @pl.when(k > 0)
        def _():
            for side in range(2):
                arrived(k, source, side)

        rows = xin[source].reshape(pair_rows, xin.shape[3])
        grads = g_ref[source].reshape(pair_rows, xin.shape[3])
        probs = router_softmax(rows, small_ref[...], experts)
        lanes = lax.broadcasted_iota(jnp.int32, probs.shape, 1)
        gate = jnp.sum(jnp.where(lanes == here, probs, 0.0), axis=1, keepdims=True)
        gated = (gate * grads.astype(single)).astype(low)
        span = pl.ds(pl.multiple_of(source * pair_rows, pair_rows), pair_rows)
        gg[span, :] = gated
        pre = nn(rows, w_in[...])
        grad_hidden = nt(gated, w_out[...])
        square = pre * pre
        wave = jnp.tanh(0.7978845608028654 * pre * (1.0 + 0.044715 * square))
        left = 0.5 + 0.5 * wave
        active = (pre * left).astype(low)
        slope = left + (0.5 * pre) * (1.0 - wave * wave) * (0.7978845608028654 + 0.10703222440890037 * square)
        grad_pre = (grad_hidden * slope).astype(low)
        hid[span, :] = active
        gpre[span, :] = grad_pre
        out = nn(active, w_out[...]).astype(low)
        out_ref[source] = out.reshape(out_ref.shape[1:])
        grad_gate = jnp.sum(grads.astype(single) * out.astype(single), axis=1, keepdims=True)
        chosen = jnp.where(lanes == here, 1.0, 0.0)
        grad_logits = jnp.where(lanes < experts, gate * grad_gate * (chosen - probs), 0.0)
        logit_grads[span, :] = grad_logits
        router = small_ref[...]
        total = nt(grad_pre, w_in[...]) + sum(nt(part, router) for part in thirds_of(grad_logits))
        gm[source] = total.astype(low).reshape(gm.shape[1:])

        def reply(side, slot):
            return send(
                gm.at[source, side], back_ref.at[chip, core], (ms.at[k, slot], mr.at[k, core]), (rep, source * 2 + side)
            )

        @pl.when(k == 0)
        def _():
            for copy in sent[5:]:
                copy.start()
            reply(1 - core, 0).start()
            pltpu.make_async_copy(gm.at[chip, core], back_ref.at[chip, core], ls).start()

        @pl.when(k > 0)
        def _():
            for side in range(2):
                reply(side, side).start()

    every = xin[...].reshape(gg.shape)
    x_t[...] = every.T
    writes = []
    for part in range(hidden // block):
        cols = slice(part * block, (part + 1) * block)
        gwin[:, cols] = nn(x_t[...], gpre[:, cols]).astype(low)
        writes.append(pltpu.make_async_copy(gwin.at[:, cols], gwin_ref.at[:, cols], os_in.at[part]))
        writes[-1].start()
        gwout[cols, :] = tn(hid[:, cols], gg[...]).astype(low)
        writes.append(pltpu.make_async_copy(gwout.at[cols], gwout_ref.at[cols], os_out.at[part]))
        writes[-1].start()
    rg_ref[...] = sum(nn(x_t[...], part) for part in thirds_of(logit_grads[...]))
    pltpu.make_async_copy(gm.at[chip, core], back_ref.at[chip, core], ls).wait()

    def replied(k, source, side):
        piece = back_ref.at[source, side]
        send(piece, piece, (ms.at[0, 0], mr.at[k, side]), twin).wait_recv()

    replied(0, chip, 1 - core)
    for k in range(1, chips):
        for side in range(2):
            replied(k, chip_across(chip, k), side)
    for copy in sent:
        copy.wait_send()
    for copy in writes:
        copy.wait()
    send(gm.at[chip, 0], back_ref.at[chip, core], (ms.at[0, 0], mr.at[0, 0]), twin).wait_send()
    for k in range(1, chips):
        for side in range(2):
            send(gm.at[chip, 0], back_ref.at[chip, core], (ms.at[k, side], mr.at[0, 0]), twin).wait_send()


def moe(rows_out, grad_in, small, w_in, w_out):
    chips, _, cap, width = rows_out.shape
    slots = chips * 2 * cap
    hidden = w_in.shape[1]
    shape = jax.ShapeDtypeStruct
    pairs = pltpu.SemaphoreType.DMA
    strips = hidden // BLOCK
    return pl.pallas_call(
        moe_kernel,
        out_shape=(
            shape(rows_out.shape, low), shape(rows_out.shape, low), shape((width, hidden), low),
            shape((hidden, width), low), shape((width, TILE), single),
        ),
        in_specs=[in_vmem] * 3 + [anywhere] * 2,
        out_specs=(anywhere, in_vmem, anywhere, anywhere, in_vmem),
        scratch_shapes=[
            pltpu.VMEM((width, hidden), low), pltpu.VMEM((hidden, width), low),
            pltpu.VMEM(rows_out.shape, low), pltpu.VMEM(rows_out.shape, low), pltpu.VMEM((slots, width), low),
            pltpu.VMEM((slots, hidden), low), pltpu.VMEM((slots, hidden), low),
            pltpu.VMEM((slots, TILE), single), pltpu.VMEM((width, slots), low), pltpu.VMEM((width, hidden), low), pltpu.VMEM((hidden, width), low),
            pairs((chips, 2)), pairs((chips, 2)), pairs((chips, 2)), pairs((chips, 2)), pairs((2,)), pairs,
            pairs((strips,)), pairs((strips,)),
        ],
        compiler_params=pltpu.CompilerParams(collective_id=3, has_side_effects=True, vmem_limit_bytes=vmem_cap),
        cost_estimate=pl.CostEstimate(flops=40_000_000_000, bytes_accessed=40_000_000, transcendentals=3_000_000),
        name="moe",
    )(rows_out, grad_in, small, w_in, w_out)


def back_kernel(
    col_ref, gain_ref, lse_ref, rev_ref, bucket_ref, rg_ref, back_hbm, mid_hbm, cot_hbm, q_hbm, k_hbm, v_hbm, o_hbm,
    every_hbm, w_hbm, n_hbm, out_hbm, gwin_hbm, gwout_hbm,
    z_ref, dense_hbm, p_hbm, e_hbm, own_hbm, gres_hbm, ret_hbm, ra_hbm, rb_hbm,
    tiles, sums, diag, kt, dqt, far_sums, dk_sum, dv_sum, g_ref, dq_ref, dk_ref, dv_ref, attn_gain,
    every_ref, w_ref, n_ref, back_ref, mid_ref, cot_ref, q_ref, k_ref, v_ref, o_ref,
    dense_ref, own_ref, gres_ref,
    o_grad, o_half, o_sum, o_in, h_grad, h_half, h_sum, h_in,
    loc, out, xs, xr, as_, ar, bs, br, os_, or_, oz_s, oz_r, hs_, hr_, hz_s, hz_r,
):
    shard_id = lax.axis_index("shard")
    shards = lax.axis_size("shard")
    rows, width = mid_ref.shape
    blocks = k_ref.shape[0] // TILE - 4
    half = TILE // 2
    experts = shards
    heads_held = rev_ref.shape[0]
    rep, slow, fast, slows, fasts = rep_places()
    _, chip, core, chips, _ = places()
    along, _, twin = peer_lists()
    loads = [
        pltpu.make_async_copy(source, target, loc.at[i])
        for i, (source, target) in enumerate((
            (back_hbm, back_ref), (mid_hbm, mid_ref), (cot_hbm, cot_ref), (w_hbm.at[3], w_ref.at[3]), (o_hbm, o_ref),
            (q_hbm, q_ref), (k_hbm, k_ref), (v_hbm, v_ref), (n_hbm, n_ref), (w_hbm.at[pl.ds(0, 3)], w_ref.at[pl.ds(0, 3)]),
            (every_hbm, every_ref), (out_hbm.at[shard_id], ret_hbm.at[shard_id]),
        ))
    ]
    for copy in loads:
        copy.start()
    writes = []

    def write(source, target):
        writes.append(pltpu.make_async_copy(source, target, out.at[len(writes)]))
        writes[-1].start()

    others = [(rep, (shard_id + k) % shards) for k in range(1, shards)]
    beside = [(slow * fasts + (fast + j) % fasts, shard_id) for j in range(1, fasts)]
    beyond = [((slow + j) % slows * fasts + fast, shard_id) for j in range(1, slows)]
    greet(others + beside + beyond)
    sent = [
        send(gwin_hbm.at[:, (fast + j + 1) % fasts], ra_hbm.at[j], (as_.at[j], ar.at[j]), device)
        for j, device in enumerate(beside)
    ] + [
        send(gwout_hbm.at[(slow + j + 1) % slows], rb_hbm.at[j], (bs.at[j], br.at[j]), device)
        for j, device in enumerate(beyond)
    ] + [
        send(out_hbm.at[device[1]], ret_hbm.at[shard_id], (xs.at[k], xr.at[k]), device)
        for k, device in enumerate(others)
    ]
    for copy in sent:
        copy.start()
    diag[...] = jnp.zeros_like(diag)
    far_sums[...] = jnp.zeros_like(far_sums)
    tile_rows = lax.broadcasted_iota(jnp.int32, (TILE, TILE), 0)
    tile_cols = lax.broadcasted_iota(jnp.int32, (TILE, TILE), 1)
    flip = (tile_rows + tile_cols == TILE - 1).astype(single)

    for copy in loads[:5]:
        copy.wait()
    slots = lax.broadcasted_iota(jnp.int32, (rows, back_ref.shape[0]), 1)
    grad_mid = nn((slots == col_ref[:, 0:1]).astype(low), back_ref[...])
    resid_mid = mid_ref[...]
    grad_gain_moe = jnp.sum(grad_mid * resid_mid * inverse_rms(resid_mid), axis=0, keepdims=True)
    grad_resid = cot_ref[...].astype(single) + norm_pull(grad_mid, resid_mid, gain_ref[1:2, :])
    gres_ref[...] = grad_resid
    write(gres_ref, gres_hbm)
    grad_attn = grad_resid.astype(low)
    g_ref[...] = nt(grad_attn, w_ref[3]).astype(low)
    o_grad[...] = nn(o_ref[...].astype(low), grad_attn).reshape(o_grad.shape).astype(low)
    o_halves = [send(o_grad.at[2 * k + 1 - core], o_half.at[k], (os_.at[k], or_.at[k]), twin) for k in range(chips)]
    o_sends = [
        send(o_sum.at[(chip + k + 1) % chips], o_in.at[k], (oz_s.at[k], oz_r.at[k]), device)
        for k, device in enumerate(along)
    ]
    for copy in o_halves:
        copy.start()
    h_halves = [send(h_grad.at[2 * k + 1 - core], h_half.at[k], (hs_.at[k], hr_.at[k]), twin) for k in range(chips)]
    h_sends = [
        send(h_sum.at[(chip + k + 1) % chips], h_in.at[k], (hz_s.at[k], hz_r.at[k]), device)
        for k, device in enumerate(along)
    ]
    for copy in loads[5:]:
        copy.wait()
    own = pl.ds(pl.multiple_of(shard_id * TILE, TILE), TILE)
    tail = slice((blocks + 2) * TILE, (blocks + 4) * TILE)
    early = width // 2

    @pl.loop(0, width // TILE)
    def pair_loop(pair):
        cols = pl.ds(pl.multiple_of(pair * TILE, TILE), TILE)
        kt[...] = k_ref[:, cols].T
        q_pair = q_ref[:, cols]
        g_pair = g_ref[:, cols]
        delta_t = g_pair.astype(single).T * o_ref[cols, :]
        for side in range(2):
            head = pair * 2 + side
            heads = slice(side * half, (side + 1) * half)
            rev_row = rev_ref[pl.ds(head, 1), :]
            fill_tiles(tiles, rev_row, rev_row[:, SPAN - 1 : SPAN], rev_row[:, SPAN : SPAN + 1])
            sums[...] = jnp.zeros_like(sums)
            mask = head_mask(rows, side)
            q_head = jnp.where(mask, q_pair, jnp.zeros_like(q_pair))
            g_head = jnp.where(mask, g_pair, jnp.zeros_like(g_pair))
            delta = jnp.sum(delta_t[heads, :], axis=0, keepdims=True)
            log_total = lse_ref[pl.ds(head, 1), :]

            def block_grads(part, first, grid):
                keys = slice(part * SPAN, (part + 1) * SPAN)
                q_rows, g_rows = q_head[first:], g_head[first:]
                scores = with_bias(nt(k_ref[keys, cols], q_rows), tiles, grid)
                weights = jnp.exp(scores - log_total[:, first:])
                grad_weights = nt(v_ref[keys, cols], g_rows)
                grad_scores = weights * (grad_weights - delta[:, first:])
                for i, row in enumerate(grid):
                    for j, kind in enumerate(row):
                        sums[kind] += grad_scores[i * TILE : (i + 1) * TILE, j * TILE : (j + 1) * TILE]
                raw = grad_scores.astype(low)
                dk = nn(raw, q_rows)
                dv = nn(weights.astype(low), g_rows)
                if side == 0:
                    dk_sum[keys, :] = dk
                    dv_sum[keys, :] = dv
                else:
                    dk_ref[keys, cols] = (dk_sum[keys, :] + dk).astype(low)
                    dv_ref[keys, cols] = (dv_sum[keys, :] + dv).astype(low)
                return nn(kt[heads, keys], raw)

            dq = jnp.zeros((half, rows), single)
            for part in range(blocks // 2):
                dq = dq + block_grads(part, 0, prompt_grid(part, shard_id, blocks))
            dq_c = dq[:, PR_DEV:]
            for part in range(2):
                dq_c = dq_c + block_grads(blocks // 2 + part, PR_DEV, local_grid(part, shard_id))
            dqt[heads, :] = jnp.concatenate([dq[:, :PR_DEV], dq_c], axis=1)
            near = jnp.concatenate(
                [sums[1] + sums[causal_tile], sums[0], jnp.zeros((TILE, TILE), single), sums[2]], axis=1
            )
            flipped = jnp.dot(flip, near, precision=lax.Precision.HIGHEST, preferred_element_type=single)
            rolled = pltpu.roll(flipped, 3 * TILE + 1, 1, stride=1, stride_axis=0)
            diag[pl.ds(head, 1), :] = jnp.sum(rolled, axis=0, keepdims=True)
            far_sums[pl.ds(head, 1), :] = jnp.concatenate(
                [jnp.sum(sums[far_before], axis=0, keepdims=True), jnp.sum(sums[far_after], axis=0, keepdims=True)],
                axis=1,
            )
        dq_ref[:, cols] = (dqt[...].T * 0.125).astype(low)

        @pl.when(pair == 0)
        def _():
            for k in range(chips):
                o_halves[k].wait_recv()
                o_sum[k] = (o_grad[2 * k + core].astype(single) + o_half[k].astype(single)).astype(low)
            for copy in o_sends:
                copy.start()

        @pl.when(pair == width // SPAN - 1)
        def _():
            normed = jnp.concatenate([n_ref[:, own], n_ref[:, tail]], axis=1)
            for i, (left, right) in enumerate(((normed, dq_ref), (n_ref[...], dk_ref), (n_ref[...], dv_ref))):
                part = nn(left, right[:, :early]).reshape(shards, h_grad.shape[1], early)
                h_grad[:, :, i * early : (i + 1) * early] = part.astype(low)
            for copy in h_halves:
                copy.start()

        @pl.when(pair == width // SPAN)
        def _():
            for k in range(chips):
                h_halves[k].wait_recv()
                h_sum[k] = (h_grad[2 * k + core].astype(single) + h_half[k].astype(single)).astype(low)
            for copy in h_sends:
                copy.start()

    lanes = lax.broadcasted_iota(jnp.int32, (heads_held, 4 * TILE), 1)
    before = jnp.sum(far_sums[:, :TILE], axis=1, keepdims=True)
    after = jnp.sum(far_sums[:, TILE:], axis=1, keepdims=True)
    by_gap = diag[...] + jnp.where(lanes == SPAN - 1, before, 0.0) + jnp.where(lanes == SPAN, after, 0.0)
    shard_rows = width // shards
    table_rows = 2 * TILE // 8 // shards
    owner = lax.broadcasted_iota(jnp.int32, (shards, shard_rows, 4 * TILE), 0)
    offset = lax.broadcasted_iota(jnp.int32, (shards, shard_rows, 4 * TILE), 1)
    held = jnp.where(offset < table_rows, owner * table_rows + offset, -1).reshape(width, 4 * TILE)
    hot = (held == bucket_ref[0:1, :]).astype(low)
    grad_table = sum(nt(part, hot) for part in thirds_of(by_gap))

    attn_gain[...] = jnp.zeros_like(attn_gain)
    normed = jnp.concatenate([n_ref[:, own], n_ref[:, tail]], axis=1)
    dense_ref[:, :early] = nn(normed, dq_ref[:, early:]).astype(low)
    grad_own = nt(dq_ref[...], w_ref[0])
    values = jnp.concatenate([every_ref[own, :], every_ref[tail, :]], axis=0).astype(single)
    attn_gain[...] += jnp.sum(fold8(grad_own * (values * inverse_rms(values))), axis=0)
    own_ref[...] = grad_own

    def pull_rows(part):
        span = pl.ds(pl.multiple_of(part * SPAN, SPAN), SPAN)
        values = every_ref[span, :].astype(single)
        grads = nt(dk_ref[span, :], w_ref[1]) + nt(dv_ref[span, :], w_ref[2])
        attn_gain[...] += jnp.sum(fold8(grads * (values * inverse_rms(values))), axis=0)
        return grads

    @pl.loop(0, blocks // 2)
    def pull_prompt(part):
        k_ref[pl.ds(pl.multiple_of(part * SPAN, SPAN), SPAN), :] = pull_rows(part).astype(low)

    write(k_ref.at[pl.ds(0, blocks * TILE)], p_hbm)
    k_ref[blocks * TILE : (blocks + 2) * TILE, :] = pull_rows(blocks // 2).astype(low)
    write(k_ref.at[pl.ds(blocks * TILE, SPAN)], e_hbm)
    own_ref[PR_DEV:, :] += pull_rows(blocks // 2 + 1)
    write(own_ref, own_hbm)

    dense_ref[:, early : 2 * early] = nn(n_ref[...], dk_ref[:, early:]).astype(low)
    dense_ref[:, 2 * early : 3 * early] = nn(n_ref[...], dv_ref[:, early:]).astype(low)

    small_t = jnp.concatenate(
        [
            jnp.zeros((experts, width), single), jnp.sum(attn_gain[...], axis=0, keepdims=True), grad_gain_moe,
            grad_table, jnp.zeros((TILE - experts - 2 - heads_held, width), single),
        ],
        axis=0,
    )
    dense_ref[:, 3 * early :] = (small_t.T + rg_ref[...]).astype(low)
    write(dense_ref, dense_hbm)
    o_total = o_sum[chip].astype(single)
    for k in range(chips - 1):
        o_sends[k].wait_recv()
        o_total = o_total + o_in[k].astype(single)
    z_ref[:, :width] = o_total.astype(low)
    h_total = h_sum[chip].astype(single)
    for k in range(chips - 1):
        h_sends[k].wait_recv()
        h_total = h_total + h_in[k].astype(single)
    z_ref[:, width:] = h_total.astype(low)
    for copy in o_halves + o_sends + h_halves + h_sends:
        copy.wait_send()
    for copy in writes:
        copy.wait()
    for k in range(shards - 1):
        piece = ret_hbm.at[(shard_id + shards - k - 1) % shards]
        send(piece, piece, (xs.at[k], xr.at[k]), others[0]).wait_recv()
    for j in range(fasts - 1):
        send(ra_hbm.at[j], ra_hbm.at[j], (as_.at[j], ar.at[j]), others[0]).wait_recv()
    for j in range(slows - 1):
        send(rb_hbm.at[j], rb_hbm.at[j], (bs.at[j], br.at[j]), others[0]).wait_recv()
    for copy in sent:
        copy.wait_send()


def back(
    returned, col_slots, mid, cotangent, gains, every_tok, weights, kept, bucket_row, router_grads, result, gwin, gwout
):
    rows, width = mid.shape
    normed, queries, keys, values, attended, lse, rev = kept
    count = keys.shape[0]
    shards = result.shape[0]
    slows, fasts = gwin.shape[:2]
    chips, lines, early = shards // 2, width // shards, width // 2
    vm = pltpu.VMEM
    shape = jax.ShapeDtypeStruct
    pairs = pltpu.SemaphoreType.DMA
    args = (
        col_slots, gains, lse, rev, bucket_row, router_grads, returned, mid, cotangent, queries, keys, values, attended,
        every_tok, weights, normed, result, gwin, gwout,
    )
    return pl.pallas_call(
        back_kernel,
        out_shape=(
            shape((lines, width + 3 * early), low), shape((width, 3 * early + TILE), low),
            shape((count - 2 * SPAN, width), low), shape((SPAN, width), low),
            shape((rows, width), single), shape((rows, width), single), shape(result.shape, low),
            shape((fasts - 1, slows) + gwin.shape[2:], low), shape((slows - 1, fasts) + gwout.shape[2:], low),
        ),
        in_specs=[in_vmem] * 6 + [anywhere] * 13,
        out_specs=(in_vmem,) + (anywhere,) * 8,
        scratch_shapes=[
            pltpu.VMEM((tile_kinds, TILE, TILE), single), pltpu.VMEM((tile_kinds, TILE, TILE), single),
            pltpu.VMEM((16, 4 * TILE), single), pltpu.VMEM((TILE, count), low), pltpu.VMEM((TILE, rows), single),
            pltpu.VMEM((16, 2 * TILE), single), pltpu.VMEM((count, TILE), single), pltpu.VMEM((count, TILE), single),
            pltpu.VMEM((rows, width), low), pltpu.VMEM((rows, width), low), pltpu.VMEM((count, width), low),
            pltpu.VMEM((count, width), low), pltpu.VMEM((8, width), single),
            pltpu.VMEM(every_tok.shape, low), pltpu.VMEM(weights.shape, low), pltpu.VMEM(normed.shape, low),
            vm(returned.shape, low), vm((rows, width), single), vm((rows, width), low), vm((rows, width), low),
            vm(keys.shape, low), vm(keys.shape, low), vm(attended.shape, single),
            vm((width, 3 * early + TILE), low),
            vm((rows, width), single), vm((rows, width), single),
            vm((shards, lines, width), low), vm((chips, lines, width), low),
            vm((chips, lines, width), low), vm((chips - 1, lines, width), low),
            vm((shards, lines, 3 * early), low), vm((chips, lines, 3 * early), low),
            vm((chips, lines, 3 * early), low), vm((chips - 1, lines, 3 * early), low),
            pairs((12,)), pairs((6,)), pairs((shards - 1,)), pairs((shards - 1,)), pairs((fasts - 1,)), pairs((fasts - 1,)),
            pairs((slows - 1,)), pairs((slows - 1,)), pairs((chips,)), pairs((chips,)), pairs((chips - 1,)),
            pairs((chips - 1,)), pairs((chips,)), pairs((chips,)), pairs((chips - 1,)), pairs((chips - 1,)),
        ],
        compiler_params=pltpu.CompilerParams(collective_id=4, has_side_effects=True, vmem_limit_bytes=vmem_cap),
        cost_estimate=pl.CostEstimate(flops=60_000_000_000, bytes_accessed=40_000_000, transcendentals=8_000_000),
        name="back",
    )(*args)


def places():
    rep, shard = lax.axis_index("rep"), lax.axis_index("shard")
    return rep, shard // 2, shard % 2, lax.axis_size("shard") // 2, rep % QUARTERS


def peer_lists():
    rep, chip, core, chips, quarter = places()
    along = [(rep, (chip + k) % chips * 2 + core) for k in range(1, chips)]
    across = [(rep - quarter + (quarter + j) % QUARTERS, chip * 2 + core) for j in range(1, QUARTERS)]
    twin = (rep, chip * 2 + 1 - core)
    return along, across, twin


def chip_across(chip, k):
    partner, bit = 0, 1
    while bit < lax.axis_size("shard") // 2:
        partner = partner + bit * ((chip // bit + k // bit) % 2)
        bit = bit * 2
    return partner


def greet(devices):
    barrier = pltpu.get_barrier_semaphore()
    for device in devices:
        pl.semaphore_signal(barrier, inc=1, device_id=device, device_id_type=mesh_ids)
    pl.semaphore_wait(barrier, len(devices))


def send(source, target, sems, device):
    return pltpu.make_async_remote_copy(
        src_ref=source, dst_ref=target, send_sem=sems[0], recv_sem=sems[1],
        device_id=device, device_id_type=mesh_ids,
    )


def rep_places():
    rep, reps = lax.axis_index("rep"), lax.axis_size("rep")
    fasts = QUARTERS if reps % (QUARTERS * QUARTERS) == 0 else 2
    return rep, rep // fasts, rep % fasts, reps // fasts, fasts


def reduce_kernel(
    gain_ref, col_ref, d_hbm, p_hbm, e_hbm, own_hbm, gres_hbm, tok_hbm, mid_hbm, gate_hbm, ret_hbm,
    gwin_hbm, ra_hbm, gwout_hbm, rb_hbm, z_hbm,
    gt_ref, mix_ref, early_ref, late_ref, ka_ref, la_hbm, kb_ref, lb_hbm,
    d_own, half, hr, tr, mr, cr, zs, tz, z_last, z_above, z_all, last, above_in, gathered,
    p_own, p_half, p_sum, p_in, e_in, own, gres, tok, mid, gate, ret,
    a_own, a_in, a_sum, b_own, b_in, b_sum,
    loc, ps_s, ps_r, ds_s, ds_r, pz_s, pz_r, rr_s, rr_r, rz_s, rz_r, zr_s, zr_r, zh_s, zh_r, za_s, za_r,
    dh_s, dh_r, da_s, da_r, ea_s, ea_r, eb_s, eb_r,
):
    rep, chip, core, chips, quarter = places()
    along, across, twin = peer_lists()
    _, slow, fast, slows, fasts = rep_places()
    classes = lax.axis_size("rep") // QUARTERS
    here = chip * 2 + core
    beside = [(slow * fasts + (fast + j) % fasts, here) for j in range(1, fasts)]
    beyond = [((slow + j) % slows * fasts + fast, here) for j in range(1, slows)]
    above = [((rep // QUARTERS + k) % classes * QUARTERS + quarter, here) for k in range(1, classes)]
    wide = lambda held: held.astype(single)
    pending = []

    def load(source, target, index):
        copy = pltpu.make_async_copy(source, target, loc.at[index])
        copy.start()
        return copy

    def go(source, target, sems, device):
        copy = send(source, target, sems, device)
        copy.start()
        pending.append(copy)

    def landed(piece, sems):
        send(piece, piece, sems, twin).wait_recv()

    early_in = load(z_hbm, zs, 12)
    a_loads = [load(gwin_hbm.at[:, fast], a_own, 0), load(ra_hbm, a_in, 1)]
    halves = [load(d_hbm.at[:, core], d_own, 5), load(p_hbm.at[:, core], p_own, 4)]
    b_loads = [load(gwout_hbm.at[slow], b_own, 2), load(rb_hbm, b_in, 3)]
    rest = [
        load(ret_hbm, ret, 6), load(mid_hbm, mid, 7), load(gate_hbm, gate, 8), load(own_hbm, own, 9),
        load(gres_hbm, gres, 10), load(tok_hbm, tok, 11),
    ]
    greets = [twin] + along
    for device in across + beside + beyond + above:
        greets.append(device)
    greet(greets)
    for k in range(chips):
        go(d_hbm.at[k, 1 - core], half.at[k], (ds_s.at[k], ds_r.at[k]), twin)
    go(p_hbm.at[:, 1 - core], p_half, (ps_s.at[0], ps_r.at[0]), twin)
    go(e_hbm, e_in, (ps_s.at[1], ps_r.at[1]), twin)
    early_in.wait()
    for j, device in enumerate(across):
        go(zs.at[(quarter + j + 1) % QUARTERS], tz.at[j], (zr_s.at[j], zr_r.at[j]), device)

    for copy in a_loads:
        copy.wait()
    for t in range(slows):
        total = wide(a_own[t])
        for j in range(fasts - 1):
            total = total + wide(a_in[j, t])
        a_sum[t] = total.astype(low)
    for j, device in enumerate(beyond):
        go(a_sum.at[(slow + j + 1) % slows], la_hbm.at[j], (ea_s.at[j], ea_r.at[j]), device)
    for copy in halves:
        copy.wait()
    for k in range(chips):
        landed(half.at[k], (ds_s.at[k], ds_r.at[k]))
        for t in range(QUARTERS):
            hr[t, k] = (wide(d_own[k, t]) + wide(half[k, t])).astype(low)
    for j, device in enumerate(across):
        go(hr.at[(quarter + j + 1) % QUARTERS], tr.at[j], (rr_s.at[j], rr_r.at[j]), device)
    landed(p_half, (ps_s.at[0], ps_r.at[0]))
    for k in range(chips):
        p_sum[k] = (wide(p_own[k]) + wide(p_half[k])).astype(low)
    for k, device in enumerate(along):
        go(p_sum.at[(chip + k + 1) % chips], p_in.at[k], (pz_s.at[k], pz_r.at[k]), device)
    for copy in b_loads:
        copy.wait()
    for t in range(fasts):
        total = wide(b_own[t])
        for j in range(slows - 1):
            total = total + wide(b_in[j, t])
        b_sum[t] = total.astype(low)
    for j, device in enumerate(beside):
        go(b_sum.at[(fast + j + 1) % fasts], lb_hbm.at[j], (eb_s.at[j], eb_r.at[j]), device)

    def class_sum(held, came, s_sems, r_sems):
        total = wide(held[...])
        for j, device in enumerate(above):
            go(held, came.at[j], (s_sems.at[j], r_sems.at[j]), device)
        for j in range(classes - 1):
            landed(came.at[j], (s_sems.at[j], r_sems.at[j]))
            total = total + wide(came[j])
        return total.astype(low)

    def hand_out(pieces, s_sems, r_sems):
        for j, device in enumerate(across):
            go(pieces.at[quarter], pieces.at[quarter], (s_sems.at[j], r_sems.at[j]), device)

    def handed(pieces, s_sems, r_sems):
        for j in range(QUARTERS - 1):
            landed(pieces.at[(quarter + QUARTERS - j - 1) % QUARTERS], (s_sems.at[j], r_sems.at[j]))

    for j in range(QUARTERS - 1):
        landed(tz.at[j], (zr_s.at[j], zr_r.at[j]))
    total = wide(zs[quarter])
    for j in range(QUARTERS - 1):
        total = total + wide(tz[j])
    z_last[...] = total.astype(low)
    z_all[quarter] = class_sum(z_last, z_above, zh_s, zh_r) if classes > 1 else z_last[...]
    hand_out(z_all, za_s, za_r)

    for copy in rest:
        copy.wait()
    slots = lax.broadcasted_iota(jnp.int32, (tok.shape[0], ret.shape[0]), 1)
    chosen = nn((slots == col_ref[:, 0:1]).astype(low), ret[...])
    mix_ref[...] = (mid[...] + gate[:, 0:1] * chosen).astype(low)
    ka_ref[...] = a_sum[slow]
    kb_ref[...] = b_sum[fast]

    for j in range(QUARTERS - 1):
        landed(tr.at[j], (rr_s.at[j], rr_r.at[j]))
    for k in range(chips):
        total = wide(hr[quarter, k])
        for j in range(QUARTERS - 1):
            total = total + wide(tr[j, k])
        mr[k] = total.astype(low)
    for k, device in enumerate(along):
        go(mr.at[(chip + k + 1) % chips], cr.at[k], (rz_s.at[k], rz_r.at[k]), device)

    for k in range(chips - 1):
        landed(p_in.at[k], (pz_s.at[k], pz_r.at[k]))
    landed(e_in, (ps_s.at[1], ps_r.at[1]))
    total = wide(p_sum[chip])
    for k in range(chips - 1):
        total = total + wide(p_in[k])
    grads = own[...] + jnp.concatenate([total, wide(e_in[...])], axis=0)
    gt_ref[...] = gres[...] + norm_pull(grads, wide(tok[...]), gain_ref[0:1, :])

    for k in range(chips - 1):
        landed(cr.at[k], (rz_s.at[k], rz_r.at[k]))
    total = wide(mr[chip])
    for k in range(chips - 1):
        total = total + wide(cr[k])
    last[...] = total.astype(low)
    gathered[quarter] = class_sum(last, above_in, dh_s, dh_r) if classes > 1 else last[...]
    hand_out(gathered, da_s, da_r)
    handed(z_all, za_s, za_r)
    early_ref[...] = z_all[...]
    handed(gathered, da_s, da_r)
    late_ref[...] = gathered[...]
    for j in range(slows - 1):
        landed(la_hbm.at[j], (ea_s.at[j], ea_r.at[j]))
    for j in range(fasts - 1):
        landed(lb_hbm.at[j], (eb_s.at[j], eb_r.at[j]))
    for copy in pending:
        copy.wait_send()


def reduce_all(gains, col_slots, dense, prompt_part, near_part, own, gres, tokens, mid, gate, returned, gwin, ra, gwout, rb, z):
    chips = lax.axis_size("shard") // 2
    classes = lax.axis_size("rep") // QUARTERS
    slows, fasts = gwin.shape[:2]
    rows, width = mid.shape
    lines, lanes = dense.shape[3:]
    wider = z.shape[2]
    shape = jax.ShapeDtypeStruct
    sem = pltpu.SemaphoreType.DMA
    vm = pltpu.VMEM
    count, others = chips - 1, QUARTERS - 1
    ours = prompt_part.shape[2:]
    extra = max(classes - 1, 1)
    args = (gains, col_slots, dense, prompt_part, near_part, own, gres, tokens, mid, gate, returned, gwin, ra, gwout, rb, z)
    return pl.pallas_call(
        reduce_kernel,
        out_shape=(
            shape((rows, width), single), shape((rows, width), low),
            shape((QUARTERS, lines, wider), low), shape((QUARTERS, lines, lanes), low),
            shape(gwin.shape[2:], low), shape((slows - 1,) + gwin.shape[2:], low),
            shape(gwout.shape[2:], low), shape((fasts - 1,) + gwout.shape[2:], low),
        ),
        in_specs=[in_vmem] * 2 + [anywhere] * 14,
        out_specs=(in_vmem,) * 5 + (anywhere, in_vmem, anywhere),
        scratch_shapes=[
            vm((chips, QUARTERS, lines, lanes), low), vm((chips, QUARTERS, lines, lanes), low),
            vm((QUARTERS, chips, lines, lanes), low), vm((others, chips, lines, lanes), low),
            vm((chips, lines, lanes), low), vm((count, lines, lanes), low),
            vm((QUARTERS, lines, wider), low), vm((others, lines, wider), low), vm((lines, wider), low),
            vm((extra, lines, wider), low), vm((QUARTERS, lines, wider), low),
            vm((lines, lanes), low), vm((extra, lines, lanes), low), vm((QUARTERS, lines, lanes), low),
            vm((chips,) + ours, low), vm((chips,) + ours, low), vm((chips,) + ours, low), vm((count,) + ours, low),
            vm(near_part.shape, low), vm((rows, width), single), vm((rows, width), single), vm((rows, width), low),
            vm((rows, width), single), vm(gate.shape, single), vm(returned.shape, low),
            vm((slows,) + gwin.shape[2:], low), vm(ra.shape, low), vm((slows,) + gwin.shape[2:], low),
            vm((fasts,) + gwout.shape[2:], low), vm(rb.shape, low), vm((fasts,) + gwout.shape[2:], low),
            sem((13,)), sem((2,)), sem((2,)), sem((chips,)), sem((chips,)), sem((count,)), sem((count,)),
            sem((others,)), sem((others,)), sem((count,)), sem((count,)),
            sem((others,)), sem((others,)), sem((extra,)), sem((extra,)), sem((others,)), sem((others,)),
            sem((extra,)), sem((extra,)), sem((others,)), sem((others,)),
            sem((slows - 1,)), sem((slows - 1,)), sem((fasts - 1,)), sem((fasts - 1,)),
        ],
        compiler_params=pltpu.CompilerParams(collective_id=1, has_side_effects=True, vmem_limit_bytes=vmem_cap),
        cost_estimate=pl.CostEstimate(flops=0, bytes_accessed=200_000_000, transcendentals=0),
        name="reduce_all",
    )(*args)


def finish_kernel(ka_ref, la_ref, kb_ref, lb_ref, early_ref, late_ref, small_ref, *outs):
    ea_ref, eb_ref, q_ref, k_ref, v_ref, o_ref, router_ref, attn_ref, moe_ref, table_ref = outs
    width = q_ref.shape[2]
    experts = router_ref.shape[1]
    ea_ref[...] = ka_ref[...].astype(single) + jnp.sum(la_ref[...].astype(single), axis=0)
    eb_ref[...] = kb_ref[...].astype(single) + jnp.sum(lb_ref[...].astype(single), axis=0)
    half = width // 2
    o_ref[...] = early_ref[:, :, :width].astype(single)
    for i, ref in enumerate((q_ref, k_ref, v_ref)):
        ref[:, :, :half] = early_ref[:, :, width + i * half : width + (i + 1) * half].astype(single)
        ref[:, :, half:] = late_ref[:, :, i * half : (i + 1) * half].astype(single)

    @pl.when(pl.program_id(0) == 0)
    def _():
        small = small_ref[...].astype(single)
        router_ref[...] = small[:, :experts]
        turned = small.T
        attn_ref[...] = turned[experts : experts + 1]
        moe_ref[...] = turned[experts + 1 : experts + 2]
        table_ref[...] = small[: table_ref.shape[0], experts + 2 : experts + 2 + table_ref.shape[1]]


def finish(ka, la, kb, lb, early, late, experts, table_rows, heads):
    shape = jax.ShapeDtypeStruct
    _, lines, wider = early.shape
    lanes = late.shape[2]
    width = kb.shape[1]
    rows = QUARTERS * lines
    small = late[:, :, lanes - TILE :].reshape(rows, TILE)
    steps = QUARTERS
    a_cols, b_rows = ka.shape[1] // steps, kb.shape[0] // steps
    part = pl.BlockSpec((1, lines, width), lambda i: (i, 0, 0))
    once = lambda *dims: pl.BlockSpec(dims, lambda i: (0,) * len(dims))
    return pl.pallas_call(
        finish_kernel,
        grid=(steps,),
        out_shape=(
            shape(ka.shape, single), shape(kb.shape, single), *(shape((QUARTERS, lines, width), single),) * 4,
            shape((rows, experts), single), shape((1, rows), single), shape((1, rows), single),
            shape((table_rows, heads), single),
        ),
        in_specs=[
            pl.BlockSpec((ka.shape[0], a_cols), lambda i: (0, i)),
            pl.BlockSpec((la.shape[0], ka.shape[0], a_cols), lambda i: (0, 0, i)),
            pl.BlockSpec((b_rows, width), lambda i: (i, 0)),
            pl.BlockSpec((lb.shape[0], b_rows, width), lambda i: (0, i, 0)),
            pl.BlockSpec((1, lines, wider), lambda i: (i, 0, 0)), pl.BlockSpec((1, lines, lanes), lambda i: (i, 0, 0)),
            once(rows, TILE),
        ],
        out_specs=(
            pl.BlockSpec((ka.shape[0], a_cols), lambda i: (0, i)), pl.BlockSpec((b_rows, width), lambda i: (i, 0)),
            part, part, part, part, once(rows, experts), once(1, rows), once(1, rows), once(table_rows, heads),
        ),
        compiler_params=pltpu.CompilerParams(vmem_limit_bytes=vmem_cap),
        cost_estimate=pl.CostEstimate(flops=0, bytes_accessed=12_000_000, transcendentals=0),
        name="finish",
    )(ka, la, kb, lb, early, late, small)


def local(
    tokens,
    routes,
    slot_ids,
    w_query,
    w_key,
    w_value,
    w_output,
    w_router,
    norm_attn,
    norm_moe,
    rel_table,
    w_in,
    w_out,
    cotangent,
):
    shard_count = lax.axis_size("shard")
    token_rows, model_width = tokens.shape
    prompt_len = PR_DEV * shard_count
    weight_rows, expert_count = w_router.shape
    table_rows, head_count = rel_table.shape
    capacity = 2 * token_rows // expert_count
    slot_count = expert_count * capacity

    small = jnp.concatenate(
        [w_router, norm_attn[:, None], norm_moe[:, None],
         jnp.pad(rel_table, ((0, weight_rows - table_rows), (0, 0)))], axis=1
    )
    small = jnp.pad(small, ((0, 0), (0, TILE - small.shape[1])))
    dispatch = routes * capacity + slot_ids

    ints = jnp.concatenate([routes[None], dispatch[None], jnp.zeros((6, token_rows), jnp.int32)])
    bucket_row = jnp.asarray(np.tile(distance_buckets(table_rows * shard_count), (8, 1)), jnp.int32)
    (
        lse, rev, gate, col_slots, gains, slots_out, grad_in, weights, every_tok, small, normed, queries, keys, values,
        attended, mid,
    ) = front(ints, bucket_row, cotangent, (w_query, w_key, w_value, w_output), tokens, small, slot_count)
    by_chip = (shard_count // 2, 2, capacity, model_width)
    grad_back, result, grad_w_in, grad_w_out, router_grads = moe(
        slots_out.reshape(by_chip), grad_in.reshape(by_chip), small, w_in[0], w_out[0]
    )
    rep_count = lax.axis_size("rep")
    slows, fasts = rep_places()[3:]
    gwin = grad_w_in.reshape(slows, fasts, model_width // rep_count, -1)
    gwout = grad_w_out.reshape(slows, fasts, -1, model_width)
    early_part, dense, prompt_part, near_part, grad_own, grad_resid, returned, ra, rb = back(
        grad_back.reshape(slot_count, model_width), col_slots, mid, cotangent, gains, every_tok, weights,
        (normed, queries, keys, values, attended, lse, rev), bucket_row, router_grads,
        result.reshape(expert_count, capacity, model_width), gwin, gwout,
    )
    chips = shard_count // 2
    lines = weight_rows // QUARTERS
    grad_tokens, mixed, early, late, ka, la, kb, lb = reduce_all(
        gains, col_slots, dense.reshape(chips, 2, QUARTERS, lines, -1),
        prompt_part.reshape(chips, 2, PR_DEV, model_width), near_part, grad_own, grad_resid, tokens, mid, gate,
        returned.reshape(slot_count, model_width), gwin, ra, gwout, rb,
        early_part.reshape(QUARTERS, lines, -1),
    )
    in_grad, out_grad, gq, gk, gv, go, router, gain_attn, gain_moe, table = finish(
        ka, la, kb, lb, early, late, expert_count, table_rows, head_count
    )
    return (
        mixed,
        grad_tokens,
        *(part.reshape(weight_rows, model_width) for part in (gq, gk, gv, go)),
        router,
        gain_attn[0],
        gain_moe[0],
        table,
        in_grad[None],
        out_grad[None],
    )


def solution(mesh):
    return jax.shard_map(
        local,
        mesh=mesh,
        in_specs=(
            P(("rep", "shard"), None),
            P(("rep", "shard")),
            P(("rep", "shard")),
            P("shard", None),
            P("shard", None),
            P("shard", None),
            P("shard", None),
            P("shard", None),
            P("shard"),
            P("shard"),
            P("shard", None),
            P("shard", None, None),
            P("shard", None, None),
            P(("rep", "shard"), None),
        ),
        out_specs=(
            P(("rep", "shard"), None),
            P(("rep", "shard"), None),
            P("shard", None),
            P("shard", None),
            P("shard", None),
            P("shard", None),
            P("shard", None),
            P("shard"),
            P("shard"),
            P("shard", None),
            P("shard", "rep", None),
            P("shard", "rep", None),
        ),
        check_vma=False,
    )
```

```python
import jax
import jax.numpy as jnp
import numpy as np
from jax import lax
from jax.experimental import pallas as pl
from jax.experimental.pallas import tpu as pltpu
from jax.sharding import PartitionSpec as P

PR_DEV = 128
TILE = 128
SPAN = 2 * TILE
BLOCK = 1536
NEAR = 3
QUARTERS = 4
far_before, far_after, causal_tile, hidden_tile, tile_kinds = 3, 4, 5, 6, 7
vmem_cap = 60 * 1024 * 1024
mesh_ids = pl.DeviceIdType.MESH
bucket_edges = (12, 16, 23, 32, 46, 64, 91)
norm_epsilon = 1e-06
masked_score = -1e30
low, single = jnp.bfloat16, jnp.float32
in_vmem = pl.BlockSpec(memory_space=pltpu.VMEM)
anywhere = pl.BlockSpec(memory_space=pl.ANY)


def inverse_rms(values):
    return lax.rsqrt(jnp.mean(values * values, axis=-1, keepdims=True) + norm_epsilon)


def norm_pull(grad, values, gain):
    scale = inverse_rms(values)
    pulled = grad * gain
    mean = jnp.mean(pulled * values, axis=-1, keepdims=True)
    return scale * pulled - values * (scale * scale * scale * mean)


def nt(left, right):
    return lax.dot_general(left, right, (((1,), (1,)), ((), ())), preferred_element_type=single)


def tn(left, right):
    return lax.dot_general(left, right, (((0,), (0,)), ((), ())), preferred_element_type=single)


def nn(left, right):
    return jnp.dot(left, right, preferred_element_type=single)


def thirds_of(values):
    first = values.astype(low)
    rest = values - first.astype(single)
    second = rest.astype(low)
    return first, second, (rest - second.astype(single)).astype(low)


def fill_tiles(tiles_ref, rev_row, low, high):
    spread = jnp.broadcast_to(rev_row, (TILE, 4 * TILE))
    rolled = pltpu.roll(spread, 0, 1, stride=1, stride_axis=0)
    keys = lax.broadcasted_iota(jnp.int32, (TILE, TILE), 0)
    rows = lax.broadcasted_iota(jnp.int32, (TILE, TILE), 1)
    tiles_ref[0] = rolled[:, TILE : 2 * TILE]
    tiles_ref[1] = rolled[:, :TILE]
    tiles_ref[2] = rolled[:, 3 * TILE :]
    tiles_ref[far_before] = jnp.broadcast_to(low, (TILE, TILE))
    tiles_ref[far_after] = jnp.broadcast_to(high, (TILE, TILE))
    tiles_ref[causal_tile] = jnp.where(keys <= rows, rolled[:, :TILE], masked_score)
    tiles_ref[hidden_tile] = jnp.full((TILE, TILE), masked_score, jnp.float32)


def prompt_tile(block, chunk, shard_id, block_count):
    if chunk == 0:
        gap = block - shard_id
        far = jnp.where(gap < 0, far_before, far_after)
        return jnp.where(jnp.abs(gap) <= 1, gap + 1, far)
    if chunk == 1 and block == block_count - 1:
        return jnp.where(shard_id % 2 == 0, 0, far_before)
    return far_before


def local_tile(block, chunk, shard_id):
    if block >= 2:
        return ((causal_tile, 0), (hidden_tile, causal_tile))[block - 2][chunk]
    kind = 0 if (block, chunk) == (1, 0) else far_before
    return jnp.where(shard_id % 2 == 1, kind, hidden_tile)


def prompt_grid(part, shard_id, block_count):
    return [
        [(side, prompt_tile(2 * part + half, chunk, shard_id, block_count)) for side in range(2) for chunk in range(3)]
        for half in range(2)
    ]


def local_grid(part, shard_id):
    return [
        [(side, local_tile(2 * part + half, chunk, shard_id)) for side in range(2) for chunk in range(2)]
        for half in range(2)
    ]


def tile_of(values, i, j):
    return values[i * TILE : (i + 1) * TILE, j * TILE : (j + 1) * TILE]


def with_bias(scores, tiles_ref, grid):
    lines = [
        jnp.concatenate(
            [tile_of(scores, i, j) + tiles_ref[side, kind] for j, (side, kind) in enumerate(row)], axis=1
        )
        for i, row in enumerate(grid)
    ]
    return jnp.concatenate(lines, axis=0)


def both_heads(values):
    first = head_mask(values.shape[0], 0)
    none = jnp.zeros_like(values)
    return jnp.concatenate([jnp.where(first, values, none), jnp.where(first, none, values)], axis=0)


def continuation(values, axis):
    rows = values.shape[axis] // 2
    pick = (lambda a, b: values[:, a:b]) if axis else (lambda a, b: values[a:b])
    return jnp.concatenate([pick(PR_DEV, rows), pick(rows + PR_DEV, 2 * rows)], axis=axis)


def fold8(values):
    return values.reshape(values.shape[0] // 8, 8, values.shape[1])


def head_mask(rows, side):
    lanes = lax.broadcasted_iota(jnp.int32, (rows, TILE), 1)
    return (lanes < TILE // 2) if side == 0 else (lanes >= TILE // 2)


def distance_buckets(bucket_count):
    steps = np.arange(4 * TILE)
    gap = -np.where(steps < 2 * TILE, steps, steps - 4 * TILE)
    size = np.abs(gap)
    far = sum((size >= edge).astype(np.int64) for edge in bucket_edges)
    exact = bucket_count // 4
    return np.where(gap > 0, bucket_count // 2, 0) + np.where(size < exact, size, exact + far)


def front_kernel(
    ints_ref, bucket_ref, cot_ref, wq_hbm, wk_hbm, wv_hbm, wo_hbm, tok_hbm, little_hbm,
    lse_ref, rev_ref, gate_ref, col_ref, gain_ref, x_ref, gin_hbm, w_hbm, every_hbm, small_hbm,
    n_hbm, q_hbm, k_hbm, v_hbm, o_hbm, mid_hbm,
    tiles, vt, sp, sl, gbuf, w_ref, every_ref, small_ref, tok_ref, shard_w, little,
    n_ref, nt_ref, q_ref, k_ref, v_ref, ot_ref, mid_ref,
    gs, gr, loc, wz_s, wz_r, tz_s, tz_r, sz_s, sz_r, wr_s, wr_r, wt_s, wt_r, tt_s, tt_r, st_s, st_r, et_s, et_r,
):
    rep, chip, core, chips, quarter = places()
    along, across, twin = peer_lists()
    shards = chips * 2
    shard_id = chip * 2 + core
    rows, width = tok_ref.shape
    experts = shards
    blocks = every_ref.shape[0] // TILE - 4
    half = TILE // 2
    heads_held = rev_ref.shape[0]
    lines = shard_w.shape[1]
    rest_rows = rows - PR_DEV
    prompt_len = blocks * TILE
    others = [(rep, (shard_id + k) % shards) for k in range(1, shards)]

    def w_rows(source, side):
        return pl.ds(pl.multiple_of((source * 2 + side) * lines, lines), lines)

    def t_rows(source, side):
        return every_ref.at[pl.ds(pl.multiple_of((source * 2 + side) * PR_DEV, PR_DEV), PR_DEV)]

    loads = [
        pltpu.make_async_copy(source, shard_w.at[i], loc.at[i])
        for i, source in enumerate((wq_hbm, wk_hbm, wv_hbm, wo_hbm))
    ] + [pltpu.make_async_copy(tok_hbm, tok_ref, loc.at[4]), pltpu.make_async_copy(little_hbm, little, loc.at[5])]
    for copy in loads:
        copy.start()
    greeted = [twin] + along
    for device in across + [(rep, (chip + k) % chips * 2 + 1 - core) for k in range(1, chips)]:
        greeted.append(device)
    greet(greeted)
    started = []

    def go(source, target, sems, device):
        copy = send(source, target, sems, device)
        copy.start()
        started.append(copy)

    def landed(piece, sems):
        send(piece, piece, sems, twin).wait_recv()

    for copy in loads:
        copy.wait()
    mine = w_rows(chip, core)
    prompt, rest = tok_ref.at[pl.ds(0, PR_DEV)], tok_ref.at[pl.ds(PR_DEV, rest_rows)]
    for k, device in enumerate(along):
        go(shard_w.at[quarter], w_ref.at[quarter, mine], (wz_s.at[k], wz_r.at[k]), device)
        go(little, small_ref.at[mine], (sz_s.at[k], sz_r.at[k]), device)
    go(little, small_ref.at[mine], (st_s.at[0], st_r.at[0]), twin)
    go(rest, every_ref.at[pl.ds(prompt_len, rest_rows)], (et_s.at[0], et_r.at[0]), twin)
    go(prompt, t_rows(chip, core), (tt_s.at[0], tt_r.at[0]), twin)
    go(shard_w, w_ref.at[:, mine], (wt_s.at[0], wt_r.at[0]), twin)
    w_ref[:, mine, :] = shard_w[...]
    small_ref[mine, :] = little[...]
    every_ref[pl.ds(pl.multiple_of(shard_id * PR_DEV, PR_DEV), PR_DEV), :] = tok_ref[:PR_DEV, :]
    every_ref[prompt_len + rest_rows :, :] = tok_ref[PR_DEV:, :]
    ints = ints_ref[...].astype(single).T
    route_col = ints[:, 0:1].astype(jnp.int32)
    col_ref[...] = jnp.broadcast_to(ints[:, 1:2].astype(jnp.int32), col_ref.shape)
    slots = lax.broadcasted_iota(jnp.int32, (x_ref.shape[0], rows), 0)
    place = (slots == ints_ref[1:2, :]).astype(low)
    gbuf[...] = nn(place, cot_ref[...]).astype(low).reshape(gbuf.shape)
    own_g = pltpu.make_async_copy(gbuf.at[shard_id], gin_hbm.at[shard_id], loc.at[6])
    own_g.start()

    for k in range(1, chips):
        source = (chip + chips - k) % chips
        piece = w_ref.at[quarter, w_rows(source, core)]
        landed(piece, (wz_s.at[k - 1], wz_r.at[k - 1]))
        for j, device in enumerate(across):
            go(piece, piece, (wr_s.at[k - 1, j], wr_r.at[k - 1, j]), device)
        go(prompt, t_rows(chip, core), (tz_s.at[k - 1], tz_r.at[k - 1]), along[k - 1])
    for k in range(1, chips):
        source = (chip + chips - k) % chips
        piece = small_ref.at[w_rows(source, core)]
        landed(piece, (sz_s.at[k - 1], sz_r.at[k - 1]))
        go(piece, piece, (st_s.at[k], st_r.at[k]), twin)
    for k in range(1, chips):
        source = (chip + chips - k) % chips
        piece = t_rows(source, core)
        landed(piece, (tz_s.at[k - 1], tz_r.at[k - 1]))
        go(piece, piece, (tt_s.at[k], tt_r.at[k]), twin)
    for k, device in enumerate(others):
        go(gbuf.at[device[1]], gin_hbm.at[shard_id], (gs.at[k], gr.at[k]), device)
    for k in range(chips):
        source = (chip + chips - k) % chips
        landed(small_ref.at[w_rows(source, 1 - core)], (st_s.at[k], st_r.at[k]))
    writes = []

    def write(source, target):
        writes.append(pltpu.make_async_copy(source, target, loc.at[7 + len(writes)]))
        writes[-1].start()

    write(small_ref, small_hbm)

    small_t = small_ref[...].astype(single).T
    gain_attn = small_t[experts : experts + 1]
    gain_moe = small_t[experts + 1 : experts + 2]
    gain_ref[...] = jnp.concatenate([gain_attn, gain_moe, jnp.zeros((6, width), single)], axis=0)
    shard_rows = width // shards
    table_rows = 2 * TILE // 8 // shards
    owner = lax.broadcasted_iota(jnp.int32, (shards, shard_rows, 4 * TILE), 0)
    offset = lax.broadcasted_iota(jnp.int32, (shards, shard_rows, 4 * TILE), 1)
    held = jnp.where(offset < table_rows, owner * table_rows + offset, -1).reshape(width, 4 * TILE)
    hot = (held == bucket_ref[0:1, :]).astype(low)
    table_t = small_t[experts + 2 : experts + 2 + heads_held].astype(low)
    rev_ref[...] = nn(table_t, hot)

    for k in range(chips):
        source = (chip + chips - k) % chips
        landed(t_rows(source, 1 - core), (tt_s.at[k], tt_r.at[k]))
    landed(every_ref.at[pl.ds(prompt_len, rest_rows)], (et_s.at[0], et_r.at[0]))
    write(every_ref, every_hbm)

    @pl.loop(0, every_ref.shape[0] // SPAN)
    def scale(part):
        span = pl.ds(pl.multiple_of(part * SPAN, SPAN), SPAN)
        values = every_ref[span, :].astype(single)
        normed = values * inverse_rms(values) * gain_attn
        n_ref[span, :] = normed.astype(low)
        nt_ref[:, span] = normed.T.astype(low)

    write(nt_ref, n_hbm)
    for k in range(1, chips):
        source = (chip + chips - k) % chips
        for j in range(1, QUARTERS):
            piece = w_ref.at[(quarter + QUARTERS - j) % QUARTERS, w_rows(source, core)]
            landed(piece, (wr_s.at[k - 1, j - 1], wr_r.at[k - 1, j - 1]))
        piece = w_ref.at[:, w_rows(source, core)]
        go(piece, piece, (wt_s.at[k], wt_r.at[k]), twin)
    for k in range(chips):
        source = (chip + chips - k) % chips
        landed(w_ref.at[:, w_rows(source, 1 - core)], (wt_s.at[k], wt_r.at[k]))
    write(w_ref, w_hbm)

    @pl.loop(0, every_ref.shape[0] // (2 * SPAN))
    def project(part):
        span = pl.ds(pl.multiple_of(part * 2 * SPAN, 2 * SPAN), 2 * SPAN)
        k_ref[span, :] = nn(n_ref[span, :], w_ref[1]).astype(low)
        v_ref[span, :] = nn(n_ref[span, :], w_ref[2]).astype(low)

    own = pl.ds(pl.multiple_of(shard_id * TILE, TILE), TILE)
    normed = jnp.concatenate([n_ref[own, :], n_ref[(blocks + 2) * TILE :, :]], axis=0)
    q_ref[...] = (nn(normed, w_ref[0]).astype(low) * jnp.asarray(0.125, low)).astype(low)
    write(k_ref, k_hbm)
    write(v_ref, v_hbm)
    write(q_ref, q_hbm)

    @pl.loop(0, width // TILE)
    def pair_loop(pair):
        cols = pl.ds(pl.multiple_of(pair * TILE, TILE), TILE)
        vt[...] = v_ref[:, cols].T
        q_both = both_heads(q_ref[:, cols])
        q_local = continuation(q_both, 0)
        for side in range(2):
            rev_row = rev_ref[pl.ds(pair * 2 + side, 1), :]
            fill_tiles(tiles.at[side], rev_row, rev_row[:, SPAN - 1 : SPAN], rev_row[:, SPAN : SPAN + 1])
        top = jnp.full((8, 2 * rows), masked_score, single)
        for part in range(blocks // 2):
            keys = slice(part * SPAN, (part + 1) * SPAN)
            scores = with_bias(nt(k_ref[keys, cols], q_both), tiles, prompt_grid(part, shard_id, blocks))
            sp[keys, :] = scores
            top = jnp.maximum(top, jnp.max(fold8(scores), axis=0))
        local = continuation(top, 1)
        for part in range(2):
            keys = slice(part * SPAN, (part + 1) * SPAN)
            held = slice((blocks // 2 + part) * SPAN, (blocks // 2 + part + 1) * SPAN)
            scores = with_bias(nt(k_ref[held, cols], q_local), tiles, local_grid(part, shard_id))
            sl[keys, :] = scores
            local = jnp.maximum(local, jnp.max(fold8(scores), axis=0))
        rest = rows - PR_DEV
        top = jnp.concatenate(
            [top[:, :PR_DEV], local[:, :rest], top[:, rows : rows + PR_DEV], local[:, rest:]], axis=1
        )
        top = jnp.max(top, axis=0, keepdims=True)
        total = jnp.zeros((8, 2 * rows), single)
        summed = [jnp.zeros((half, rows), single)] * 2
        for part in range(blocks // 2):
            keys = slice(part * SPAN, (part + 1) * SPAN)
            weights = jnp.exp(sp[keys, :] - top)
            total = total + jnp.sum(fold8(weights), axis=0)
            weights = weights.astype(low)
            for side in range(2):
                heads = slice(side * half, (side + 1) * half)
                summed[side] = summed[side] + nn(vt[heads, keys], weights[:, side * rows : (side + 1) * rows])
        top_local, total_local = continuation(top, 1), continuation(total, 1)
        summed_local = [part_sum[:, PR_DEV:] for part_sum in summed]
        for part in range(2):
            keys = slice(part * SPAN, (part + 1) * SPAN)
            held = slice((blocks // 2 + part) * SPAN, (blocks // 2 + part + 1) * SPAN)
            weights = jnp.exp(sl[keys, :] - top_local)
            total_local = total_local + jnp.sum(fold8(weights), axis=0)
            weights = weights.astype(low)
            for side in range(2):
                heads = slice(side * half, (side + 1) * half)
                summed_local[side] = summed_local[side] + nn(
                    vt[heads, held], weights[:, side * rest : (side + 1) * rest]
                )
        for side in range(2):
            head = pair * 2 + side
            ours = slice(side * rows, (side + 1) * rows)
            sums = jnp.concatenate(
                [total[:, side * rows : side * rows + PR_DEV], total_local[:, side * rest : (side + 1) * rest]], axis=1
            )
            sums = jnp.sum(sums, axis=0, keepdims=True)
            mixed = jnp.concatenate([summed[side][:, :PR_DEV], summed_local[side]], axis=1)
            ot_ref[pl.ds(pl.multiple_of(head * half, half), half), :] = mixed / sums
            lse_ref[pl.ds(head, 1), :] = top[:, ours] + jnp.log(sums)

    resid_mid = tok_ref[...].astype(single) + nn(ot_ref[...].T.astype(low), w_ref[3])
    mid_ref[...] = resid_mid
    write(ot_ref, o_hbm)
    write(mid_ref, mid_hbm)
    mid_low = (resid_mid * inverse_rms(resid_mid) * gain_moe).astype(low)
    probs = router_softmax(mid_low, small_ref[...], experts)
    lanes = lax.broadcasted_iota(jnp.int32, probs.shape, 1)
    gate = jnp.sum(jnp.where(lanes == route_col, probs, 0.0), axis=1, keepdims=True)
    gate_ref[...] = jnp.broadcast_to(gate, gate_ref.shape)
    x_ref[...] = nn(place, mid_low).astype(low)
    own_g.wait()
    for k in range(shards - 1):
        landed(gin_hbm.at[(shard_id + shards - k - 1) % shards], (gs.at[k], gr.at[k]))
    for copy in writes:
        copy.wait()
    for copy in started:
        copy.wait_send()


def router_softmax(rows_low, small, experts):
    logits = nn(rows_low, small)
    lanes = lax.broadcasted_iota(jnp.int32, logits.shape, 1)
    logits = jnp.where(lanes < experts, logits, masked_score)
    powers = jnp.exp(logits - jnp.max(logits, axis=1, keepdims=True))
    return powers / jnp.sum(powers, axis=1, keepdims=True)


def front(ints, bucket_row, cotangent, weights, tokens, small, slot_count):
    rows, width = tokens.shape
    shards = lax.axis_size("shard")
    chips, count = shards // 2, shards // 2 - 1
    keys = shards * PR_DEV + 2 * (rows - PR_DEV)
    lines = small.shape[0]
    shape = jax.ShapeDtypeStruct
    sem = pltpu.SemaphoreType.DMA
    vm = pltpu.VMEM
    return pl.pallas_call(
        front_kernel,
        out_shape=(
            shape((16, rows), single), shape((16, 4 * TILE), single), shape((rows, TILE), single),
            shape((rows, TILE), jnp.int32), shape((8, width), single), shape((slot_count, width), low),
            shape((shards, slot_count // shards, width), low), shape((4, width, width), low),
            shape((keys, width), low), shape((width, TILE), low),
            shape((width, keys), low), shape((rows, width), low), shape((keys, width), low),
            shape((keys, width), low), shape((width, rows), single), shape((rows, width), single),
        ),
        in_specs=[in_vmem] * 3 + [anywhere] * 6,
        out_specs=(in_vmem,) * 6 + (anywhere,) * 10,
        scratch_shapes=[
            vm((2, tile_kinds, TILE, TILE), single), vm((TILE, keys), low), vm((keys - 2 * SPAN, 2 * rows), single),
            vm((2 * SPAN, 2 * (rows - TILE)), single),
            vm((shards, slot_count // shards, width), low), vm((4, width, width), low), vm((keys, width), low),
            vm((width, TILE), low), vm((rows, width), low), vm((4, lines, width), low), vm((lines, TILE), low),
            vm((keys, width), low), vm((width, keys), low), vm((rows, width), low), vm((keys, width), low),
            vm((keys, width), low), vm((width, rows), single), vm((rows, width), single),
            sem((shards - 1,)), sem((shards - 1,)), sem((16,)), sem((count,)), sem((count,)), sem((count,)),
            sem((count,)), sem((count,)), sem((count,)), sem((count, 3)), sem((count, 3)), sem((chips,)), sem((chips,)),
            sem((chips,)), sem((chips,)), sem((chips,)), sem((chips,)), sem((1,)), sem((1,)),
        ],
        compiler_params=pltpu.CompilerParams(collective_id=2, has_side_effects=True, vmem_limit_bytes=vmem_cap),
        cost_estimate=pl.CostEstimate(flops=30_000_000_000, bytes_accessed=20_000_000, transcendentals=8_000_000),
        name="front",
    )(ints, bucket_row, cotangent, *weights, tokens, small)


def moe_kernel(
    x_ref, g_ref, small_ref, w_in_ref, w_out_ref,
    back_ref, out_ref, gwin_ref, gwout_ref, rg_ref,
    w_in, w_out, xin, gm, gg, hid, gpre, logit_grads, x_t, gwin, gwout,
    xs, xr, ms, mr, ws, ls, os_in, os_out,
):
    rep, chip, core, chips, quarter = places()
    experts = chips * 2
    here = chip * 2 + core
    pair_rows = 2 * xin.shape[2]
    hidden = w_in_ref.shape[1]
    block = BLOCK
    loads = [
        pltpu.make_async_copy(w_in_ref, w_in, ws.at[0]),
        pltpu.make_async_copy(w_out_ref, w_out, ws.at[1]),
    ]
    for copy in loads:
        copy.start()
    twin = (rep, chip * 2 + 1 - core)
    targets = [
        (k, side, (rep, chip_across(chip, k) * 2 + side)) for k in range(1, chips) for side in range(2)
    ]
    greet([twin] + [device for _, _, device in targets])
    sent = [send(x_ref.at[chip, 1 - core], xin.at[chip, core], (xs.at[0, 0], xr.at[0, core]), twin)]
    for k, side, device in targets:
        sent.append(
            send(x_ref.at[chip_across(chip, k), side], xin.at[chip, core], (xs.at[k, side], xr.at[k, core]), device)
        )
    for copy in sent[:5]:
        copy.start()
    xin[chip, core] = x_ref[chip, core]
    for copy in loads:
        copy.wait()

    def arrived(k, source, side):
        piece = xin.at[source, side]
        send(piece, piece, (xs.at[0, 0], xr.at[k, side]), twin).wait_recv()

    @pl.loop(0, chips)
    def chunk(k):
        source = chip_across(chip, k)

        @pl.when(k == 0)
        def _():
            arrived(0, chip, 1 - core)

        @pl.when(k > 0)
        def _():
            for side in range(2):
                arrived(k, source, side)

        rows = xin[source].reshape(pair_rows, xin.shape[3])
        grads = g_ref[source].reshape(pair_rows, xin.shape[3])
        probs = router_softmax(rows, small_ref[...], experts)
        lanes = lax.broadcasted_iota(jnp.int32, probs.shape, 1)
        gate = jnp.sum(jnp.where(lanes == here, probs, 0.0), axis=1, keepdims=True)
        gated = (gate * grads.astype(single)).astype(low)
        span = pl.ds(pl.multiple_of(source * pair_rows, pair_rows), pair_rows)
        gg[span, :] = gated
        pre = nn(rows, w_in[...])
        grad_hidden = nt(gated, w_out[...])
        square = pre * pre
        wave = jnp.tanh(0.7978845608028654 * pre * (1.0 + 0.044715 * square))
        left = 0.5 + 0.5 * wave
        active = (pre * left).astype(low)
        slope = left + (0.5 * pre) * (1.0 - wave * wave) * (0.7978845608028654 + 0.10703222440890037 * square)
        grad_pre = (grad_hidden * slope).astype(low)
        hid[span, :] = active
        gpre[span, :] = grad_pre
        out = nn(active, w_out[...]).astype(low)
        out_ref[source] = out.reshape(out_ref.shape[1:])
        grad_gate = jnp.sum(grads.astype(single) * out.astype(single), axis=1, keepdims=True)
        chosen = jnp.where(lanes == here, 1.0, 0.0)
        grad_logits = jnp.where(lanes < experts, gate * grad_gate * (chosen - probs), 0.0)
        logit_grads[span, :] = grad_logits
        router = small_ref[...]
        total = nt(grad_pre, w_in[...]) + sum(nt(part, router) for part in thirds_of(grad_logits))
        gm[source] = total.astype(low).reshape(gm.shape[1:])

        def reply(side, slot):
            return send(
                gm.at[source, side], back_ref.at[chip, core], (ms.at[k, slot], mr.at[k, core]), (rep, source * 2 + side)
            )

        @pl.when(k == 0)
        def _():
            for copy in sent[5:]:
                copy.start()
            reply(1 - core, 0).start()
            pltpu.make_async_copy(gm.at[chip, core], back_ref.at[chip, core], ls).start()

        @pl.when(k > 0)
        def _():
            for side in range(2):
                reply(side, side).start()

    every = xin[...].reshape(gg.shape)
    x_t[...] = every.T

    def strip_writes(part):
        cols = pl.ds(pl.multiple_of(part * block, block), block)
        return [
            pltpu.make_async_copy(gwin.at[:, cols], gwin_ref.at[:, cols], os_in.at[part]),
            pltpu.make_async_copy(gwout.at[cols], gwout_ref.at[cols], os_out.at[part]),
        ]

    @pl.loop(0, hidden // block)
    def strip(part):
        cols = pl.ds(pl.multiple_of(part * block, block), block)
        first, second = strip_writes(part)
        gwin[:, cols] = nn(x_t[...], gpre[:, cols]).astype(low)
        first.start()
        gwout[cols, :] = tn(hid[:, cols], gg[...]).astype(low)
        second.start()

    rg_ref[...] = sum(nn(x_t[...], part) for part in thirds_of(logit_grads[...]))
    pltpu.make_async_copy(gm.at[chip, core], back_ref.at[chip, core], ls).wait()

    def replied(k, source, side):
        piece = back_ref.at[source, side]
        send(piece, piece, (ms.at[0, 0], mr.at[k, side]), twin).wait_recv()

    replied(0, chip, 1 - core)
    for k in range(1, chips):
        for side in range(2):
            replied(k, chip_across(chip, k), side)
    for copy in sent:
        copy.wait_send()
    for part in range(hidden // block):
        for copy in strip_writes(part):
            copy.wait()
    send(gm.at[chip, 0], back_ref.at[chip, core], (ms.at[0, 0], mr.at[0, 0]), twin).wait_send()
    for k in range(1, chips):
        for side in range(2):
            send(gm.at[chip, 0], back_ref.at[chip, core], (ms.at[k, side], mr.at[0, 0]), twin).wait_send()


def moe(rows_out, grad_in, small, w_in, w_out):
    chips, _, cap, width = rows_out.shape
    slots = chips * 2 * cap
    hidden = w_in.shape[1]
    shape = jax.ShapeDtypeStruct
    pairs = pltpu.SemaphoreType.DMA
    strips = hidden // BLOCK
    return pl.pallas_call(
        moe_kernel,
        out_shape=(
            shape(rows_out.shape, low), shape(rows_out.shape, low), shape((width, hidden), low),
            shape((hidden, width), low), shape((width, TILE), single),
        ),
        in_specs=[in_vmem] * 3 + [anywhere] * 2,
        out_specs=(anywhere, in_vmem, anywhere, anywhere, in_vmem),
        scratch_shapes=[
            pltpu.VMEM((width, hidden), low), pltpu.VMEM((hidden, width), low),
            pltpu.VMEM(rows_out.shape, low), pltpu.VMEM(rows_out.shape, low), pltpu.VMEM((slots, width), low),
            pltpu.VMEM((slots, hidden), low), pltpu.VMEM((slots, hidden), low),
            pltpu.VMEM((slots, TILE), single), pltpu.VMEM((width, slots), low), pltpu.VMEM((width, hidden), low), pltpu.VMEM((hidden, width), low),
            pairs((chips, 2)), pairs((chips, 2)), pairs((chips, 2)), pairs((chips, 2)), pairs((2,)), pairs,
            pairs((strips,)), pairs((strips,)),
        ],
        compiler_params=pltpu.CompilerParams(collective_id=3, has_side_effects=True, vmem_limit_bytes=vmem_cap),
        cost_estimate=pl.CostEstimate(flops=40_000_000_000, bytes_accessed=40_000_000, transcendentals=3_000_000),
        name="moe",
    )(rows_out, grad_in, small, w_in, w_out)


def back_kernel(
    col_ref, gain_ref, lse_ref, rev_ref, bucket_ref, rg_ref, back_hbm, mid_hbm, cot_hbm, q_hbm, k_hbm, v_hbm, o_hbm,
    every_hbm, w_hbm, n_hbm, gwin_hbm, gwout_hbm, out_hbm,
    z_ref, dense_hbm, p_hbm, e_hbm, own_hbm, gres_hbm, ra_hbm, rb_hbm, ret_hbm,
    tiles, sums, diag, kt, dqt, far_sums, g_ref, dq_ref, dk_ref, dv_ref, attn_gain,
    every_ref, w_ref, n_ref, back_ref, mid_ref, cot_ref, q_ref, k_ref, v_ref, o_ref,
    dense_ref, own_ref, gres_ref,
    o_grad, o_half, o_sum, o_in, h_grad, h_half, h_sum, h_in,
    loc, out, xs, xr, as_, ar, bs, br, os_, or_, oz_s, oz_r, hs_, hr_, hz_s, hz_r,
):
    shard_id = lax.axis_index("shard")
    shards = lax.axis_size("shard")
    rows, width = mid_ref.shape
    blocks = k_ref.shape[0] // TILE - 4
    half = TILE // 2
    experts = shards
    heads_held = rev_ref.shape[0]
    rep, slow, fast, slows, fasts = rep_places()
    _, chip, core, chips, _ = places()
    along, _, twin = peer_lists()
    loads = [
        pltpu.make_async_copy(source, target, loc.at[i])
        for i, (source, target) in enumerate((
            (back_hbm, back_ref), (mid_hbm, mid_ref), (cot_hbm, cot_ref), (w_hbm.at[3], w_ref.at[3]), (o_hbm, o_ref),
            (q_hbm, q_ref), (k_hbm, k_ref), (v_hbm, v_ref), (n_hbm, n_ref), (w_hbm.at[pl.ds(0, 3)], w_ref.at[pl.ds(0, 3)]),
            (every_hbm, every_ref), (out_hbm.at[chip, core], ret_hbm.at[chip, core]),
        ))
    ]
    for copy in loads:
        copy.start()
    writes = []

    def write(source, target):
        writes.append(pltpu.make_async_copy(source, target, out.at[len(writes)]))
        writes[-1].start()

    beside = [(slow * fasts + (fast + j) % fasts, shard_id) for j in range(1, fasts)]
    beyond = [((slow + j) % slows * fasts + fast, shard_id) for j in range(1, slows)]
    nearby = result_peers(rep, chip, core, range(NEAR))
    far_twins = [(rep, (chip + k) % chips * 2 + 1 - core) for k in range(1, chips)]
    greet([twin] + along + far_twins + beside + beyond)
    sent = [
        send(gwin_hbm.at[:, (fast + j + 1) % fasts], ra_hbm.at[j], (as_.at[j], ar.at[j]), device)
        for j, device in enumerate(beside)
    ] + [
        send(gwout_hbm.at[(slow + j + 1) % slows], rb_hbm.at[j], (bs.at[j], br.at[j]), device)
        for j, device in enumerate(beyond)
    ] + [
        send(out_hbm.at[chip_across(chip, k), side if k else 1 - core], ret_hbm.at[chip, core], (xs.at[k, side], xr.at[k, core]), device)
        for k, side, device in nearby
    ]
    for copy in sent:
        copy.start()
    diag[...] = jnp.zeros_like(diag)
    far_sums[...] = jnp.zeros_like(far_sums)
    tile_rows = lax.broadcasted_iota(jnp.int32, (TILE, TILE), 0)
    tile_cols = lax.broadcasted_iota(jnp.int32, (TILE, TILE), 1)
    flip = (tile_rows + tile_cols == TILE - 1).astype(single)

    for copy in loads[:5]:
        copy.wait()
    slots = lax.broadcasted_iota(jnp.int32, (rows, back_ref.shape[0]), 1)
    grad_mid = nn((slots == col_ref[:, 0:1]).astype(low), back_ref[...])
    resid_mid = mid_ref[...]
    grad_gain_moe = jnp.sum(grad_mid * resid_mid * inverse_rms(resid_mid), axis=0, keepdims=True)
    grad_resid = cot_ref[...].astype(single) + norm_pull(grad_mid, resid_mid, gain_ref[1:2, :])
    gres_ref[...] = grad_resid
    write(gres_ref, gres_hbm)
    grad_attn = grad_resid.astype(low)
    g_ref[...] = nt(grad_attn, w_ref[3]).astype(low)
    o_grad[...] = nn(o_ref[...].astype(low), grad_attn).reshape(o_grad.shape).astype(low)
    o_halves = [send(o_grad.at[2 * k + 1 - core], o_half.at[k], (os_.at[k], or_.at[k]), twin) for k in range(chips)]
    o_sends = [
        send(o_sum.at[(chip + k + 1) % chips], o_in.at[k], (oz_s.at[k], oz_r.at[k]), device)
        for k, device in enumerate(along)
    ]
    for copy in o_halves:
        copy.start()
    h_halves = [send(h_grad.at[2 * k + 1 - core], h_half.at[k], (hs_.at[k], hr_.at[k]), twin) for k in range(chips)]
    h_sends = [
        send(h_sum.at[(chip + k + 1) % chips], h_in.at[k], (hz_s.at[k], hz_r.at[k]), device)
        for k, device in enumerate(along)
    ]
    for copy in loads[5:]:
        copy.wait()
    own = pl.ds(pl.multiple_of(shard_id * TILE, TILE), TILE)
    tail = slice((blocks + 2) * TILE, (blocks + 4) * TILE)
    early = width // 2

    @pl.loop(0, width // TILE)
    def pair_loop(pair):
        cols = pl.ds(pl.multiple_of(pair * TILE, TILE), TILE)
        kt[...] = k_ref[:, cols].T
        g_pair = g_ref[:, cols]
        q_both, g_both = both_heads(q_ref[:, cols]), both_heads(g_pair)
        delta_t = g_pair.astype(single).T * o_ref[cols, :]
        delta = jnp.concatenate(
            [jnp.sum(delta_t[:half], axis=0, keepdims=True), jnp.sum(delta_t[half:], axis=0, keepdims=True)], axis=1
        )
        log_total = jnp.concatenate([lse_ref[pl.ds(pair * 2, 1), :], lse_ref[pl.ds(pair * 2 + 1, 1), :]], axis=1)
        for side in range(2):
            rev_row = rev_ref[pl.ds(pair * 2 + side, 1), :]
            fill_tiles(tiles.at[side], rev_row, rev_row[:, SPAN - 1 : SPAN], rev_row[:, SPAN : SPAN + 1])
        sums[...] = jnp.zeros_like(sums)

        def block_grads(part, q_rows, g_rows, shift, scale, grid):
            keys = slice(part * SPAN, (part + 1) * SPAN)
            count = q_rows.shape[0] // 2
            scores = with_bias(nt(k_ref[keys, cols], q_rows), tiles, grid)
            weights = jnp.exp(scores - shift)
            grad_scores = weights * (nt(v_ref[keys, cols], g_rows) - scale)
            for i, row in enumerate(grid):
                for j, (side, kind) in enumerate(row):
                    sums[side, kind] += tile_of(grad_scores, i, j)
            raw = grad_scores.astype(low)
            dk_ref[keys, cols] = nn(raw, q_rows).astype(low)
            dv_ref[keys, cols] = nn(weights.astype(low), g_rows).astype(low)
            return [nn(kt[:half, keys], raw[:, :count]), nn(kt[half:, keys], raw[:, count:])]

        grads = [jnp.zeros((half, rows), single)] * 2
        for part in range(blocks // 2):
            more = block_grads(part, q_both, g_both, log_total, delta, prompt_grid(part, shard_id, blocks))
            grads = [old + new for old, new in zip(grads, more)]
        local = [old[:, PR_DEV:] for old in grads]
        held = (continuation(q_both, 0), continuation(g_both, 0), continuation(log_total, 1), continuation(delta, 1))
        for part in range(2):
            more = block_grads(blocks // 2 + part, *held, local_grid(part, shard_id))
            local = [old + new for old, new in zip(local, more)]
        for side in range(2):
            head = pair * 2 + side
            dqt[side * half : (side + 1) * half, :] = jnp.concatenate([grads[side][:, :PR_DEV], local[side]], axis=1)
            near = jnp.concatenate(
                [
                    sums[side, 1] + sums[side, causal_tile], sums[side, 0], jnp.zeros((TILE, TILE), single),
                    sums[side, 2],
                ],
                axis=1,
            )
            flipped = jnp.dot(flip, near, precision=lax.Precision.HIGHEST, preferred_element_type=single)
            rolled = pltpu.roll(flipped, 3 * TILE + 1, 1, stride=1, stride_axis=0)
            diag[pl.ds(head, 1), :] = jnp.sum(rolled, axis=0, keepdims=True)
            far_sums[pl.ds(head, 1), :] = jnp.concatenate(
                [
                    jnp.sum(sums[side, far_before], axis=0, keepdims=True),
                    jnp.sum(sums[side, far_after], axis=0, keepdims=True),
                ],
                axis=1,
            )
        dq_ref[:, cols] = (dqt[...].T * 0.125).astype(low)

        @pl.when(pair == 0)
        def _():
            for k in range(chips):
                o_halves[k].wait_recv()
                o_sum[k] = (o_grad[2 * k + core].astype(single) + o_half[k].astype(single)).astype(low)
            for copy in o_sends:
                copy.start()

        @pl.when(pair == width // SPAN - 1)
        def _():
            normed = jnp.concatenate([n_ref[:, own], n_ref[:, tail]], axis=1)
            for i, (left, right) in enumerate(((normed, dq_ref), (n_ref[...], dk_ref), (n_ref[...], dv_ref))):
                part = nn(left, right[:, :early]).reshape(shards, h_grad.shape[1], early)
                h_grad[:, :, i * early : (i + 1) * early] = part.astype(low)
            for copy in h_halves:
                copy.start()

        @pl.when(pair == width // SPAN)
        def _():
            for k in range(chips):
                h_halves[k].wait_recv()
                h_sum[k] = (h_grad[2 * k + core].astype(single) + h_half[k].astype(single)).astype(low)
            for copy in h_sends:
                copy.start()

    lanes = lax.broadcasted_iota(jnp.int32, (heads_held, 4 * TILE), 1)
    before = jnp.sum(far_sums[:, :TILE], axis=1, keepdims=True)
    after = jnp.sum(far_sums[:, TILE:], axis=1, keepdims=True)
    by_gap = diag[...] + jnp.where(lanes == SPAN - 1, before, 0.0) + jnp.where(lanes == SPAN, after, 0.0)
    shard_rows = width // shards
    table_rows = 2 * TILE // 8 // shards
    owner = lax.broadcasted_iota(jnp.int32, (shards, shard_rows, 4 * TILE), 0)
    offset = lax.broadcasted_iota(jnp.int32, (shards, shard_rows, 4 * TILE), 1)
    held = jnp.where(offset < table_rows, owner * table_rows + offset, -1).reshape(width, 4 * TILE)
    hot = (held == bucket_ref[0:1, :]).astype(low)
    grad_table = sum(nt(part, hot) for part in thirds_of(by_gap))

    attn_gain[...] = jnp.zeros_like(attn_gain)
    normed = jnp.concatenate([n_ref[:, own], n_ref[:, tail]], axis=1)
    dense_ref[:, :early] = nn(normed, dq_ref[:, early:]).astype(low)
    grad_own = nt(dq_ref[...], w_ref[0])
    values = jnp.concatenate([every_ref[own, :], every_ref[tail, :]], axis=0).astype(single)
    attn_gain[...] += jnp.sum(fold8(grad_own * (values * inverse_rms(values))), axis=0)
    own_ref[...] = grad_own

    def pull_rows(part):
        span = pl.ds(pl.multiple_of(part * SPAN, SPAN), SPAN)
        values = every_ref[span, :].astype(single)
        grads = nt(dk_ref[span, :], w_ref[1]) + nt(dv_ref[span, :], w_ref[2])
        attn_gain[...] += jnp.sum(fold8(grads * (values * inverse_rms(values))), axis=0)
        return grads

    @pl.loop(0, blocks // 2)
    def pull_prompt(part):
        k_ref[pl.ds(pl.multiple_of(part * SPAN, SPAN), SPAN), :] = pull_rows(part).astype(low)

    write(k_ref.at[pl.ds(0, blocks * TILE)], p_hbm)
    k_ref[blocks * TILE : (blocks + 2) * TILE, :] = pull_rows(blocks // 2).astype(low)
    write(k_ref.at[pl.ds(blocks * TILE, SPAN)], e_hbm)
    own_ref[PR_DEV:, :] += pull_rows(blocks // 2 + 1)
    write(own_ref, own_hbm)

    dense_ref[:, early : 2 * early] = nn(n_ref[...], dk_ref[:, early:]).astype(low)
    dense_ref[:, 2 * early : 3 * early] = nn(n_ref[...], dv_ref[:, early:]).astype(low)

    small_t = jnp.concatenate(
        [
            jnp.zeros((experts, width), single), jnp.sum(attn_gain[...], axis=0, keepdims=True), grad_gain_moe,
            grad_table, jnp.zeros((TILE - experts - 2 - heads_held, width), single),
        ],
        axis=0,
    )
    dense_ref[:, 3 * early :] = (small_t.T + rg_ref[...]).astype(low)
    write(dense_ref, dense_hbm)
    o_total = o_sum[chip].astype(single)
    for k in range(chips - 1):
        o_sends[k].wait_recv()
        o_total = o_total + o_in[k].astype(single)
    z_ref[:, :width] = o_total.astype(low)
    h_total = h_sum[chip].astype(single)
    for k in range(chips - 1):
        h_sends[k].wait_recv()
        h_total = h_total + h_in[k].astype(single)
    z_ref[:, width:] = h_total.astype(low)
    for copy in o_halves + o_sends + h_halves + h_sends:
        copy.wait_send()
    for copy in writes:
        copy.wait()
    for k, side in result_slots(core, range(NEAR)):
        piece = ret_hbm.at[chip_across(chip, k), side]
        send(piece, piece, (xs.at[0, 0], xr.at[k, side]), twin).wait_recv()
    for j in range(fasts - 1):
        send(ra_hbm.at[j], ra_hbm.at[j], (as_.at[j], ar.at[j]), twin).wait_recv()
    for j in range(slows - 1):
        send(rb_hbm.at[j], rb_hbm.at[j], (bs.at[j], br.at[j]), twin).wait_recv()
    for copy in sent:
        copy.wait_send()


def back(
    returned, col_slots, mid, cotangent, gains, every_tok, weights, kept, bucket_row, router_grads, gwin, gwout, result
):
    rows, width = mid.shape
    normed, queries, keys, values, attended, lse, rev = kept
    count = keys.shape[0]
    shards = lax.axis_size("shard")
    slows, fasts = gwin.shape[:2]
    chips, lines, early = shards // 2, width // shards, width // 2
    vm = pltpu.VMEM
    shape = jax.ShapeDtypeStruct
    pairs = pltpu.SemaphoreType.DMA
    args = (
        col_slots, gains, lse, rev, bucket_row, router_grads, returned, mid, cotangent, queries, keys, values, attended,
        every_tok, weights, normed, gwin, gwout, result,
    )
    return pl.pallas_call(
        back_kernel,
        out_shape=(
            shape((lines, width + 3 * early), low), shape((width, 3 * early + TILE), low),
            shape((count - 2 * SPAN, width), low), shape((SPAN, width), low),
            shape((rows, width), single), shape((rows, width), single),
            shape((fasts - 1, slows) + gwin.shape[2:], low), shape((slows - 1, fasts) + gwout.shape[2:], low),
            shape(result.shape, low),
        ),
        in_specs=[in_vmem] * 6 + [anywhere] * 13,
        out_specs=(in_vmem,) + (anywhere,) * 8,
        scratch_shapes=[
            pltpu.VMEM((2, tile_kinds, TILE, TILE), single), pltpu.VMEM((2, tile_kinds, TILE, TILE), single),
            pltpu.VMEM((16, 4 * TILE), single), pltpu.VMEM((TILE, count), low), pltpu.VMEM((TILE, rows), single),
            pltpu.VMEM((16, 2 * TILE), single),
            pltpu.VMEM((rows, width), low), pltpu.VMEM((rows, width), low), pltpu.VMEM((count, width), low),
            pltpu.VMEM((count, width), low), pltpu.VMEM((8, width), single),
            pltpu.VMEM(every_tok.shape, low), pltpu.VMEM(weights.shape, low), pltpu.VMEM(normed.shape, low),
            vm(returned.shape, low), vm((rows, width), single), vm((rows, width), low), vm((rows, width), low),
            vm(keys.shape, low), vm(keys.shape, low), vm(attended.shape, single),
            vm((width, 3 * early + TILE), low),
            vm((rows, width), single), vm((rows, width), single),
            vm((shards, lines, width), low), vm((chips, lines, width), low),
            vm((chips, lines, width), low), vm((chips - 1, lines, width), low),
            vm((shards, lines, 3 * early), low), vm((chips, lines, 3 * early), low),
            vm((chips, lines, 3 * early), low), vm((chips - 1, lines, 3 * early), low),
            pairs((12,)), pairs((6,)), pairs((NEAR, 2)), pairs((NEAR, 2)), pairs((fasts - 1,)), pairs((fasts - 1,)),
            pairs((slows - 1,)), pairs((slows - 1,)), pairs((chips,)), pairs((chips,)), pairs((chips - 1,)),
            pairs((chips - 1,)), pairs((chips,)), pairs((chips,)), pairs((chips - 1,)), pairs((chips - 1,)),
        ],
        compiler_params=pltpu.CompilerParams(collective_id=4, has_side_effects=True, vmem_limit_bytes=vmem_cap),
        cost_estimate=pl.CostEstimate(flops=60_000_000_000, bytes_accessed=40_000_000, transcendentals=8_000_000),
        name="back",
    )(*args)


def places():
    rep, shard = lax.axis_index("rep"), lax.axis_index("shard")
    return rep, shard // 2, shard % 2, lax.axis_size("shard") // 2, rep % QUARTERS


def peer_lists():
    rep, chip, core, chips, quarter = places()
    along = [(rep, (chip + k) % chips * 2 + core) for k in range(1, chips)]
    across = [(rep - quarter + (quarter + j) % QUARTERS, chip * 2 + core) for j in range(1, QUARTERS)]
    twin = (rep, chip * 2 + 1 - core)
    return along, across, twin


def chip_across(chip, k):
    partner, bit = 0, 1
    while bit < lax.axis_size("shard") // 2:
        partner = partner + bit * ((chip // bit + k // bit) % 2)
        bit = bit * 2
    return partner


def result_peers(rep, chip, core, chosen):
    return [
        (k, side, (rep, chip_across(chip, k) * 2 + (side if k else 1 - core)))
        for k in chosen for side in range(2 if k else 1)
    ]


def result_slots(core, chosen):
    return [(k, side if k else 1 - core) for k in chosen for side in range(2 if k else 1)]


def greet(devices):
    barrier = pltpu.get_barrier_semaphore()
    for device in devices:
        pl.semaphore_signal(barrier, inc=1, device_id=device, device_id_type=mesh_ids)
    pl.semaphore_wait(barrier, len(devices))


def send(source, target, sems, device):
    return pltpu.make_async_remote_copy(
        src_ref=source, dst_ref=target, send_sem=sems[0], recv_sem=sems[1],
        device_id=device, device_id_type=mesh_ids,
    )


def rep_places():
    rep, reps = lax.axis_index("rep"), lax.axis_size("rep")
    fasts = QUARTERS if reps % (QUARTERS * QUARTERS) == 0 else 2
    return rep, rep // fasts, rep % fasts, reps // fasts, fasts


def reduce_kernel(
    gain_ref, col_ref, d_hbm, p_hbm, e_hbm, own_hbm, gres_hbm, tok_hbm, mid_hbm, gate_hbm, out_hbm, ret_hbm,
    gwin_hbm, ra_hbm, gwout_hbm, rb_hbm, z_hbm,
    gt_ref, mix_ref, early_ref, late_ref, ka_ref, la_hbm, kb_ref, lb_hbm,
    d_own, half, hr, tr, mr, cr, zs, tz, z_last, z_above, z_all, last, above_in, gathered,
    p_own, p_half, p_sum, p_in, e_in, own, gres, tok, mid, gate, ret,
    a_own, a_in, a_sum, b_own, b_in, b_sum,
    loc, ps_s, ps_r, ds_s, ds_r, pz_s, pz_r, rr_s, rr_r, rz_s, rz_r, zr_s, zr_r, zh_s, zh_r, za_s, za_r,
    dh_s, dh_r, da_s, da_r, ea_s, ea_r, eb_s, eb_r, xs, xr,
):
    rep, chip, core, chips, quarter = places()
    along, across, twin = peer_lists()
    _, slow, fast, slows, fasts = rep_places()
    classes = lax.axis_size("rep") // QUARTERS
    here = chip * 2 + core
    beside = [(slow * fasts + (fast + j) % fasts, here) for j in range(1, fasts)]
    beyond = [((slow + j) % slows * fasts + fast, here) for j in range(1, slows)]
    above = [((rep // QUARTERS + k) % classes * QUARTERS + quarter, here) for k in range(1, classes)]
    wide = lambda held: held.astype(single)
    pending = []

    def load(source, target, index):
        copy = pltpu.make_async_copy(source, target, loc.at[index])
        copy.start()
        return copy

    def go(source, target, sems, device):
        copy = send(source, target, sems, device)
        copy.start()
        pending.append(copy)

    def landed(piece, sems):
        send(piece, piece, sems, twin).wait_recv()

    early_in = load(z_hbm, zs, 12)
    a_loads = [load(gwin_hbm.at[:, fast], a_own, 0), load(ra_hbm, a_in, 1)]
    halves = [load(d_hbm.at[:, core], d_own, 5), load(p_hbm.at[:, core], p_own, 4)]
    b_loads = [load(gwout_hbm.at[slow], b_own, 2), load(rb_hbm, b_in, 3)]
    rest = [
        load(ret_hbm.at[chip_across(chip, k)], ret.at[chip_across(chip, k)], 13 + k) for k in range(NEAR)
    ] + [
        load(mid_hbm, mid, 7), load(gate_hbm, gate, 8), load(own_hbm, own, 9),
        load(gres_hbm, gres, 10), load(tok_hbm, tok, 11),
    ]
    others = [(rep, (here + k) % (2 * chips)) for k in range(1, 2 * chips)]
    greets = list(others)
    for device in across + beside + beyond + above:
        greets.append(device)
    greet(greets)
    for k in range(chips):
        go(d_hbm.at[k, 1 - core], half.at[k], (ds_s.at[k], ds_r.at[k]), twin)
    go(p_hbm.at[:, 1 - core], p_half, (ps_s.at[0], ps_r.at[0]), twin)
    go(e_hbm, e_in, (ps_s.at[1], ps_r.at[1]), twin)
    for k, side, device in result_peers(rep, chip, core, range(NEAR, chips)):
        go(out_hbm.at[chip_across(chip, k), side], ret.at[chip, core], (xs.at[k - NEAR, side], xr.at[k - NEAR, core]), device)
    early_in.wait()
    for j, device in enumerate(across):
        go(zs.at[(quarter + j + 1) % QUARTERS], tz.at[j], (zr_s.at[j], zr_r.at[j]), device)

    for copy in a_loads:
        copy.wait()
    for t in range(slows):
        total = wide(a_own[t])
        for j in range(fasts - 1):
            total = total + wide(a_in[j, t])
        a_sum[t] = total.astype(low)
    for j, device in enumerate(beyond):
        go(a_sum.at[(slow + j + 1) % slows], la_hbm.at[j], (ea_s.at[j], ea_r.at[j]), device)
    for copy in halves:
        copy.wait()
    for k in range(chips):
        landed(half.at[k], (ds_s.at[k], ds_r.at[k]))
        for t in range(QUARTERS):
            hr[t, k] = (wide(d_own[k, t]) + wide(half[k, t])).astype(low)
    for j, device in enumerate(across):
        go(hr.at[(quarter + j + 1) % QUARTERS], tr.at[j], (rr_s.at[j], rr_r.at[j]), device)
    landed(p_half, (ps_s.at[0], ps_r.at[0]))
    for k in range(chips):
        p_sum[k] = (wide(p_own[k]) + wide(p_half[k])).astype(low)
    for k, device in enumerate(along):
        go(p_sum.at[(chip + k + 1) % chips], p_in.at[k], (pz_s.at[k], pz_r.at[k]), device)
    for copy in b_loads:
        copy.wait()
    for t in range(fasts):
        total = wide(b_own[t])
        for j in range(slows - 1):
            total = total + wide(b_in[j, t])
        b_sum[t] = total.astype(low)
    for j, device in enumerate(beside):
        go(b_sum.at[(fast + j + 1) % fasts], lb_hbm.at[j], (eb_s.at[j], eb_r.at[j]), device)

    def class_sum(held, came, s_sems, r_sems):
        total = wide(held[...])
        for j, device in enumerate(above):
            go(held, came.at[j], (s_sems.at[j], r_sems.at[j]), device)
        for j in range(classes - 1):
            landed(came.at[j], (s_sems.at[j], r_sems.at[j]))
            total = total + wide(came[j])
        return total.astype(low)

    def hand_out(pieces, s_sems, r_sems):
        for j, device in enumerate(across):
            go(pieces.at[quarter], pieces.at[quarter], (s_sems.at[j], r_sems.at[j]), device)

    def handed(pieces, s_sems, r_sems):
        for j in range(QUARTERS - 1):
            landed(pieces.at[(quarter + QUARTERS - j - 1) % QUARTERS], (s_sems.at[j], r_sems.at[j]))

    for j in range(QUARTERS - 1):
        landed(tz.at[j], (zr_s.at[j], zr_r.at[j]))
    total = wide(zs[quarter])
    for j in range(QUARTERS - 1):
        total = total + wide(tz[j])
    z_last[...] = total.astype(low)
    z_all[quarter] = class_sum(z_last, z_above, zh_s, zh_r) if classes > 1 else z_last[...]
    hand_out(z_all, za_s, za_r)

    for copy in rest:
        copy.wait()
    ka_ref[...] = a_sum[slow]
    kb_ref[...] = b_sum[fast]

    for j in range(QUARTERS - 1):
        landed(tr.at[j], (rr_s.at[j], rr_r.at[j]))
    for k in range(chips):
        total = wide(hr[quarter, k])
        for j in range(QUARTERS - 1):
            total = total + wide(tr[j, k])
        mr[k] = total.astype(low)
    for k, device in enumerate(along):
        go(mr.at[(chip + k + 1) % chips], cr.at[k], (rz_s.at[k], rz_r.at[k]), device)

    for k in range(chips - 1):
        landed(p_in.at[k], (pz_s.at[k], pz_r.at[k]))
    landed(e_in, (ps_s.at[1], ps_r.at[1]))
    total = wide(p_sum[chip])
    for k in range(chips - 1):
        total = total + wide(p_in[k])
    grads = own[...] + jnp.concatenate([total, wide(e_in[...])], axis=0)
    gt_ref[...] = gres[...] + norm_pull(grads, wide(tok[...]), gain_ref[0:1, :])

    for k in range(chips - 1):
        landed(cr.at[k], (rz_s.at[k], rz_r.at[k]))
    total = wide(mr[chip])
    for k in range(chips - 1):
        total = total + wide(cr[k])
    last[...] = total.astype(low)
    gathered[quarter] = class_sum(last, above_in, dh_s, dh_r) if classes > 1 else last[...]
    hand_out(gathered, da_s, da_r)
    for k, side in result_slots(core, range(NEAR, chips)):
        landed(ret.at[chip_across(chip, k), side], (xs.at[k - NEAR, side], xr.at[k - NEAR, side]))
    slots = lax.broadcasted_iota(jnp.int32, (tok.shape[0], 2 * chips * ret.shape[2]), 1)
    chosen = nn((slots == col_ref[:, 0:1]).astype(low), ret[...].reshape(slots.shape[1], tok.shape[1]))
    mix_ref[...] = (mid[...] + gate[:, 0:1] * chosen).astype(low)
    handed(z_all, za_s, za_r)
    early_ref[...] = z_all[...]
    handed(gathered, da_s, da_r)
    late_ref[...] = gathered[...]
    for j in range(slows - 1):
        landed(la_hbm.at[j], (ea_s.at[j], ea_r.at[j]))
    for j in range(fasts - 1):
        landed(lb_hbm.at[j], (eb_s.at[j], eb_r.at[j]))
    for copy in pending:
        copy.wait_send()


def reduce_all(gains, col_slots, dense, prompt_part, near_part, own, gres, tokens, mid, gate, result, returned, gwin, ra, gwout, rb, z):
    chips = lax.axis_size("shard") // 2
    classes = lax.axis_size("rep") // QUARTERS
    slows, fasts = gwin.shape[:2]
    rows, width = mid.shape
    lines, lanes = dense.shape[3:]
    wider = z.shape[2]
    shape = jax.ShapeDtypeStruct
    sem = pltpu.SemaphoreType.DMA
    vm = pltpu.VMEM
    count, others = chips - 1, QUARTERS - 1
    ours = prompt_part.shape[2:]
    extra = max(classes - 1, 1)
    args = (gains, col_slots, dense, prompt_part, near_part, own, gres, tokens, mid, gate, result, returned, gwin, ra, gwout, rb, z)
    return pl.pallas_call(
        reduce_kernel,
        out_shape=(
            shape((rows, width), single), shape((rows, width), low),
            shape((QUARTERS, lines, wider), low), shape((QUARTERS, lines, lanes), low),
            shape(gwin.shape[2:], low), shape((slows - 1,) + gwin.shape[2:], low),
            shape(gwout.shape[2:], low), shape((fasts - 1,) + gwout.shape[2:], low),
        ),
        in_specs=[in_vmem] * 2 + [anywhere] * 15,
        out_specs=(in_vmem,) * 5 + (anywhere, in_vmem, anywhere),
        scratch_shapes=[
            vm((chips, QUARTERS, lines, lanes), low), vm((chips, QUARTERS, lines, lanes), low),
            vm((QUARTERS, chips, lines, lanes), low), vm((others, chips, lines, lanes), low),
            vm((chips, lines, lanes), low), vm((count, lines, lanes), low),
            vm((QUARTERS, lines, wider), low), vm((others, lines, wider), low), vm((lines, wider), low),
            vm((extra, lines, wider), low), vm((QUARTERS, lines, wider), low),
            vm((lines, lanes), low), vm((extra, lines, lanes), low), vm((QUARTERS, lines, lanes), low),
            vm((chips,) + ours, low), vm((chips,) + ours, low), vm((chips,) + ours, low), vm((count,) + ours, low),
            vm(near_part.shape, low), vm((rows, width), single), vm((rows, width), single), vm((rows, width), low),
            vm((rows, width), single), vm(gate.shape, single), vm(result.shape, low),
            vm((slows,) + gwin.shape[2:], low), vm(ra.shape, low), vm((slows,) + gwin.shape[2:], low),
            vm((fasts,) + gwout.shape[2:], low), vm(rb.shape, low), vm((fasts,) + gwout.shape[2:], low),
            sem((13 + NEAR,)), sem((2,)), sem((2,)), sem((chips,)), sem((chips,)), sem((count,)), sem((count,)),
            sem((others,)), sem((others,)), sem((count,)), sem((count,)),
            sem((others,)), sem((others,)), sem((extra,)), sem((extra,)), sem((others,)), sem((others,)),
            sem((extra,)), sem((extra,)), sem((others,)), sem((others,)),
            sem((slows - 1,)), sem((slows - 1,)), sem((fasts - 1,)), sem((fasts - 1,)),
            sem((chips - NEAR, 2)), sem((chips - NEAR, 2)),
        ],
        compiler_params=pltpu.CompilerParams(collective_id=1, has_side_effects=True, vmem_limit_bytes=vmem_cap),
        cost_estimate=pl.CostEstimate(flops=0, bytes_accessed=200_000_000, transcendentals=0),
        name="reduce_all",
    )(*args)


def finish_kernel(ka_ref, la_ref, kb_ref, lb_ref, early_ref, late_ref, small_ref, gt_ref, mix_ref, *outs):
    ea_ref, eb_ref, q_ref, k_ref, v_ref, o_ref, router_ref, attn_ref, moe_ref, table_ref, gt_out, mix_out = outs
    gt_out[...] = gt_ref[...]
    mix_out[...] = mix_ref[...]
    width = q_ref.shape[2]
    experts = router_ref.shape[0]
    ea_ref[...] = ka_ref[...].astype(single) + jnp.sum(la_ref[...].astype(single), axis=0)
    eb_ref[...] = kb_ref[...].astype(single) + jnp.sum(lb_ref[...].astype(single), axis=0)
    half = width // 2
    o_ref[...] = early_ref[:, :, :width].astype(single)
    for i, ref in enumerate((q_ref, k_ref, v_ref)):
        ref[:, :, :half] = early_ref[:, :, width + i * half : width + (i + 1) * half].astype(single)
        ref[:, :, half:] = late_ref[:, :, i * half : (i + 1) * half].astype(single)

    @pl.when(pl.program_id(0) == 0)
    def _():
        small = small_ref[...].astype(single).reshape(router_ref.shape[1], TILE)
        turned = small.T
        router_ref[...] = turned[:experts]
        attn_ref[...] = turned[experts : experts + 1]
        moe_ref[...] = turned[experts + 1 : experts + 2]
        table_ref[...] = small[: table_ref.shape[0], experts + 2 : experts + 2 + table_ref.shape[1]]


def finish(ka, la, kb, lb, early, late, grad_tokens, mixed, experts, table_rows, heads):
    shape = jax.ShapeDtypeStruct
    _, lines, wider = early.shape
    lanes = late.shape[2]
    width = kb.shape[1]
    rows = QUARTERS * lines
    steps = QUARTERS
    a_cols, b_rows = ka.shape[1] // steps, kb.shape[0] // steps
    part = pl.BlockSpec((1, lines, width), lambda i: (i, 0, 0))
    once = lambda *dims: pl.BlockSpec(dims, lambda i: (0,) * len(dims))
    some = pl.BlockSpec((mixed.shape[0] // steps, width), lambda i: (i, 0))
    return pl.pallas_call(
        finish_kernel,
        grid=(steps,),
        out_shape=(
            shape(ka.shape, single), shape(kb.shape, single), *(shape((QUARTERS, lines, width), single),) * 4,
            shape((experts, rows), single), shape((1, rows), single), shape((1, rows), single),
            shape((table_rows, heads), single), shape(grad_tokens.shape, single), shape(mixed.shape, low),
        ),
        in_specs=[
            pl.BlockSpec((ka.shape[0], a_cols), lambda i: (0, i)),
            pl.BlockSpec((la.shape[0], ka.shape[0], a_cols), lambda i: (0, 0, i)),
            pl.BlockSpec((b_rows, width), lambda i: (i, 0)),
            pl.BlockSpec((lb.shape[0], b_rows, width), lambda i: (0, i, 0)),
            pl.BlockSpec((1, lines, wider), lambda i: (i, 0, 0)), pl.BlockSpec((1, lines, lanes), lambda i: (i, 0, 0)),
            pl.BlockSpec((QUARTERS, lines, TILE), lambda i: (0, 0, lanes // TILE - 1)), some, some,
        ],
        out_specs=(
            pl.BlockSpec((ka.shape[0], a_cols), lambda i: (0, i)), pl.BlockSpec((b_rows, width), lambda i: (i, 0)),
            part, part, part, part, once(experts, rows), once(1, rows), once(1, rows), once(table_rows, heads),
            some, some,
        ),
        compiler_params=pltpu.CompilerParams(vmem_limit_bytes=vmem_cap),
        cost_estimate=pl.CostEstimate(flops=0, bytes_accessed=12_000_000, transcendentals=0),
        name="finish",
    )(ka, la, kb, lb, early, late, late, grad_tokens, mixed)


def local(
    tokens,
    routes,
    slot_ids,
    w_query,
    w_key,
    w_value,
    w_output,
    w_router,
    norm_attn,
    norm_moe,
    rel_table,
    w_in,
    w_out,
    cotangent,
):
    shard_count = lax.axis_size("shard")
    token_rows, model_width = tokens.shape
    prompt_len = PR_DEV * shard_count
    weight_rows, expert_count = w_router.shape
    table_rows, head_count = rel_table.shape
    capacity = 2 * token_rows // expert_count
    slot_count = expert_count * capacity

    small = jnp.concatenate(
        [w_router, norm_attn[:, None], norm_moe[:, None],
         jnp.pad(rel_table, ((0, weight_rows - table_rows), (0, 0)))], axis=1
    )
    small = jnp.pad(small, ((0, 0), (0, TILE - small.shape[1])))
    dispatch = routes * capacity + slot_ids

    ints = jnp.concatenate([routes[None], dispatch[None], jnp.zeros((6, token_rows), jnp.int32)])
    bucket_row = jnp.asarray(np.tile(distance_buckets(table_rows * shard_count), (8, 1)), jnp.int32)
    (
        lse, rev, gate, col_slots, gains, slots_out, grad_in, weights, every_tok, small, normed, queries, keys, values,
        attended, mid,
    ) = front(ints, bucket_row, cotangent, (w_query, w_key, w_value, w_output), tokens, small, slot_count)
    by_chip = (shard_count // 2, 2, capacity, model_width)
    grad_back, result, grad_w_in, grad_w_out, router_grads = moe(
        slots_out.reshape(by_chip), grad_in.reshape(by_chip), small, w_in[0], w_out[0]
    )
    rep_count = lax.axis_size("rep")
    slows, fasts = rep_places()[3:]
    gwin = grad_w_in.reshape(slows, fasts, model_width // rep_count, -1)
    gwout = grad_w_out.reshape(slows, fasts, -1, model_width)
    early_part, dense, prompt_part, near_part, grad_own, grad_resid, ra, rb, returned = back(
        grad_back.reshape(slot_count, model_width), col_slots, mid, cotangent, gains, every_tok, weights,
        (normed, queries, keys, values, attended, lse, rev), bucket_row, router_grads, gwin, gwout, result,
    )
    chips = shard_count // 2
    lines = weight_rows // QUARTERS
    grad_tokens, mixed, early, late, ka, la, kb, lb = reduce_all(
        gains, col_slots, dense.reshape(chips, 2, QUARTERS, lines, -1),
        prompt_part.reshape(chips, 2, PR_DEV, model_width), near_part, grad_own, grad_resid, tokens, mid, gate,
        result, returned, gwin, ra, gwout, rb,
        early_part.reshape(QUARTERS, lines, -1),
    )
    in_grad, out_grad, gq, gk, gv, go, router, gain_attn, gain_moe, table, grad_tokens, mixed = finish(
        ka, la, kb, lb, early, late, grad_tokens, mixed, expert_count, table_rows, head_count
    )
    return (
        mixed,
        grad_tokens,
        *(part.reshape(weight_rows, model_width) for part in (gq, gk, gv, go)),
        router.T,
        gain_attn[0],
        gain_moe[0],
        table,
        in_grad[None],
        out_grad[None],
    )


def solution(mesh):
    return jax.shard_map(
        local,
        mesh=mesh,
        in_specs=(
            P(("rep", "shard"), None),
            P(("rep", "shard")),
            P(("rep", "shard")),
            P("shard", None),
            P("shard", None),
            P("shard", None),
            P("shard", None),
            P("shard", None),
            P("shard"),
            P("shard"),
            P("shard", None),
            P("shard", None, None),
            P("shard", None, None),
            P(("rep", "shard"), None),
        ),
        out_specs=(
            P(("rep", "shard"), None),
            P(("rep", "shard"), None),
            P("shard", None),
            P("shard", None),
            P("shard", None),
            P("shard", None),
            P("shard", None),
            P("shard"),
            P("shard"),
            P("shard", None),
            P("shard", "rep", None),
            P("shard", "rep", None),
        ),
        check_vma=False,
    )
```

```python
import jax
import jax.numpy as jnp
import numpy as np
from jax import lax
from jax.experimental import pallas as pl
from jax.experimental.pallas import tpu as pltpu
from jax.sharding import PartitionSpec as P

PR_DEV = 128
TILE = 128
SPAN = 2 * TILE
NEAR = 3
QUARTERS = 4
far_before, far_after, causal_tile, hidden_tile, tile_kinds = 3, 4, 5, 6, 7
vmem_cap = 60 * 1024 * 1024
mesh_ids = pl.DeviceIdType.MESH
bucket_edges = (12, 16, 23, 32, 46, 64, 91)
norm_epsilon = 1e-06
masked_score = -1e30
low, single = jnp.bfloat16, jnp.float32
in_vmem = pl.BlockSpec(memory_space=pltpu.VMEM)
anywhere = pl.BlockSpec(memory_space=pl.ANY)


def inverse_rms(values):
    return lax.rsqrt(jnp.mean(values * values, axis=-1, keepdims=True) + norm_epsilon)


def norm_pull(grad, values, gain):
    scale = inverse_rms(values)
    pulled = grad * gain
    mean = jnp.mean(pulled * values, axis=-1, keepdims=True)
    return scale * pulled - values * (scale * scale * scale * mean)


def nt(left, right):
    return lax.dot_general(left, right, (((1,), (1,)), ((), ())), preferred_element_type=single)


def tn(left, right):
    return lax.dot_general(left, right, (((0,), (0,)), ((), ())), preferred_element_type=single)


def nn(left, right):
    return jnp.dot(left, right, preferred_element_type=single)


def thirds_of(values):
    first = values.astype(low)
    rest = values - first.astype(single)
    second = rest.astype(low)
    return first, second, (rest - second.astype(single)).astype(low)


def fill_tiles(tiles_ref, rev_row, low, high):
    spread = jnp.broadcast_to(rev_row, (TILE, 4 * TILE))
    rolled = pltpu.roll(spread, 0, 1, stride=1, stride_axis=0)
    keys = lax.broadcasted_iota(jnp.int32, (TILE, TILE), 0)
    rows = lax.broadcasted_iota(jnp.int32, (TILE, TILE), 1)
    tiles_ref[0] = rolled[:, TILE : 2 * TILE]
    tiles_ref[1] = rolled[:, :TILE]
    tiles_ref[2] = rolled[:, 3 * TILE :]
    tiles_ref[far_before] = jnp.broadcast_to(low, (TILE, TILE))
    tiles_ref[far_after] = jnp.broadcast_to(high, (TILE, TILE))
    tiles_ref[causal_tile] = jnp.where(keys <= rows, rolled[:, :TILE], masked_score)
    tiles_ref[hidden_tile] = jnp.full((TILE, TILE), masked_score, jnp.float32)


def prompt_tile(block, chunk, shard_id, block_count):
    if chunk == 0:
        gap = block - shard_id
        far = jnp.where(gap < 0, far_before, far_after)
        return jnp.where(jnp.abs(gap) <= 1, gap + 1, far)
    if chunk == 1 and block == block_count - 1:
        return jnp.where(shard_id % 2 == 0, 0, far_before)
    return far_before


def local_tile(block, chunk, shard_id):
    if block >= 2:
        return ((causal_tile, 0), (hidden_tile, causal_tile))[block - 2][chunk]
    kind = 0 if (block, chunk) == (1, 0) else far_before
    return jnp.where(shard_id % 2 == 1, kind, hidden_tile)


def prompt_grid(part, shard_id, block_count):
    return [
        [(side, prompt_tile(2 * part + half, chunk, shard_id, block_count)) for side in range(2) for chunk in range(3)]
        for half in range(2)
    ]


def local_grid(part, shard_id):
    return [
        [(side, local_tile(2 * part + half, chunk, shard_id)) for side in range(2) for chunk in range(2)]
        for half in range(2)
    ]


def tile_of(values, i, j):
    return values[i * TILE : (i + 1) * TILE, j * TILE : (j + 1) * TILE]


def with_bias(scores, tiles_ref, grid):
    lines = [
        jnp.concatenate(
            [tile_of(scores, i, j) + tiles_ref[side, kind] for j, (side, kind) in enumerate(row)], axis=1
        )
        for i, row in enumerate(grid)
    ]
    return jnp.concatenate(lines, axis=0)


def both_heads(values):
    first = head_mask(values.shape[0], 0)
    none = jnp.zeros_like(values)
    return jnp.concatenate([jnp.where(first, values, none), jnp.where(first, none, values)], axis=0)


def continuation(values, axis):
    rows = values.shape[axis] // 2
    pick = (lambda a, b: values[:, a:b]) if axis else (lambda a, b: values[a:b])
    return jnp.concatenate([pick(PR_DEV, rows), pick(rows + PR_DEV, 2 * rows)], axis=axis)


def fold8(values):
    return values.reshape(values.shape[0] // 8, 8, values.shape[1])


def head_mask(rows, side):
    lanes = lax.broadcasted_iota(jnp.int32, (rows, TILE), 1)
    return (lanes < TILE // 2) if side == 0 else (lanes >= TILE // 2)


def distance_buckets(bucket_count):
    steps = np.arange(4 * TILE)
    gap = -np.where(steps < 2 * TILE, steps, steps - 4 * TILE)
    size = np.abs(gap)
    far = sum((size >= edge).astype(np.int64) for edge in bucket_edges)
    exact = bucket_count // 4
    return np.where(gap > 0, bucket_count // 2, 0) + np.where(size < exact, size, exact + far)


def front_kernel(
    ints_ref, bucket_ref, cot_ref, wq_hbm, wk_hbm, wv_hbm, wo_hbm, tok_hbm, little_hbm,
    lse_ref, rev_ref, gate_ref, col_ref, gain_ref, x_ref, gin_hbm, w_hbm, every_hbm, small_hbm,
    n_hbm, q_hbm, k_hbm, v_hbm, o_hbm, mid_hbm,
    tiles, vt, sp, sl, gbuf, w_ref, every_ref, small_ref, tok_ref, shard_w, little,
    n_ref, nt_ref, q_ref, k_ref, v_ref, ot_ref, mid_ref,
    gs, gr, loc, wz_s, wz_r, tz_s, tz_r, sz_s, sz_r, wr_s, wr_r, wt_s, wt_r, tt_s, tt_r, st_s, st_r, et_s, et_r,
):
    rep, chip, core, chips, quarter = places()
    along, across, twin = peer_lists()
    shards = chips * 2
    shard_id = chip * 2 + core
    rows, width = tok_ref.shape
    experts = shards
    blocks = every_ref.shape[0] // TILE - 4
    half = TILE // 2
    heads_held = rev_ref.shape[0]
    lines = shard_w.shape[1]
    rest_rows = rows - PR_DEV
    prompt_len = blocks * TILE
    others = [(rep, (shard_id + k) % shards) for k in range(1, shards)]

    def w_rows(source, side):
        return pl.ds(pl.multiple_of((source * 2 + side) * lines, lines), lines)

    def t_rows(source, side):
        return every_ref.at[pl.ds(pl.multiple_of((source * 2 + side) * PR_DEV, PR_DEV), PR_DEV)]

    loads = [
        pltpu.make_async_copy(source, shard_w.at[i], loc.at[i])
        for i, source in enumerate((wq_hbm, wk_hbm, wv_hbm, wo_hbm))
    ] + [pltpu.make_async_copy(tok_hbm, tok_ref, loc.at[4]), pltpu.make_async_copy(little_hbm, little, loc.at[5])]
    for copy in loads:
        copy.start()
    greeted = [twin] + along
    for device in across + [(rep, (chip + k) % chips * 2 + 1 - core) for k in range(1, chips)]:
        greeted.append(device)
    greet(greeted)
    started = []

    def go(source, target, sems, device):
        copy = send(source, target, sems, device)
        copy.start()
        started.append(copy)

    def landed(piece, sems):
        send(piece, piece, sems, twin).wait_recv()

    for copy in loads:
        copy.wait()
    mine = w_rows(chip, core)
    prompt, rest = tok_ref.at[pl.ds(0, PR_DEV)], tok_ref.at[pl.ds(PR_DEV, rest_rows)]
    for k, device in enumerate(along):
        go(shard_w.at[quarter], w_ref.at[quarter, mine], (wz_s.at[k], wz_r.at[k]), device)
        go(little, small_ref.at[mine], (sz_s.at[k], sz_r.at[k]), device)
    go(little, small_ref.at[mine], (st_s.at[0], st_r.at[0]), twin)
    go(rest, every_ref.at[pl.ds(prompt_len, rest_rows)], (et_s.at[0], et_r.at[0]), twin)
    go(prompt, t_rows(chip, core), (tt_s.at[0], tt_r.at[0]), twin)
    go(shard_w, w_ref.at[:, mine], (wt_s.at[0], wt_r.at[0]), twin)
    w_ref[:, mine, :] = shard_w[...]
    small_ref[mine, :] = little[...]
    every_ref[pl.ds(pl.multiple_of(shard_id * PR_DEV, PR_DEV), PR_DEV), :] = tok_ref[:PR_DEV, :]
    every_ref[prompt_len + rest_rows :, :] = tok_ref[PR_DEV:, :]
    ints = ints_ref[...].astype(single).T
    route_col = ints[:, 0:1].astype(jnp.int32)
    col_ref[...] = jnp.broadcast_to(ints[:, 1:2].astype(jnp.int32), col_ref.shape)
    slots = lax.broadcasted_iota(jnp.int32, (x_ref.shape[0], rows), 0)
    place = (slots == ints_ref[1:2, :]).astype(low)
    gbuf[...] = nn(place, cot_ref[...]).astype(low).reshape(gbuf.shape)
    own_g = pltpu.make_async_copy(gbuf.at[shard_id], gin_hbm.at[shard_id], loc.at[6])
    own_g.start()

    for k in range(1, chips):
        source = (chip + chips - k) % chips
        piece = w_ref.at[quarter, w_rows(source, core)]
        landed(piece, (wz_s.at[k - 1], wz_r.at[k - 1]))
        for j, device in enumerate(across):
            go(piece, piece, (wr_s.at[k - 1, j], wr_r.at[k - 1, j]), device)
        go(prompt, t_rows(chip, core), (tz_s.at[k - 1], tz_r.at[k - 1]), along[k - 1])
    for k in range(1, chips):
        source = (chip + chips - k) % chips
        piece = small_ref.at[w_rows(source, core)]
        landed(piece, (sz_s.at[k - 1], sz_r.at[k - 1]))
        go(piece, piece, (st_s.at[k], st_r.at[k]), twin)
    for k in range(1, chips):
        source = (chip + chips - k) % chips
        piece = t_rows(source, core)
        landed(piece, (tz_s.at[k - 1], tz_r.at[k - 1]))
        go(piece, piece, (tt_s.at[k], tt_r.at[k]), twin)
    for k, device in enumerate(others):
        go(gbuf.at[device[1]], gin_hbm.at[shard_id], (gs.at[k], gr.at[k]), device)
    for k in range(chips):
        source = (chip + chips - k) % chips
        landed(small_ref.at[w_rows(source, 1 - core)], (st_s.at[k], st_r.at[k]))
    writes = []

    def write(source, target):
        writes.append(pltpu.make_async_copy(source, target, loc.at[7 + len(writes)]))
        writes[-1].start()

    write(small_ref, small_hbm)

    small_t = small_ref[...].astype(single).T
    gain_attn = small_t[experts : experts + 1]
    gain_moe = small_t[experts + 1 : experts + 2]
    gain_ref[...] = jnp.concatenate([gain_attn, gain_moe, jnp.zeros((6, width), single)], axis=0)
    shard_rows = width // shards
    table_rows = 2 * TILE // 8 // shards
    owner = lax.broadcasted_iota(jnp.int32, (shards, shard_rows, 4 * TILE), 0)
    offset = lax.broadcasted_iota(jnp.int32, (shards, shard_rows, 4 * TILE), 1)
    held = jnp.where(offset < table_rows, owner * table_rows + offset, -1).reshape(width, 4 * TILE)
    hot = (held == bucket_ref[0:1, :]).astype(low)
    table_t = small_t[experts + 2 : experts + 2 + heads_held].astype(low)
    rev_ref[...] = nn(table_t, hot)

    for k in range(chips):
        source = (chip + chips - k) % chips
        landed(t_rows(source, 1 - core), (tt_s.at[k], tt_r.at[k]))
    landed(every_ref.at[pl.ds(prompt_len, rest_rows)], (et_s.at[0], et_r.at[0]))
    write(every_ref, every_hbm)

    @pl.loop(0, every_ref.shape[0] // SPAN)
    def scale(part):
        span = pl.ds(pl.multiple_of(part * SPAN, SPAN), SPAN)
        values = every_ref[span, :].astype(single)
        normed = values * inverse_rms(values) * gain_attn
        n_ref[span, :] = normed.astype(low)
        nt_ref[:, span] = normed.T.astype(low)

    write(nt_ref, n_hbm)
    for k in range(1, chips):
        source = (chip + chips - k) % chips
        for j in range(1, QUARTERS):
            piece = w_ref.at[(quarter + QUARTERS - j) % QUARTERS, w_rows(source, core)]
            landed(piece, (wr_s.at[k - 1, j - 1], wr_r.at[k - 1, j - 1]))
        piece = w_ref.at[:, w_rows(source, core)]
        go(piece, piece, (wt_s.at[k], wt_r.at[k]), twin)
    for k in range(chips):
        source = (chip + chips - k) % chips
        landed(w_ref.at[:, w_rows(source, 1 - core)], (wt_s.at[k], wt_r.at[k]))
    write(w_ref, w_hbm)

    @pl.loop(0, every_ref.shape[0] // (2 * SPAN))
    def project(part):
        span = pl.ds(pl.multiple_of(part * 2 * SPAN, 2 * SPAN), 2 * SPAN)
        k_ref[span, :] = nn(n_ref[span, :], w_ref[1]).astype(low)
        v_ref[span, :] = nn(n_ref[span, :], w_ref[2]).astype(low)

    own = pl.ds(pl.multiple_of(shard_id * TILE, TILE), TILE)
    normed = jnp.concatenate([n_ref[own, :], n_ref[(blocks + 2) * TILE :, :]], axis=0)
    q_ref[...] = (nn(normed, w_ref[0]).astype(low) * jnp.asarray(0.125, low)).astype(low)
    write(k_ref, k_hbm)
    write(v_ref, v_hbm)
    write(q_ref, q_hbm)

    @pl.loop(0, width // TILE)
    def pair_loop(pair):
        cols = pl.ds(pl.multiple_of(pair * TILE, TILE), TILE)
        vt[...] = v_ref[:, cols].T
        q_both = both_heads(q_ref[:, cols])
        q_local = continuation(q_both, 0)
        for side in range(2):
            rev_row = rev_ref[pl.ds(pair * 2 + side, 1), :]
            fill_tiles(tiles.at[side], rev_row, rev_row[:, SPAN - 1 : SPAN], rev_row[:, SPAN : SPAN + 1])
        top = jnp.full((8, 2 * rows), masked_score, single)
        for part in range(blocks // 2):
            keys = slice(part * SPAN, (part + 1) * SPAN)
            scores = with_bias(nt(k_ref[keys, cols], q_both), tiles, prompt_grid(part, shard_id, blocks))
            sp[keys, :] = scores
            top = jnp.maximum(top, jnp.max(fold8(scores), axis=0))
        local = continuation(top, 1)
        for part in range(2):
            keys = slice(part * SPAN, (part + 1) * SPAN)
            held = slice((blocks // 2 + part) * SPAN, (blocks // 2 + part + 1) * SPAN)
            scores = with_bias(nt(k_ref[held, cols], q_local), tiles, local_grid(part, shard_id))
            sl[keys, :] = scores
            local = jnp.maximum(local, jnp.max(fold8(scores), axis=0))
        rest = rows - PR_DEV
        top = jnp.concatenate(
            [top[:, :PR_DEV], local[:, :rest], top[:, rows : rows + PR_DEV], local[:, rest:]], axis=1
        )
        top = jnp.max(top, axis=0, keepdims=True)
        total = jnp.zeros((8, 2 * rows), single)
        summed = [jnp.zeros((half, rows), single)] * 2
        for part in range(blocks // 2):
            keys = slice(part * SPAN, (part + 1) * SPAN)
            weights = jnp.exp(sp[keys, :] - top)
            total = total + jnp.sum(fold8(weights), axis=0)
            weights = weights.astype(low)
            for side in range(2):
                heads = slice(side * half, (side + 1) * half)
                summed[side] = summed[side] + nn(vt[heads, keys], weights[:, side * rows : (side + 1) * rows])
        top_local, total_local = continuation(top, 1), continuation(total, 1)
        summed_local = [part_sum[:, PR_DEV:] for part_sum in summed]
        for part in range(2):
            keys = slice(part * SPAN, (part + 1) * SPAN)
            held = slice((blocks // 2 + part) * SPAN, (blocks // 2 + part + 1) * SPAN)
            weights = jnp.exp(sl[keys, :] - top_local)
            total_local = total_local + jnp.sum(fold8(weights), axis=0)
            weights = weights.astype(low)
            for side in range(2):
                heads = slice(side * half, (side + 1) * half)
                summed_local[side] = summed_local[side] + nn(
                    vt[heads, held], weights[:, side * rest : (side + 1) * rest]
                )
        for side in range(2):
            head = pair * 2 + side
            ours = slice(side * rows, (side + 1) * rows)
            sums = jnp.concatenate(
                [total[:, side * rows : side * rows + PR_DEV], total_local[:, side * rest : (side + 1) * rest]], axis=1
            )
            sums = jnp.sum(sums, axis=0, keepdims=True)
            mixed = jnp.concatenate([summed[side][:, :PR_DEV], summed_local[side]], axis=1)
            ot_ref[pl.ds(pl.multiple_of(head * half, half), half), :] = mixed / sums
            lse_ref[pl.ds(head, 1), :] = top[:, ours] + jnp.log(sums)

    resid_mid = tok_ref[...].astype(single) + nn(ot_ref[...].T.astype(low), w_ref[3])
    mid_ref[...] = resid_mid
    write(ot_ref, o_hbm)
    write(mid_ref, mid_hbm)
    mid_low = (resid_mid * inverse_rms(resid_mid) * gain_moe).astype(low)
    probs = router_softmax(mid_low, small_ref[...], experts)
    lanes = lax.broadcasted_iota(jnp.int32, probs.shape, 1)
    gate = jnp.sum(jnp.where(lanes == route_col, probs, 0.0), axis=1, keepdims=True)
    gate_ref[...] = jnp.broadcast_to(gate, gate_ref.shape)
    x_ref[...] = nn(place, mid_low).astype(low)
    own_g.wait()
    for k in range(shards - 1):
        landed(gin_hbm.at[(shard_id + shards - k - 1) % shards], (gs.at[k], gr.at[k]))
    for copy in writes:
        copy.wait()
    for copy in started:
        copy.wait_send()


def router_softmax(rows_low, small, experts):
    logits = nn(rows_low, small)
    lanes = lax.broadcasted_iota(jnp.int32, logits.shape, 1)
    logits = jnp.where(lanes < experts, logits, masked_score)
    powers = jnp.exp(logits - jnp.max(logits, axis=1, keepdims=True))
    return powers / jnp.sum(powers, axis=1, keepdims=True)


def front(ints, bucket_row, cotangent, weights, tokens, small, slot_count):
    rows, width = tokens.shape
    shards = lax.axis_size("shard")
    chips, count = shards // 2, shards // 2 - 1
    keys = shards * PR_DEV + 2 * (rows - PR_DEV)
    lines = small.shape[0]
    shape = jax.ShapeDtypeStruct
    sem = pltpu.SemaphoreType.DMA
    vm = pltpu.VMEM
    return pl.pallas_call(
        front_kernel,
        out_shape=(
            shape((16, rows), single), shape((16, 4 * TILE), single), shape((rows, TILE), single),
            shape((rows, TILE), jnp.int32), shape((8, width), single), shape((slot_count, width), low),
            shape((shards, slot_count // shards, width), low), shape((4, width, width), low),
            shape((keys, width), low), shape((width, TILE), low),
            shape((width, keys), low), shape((rows, width), low), shape((keys, width), low),
            shape((keys, width), low), shape((width, rows), single), shape((rows, width), single),
        ),
        in_specs=[in_vmem] * 3 + [anywhere] * 6,
        out_specs=(in_vmem,) * 6 + (anywhere,) * 10,
        scratch_shapes=[
            vm((2, tile_kinds, TILE, TILE), single), vm((TILE, keys), low), vm((keys - 2 * SPAN, 2 * rows), single),
            vm((2 * SPAN, 2 * (rows - TILE)), single),
            vm((shards, slot_count // shards, width), low), vm((4, width, width), low), vm((keys, width), low),
            vm((width, TILE), low), vm((rows, width), low), vm((4, lines, width), low), vm((lines, TILE), low),
            vm((keys, width), low), vm((width, keys), low), vm((rows, width), low), vm((keys, width), low),
            vm((keys, width), low), vm((width, rows), single), vm((rows, width), single),
            sem((shards - 1,)), sem((shards - 1,)), sem((16,)), sem((count,)), sem((count,)), sem((count,)),
            sem((count,)), sem((count,)), sem((count,)), sem((count, 3)), sem((count, 3)), sem((chips,)), sem((chips,)),
            sem((chips,)), sem((chips,)), sem((chips,)), sem((chips,)), sem((1,)), sem((1,)),
        ],
        compiler_params=pltpu.CompilerParams(collective_id=2, has_side_effects=True, vmem_limit_bytes=vmem_cap),
        cost_estimate=pl.CostEstimate(flops=30_000_000_000, bytes_accessed=20_000_000, transcendentals=8_000_000),
        name="front",
    )(ints, bucket_row, cotangent, *weights, tokens, small)


def moe_kernel(
    x_ref, g_ref, small_ref, w_in_ref, w_out_ref,
    back_ref, out_ref, ge_hbm, rx_hbm, ry_hbm, rg_ref,
    w_in, w_out, xin, gm, gg, hid, gpre, logit_grads, x_t, gw_in, gw_out,
    xs, xr, ms, mr, ws, ls, os_in, os_out, ex_s, ex_r, ey_s, ey_r,
):
    rep, chip, core, chips, quarter = places()
    experts = chips * 2
    here = chip * 2 + core
    pair_rows = 2 * xin.shape[2]
    hidden = w_in_ref.shape[1]
    width = w_in_ref.shape[0]
    _, slow, fast, slows, fasts = rep_places()
    lines = gw_in.shape[3]
    beside = [(slow * fasts + (fast + j) % fasts, here) for j in range(1, fasts)]
    beyond = [((slow + j) % slows * fasts + fast, here) for j in range(1, slows)]
    loads = [
        pltpu.make_async_copy(w_in_ref, w_in, ws.at[0]),
        pltpu.make_async_copy(w_out_ref, w_out, ws.at[1]),
    ]
    for copy in loads:
        copy.start()
    twin = (rep, chip * 2 + 1 - core)
    targets = [
        (k, side, (rep, chip_across(chip, k) * 2 + side)) for k in range(1, chips) for side in range(2)
    ]
    greet([twin] + [device for _, _, device in targets] + beside + beyond)
    sent = [send(x_ref.at[chip, 1 - core], xin.at[chip, core], (xs.at[0, 0], xr.at[0, core]), twin)]
    for k, side, device in targets:
        sent.append(
            send(x_ref.at[chip_across(chip, k), side], xin.at[chip, core], (xs.at[k, side], xr.at[k, core]), device)
        )
    for copy in sent[:5]:
        copy.start()
    xin[chip, core] = x_ref[chip, core]
    for copy in loads:
        copy.wait()

    def arrived(k, source, side):
        piece = xin.at[source, side]
        send(piece, piece, (xs.at[0, 0], xr.at[k, side]), twin).wait_recv()

    @pl.loop(0, chips)
    def chunk(k):
        source = chip_across(chip, k)

        @pl.when(k == 0)
        def _():
            arrived(0, chip, 1 - core)

        @pl.when(k > 0)
        def _():
            for side in range(2):
                arrived(k, source, side)

        rows = xin[source].reshape(pair_rows, xin.shape[3])
        grads = g_ref[source].reshape(pair_rows, xin.shape[3])
        probs = router_softmax(rows, small_ref[...], experts)
        lanes = lax.broadcasted_iota(jnp.int32, probs.shape, 1)
        gate = jnp.sum(jnp.where(lanes == here, probs, 0.0), axis=1, keepdims=True)
        gated = (gate * grads.astype(single)).astype(low)
        span = pl.ds(pl.multiple_of(source * pair_rows, pair_rows), pair_rows)
        gg[span, :] = gated
        pre = nn(rows, w_in[...])
        grad_hidden = nt(gated, w_out[...])
        square = pre * pre
        wave = jnp.tanh(0.7978845608028654 * pre * (1.0 + 0.044715 * square))
        left = 0.5 + 0.5 * wave
        active = (pre * left).astype(low)
        slope = left + (0.5 * pre) * (1.0 - wave * wave) * (0.7978845608028654 + 0.10703222440890037 * square)
        grad_pre = (grad_hidden * slope).astype(low)
        hid[span, :] = active
        gpre[span, :] = grad_pre
        out = nn(active, w_out[...]).astype(low)
        out_ref[source] = out.reshape(out_ref.shape[1:])
        grad_gate = jnp.sum(grads.astype(single) * out.astype(single), axis=1, keepdims=True)
        chosen = jnp.where(lanes == here, 1.0, 0.0)
        grad_logits = jnp.where(lanes < experts, gate * grad_gate * (chosen - probs), 0.0)
        logit_grads[span, :] = grad_logits
        router = small_ref[...]
        total = nt(grad_pre, w_in[...]) + sum(nt(part, router) for part in thirds_of(grad_logits))
        gm[source] = total.astype(low).reshape(gm.shape[1:])

        def reply(side, slot):
            return send(
                gm.at[source, side], back_ref.at[chip, core], (ms.at[k, slot], mr.at[k, core]), (rep, source * 2 + side)
            )

        @pl.when(k == 0)
        def _():
            for copy in sent[5:]:
                copy.start()
            reply(1 - core, 0).start()
            pltpu.make_async_copy(gm.at[chip, core], back_ref.at[chip, core], ls).start()

        @pl.when(k > 0)
        def _():
            for side in range(2):
                reply(side, side).start()

    every = xin[...].reshape(gg.shape)
    x_t[...] = every.T

    def strip_writes(part):
        rows = pl.ds(pl.multiple_of(part * lines, lines), lines)
        tail = pl.ds(4 * lines, 4 * lines)
        if gw_out.shape[1] == 1:
            second = (gw_out.at[part, 0], ge_hbm.at[part // fasts, part % fasts, tail])
        else:
            second = (gw_out.at[part], ge_hbm.at[part, :, tail])
        return [
            pltpu.make_async_copy(gw_in.at[part], ge_hbm.at[:, :, rows], os_in.at[part]),
            pltpu.make_async_copy(*second, os_out.at[part]),
        ]

    grads_out = [
        send(gw_in.at[0, :, (fast + j + 1) % fasts], rx_hbm.at[j], (ex_s.at[j], ex_r.at[j]), device)
        for j, device in enumerate(beside)
    ], [
        send(gw_in.at[1, (slow + j + 1) % slows], ry_hbm.at[j], (ey_s.at[j], ey_r.at[j]), device)
        for j, device in enumerate(beyond)
    ]

    @pl.loop(0, hidden // width)
    def strip(part):
        cols = pl.ds(pl.multiple_of(part * width, width), width)
        first, second = strip_writes(part)
        gw_in[part] = nn(x_t[...], gpre[:, cols]).astype(low).reshape(gw_in.shape[1:])
        first.start()
        for turn in range(2):

            @pl.when(part == turn)
            def _():
                for copy in grads_out[turn]:
                    copy.start()

        gw_out[part] = tn(hid[:, cols], gg[...]).astype(low).reshape(gw_out.shape[1:])
        second.start()

    rg_ref[...] = sum(nn(x_t[...], part) for part in thirds_of(logit_grads[...]))
    pltpu.make_async_copy(gm.at[chip, core], back_ref.at[chip, core], ls).wait()

    def replied(k, source, side):
        piece = back_ref.at[source, side]
        send(piece, piece, (ms.at[0, 0], mr.at[k, side]), twin).wait_recv()

    replied(0, chip, 1 - core)
    for k in range(1, chips):
        for side in range(2):
            replied(k, chip_across(chip, k), side)
    for copy in sent:
        copy.wait_send()
    for part in range(hidden // width):
        for copy in strip_writes(part):
            copy.wait()
    for copy in grads_out[0] + grads_out[1]:
        copy.wait()
    send(gm.at[chip, 0], back_ref.at[chip, core], (ms.at[0, 0], mr.at[0, 0]), twin).wait_send()
    for k in range(1, chips):
        for side in range(2):
            send(gm.at[chip, 0], back_ref.at[chip, core], (ms.at[k, side], mr.at[0, 0]), twin).wait_send()


def moe(rows_out, grad_in, small, w_in, w_out):
    chips, _, cap, width = rows_out.shape
    slots = chips * 2 * cap
    hidden = w_in.shape[1]
    shape = jax.ShapeDtypeStruct
    pairs = pltpu.SemaphoreType.DMA
    strips = hidden // width
    slows, fasts = rep_places()[3:]
    lines = width // (slows * fasts)
    return pl.pallas_call(
        moe_kernel,
        out_shape=(
            shape(rows_out.shape, low), shape(rows_out.shape, low), shape((slows, fasts, 8 * lines, width), low),
            shape((fasts - 1, slows, lines, width), low), shape((slows - 1, fasts, lines, width), low),
            shape((width, TILE), single),
        ),
        in_specs=[in_vmem] * 3 + [anywhere] * 2,
        out_specs=(anywhere, in_vmem, anywhere, anywhere, anywhere, in_vmem),
        scratch_shapes=[
            pltpu.VMEM((width, hidden), low), pltpu.VMEM((hidden, width), low),
            pltpu.VMEM(rows_out.shape, low), pltpu.VMEM(rows_out.shape, low), pltpu.VMEM((slots, width), low),
            pltpu.VMEM((slots, hidden), low), pltpu.VMEM((slots, hidden), low),
            pltpu.VMEM((slots, TILE), single), pltpu.VMEM((width, slots), low),
            pltpu.VMEM((strips, slows, fasts, lines, width), low),
            pltpu.VMEM((strips, width // (4 * lines), 4 * lines, width), low),
            pairs((chips, 2)), pairs((chips, 2)), pairs((chips, 2)), pairs((chips, 2)), pairs((2,)), pairs,
            pairs((strips,)), pairs((strips,)), pairs((fasts - 1,)), pairs((fasts - 1,)), pairs((slows - 1,)),
            pairs((slows - 1,)),
        ],
        compiler_params=pltpu.CompilerParams(collective_id=3, has_side_effects=True, vmem_limit_bytes=vmem_cap),
        cost_estimate=pl.CostEstimate(flops=40_000_000_000, bytes_accessed=40_000_000, transcendentals=3_000_000),
        name="moe",
    )(rows_out, grad_in, small, w_in, w_out)


def back_kernel(
    col_ref, gain_ref, lse_ref, rev_ref, bucket_ref, rg_ref, back_hbm, mid_hbm, cot_hbm, q_hbm, k_hbm, v_hbm, o_hbm,
    every_hbm, w_hbm, n_hbm, ge_hbm, rx_hbm, ry_hbm, out_hbm,
    z_ref, kx_ref, ky_ref, dense_hbm, p_hbm, e_hbm, own_hbm, gres_hbm, ra_hbm, rb_hbm, ret_hbm, lx_hbm, ly_hbm,
    tiles, sums, diag, kt, dqt, far_sums, g_ref, dq_ref, dk_ref, dv_ref, attn_gain,
    every_ref, w_ref, n_ref, back_ref, mid_ref, cot_ref, q_ref, k_ref, v_ref, o_ref,
    dense_ref, own_ref, gres_ref,
    x_own, x_in, x_sum, y_own, y_in, y_sum, o_grad, o_half, o_sum, o_in, h_grad, h_half, h_sum, h_in,
    loc, out, lx_s, lx_r, ly_s, ly_r, xs, xr, as_, ar, bs, br, os_, or_, oz_s, oz_r, hs_, hr_, hz_s, hz_r,
):
    shard_id = lax.axis_index("shard")
    shards = lax.axis_size("shard")
    rows, width = mid_ref.shape
    blocks = k_ref.shape[0] // TILE - 4
    half = TILE // 2
    experts = shards
    heads_held = rev_ref.shape[0]
    rep, slow, fast, slows, fasts = rep_places()
    _, chip, core, chips, _ = places()
    along, _, twin = peer_lists()
    lines = x_own.shape[1]
    loads = [
        pltpu.make_async_copy(source, target, loc.at[i])
        for i, (source, target) in enumerate((
            (back_hbm, back_ref), (mid_hbm, mid_ref), (cot_hbm, cot_ref), (w_hbm.at[3], w_ref.at[3]), (o_hbm, o_ref),
            (q_hbm, q_ref), (k_hbm, k_ref), (v_hbm, v_ref), (n_hbm, n_ref), (w_hbm.at[pl.ds(0, 3)], w_ref.at[pl.ds(0, 3)]),
            (every_hbm, every_ref), (out_hbm.at[chip, core], ret_hbm.at[chip, core]),
            (ge_hbm.at[:, fast, pl.ds(0, lines)], x_own), (rx_hbm, x_in),
            (ge_hbm.at[slow, :, pl.ds(lines, lines)], y_own), (ry_hbm, y_in),
        ))
    ]
    for copy in loads:
        copy.start()
    writes = []

    def write(source, target):
        writes.append(pltpu.make_async_copy(source, target, out.at[len(writes)]))
        writes[-1].start()

    beside = [(slow * fasts + (fast + j) % fasts, shard_id) for j in range(1, fasts)]
    beyond = [((slow + j) % slows * fasts + fast, shard_id) for j in range(1, slows)]
    nearby = result_peers(rep, chip, core, range(NEAR))
    far_twins = [(rep, (chip + k) % chips * 2 + 1 - core) for k in range(1, chips)]
    greet([twin] + along + far_twins + beside + beyond)
    sent = [
        send(ge_hbm.at[:, (fast + j + 1) % fasts, pl.ds(2 * lines, 3 * lines)], ra_hbm.at[j], (as_.at[j], ar.at[j]), device)
        for j, device in enumerate(beside)
    ] + [
        send(ge_hbm.at[(slow + j + 1) % slows, :, pl.ds(5 * lines, 3 * lines)], rb_hbm.at[j], (bs.at[j], br.at[j]), device)
        for j, device in enumerate(beyond)
    ] + [
        send(out_hbm.at[chip_across(chip, k), side if k else 1 - core], ret_hbm.at[chip, core], (xs.at[k, side], xr.at[k, core]), device)
        for k, side, device in nearby
    ]
    for copy in sent:
        copy.start()
    for copy in loads[12:]:
        copy.wait()
    for held, came, total in ((x_own, x_in, x_sum), (y_own, y_in, y_sum)):
        value = held[...].astype(single)
        for j in range(came.shape[0]):
            value = value + came[j].astype(single)
        total[...] = value.astype(low)
    second = [
        send(x_sum.at[(slow + j + 1) % slows], lx_hbm.at[j], (lx_s.at[j], lx_r.at[j]), device)
        for j, device in enumerate(beyond)
    ] + [
        send(y_sum.at[(fast + j + 1) % fasts], ly_hbm.at[j], (ly_s.at[j], ly_r.at[j]), device)
        for j, device in enumerate(beside)
    ]
    for copy in second:
        copy.start()
    kx_ref[...] = x_sum[slow]
    ky_ref[...] = y_sum[fast]
    diag[...] = jnp.zeros_like(diag)
    far_sums[...] = jnp.zeros_like(far_sums)
    tile_rows = lax.broadcasted_iota(jnp.int32, (TILE, TILE), 0)
    tile_cols = lax.broadcasted_iota(jnp.int32, (TILE, TILE), 1)
    flip = (tile_rows + tile_cols == TILE - 1).astype(single)

    for copy in loads[:5]:
        copy.wait()
    slots = lax.broadcasted_iota(jnp.int32, (rows, back_ref.shape[0]), 1)
    grad_mid = nn((slots == col_ref[:, 0:1]).astype(low), back_ref[...])
    resid_mid = mid_ref[...]
    grad_gain_moe = jnp.sum(grad_mid * resid_mid * inverse_rms(resid_mid), axis=0, keepdims=True)
    grad_resid = cot_ref[...].astype(single) + norm_pull(grad_mid, resid_mid, gain_ref[1:2, :])
    gres_ref[...] = grad_resid
    write(gres_ref, gres_hbm)
    grad_attn = grad_resid.astype(low)
    g_ref[...] = nt(grad_attn, w_ref[3]).astype(low)
    o_grad[...] = nn(o_ref[...].astype(low), grad_attn).reshape(o_grad.shape).astype(low)
    o_halves = [send(o_grad.at[2 * k + 1 - core], o_half.at[k], (os_.at[k], or_.at[k]), twin) for k in range(chips)]
    o_sends = [
        send(o_sum.at[(chip + k + 1) % chips], o_in.at[k], (oz_s.at[k], oz_r.at[k]), device)
        for k, device in enumerate(along)
    ]
    for copy in o_halves:
        copy.start()
    h_halves = [send(h_grad.at[2 * k + 1 - core], h_half.at[k], (hs_.at[k], hr_.at[k]), twin) for k in range(chips)]
    h_sends = [
        send(h_sum.at[(chip + k + 1) % chips], h_in.at[k], (hz_s.at[k], hz_r.at[k]), device)
        for k, device in enumerate(along)
    ]
    for copy in loads[5:12]:
        copy.wait()
    own = pl.ds(pl.multiple_of(shard_id * TILE, TILE), TILE)
    tail = slice((blocks + 2) * TILE, (blocks + 4) * TILE)
    early = width // 2

    @pl.loop(0, width // TILE)
    def pair_loop(pair):
        cols = pl.ds(pl.multiple_of(pair * TILE, TILE), TILE)
        kt[...] = k_ref[:, cols].T
        g_pair = g_ref[:, cols]
        q_both, g_both = both_heads(q_ref[:, cols]), both_heads(g_pair)
        delta_t = g_pair.astype(single).T * o_ref[cols, :]
        delta = jnp.concatenate(
            [jnp.sum(delta_t[:half], axis=0, keepdims=True), jnp.sum(delta_t[half:], axis=0, keepdims=True)], axis=1
        )
        log_total = jnp.concatenate([lse_ref[pl.ds(pair * 2, 1), :], lse_ref[pl.ds(pair * 2 + 1, 1), :]], axis=1)
        for side in range(2):
            rev_row = rev_ref[pl.ds(pair * 2 + side, 1), :]
            fill_tiles(tiles.at[side], rev_row, rev_row[:, SPAN - 1 : SPAN], rev_row[:, SPAN : SPAN + 1])
        sums[...] = jnp.zeros_like(sums)

        def block_grads(part, q_rows, g_rows, shift, scale, grid):
            keys = slice(part * SPAN, (part + 1) * SPAN)
            count = q_rows.shape[0] // 2
            scores = with_bias(nt(k_ref[keys, cols], q_rows), tiles, grid)
            weights = jnp.exp(scores - shift)
            grad_scores = weights * (nt(v_ref[keys, cols], g_rows) - scale)
            for i, row in enumerate(grid):
                for j, (side, kind) in enumerate(row):
                    sums[side, kind] += tile_of(grad_scores, i, j)
            raw = grad_scores.astype(low)
            dk_ref[keys, cols] = nn(raw, q_rows).astype(low)
            dv_ref[keys, cols] = nn(weights.astype(low), g_rows).astype(low)
            return [nn(kt[:half, keys], raw[:, :count]), nn(kt[half:, keys], raw[:, count:])]

        grads = [jnp.zeros((half, rows), single)] * 2
        for part in range(blocks // 2):
            more = block_grads(part, q_both, g_both, log_total, delta, prompt_grid(part, shard_id, blocks))
            grads = [old + new for old, new in zip(grads, more)]
        local = [old[:, PR_DEV:] for old in grads]
        held = (continuation(q_both, 0), continuation(g_both, 0), continuation(log_total, 1), continuation(delta, 1))
        for part in range(2):
            more = block_grads(blocks // 2 + part, *held, local_grid(part, shard_id))
            local = [old + new for old, new in zip(local, more)]
        for side in range(2):
            head = pair * 2 + side
            dqt[side * half : (side + 1) * half, :] = jnp.concatenate([grads[side][:, :PR_DEV], local[side]], axis=1)
            near = jnp.concatenate(
                [
                    sums[side, 1] + sums[side, causal_tile], sums[side, 0], jnp.zeros((TILE, TILE), single),
                    sums[side, 2],
                ],
                axis=1,
            )
            flipped = jnp.dot(flip, near, precision=lax.Precision.HIGHEST, preferred_element_type=single)
            rolled = pltpu.roll(flipped, 3 * TILE + 1, 1, stride=1, stride_axis=0)
            diag[pl.ds(head, 1), :] = jnp.sum(rolled, axis=0, keepdims=True)
            far_sums[pl.ds(head, 1), :] = jnp.concatenate(
                [
                    jnp.sum(sums[side, far_before], axis=0, keepdims=True),
                    jnp.sum(sums[side, far_after], axis=0, keepdims=True),
                ],
                axis=1,
            )
        dq_ref[:, cols] = (dqt[...].T * 0.125).astype(low)

        @pl.when(pair == 0)
        def _():
            for k in range(chips):
                o_halves[k].wait_recv()
                o_sum[k] = (o_grad[2 * k + core].astype(single) + o_half[k].astype(single)).astype(low)
            for copy in o_sends:
                copy.start()

        @pl.when(pair == width // SPAN - 1)
        def _():
            normed = jnp.concatenate([n_ref[:, own], n_ref[:, tail]], axis=1)
            for i, (left, right) in enumerate(((normed, dq_ref), (n_ref[...], dk_ref), (n_ref[...], dv_ref))):
                part = nn(left, right[:, :early]).reshape(shards, h_grad.shape[1], early)
                h_grad[:, :, i * early : (i + 1) * early] = part.astype(low)
            for copy in h_halves:
                copy.start()

        @pl.when(pair == width // SPAN)
        def _():
            for k in range(chips):
                h_halves[k].wait_recv()
                h_sum[k] = (h_grad[2 * k + core].astype(single) + h_half[k].astype(single)).astype(low)
            for copy in h_sends:
                copy.start()

    lanes = lax.broadcasted_iota(jnp.int32, (heads_held, 4 * TILE), 1)
    before = jnp.sum(far_sums[:, :TILE], axis=1, keepdims=True)
    after = jnp.sum(far_sums[:, TILE:], axis=1, keepdims=True)
    by_gap = diag[...] + jnp.where(lanes == SPAN - 1, before, 0.0) + jnp.where(lanes == SPAN, after, 0.0)
    shard_rows = width // shards
    table_rows = 2 * TILE // 8 // shards
    owner = lax.broadcasted_iota(jnp.int32, (shards, shard_rows, 4 * TILE), 0)
    offset = lax.broadcasted_iota(jnp.int32, (shards, shard_rows, 4 * TILE), 1)
    held = jnp.where(offset < table_rows, owner * table_rows + offset, -1).reshape(width, 4 * TILE)
    hot = (held == bucket_ref[0:1, :]).astype(low)
    grad_table = sum(nt(part, hot) for part in thirds_of(by_gap))

    attn_gain[...] = jnp.zeros_like(attn_gain)
    normed = jnp.concatenate([n_ref[:, own], n_ref[:, tail]], axis=1)
    dense_ref[:, :early] = nn(normed, dq_ref[:, early:]).astype(low)
    grad_own = nt(dq_ref[...], w_ref[0])
    values = jnp.concatenate([every_ref[own, :], every_ref[tail, :]], axis=0).astype(single)
    attn_gain[...] += jnp.sum(fold8(grad_own * (values * inverse_rms(values))), axis=0)
    own_ref[...] = grad_own

    def pull_rows(part):
        span = pl.ds(pl.multiple_of(part * SPAN, SPAN), SPAN)
        values = every_ref[span, :].astype(single)
        grads = nt(dk_ref[span, :], w_ref[1]) + nt(dv_ref[span, :], w_ref[2])
        attn_gain[...] += jnp.sum(fold8(grads * (values * inverse_rms(values))), axis=0)
        return grads

    @pl.loop(0, blocks // 2)
    def pull_prompt(part):
        k_ref[pl.ds(pl.multiple_of(part * SPAN, SPAN), SPAN), :] = pull_rows(part).astype(low)

    write(k_ref.at[pl.ds(0, blocks * TILE)], p_hbm)
    k_ref[blocks * TILE : (blocks + 2) * TILE, :] = pull_rows(blocks // 2).astype(low)
    write(k_ref.at[pl.ds(blocks * TILE, SPAN)], e_hbm)
    own_ref[PR_DEV:, :] += pull_rows(blocks // 2 + 1)
    write(own_ref, own_hbm)

    dense_ref[:, early : 2 * early] = nn(n_ref[...], dk_ref[:, early:]).astype(low)
    dense_ref[:, 2 * early : 3 * early] = nn(n_ref[...], dv_ref[:, early:]).astype(low)

    small_t = jnp.concatenate(
        [
            jnp.zeros((experts, width), single), jnp.sum(attn_gain[...], axis=0, keepdims=True), grad_gain_moe,
            grad_table, jnp.zeros((TILE - experts - 2 - heads_held, width), single),
        ],
        axis=0,
    )
    dense_ref[:, 3 * early :] = (small_t.T + rg_ref[...]).astype(low)
    write(dense_ref, dense_hbm)
    o_total = o_sum[chip].astype(single)
    for k in range(chips - 1):
        o_sends[k].wait_recv()
        o_total = o_total + o_in[k].astype(single)
    z_ref[:, :width] = o_total.astype(low)
    h_total = h_sum[chip].astype(single)
    for k in range(chips - 1):
        h_sends[k].wait_recv()
        h_total = h_total + h_in[k].astype(single)
    z_ref[:, width:] = h_total.astype(low)
    for copy in o_halves + o_sends + h_halves + h_sends:
        copy.wait_send()
    for copy in writes:
        copy.wait()
    for k, side in result_slots(core, range(NEAR)):
        piece = ret_hbm.at[chip_across(chip, k), side]
        send(piece, piece, (xs.at[0, 0], xr.at[k, side]), twin).wait_recv()
    for j in range(fasts - 1):
        send(ra_hbm.at[j], ra_hbm.at[j], (as_.at[j], ar.at[j]), twin).wait_recv()
    for j in range(slows - 1):
        send(rb_hbm.at[j], rb_hbm.at[j], (bs.at[j], br.at[j]), twin).wait_recv()
    for copy in second:
        copy.wait()
    for copy in sent:
        copy.wait_send()


def back(
    returned, col_slots, mid, cotangent, gains, every_tok, weights, kept, bucket_row, router_grads, grads, rx, ry, result
):
    rows, width = mid.shape
    normed, queries, keys, values, attended, lse, rev = kept
    count = keys.shape[0]
    shards = lax.axis_size("shard")
    slows, fasts, eighths = grads.shape[:3]
    m = eighths // 8
    chips, lines, early = shards // 2, width // shards, width // 2
    vm = pltpu.VMEM
    shape = jax.ShapeDtypeStruct
    pairs = pltpu.SemaphoreType.DMA
    args = (
        col_slots, gains, lse, rev, bucket_row, router_grads, returned, mid, cotangent, queries, keys, values, attended,
        every_tok, weights, normed, grads, rx, ry, result,
    )
    return pl.pallas_call(
        back_kernel,
        out_shape=(
            shape((lines, width + 3 * early), low), shape((m, width), low), shape((m, width), low),
            shape((width, 3 * early + TILE), low),
            shape((count - 2 * SPAN, width), low), shape((SPAN, width), low),
            shape((rows, width), single), shape((rows, width), single),
            shape((fasts - 1, slows, 3 * m, width), low), shape((slows - 1, fasts, 3 * m, width), low),
            shape(result.shape, low), shape((slows - 1, m, width), low), shape((fasts - 1, m, width), low),
        ),
        in_specs=[in_vmem] * 6 + [anywhere] * 14,
        out_specs=(in_vmem,) * 3 + (anywhere,) * 10,
        scratch_shapes=[
            pltpu.VMEM((2, tile_kinds, TILE, TILE), single), pltpu.VMEM((2, tile_kinds, TILE, TILE), single),
            pltpu.VMEM((16, 4 * TILE), single), pltpu.VMEM((TILE, count), low), pltpu.VMEM((TILE, rows), single),
            pltpu.VMEM((16, 2 * TILE), single),
            pltpu.VMEM((rows, width), low), pltpu.VMEM((rows, width), low), pltpu.VMEM((count, width), low),
            pltpu.VMEM((count, width), low), pltpu.VMEM((8, width), single),
            pltpu.VMEM(every_tok.shape, low), pltpu.VMEM(weights.shape, low), pltpu.VMEM(normed.shape, low),
            vm(returned.shape, low), vm((rows, width), single), vm((rows, width), low), vm((rows, width), low),
            vm(keys.shape, low), vm(keys.shape, low), vm(attended.shape, single),
            vm((width, 3 * early + TILE), low),
            vm((rows, width), single), vm((rows, width), single),
            vm((slows, m, width), low), vm((fasts - 1, slows, m, width), low), vm((slows, m, width), low),
            vm((fasts, m, width), low), vm((slows - 1, fasts, m, width), low), vm((fasts, m, width), low),
            vm((shards, lines, width), low), vm((chips, lines, width), low),
            vm((chips, lines, width), low), vm((chips - 1, lines, width), low),
            vm((shards, lines, 3 * early), low), vm((chips, lines, 3 * early), low),
            vm((chips, lines, 3 * early), low), vm((chips - 1, lines, 3 * early), low),
            pairs((16,)), pairs((6,)), pairs((slows - 1,)), pairs((slows - 1,)), pairs((fasts - 1,)), pairs((fasts - 1,)),
            pairs((NEAR, 2)), pairs((NEAR, 2)), pairs((fasts - 1,)), pairs((fasts - 1,)),
            pairs((slows - 1,)), pairs((slows - 1,)), pairs((chips,)), pairs((chips,)), pairs((chips - 1,)),
            pairs((chips - 1,)), pairs((chips,)), pairs((chips,)), pairs((chips - 1,)), pairs((chips - 1,)),
        ],
        compiler_params=pltpu.CompilerParams(collective_id=4, has_side_effects=True, vmem_limit_bytes=vmem_cap),
        cost_estimate=pl.CostEstimate(flops=60_000_000_000, bytes_accessed=40_000_000, transcendentals=8_000_000),
        name="back",
    )(*args)


def places():
    rep, shard = lax.axis_index("rep"), lax.axis_index("shard")
    return rep, shard // 2, shard % 2, lax.axis_size("shard") // 2, rep % QUARTERS


def peer_lists():
    rep, chip, core, chips, quarter = places()
    along = [(rep, (chip + k) % chips * 2 + core) for k in range(1, chips)]
    across = [(rep - quarter + (quarter + j) % QUARTERS, chip * 2 + core) for j in range(1, QUARTERS)]
    twin = (rep, chip * 2 + 1 - core)
    return along, across, twin


def chip_across(chip, k):
    partner, bit = 0, 1
    while bit < lax.axis_size("shard") // 2:
        partner = partner + bit * ((chip // bit + k // bit) % 2)
        bit = bit * 2
    return partner


def result_peers(rep, chip, core, chosen):
    return [
        (k, side, (rep, chip_across(chip, k) * 2 + (side if k else 1 - core)))
        for k in chosen for side in range(2 if k else 1)
    ]


def result_slots(core, chosen):
    return [(k, side if k else 1 - core) for k in chosen for side in range(2 if k else 1)]


def greet(devices):
    barrier = pltpu.get_barrier_semaphore()
    for device in devices:
        pl.semaphore_signal(barrier, inc=1, device_id=device, device_id_type=mesh_ids)
    pl.semaphore_wait(barrier, len(devices))


def send(source, target, sems, device):
    return pltpu.make_async_remote_copy(
        src_ref=source, dst_ref=target, send_sem=sems[0], recv_sem=sems[1],
        device_id=device, device_id_type=mesh_ids,
    )


def rep_places():
    rep, reps = lax.axis_index("rep"), lax.axis_size("rep")
    fasts = QUARTERS if reps % (QUARTERS * QUARTERS) == 0 else 2
    return rep, rep // fasts, rep % fasts, reps // fasts, fasts


def reduce_kernel(
    gain_ref, col_ref, d_hbm, p_hbm, e_hbm, own_hbm, gres_hbm, tok_hbm, mid_hbm, gate_hbm, out_hbm, ret_hbm,
    ge_hbm, ra_hbm, rb_hbm, z_hbm,
    gt_ref, mix_ref, early_ref, late_ref, ka_ref, la_hbm, kb_ref, lb_hbm,
    d_own, half, hr, tr, mr, cr, zs, tz, z_last, z_above, z_all, last, above_in, gathered,
    p_own, p_half, p_sum, p_in, e_in, own, gres, tok, mid, gate, ret,
    a_own, a_in, a_sum, b_own, b_in, b_sum,
    loc, ps_s, ps_r, ds_s, ds_r, pz_s, pz_r, rr_s, rr_r, rz_s, rz_r, zr_s, zr_r, zh_s, zh_r, za_s, za_r,
    dh_s, dh_r, da_s, da_r, ea_s, ea_r, eb_s, eb_r, xs, xr,
):
    rep, chip, core, chips, quarter = places()
    along, across, twin = peer_lists()
    _, slow, fast, slows, fasts = rep_places()
    classes = lax.axis_size("rep") // QUARTERS
    here = chip * 2 + core
    beside = [(slow * fasts + (fast + j) % fasts, here) for j in range(1, fasts)]
    beyond = [((slow + j) % slows * fasts + fast, here) for j in range(1, slows)]
    above = [((rep // QUARTERS + k) % classes * QUARTERS + quarter, here) for k in range(1, classes)]
    wide = lambda held: held.astype(single)
    lines = ge_hbm.shape[2] // 8
    pending = []

    def load(source, target, index):
        copy = pltpu.make_async_copy(source, target, loc.at[index])
        copy.start()
        return copy

    def go(source, target, sems, device):
        copy = send(source, target, sems, device)
        copy.start()
        pending.append(copy)

    def landed(piece, sems):
        send(piece, piece, sems, twin).wait_recv()

    early_in = load(z_hbm, zs, 12)
    a_loads = [load(ge_hbm.at[:, fast, pl.ds(2 * lines, 3 * lines)], a_own, 0), load(ra_hbm, a_in, 1)]
    halves = [load(d_hbm.at[:, core], d_own, 5), load(p_hbm.at[:, core], p_own, 4)]
    b_loads = [load(ge_hbm.at[slow, :, pl.ds(5 * lines, 3 * lines)], b_own, 2), load(rb_hbm, b_in, 3)]
    rest = [
        load(ret_hbm.at[chip_across(chip, k)], ret.at[chip_across(chip, k)], 13 + k) for k in range(NEAR)
    ] + [
        load(mid_hbm, mid, 7), load(gate_hbm, gate, 8), load(own_hbm, own, 9),
        load(gres_hbm, gres, 10), load(tok_hbm, tok, 11),
    ]
    others = [(rep, (here + k) % (2 * chips)) for k in range(1, 2 * chips)]
    greets = list(others)
    for device in across + beside + beyond + above:
        greets.append(device)
    greet(greets)
    for k in range(chips):
        go(d_hbm.at[k, 1 - core], half.at[k], (ds_s.at[k], ds_r.at[k]), twin)
    go(p_hbm.at[:, 1 - core], p_half, (ps_s.at[0], ps_r.at[0]), twin)
    go(e_hbm, e_in, (ps_s.at[1], ps_r.at[1]), twin)
    for k, side, device in result_peers(rep, chip, core, range(NEAR, chips)):
        go(out_hbm.at[chip_across(chip, k), side], ret.at[chip, core], (xs.at[k - NEAR, side], xr.at[k - NEAR, core]), device)
    early_in.wait()
    for j, device in enumerate(across):
        go(zs.at[(quarter + j + 1) % QUARTERS], tz.at[j], (zr_s.at[j], zr_r.at[j]), device)

    for copy in a_loads:
        copy.wait()
    for t in range(slows):
        total = wide(a_own[t])
        for j in range(fasts - 1):
            total = total + wide(a_in[j, t])
        a_sum[t] = total.astype(low)
    for j, device in enumerate(beyond):
        go(a_sum.at[(slow + j + 1) % slows], la_hbm.at[j], (ea_s.at[j], ea_r.at[j]), device)
    for copy in halves:
        copy.wait()
    for k in range(chips):
        landed(half.at[k], (ds_s.at[k], ds_r.at[k]))
        for t in range(QUARTERS):
            hr[t, k] = (wide(d_own[k, t]) + wide(half[k, t])).astype(low)
    for j, device in enumerate(across):
        go(hr.at[(quarter + j + 1) % QUARTERS], tr.at[j], (rr_s.at[j], rr_r.at[j]), device)
    landed(p_half, (ps_s.at[0], ps_r.at[0]))
    for k in range(chips):
        p_sum[k] = (wide(p_own[k]) + wide(p_half[k])).astype(low)
    for k, device in enumerate(along):
        go(p_sum.at[(chip + k + 1) % chips], p_in.at[k], (pz_s.at[k], pz_r.at[k]), device)
    for copy in b_loads:
        copy.wait()
    for t in range(fasts):
        total = wide(b_own[t])
        for j in range(slows - 1):
            total = total + wide(b_in[j, t])
        b_sum[t] = total.astype(low)
    for j, device in enumerate(beside):
        go(b_sum.at[(fast + j + 1) % fasts], lb_hbm.at[j], (eb_s.at[j], eb_r.at[j]), device)

    def class_sum(held, came, s_sems, r_sems):
        total = wide(held[...])
        for j, device in enumerate(above):
            go(held, came.at[j], (s_sems.at[j], r_sems.at[j]), device)
        for j in range(classes - 1):
            landed(came.at[j], (s_sems.at[j], r_sems.at[j]))
            total = total + wide(came[j])
        return total.astype(low)

    def hand_out(pieces, s_sems, r_sems):
        for j, device in enumerate(across):
            go(pieces.at[quarter], pieces.at[quarter], (s_sems.at[j], r_sems.at[j]), device)

    def handed(pieces, s_sems, r_sems):
        for j in range(QUARTERS - 1):
            landed(pieces.at[(quarter + QUARTERS - j - 1) % QUARTERS], (s_sems.at[j], r_sems.at[j]))

    for j in range(QUARTERS - 1):
        landed(tz.at[j], (zr_s.at[j], zr_r.at[j]))
    total = wide(zs[quarter])
    for j in range(QUARTERS - 1):
        total = total + wide(tz[j])
    z_last[...] = total.astype(low)
    z_all[quarter] = class_sum(z_last, z_above, zh_s, zh_r) if classes > 1 else z_last[...]
    hand_out(z_all, za_s, za_r)

    for copy in rest:
        copy.wait()
    ka_ref[...] = a_sum[slow]
    kb_ref[...] = b_sum[fast]

    for j in range(QUARTERS - 1):
        landed(tr.at[j], (rr_s.at[j], rr_r.at[j]))
    for k in range(chips):
        total = wide(hr[quarter, k])
        for j in range(QUARTERS - 1):
            total = total + wide(tr[j, k])
        mr[k] = total.astype(low)
    for k, device in enumerate(along):
        go(mr.at[(chip + k + 1) % chips], cr.at[k], (rz_s.at[k], rz_r.at[k]), device)

    for k in range(chips - 1):
        landed(p_in.at[k], (pz_s.at[k], pz_r.at[k]))
    landed(e_in, (ps_s.at[1], ps_r.at[1]))
    total = wide(p_sum[chip])
    for k in range(chips - 1):
        total = total + wide(p_in[k])
    grads = own[...] + jnp.concatenate([total, wide(e_in[...])], axis=0)
    gt_ref[...] = gres[...] + norm_pull(grads, wide(tok[...]), gain_ref[0:1, :])

    for k in range(chips - 1):
        landed(cr.at[k], (rz_s.at[k], rz_r.at[k]))
    total = wide(mr[chip])
    for k in range(chips - 1):
        total = total + wide(cr[k])
    last[...] = total.astype(low)
    gathered[quarter] = class_sum(last, above_in, dh_s, dh_r) if classes > 1 else last[...]
    hand_out(gathered, da_s, da_r)
    for k, side in result_slots(core, range(NEAR, chips)):
        landed(ret.at[chip_across(chip, k), side], (xs.at[k - NEAR, side], xr.at[k - NEAR, side]))
    slots = lax.broadcasted_iota(jnp.int32, (tok.shape[0], 2 * chips * ret.shape[2]), 1)
    chosen = nn((slots == col_ref[:, 0:1]).astype(low), ret[...].reshape(slots.shape[1], tok.shape[1]))
    mix_ref[...] = (mid[...] + gate[:, 0:1] * chosen).astype(low)
    handed(z_all, za_s, za_r)
    early_ref[...] = z_all[...]
    handed(gathered, da_s, da_r)
    late_ref[...] = gathered[...]
    for j in range(slows - 1):
        landed(la_hbm.at[j], (ea_s.at[j], ea_r.at[j]))
    for j in range(fasts - 1):
        landed(lb_hbm.at[j], (eb_s.at[j], eb_r.at[j]))
    for copy in pending:
        copy.wait_send()


def reduce_all(gains, col_slots, dense, prompt_part, near_part, own, gres, tokens, mid, gate, result, returned, grads, ra, rb, z):
    chips = lax.axis_size("shard") // 2
    classes = lax.axis_size("rep") // QUARTERS
    slows, fasts, eighths = grads.shape[:3]
    part = (3 * eighths // 8, mid.shape[1])
    rows, width = mid.shape
    lines, lanes = dense.shape[3:]
    wider = z.shape[2]
    shape = jax.ShapeDtypeStruct
    sem = pltpu.SemaphoreType.DMA
    vm = pltpu.VMEM
    count, others = chips - 1, QUARTERS - 1
    ours = prompt_part.shape[2:]
    extra = max(classes - 1, 1)
    args = (gains, col_slots, dense, prompt_part, near_part, own, gres, tokens, mid, gate, result, returned, grads, ra, rb, z)
    return pl.pallas_call(
        reduce_kernel,
        out_shape=(
            shape((rows, width), single), shape((rows, width), low),
            shape((QUARTERS, lines, wider), low), shape((QUARTERS, lines, lanes), low),
            shape(part, low), shape((slows - 1,) + part, low), shape(part, low), shape((fasts - 1,) + part, low),
        ),
        in_specs=[in_vmem] * 2 + [anywhere] * 14,
        out_specs=(in_vmem,) * 5 + (anywhere, in_vmem, anywhere),
        scratch_shapes=[
            vm((chips, QUARTERS, lines, lanes), low), vm((chips, QUARTERS, lines, lanes), low),
            vm((QUARTERS, chips, lines, lanes), low), vm((others, chips, lines, lanes), low),
            vm((chips, lines, lanes), low), vm((count, lines, lanes), low),
            vm((QUARTERS, lines, wider), low), vm((others, lines, wider), low), vm((lines, wider), low),
            vm((extra, lines, wider), low), vm((QUARTERS, lines, wider), low),
            vm((lines, lanes), low), vm((extra, lines, lanes), low), vm((QUARTERS, lines, lanes), low),
            vm((chips,) + ours, low), vm((chips,) + ours, low), vm((chips,) + ours, low), vm((count,) + ours, low),
            vm(near_part.shape, low), vm((rows, width), single), vm((rows, width), single), vm((rows, width), low),
            vm((rows, width), single), vm(gate.shape, single), vm(result.shape, low),
            vm((slows,) + part, low), vm(ra.shape, low), vm((slows,) + part, low),
            vm((fasts,) + part, low), vm(rb.shape, low), vm((fasts,) + part, low),
            sem((13 + NEAR,)), sem((2,)), sem((2,)), sem((chips,)), sem((chips,)), sem((count,)), sem((count,)),
            sem((others,)), sem((others,)), sem((count,)), sem((count,)),
            sem((others,)), sem((others,)), sem((extra,)), sem((extra,)), sem((others,)), sem((others,)),
            sem((extra,)), sem((extra,)), sem((others,)), sem((others,)),
            sem((slows - 1,)), sem((slows - 1,)), sem((fasts - 1,)), sem((fasts - 1,)),
            sem((chips - NEAR, 2)), sem((chips - NEAR, 2)),
        ],
        compiler_params=pltpu.CompilerParams(collective_id=1, has_side_effects=True, vmem_limit_bytes=vmem_cap),
        cost_estimate=pl.CostEstimate(flops=0, bytes_accessed=200_000_000, transcendentals=0),
        name="reduce_all",
    )(*args)


def finish_kernel(
    kx_ref, lx_ref, ky_ref, ly_ref, ka_ref, la_ref, kc_ref, lc_ref, kb_ref, lb_ref, early_ref, late_ref, small_ref, gt_ref, mix_ref, *outs
):
    ea_ref, eb_ref, q_ref, k_ref, v_ref, o_ref, router_ref, attn_ref, moe_ref, table_ref, gt_out, mix_out = outs
    gt_out[...] = gt_ref[...]
    mix_out[...] = mix_ref[...]
    width = q_ref.shape[2]
    experts = router_ref.shape[0]
    step = pl.program_id(0)

    def total(held, came):
        value = held[...].reshape(ea_ref.shape).astype(single)
        for j in range(came.shape[0]):
            value = value + came[j].reshape(ea_ref.shape).astype(single)
        return value

    for target, first, last, sources in (
        (ea_ref, 0, 0, (kx_ref, lx_ref)), (ea_ref, 1, 1, (ky_ref, ly_ref)), (ea_ref, 2, 3, (ka_ref, la_ref)),
        (eb_ref, 0, 0, (kc_ref, lc_ref)), (eb_ref, 1, 3, (kb_ref, lb_ref)),
    ):

        @pl.when((step >= first) & (step <= last))
        def _():
            target[...] = total(*sources)

    half = width // 2
    o_ref[...] = early_ref[:, :, :width].astype(single)
    for i, ref in enumerate((q_ref, k_ref, v_ref)):
        ref[:, :, :half] = early_ref[:, :, width + i * half : width + (i + 1) * half].astype(single)
        ref[:, :, half:] = late_ref[:, :, i * half : (i + 1) * half].astype(single)

    @pl.when(pl.program_id(0) == 0)
    def _():
        small = small_ref[...].astype(single).reshape(router_ref.shape[1], TILE)
        turned = small.T
        router_ref[...] = turned[:experts]
        attn_ref[...] = turned[experts : experts + 1]
        moe_ref[...] = turned[experts + 1 : experts + 2]
        table_ref[...] = small[: table_ref.shape[0], experts + 2 : experts + 2 + table_ref.shape[1]]


def finish(kx, lx, ky, ly, ka, la, kb, lb, early, late, grad_tokens, mixed, experts, table_rows, heads):
    shape = jax.ShapeDtypeStruct
    _, lines, wider = early.shape
    lanes = late.shape[2]
    width = kb.shape[1]
    rows = QUARTERS * lines
    steps = QUARTERS
    m = kx.shape[0]
    ka, kb = (part.reshape(3, m, width) for part in (ka, kb))
    la, lb = (part.reshape(-1, 3, m, width) for part in (la, lb))
    block = lambda pick: pl.BlockSpec((1, m, width), lambda i: (pick(i), 0, 0))
    blocks = lambda array, pick: pl.BlockSpec((array.shape[0], 1, m, width), lambda i: (0, pick(i), 0, 0))
    strip, rest = (lambda i: jnp.maximum(i - 2, 0)), (lambda i: jnp.maximum(i - 1, 0))
    part = pl.BlockSpec((1, lines, width), lambda i: (i, 0, 0))
    once = lambda *dims: pl.BlockSpec(dims, lambda i: (0,) * len(dims))
    some = pl.BlockSpec((mixed.shape[0] // steps, width), lambda i: (i, 0))
    return pl.pallas_call(
        finish_kernel,
        grid=(steps,),
        out_shape=(
            shape((m, steps * width), single), shape((steps * m, width), single), *(shape((QUARTERS, lines, width), single),) * 4,
            shape((experts, rows), single), shape((1, rows), single), shape((1, rows), single),
            shape((table_rows, heads), single), shape(grad_tokens.shape, single), shape(mixed.shape, low),
        ),
        in_specs=[
            once(*kx.shape), once(*lx.shape), once(*ky.shape), once(*ly.shape),
            block(strip), blocks(la, strip), block(lambda i: 2), blocks(la, lambda i: 2), block(rest), blocks(lb, rest),
            pl.BlockSpec((1, lines, wider), lambda i: (i, 0, 0)), pl.BlockSpec((1, lines, lanes), lambda i: (i, 0, 0)),
            pl.BlockSpec((QUARTERS, lines, TILE), lambda i: (0, 0, lanes // TILE - 1)), some, some,
        ],
        out_specs=(
            pl.BlockSpec((m, width), lambda i: (0, i)), pl.BlockSpec((m, width), lambda i: (i, 0)),
            part, part, part, part, once(experts, rows), once(1, rows), once(1, rows), once(table_rows, heads),
            some, some,
        ),
        compiler_params=pltpu.CompilerParams(vmem_limit_bytes=vmem_cap),
        cost_estimate=pl.CostEstimate(flops=0, bytes_accessed=12_000_000, transcendentals=0),
        name="finish",
    )(kx, lx, ky, ly, ka, la, ka, la, kb, lb, early, late, late, grad_tokens, mixed)


def local(
    tokens,
    routes,
    slot_ids,
    w_query,
    w_key,
    w_value,
    w_output,
    w_router,
    norm_attn,
    norm_moe,
    rel_table,
    w_in,
    w_out,
    cotangent,
):
    shard_count = lax.axis_size("shard")
    token_rows, model_width = tokens.shape
    prompt_len = PR_DEV * shard_count
    weight_rows, expert_count = w_router.shape
    table_rows, head_count = rel_table.shape
    capacity = 2 * token_rows // expert_count
    slot_count = expert_count * capacity

    small = jnp.concatenate(
        [w_router, norm_attn[:, None], norm_moe[:, None],
         jnp.pad(rel_table, ((0, weight_rows - table_rows), (0, 0)))], axis=1
    )
    small = jnp.pad(small, ((0, 0), (0, TILE - small.shape[1])))
    dispatch = routes * capacity + slot_ids

    ints = jnp.concatenate([routes[None], dispatch[None], jnp.zeros((6, token_rows), jnp.int32)])
    bucket_row = jnp.asarray(np.tile(distance_buckets(table_rows * shard_count), (8, 1)), jnp.int32)
    (
        lse, rev, gate, col_slots, gains, slots_out, grad_in, weights, every_tok, small, normed, queries, keys, values,
        attended, mid,
    ) = front(ints, bucket_row, cotangent, (w_query, w_key, w_value, w_output), tokens, small, slot_count)
    by_chip = (shard_count // 2, 2, capacity, model_width)
    grad_back, result, grads, rx, ry, router_grads = moe(
        slots_out.reshape(by_chip), grad_in.reshape(by_chip), small, w_in[0], w_out[0]
    )
    early_part, kx, ky, dense, prompt_part, near_part, grad_own, grad_resid, ra, rb, returned, lx, ly = back(
        grad_back.reshape(slot_count, model_width), col_slots, mid, cotangent, gains, every_tok, weights,
        (normed, queries, keys, values, attended, lse, rev), bucket_row, router_grads, grads, rx, ry, result,
    )
    chips = shard_count // 2
    lines = weight_rows // QUARTERS
    grad_tokens, mixed, early, late, ka, la, kb, lb = reduce_all(
        gains, col_slots, dense.reshape(chips, 2, QUARTERS, lines, -1),
        prompt_part.reshape(chips, 2, PR_DEV, model_width), near_part, grad_own, grad_resid, tokens, mid, gate,
        result, returned, grads, ra, rb,
        early_part.reshape(QUARTERS, lines, -1),
    )
    in_grad, out_grad, gq, gk, gv, go, router, gain_attn, gain_moe, table, grad_tokens, mixed = finish(
        kx, lx, ky, ly, ka, la, kb, lb, early, late, grad_tokens, mixed, expert_count, table_rows, head_count
    )
    return (
        mixed,
        grad_tokens,
        *(part.reshape(weight_rows, model_width) for part in (gq, gk, gv, go)),
        router.T,
        gain_attn[0],
        gain_moe[0],
        table,
        in_grad[None],
        out_grad[None],
    )


def solution(mesh):
    return jax.shard_map(
        local,
        mesh=mesh,
        in_specs=(
            P(("rep", "shard"), None),
            P(("rep", "shard")),
            P(("rep", "shard")),
            P("shard", None),
            P("shard", None),
            P("shard", None),
            P("shard", None),
            P("shard", None),
            P("shard"),
            P("shard"),
            P("shard", None),
            P("shard", None, None),
            P("shard", None, None),
            P(("rep", "shard"), None),
        ),
        out_specs=(
            P(("rep", "shard"), None),
            P(("rep", "shard"), None),
            P("shard", None),
            P("shard", None),
            P("shard", None),
            P("shard", None),
            P("shard", None),
            P("shard"),
            P("shard"),
            P("shard", None),
            P("shard", "rep", None),
            P("shard", "rep", None),
        ),
        check_vma=False,
    )
```

```python
import jax
import jax.numpy as jnp
import numpy as np
from jax import lax
from jax.experimental import pallas as pl
from jax.experimental.pallas import tpu as pltpu
from jax.sharding import PartitionSpec as P

PR_DEV = 128
TILE = 128
SPAN = 2 * TILE
NEAR = 3
QUARTERS = 4
far_before, far_after, causal_tile, hidden_tile, tile_kinds = 3, 4, 5, 6, 7
vmem_cap = 60 * 1024 * 1024
mesh_ids = pl.DeviceIdType.MESH
bucket_edges = (12, 16, 23, 32, 46, 64, 91)
norm_epsilon = 1e-06
masked_score = -1e30
low, single = jnp.bfloat16, jnp.float32
in_vmem = pl.BlockSpec(memory_space=pltpu.VMEM)
anywhere = pl.BlockSpec(memory_space=pl.ANY)


def inverse_rms(values):
    return lax.rsqrt(jnp.mean(values * values, axis=-1, keepdims=True) + norm_epsilon)


def norm_pull(grad, values, gain):
    scale = inverse_rms(values)
    pulled = grad * gain
    mean = jnp.mean(pulled * values, axis=-1, keepdims=True)
    return scale * pulled - values * (scale * scale * scale * mean)


def nt(left, right):
    return lax.dot_general(left, right, (((1,), (1,)), ((), ())), preferred_element_type=single)


def tn(left, right):
    return lax.dot_general(left, right, (((0,), (0,)), ((), ())), preferred_element_type=single)


def nn(left, right):
    return jnp.dot(left, right, preferred_element_type=single)


def thirds_of(values):
    first = values.astype(low)
    rest = values - first.astype(single)
    second = rest.astype(low)
    return first, second, (rest - second.astype(single)).astype(low)


def fill_tiles(tiles_ref, rev_row, low, high):
    spread = jnp.broadcast_to(rev_row, (TILE, 4 * TILE))
    rolled = pltpu.roll(spread, 0, 1, stride=1, stride_axis=0)
    keys = lax.broadcasted_iota(jnp.int32, (TILE, TILE), 0)
    rows = lax.broadcasted_iota(jnp.int32, (TILE, TILE), 1)
    tiles_ref[0] = rolled[:, TILE : 2 * TILE]
    tiles_ref[1] = rolled[:, :TILE]
    tiles_ref[2] = rolled[:, 3 * TILE :]
    tiles_ref[far_before] = jnp.broadcast_to(low, (TILE, TILE))
    tiles_ref[far_after] = jnp.broadcast_to(high, (TILE, TILE))
    tiles_ref[causal_tile] = jnp.where(keys <= rows, rolled[:, :TILE], masked_score)
    tiles_ref[hidden_tile] = jnp.full((TILE, TILE), masked_score, jnp.float32)


def prompt_tile(block, chunk, shard_id, block_count):
    if chunk == 0:
        gap = block - shard_id
        far = jnp.where(gap < 0, far_before, far_after)
        return jnp.where(jnp.abs(gap) <= 1, gap + 1, far)
    if chunk == 1 and block == block_count - 1:
        return jnp.where(shard_id % 2 == 0, 0, far_before)
    return far_before


def local_tile(block, chunk, shard_id):
    if block >= 2:
        return ((causal_tile, 0), (hidden_tile, causal_tile))[block - 2][chunk]
    kind = 0 if (block, chunk) == (1, 0) else far_before
    return jnp.where(shard_id % 2 == 1, kind, hidden_tile)


def prompt_grid(part, shard_id, block_count):
    return [
        [(side, prompt_tile(2 * part + half, chunk, shard_id, block_count)) for side in range(2) for chunk in range(3)]
        for half in range(2)
    ]


def local_grid(part, shard_id):
    return [
        [(side, local_tile(2 * part + half, chunk, shard_id)) for side in range(2) for chunk in range(2)]
        for half in range(2)
    ]


def tile_of(values, i, j):
    return values[i * TILE : (i + 1) * TILE, j * TILE : (j + 1) * TILE]


def with_bias(scores, tiles_ref, grid):
    lines = [
        jnp.concatenate(
            [tile_of(scores, i, j) + tiles_ref[side, kind] for j, (side, kind) in enumerate(row)], axis=1
        )
        for i, row in enumerate(grid)
    ]
    return jnp.concatenate(lines, axis=0)


def both_heads(values):
    first = head_mask(values.shape[0], 0)
    none = jnp.zeros_like(values)
    return jnp.concatenate([jnp.where(first, values, none), jnp.where(first, none, values)], axis=0)


def continuation(values, axis):
    rows = values.shape[axis] // 2
    pick = (lambda a, b: values[:, a:b]) if axis else (lambda a, b: values[a:b])
    return jnp.concatenate([pick(PR_DEV, rows), pick(rows + PR_DEV, 2 * rows)], axis=axis)


def fold8(values):
    return values.reshape(values.shape[0] // 8, 8, values.shape[1])


def head_mask(rows, side):
    lanes = lax.broadcasted_iota(jnp.int32, (rows, TILE), 1)
    return (lanes < TILE // 2) if side == 0 else (lanes >= TILE // 2)


def distance_buckets(bucket_count):
    steps = np.arange(4 * TILE)
    gap = -np.where(steps < 2 * TILE, steps, steps - 4 * TILE)
    size = np.abs(gap)
    far = sum((size >= edge).astype(np.int64) for edge in bucket_edges)
    exact = bucket_count // 4
    return np.where(gap > 0, bucket_count // 2, 0) + np.where(size < exact, size, exact + far)


def front_kernel(
    ints_ref, bucket_ref, cot_ref, little_ref, wq_hbm, wk_hbm, wv_hbm, wo_hbm, tok_hbm,
    lse_ref, rev_ref, gate_ref, col_ref, gain_ref, x_ref, gin_hbm, w_hbm, every_hbm, small_hbm,
    n_hbm, q_hbm, k_hbm, v_hbm, o_hbm, mid_hbm,
    tiles, vt, sp, sl, gbuf, w_ref, every_ref, small_ref, tok_ref, shard_w, little,
    n_ref, nt_ref, q_ref, k_ref, v_ref, ot_ref, mid_ref,
    gs, gr, loc, wz_s, wz_r, tz_s, tz_r, sz_s, sz_r, wr_s, wr_r, wt_s, wt_r, tt_s, tt_r, st_s, st_r, et_s, et_r,
):
    rep, chip, core, chips, quarter = places()
    along, across, twin = peer_lists()
    shards = chips * 2
    shard_id = chip * 2 + core
    rows, width = tok_ref.shape
    experts = shards
    blocks = every_ref.shape[0] // TILE - 4
    half = TILE // 2
    heads_held = rev_ref.shape[0]
    lines = shard_w.shape[1]
    rest_rows = rows - PR_DEV
    prompt_len = blocks * TILE
    others = [(rep, (shard_id + k) % shards) for k in range(1, shards)]

    def w_rows(source, side):
        return pl.ds(pl.multiple_of((source * 2 + side) * lines, lines), lines)

    def t_rows(source, side):
        return every_ref.at[pl.ds(pl.multiple_of((source * 2 + side) * PR_DEV, PR_DEV), PR_DEV)]

    loads = [
        pltpu.make_async_copy(source, shard_w.at[i], loc.at[i])
        for i, source in enumerate((wq_hbm, wk_hbm, wv_hbm, wo_hbm))
    ] + [pltpu.make_async_copy(tok_hbm, tok_ref, loc.at[4])]
    for copy in loads:
        copy.start()
    little[...] = little_ref[...].astype(single).T[:lines].astype(low)
    greeted = [twin] + along
    for device in across + [(rep, (chip + k) % chips * 2 + 1 - core) for k in range(1, chips)]:
        greeted.append(device)
    greet(greeted)
    started = []

    def go(source, target, sems, device):
        copy = send(source, target, sems, device)
        copy.start()
        started.append(copy)

    def landed(piece, sems):
        send(piece, piece, sems, twin).wait_recv()

    for copy in loads:
        copy.wait()
    mine = w_rows(chip, core)
    prompt, rest = tok_ref.at[pl.ds(0, PR_DEV)], tok_ref.at[pl.ds(PR_DEV, rest_rows)]
    for k, device in enumerate(along):
        go(shard_w.at[quarter], w_ref.at[quarter, mine], (wz_s.at[k], wz_r.at[k]), device)
        go(little, small_ref.at[mine], (sz_s.at[k], sz_r.at[k]), device)
    go(little, small_ref.at[mine], (st_s.at[0], st_r.at[0]), twin)
    go(rest, every_ref.at[pl.ds(prompt_len, rest_rows)], (et_s.at[0], et_r.at[0]), twin)
    go(prompt, t_rows(chip, core), (tt_s.at[0], tt_r.at[0]), twin)
    go(shard_w, w_ref.at[:, mine], (wt_s.at[0], wt_r.at[0]), twin)
    w_ref[:, mine, :] = shard_w[...]
    small_ref[mine, :] = little[...]
    every_ref[pl.ds(pl.multiple_of(shard_id * PR_DEV, PR_DEV), PR_DEV), :] = tok_ref[:PR_DEV, :]
    every_ref[prompt_len + rest_rows :, :] = tok_ref[PR_DEV:, :]
    dispatch = ints_ref[0:1, :] * (x_ref.shape[0] // experts) + ints_ref[1:2, :]
    ints = jnp.concatenate([ints_ref[0:1, :], dispatch, jnp.zeros((6, rows), jnp.int32)], axis=0).astype(single).T
    route_col = ints[:, 0:1].astype(jnp.int32)
    col_ref[...] = jnp.broadcast_to(ints[:, 1:2].astype(jnp.int32), col_ref.shape)
    slots = lax.broadcasted_iota(jnp.int32, (x_ref.shape[0], rows), 0)
    place = (slots == dispatch).astype(low)
    gbuf[...] = nn(place, cot_ref[...]).astype(low).reshape(gbuf.shape)
    own_g = pltpu.make_async_copy(gbuf.at[shard_id], gin_hbm.at[shard_id], loc.at[6])
    own_g.start()

    for k in range(1, chips):
        source = (chip + chips - k) % chips
        piece = w_ref.at[quarter, w_rows(source, core)]
        landed(piece, (wz_s.at[k - 1], wz_r.at[k - 1]))
        for j, device in enumerate(across):
            go(piece, piece, (wr_s.at[k - 1, j], wr_r.at[k - 1, j]), device)
        go(prompt, t_rows(chip, core), (tz_s.at[k - 1], tz_r.at[k - 1]), along[k - 1])
    for k in range(1, chips):
        source = (chip + chips - k) % chips
        piece = small_ref.at[w_rows(source, core)]
        landed(piece, (sz_s.at[k - 1], sz_r.at[k - 1]))
        go(piece, piece, (st_s.at[k], st_r.at[k]), twin)
    for k in range(1, chips):
        source = (chip + chips - k) % chips
        piece = t_rows(source, core)
        landed(piece, (tz_s.at[k - 1], tz_r.at[k - 1]))
        go(piece, piece, (tt_s.at[k], tt_r.at[k]), twin)
    for k, device in enumerate(others):
        go(gbuf.at[device[1]], gin_hbm.at[shard_id], (gs.at[k], gr.at[k]), device)
    for k in range(chips):
        source = (chip + chips - k) % chips
        landed(small_ref.at[w_rows(source, 1 - core)], (st_s.at[k], st_r.at[k]))
    writes = []

    def write(source, target):
        writes.append(pltpu.make_async_copy(source, target, loc.at[7 + len(writes)]))
        writes[-1].start()

    write(small_ref, small_hbm)

    small_t = small_ref[...].astype(single).T
    gain_attn = small_t[experts : experts + 1]
    gain_moe = small_t[experts + 1 : experts + 2]
    gain_ref[...] = jnp.concatenate([gain_attn, gain_moe, jnp.zeros((6, width), single)], axis=0)
    shard_rows = width // shards
    table_rows = 2 * TILE // 8 // shards
    owner = lax.broadcasted_iota(jnp.int32, (shards, shard_rows, 4 * TILE), 0)
    offset = lax.broadcasted_iota(jnp.int32, (shards, shard_rows, 4 * TILE), 1)
    held = jnp.where(offset < table_rows, owner * table_rows + offset, -1).reshape(width, 4 * TILE)
    hot = (held == bucket_ref[0:1, :]).astype(low)
    table_t = small_t[experts + 2 : experts + 2 + heads_held].astype(low)
    rev_ref[...] = nn(table_t, hot)

    for k in range(chips):
        source = (chip + chips - k) % chips
        landed(t_rows(source, 1 - core), (tt_s.at[k], tt_r.at[k]))
    landed(every_ref.at[pl.ds(prompt_len, rest_rows)], (et_s.at[0], et_r.at[0]))
    write(every_ref, every_hbm)

    @pl.loop(0, every_ref.shape[0] // SPAN)
    def scale(part):
        span = pl.ds(pl.multiple_of(part * SPAN, SPAN), SPAN)
        values = every_ref[span, :].astype(single)
        normed = values * inverse_rms(values) * gain_attn
        n_ref[span, :] = normed.astype(low)
        nt_ref[:, span] = normed.T.astype(low)

    write(nt_ref, n_hbm)
    for k in range(1, chips):
        source = (chip + chips - k) % chips
        for j in range(1, QUARTERS):
            piece = w_ref.at[(quarter + QUARTERS - j) % QUARTERS, w_rows(source, core)]
            landed(piece, (wr_s.at[k - 1, j - 1], wr_r.at[k - 1, j - 1]))
        piece = w_ref.at[:, w_rows(source, core)]
        go(piece, piece, (wt_s.at[k], wt_r.at[k]), twin)
    for k in range(chips):
        source = (chip + chips - k) % chips
        landed(w_ref.at[:, w_rows(source, 1 - core)], (wt_s.at[k], wt_r.at[k]))
    write(w_ref, w_hbm)

    @pl.loop(0, every_ref.shape[0] // (2 * SPAN))
    def project(part):
        span = pl.ds(pl.multiple_of(part * 2 * SPAN, 2 * SPAN), 2 * SPAN)
        k_ref[span, :] = nn(n_ref[span, :], w_ref[1]).astype(low)
        v_ref[span, :] = nn(n_ref[span, :], w_ref[2]).astype(low)

    own = pl.ds(pl.multiple_of(shard_id * TILE, TILE), TILE)
    normed = jnp.concatenate([n_ref[own, :], n_ref[(blocks + 2) * TILE :, :]], axis=0)
    q_ref[...] = (nn(normed, w_ref[0]).astype(low) * jnp.asarray(0.125, low)).astype(low)
    write(k_ref, k_hbm)
    write(v_ref, v_hbm)
    write(q_ref, q_hbm)

    @pl.loop(0, width // TILE)
    def pair_loop(pair):
        cols = pl.ds(pl.multiple_of(pair * TILE, TILE), TILE)
        vt[...] = v_ref[:, cols].T
        q_both = both_heads(q_ref[:, cols])
        q_local = continuation(q_both, 0)
        for side in range(2):
            rev_row = rev_ref[pl.ds(pair * 2 + side, 1), :]
            fill_tiles(tiles.at[side], rev_row, rev_row[:, SPAN - 1 : SPAN], rev_row[:, SPAN : SPAN + 1])
        top = jnp.full((8, 2 * rows), masked_score, single)
        for part in range(blocks // 2):
            keys = slice(part * SPAN, (part + 1) * SPAN)
            scores = with_bias(nt(k_ref[keys, cols], q_both), tiles, prompt_grid(part, shard_id, blocks))
            sp[keys, :] = scores
            top = jnp.maximum(top, jnp.max(fold8(scores), axis=0))
        local = continuation(top, 1)
        for part in range(2):
            keys = slice(part * SPAN, (part + 1) * SPAN)
            held = slice((blocks // 2 + part) * SPAN, (blocks // 2 + part + 1) * SPAN)
            scores = with_bias(nt(k_ref[held, cols], q_local), tiles, local_grid(part, shard_id))
            sl[keys, :] = scores
            local = jnp.maximum(local, jnp.max(fold8(scores), axis=0))
        rest = rows - PR_DEV
        top = jnp.concatenate(
            [top[:, :PR_DEV], local[:, :rest], top[:, rows : rows + PR_DEV], local[:, rest:]], axis=1
        )
        top = jnp.max(top, axis=0, keepdims=True)
        total = jnp.zeros((8, 2 * rows), single)
        summed = [jnp.zeros((half, rows), single)] * 2
        for part in range(blocks // 2):
            keys = slice(part * SPAN, (part + 1) * SPAN)
            weights = jnp.exp(sp[keys, :] - top)
            total = total + jnp.sum(fold8(weights), axis=0)
            weights = weights.astype(low)
            for side in range(2):
                heads = slice(side * half, (side + 1) * half)
                summed[side] = summed[side] + nn(vt[heads, keys], weights[:, side * rows : (side + 1) * rows])
        top_local, total_local = continuation(top, 1), continuation(total, 1)
        summed_local = [part_sum[:, PR_DEV:] for part_sum in summed]
        for part in range(2):
            keys = slice(part * SPAN, (part + 1) * SPAN)
            held = slice((blocks // 2 + part) * SPAN, (blocks // 2 + part + 1) * SPAN)
            weights = jnp.exp(sl[keys, :] - top_local)
            total_local = total_local + jnp.sum(fold8(weights), axis=0)
            weights = weights.astype(low)
            for side in range(2):
                heads = slice(side * half, (side + 1) * half)
                summed_local[side] = summed_local[side] + nn(
                    vt[heads, held], weights[:, side * rest : (side + 1) * rest]
                )
        for side in range(2):
            head = pair * 2 + side
            ours = slice(side * rows, (side + 1) * rows)
            sums = jnp.concatenate(
                [total[:, side * rows : side * rows + PR_DEV], total_local[:, side * rest : (side + 1) * rest]], axis=1
            )
            sums = jnp.sum(sums, axis=0, keepdims=True)
            mixed = jnp.concatenate([summed[side][:, :PR_DEV], summed_local[side]], axis=1)
            ot_ref[pl.ds(pl.multiple_of(head * half, half), half), :] = mixed / sums
            lse_ref[pl.ds(head, 1), :] = top[:, ours] + jnp.log(sums)

    resid_mid = tok_ref[...].astype(single) + nn(ot_ref[...].T.astype(low), w_ref[3])
    mid_ref[...] = resid_mid
    write(ot_ref, o_hbm)
    write(mid_ref, mid_hbm)
    mid_low = (resid_mid * inverse_rms(resid_mid) * gain_moe).astype(low)
    probs = router_softmax(mid_low, small_ref[...], experts)
    lanes = lax.broadcasted_iota(jnp.int32, probs.shape, 1)
    gate = jnp.sum(jnp.where(lanes == route_col, probs, 0.0), axis=1, keepdims=True)
    gate_ref[...] = jnp.broadcast_to(gate, gate_ref.shape)
    x_ref[...] = nn(place, mid_low).astype(low)
    own_g.wait()
    for k in range(shards - 1):
        landed(gin_hbm.at[(shard_id + shards - k - 1) % shards], (gs.at[k], gr.at[k]))
    for copy in writes:
        copy.wait()
    for copy in started:
        copy.wait_send()


def router_softmax(rows_low, small, experts):
    logits = nn(rows_low, small)
    lanes = lax.broadcasted_iota(jnp.int32, logits.shape, 1)
    logits = jnp.where(lanes < experts, logits, masked_score)
    powers = jnp.exp(logits - jnp.max(logits, axis=1, keepdims=True))
    return powers / jnp.sum(powers, axis=1, keepdims=True)


def front(ints, bucket_row, cotangent, weights, tokens, small, slot_count):
    rows, width = tokens.shape
    shards = lax.axis_size("shard")
    chips, count = shards // 2, shards // 2 - 1
    keys = shards * PR_DEV + 2 * (rows - PR_DEV)
    lines = width // shards
    shape = jax.ShapeDtypeStruct
    sem = pltpu.SemaphoreType.DMA
    vm = pltpu.VMEM
    return pl.pallas_call(
        front_kernel,
        out_shape=(
            shape((16, rows), single), shape((16, 4 * TILE), single), shape((rows, TILE), single),
            shape((rows, TILE), jnp.int32), shape((8, width), single), shape((slot_count, width), low),
            shape((shards, slot_count // shards, width), low), shape((4, width, width), low),
            shape((keys, width), low), shape((width, TILE), low),
            shape((width, keys), low), shape((rows, width), low), shape((keys, width), low),
            shape((keys, width), low), shape((width, rows), single), shape((rows, width), single),
        ),
        in_specs=[in_vmem] * 4 + [anywhere] * 5,
        out_specs=(in_vmem,) * 6 + (anywhere,) * 10,
        scratch_shapes=[
            vm((2, tile_kinds, TILE, TILE), single), vm((TILE, keys), low), vm((keys - 2 * SPAN, 2 * rows), single),
            vm((2 * SPAN, 2 * (rows - TILE)), single),
            vm((shards, slot_count // shards, width), low), vm((4, width, width), low), vm((keys, width), low),
            vm((width, TILE), low), vm((rows, width), low), vm((4, lines, width), low), vm((lines, TILE), low),
            vm((keys, width), low), vm((width, keys), low), vm((rows, width), low), vm((keys, width), low),
            vm((keys, width), low), vm((width, rows), single), vm((rows, width), single),
            sem((shards - 1,)), sem((shards - 1,)), sem((16,)), sem((count,)), sem((count,)), sem((count,)),
            sem((count,)), sem((count,)), sem((count,)), sem((count, 3)), sem((count, 3)), sem((chips,)), sem((chips,)),
            sem((chips,)), sem((chips,)), sem((chips,)), sem((chips,)), sem((1,)), sem((1,)),
        ],
        compiler_params=pltpu.CompilerParams(collective_id=2, has_side_effects=True, vmem_limit_bytes=vmem_cap),
        cost_estimate=pl.CostEstimate(flops=30_000_000_000, bytes_accessed=20_000_000, transcendentals=8_000_000),
        name="front",
    )(ints, bucket_row, cotangent, small, *weights, tokens)


def moe_kernel(
    small_ref, x_ref, g_hbm, w_in_ref, w_out_ref,
    back_ref, out_hbm, ge_hbm, rx_hbm, ry_hbm, rg_ref,
    w_in, w_out, xin, gm, gg, hid, gpre, logit_grads, x_t, gw_in, gw_out, g_ref, out_ref,
    xs, xr, ms, mr, ws, ls, os_in, os_out, ex_s, ex_r, ey_s, ey_r, own, os_result,
):
    rep, chip, core, chips, quarter = places()
    experts = chips * 2
    here = chip * 2 + core
    pair_rows = 2 * xin.shape[2]
    hidden = w_in_ref.shape[1]
    width = w_in_ref.shape[0]
    _, slow, fast, slows, fasts = rep_places()
    lines = gw_in.shape[3]
    beside = [(slow * fasts + (fast + j) % fasts, here) for j in range(1, fasts)]
    beyond = [((slow + j) % slows * fasts + fast, here) for j in range(1, slows)]
    loads = [
        pltpu.make_async_copy(w_in_ref, w_in, ws.at[0]),
        pltpu.make_async_copy(w_out_ref, w_out, ws.at[1]),
    ]
    held = [
        pltpu.make_async_copy(x_ref.at[chip, core], xin.at[chip, core], own.at[0]),
        pltpu.make_async_copy(g_hbm, g_ref, own.at[1]),
    ]
    for copy in held + loads:
        copy.start()
    twin = (rep, chip * 2 + 1 - core)
    targets = [
        (k, side, (rep, chip_across(chip, k) * 2 + side)) for k in range(1, chips) for side in range(2)
    ]
    greet([twin] + [device for _, _, device in targets] + beside + beyond)
    sent = [send(x_ref.at[chip, 1 - core], xin.at[chip, core], (xs.at[0, 0], xr.at[0, core]), twin)]
    for k, side, device in targets:
        sent.append(
            send(x_ref.at[chip_across(chip, k), side], xin.at[chip, core], (xs.at[k, side], xr.at[k, core]), device)
        )
    for copy in sent[:5]:
        copy.start()
    for copy in held + loads:
        copy.wait()

    def arrived(k, source, side):
        piece = xin.at[source, side]
        send(piece, piece, (xs.at[0, 0], xr.at[k, side]), twin).wait_recv()

    @pl.loop(0, chips)
    def chunk(k):
        source = chip_across(chip, k)

        @pl.when(k == 0)
        def _():
            arrived(0, chip, 1 - core)

        @pl.when(k > 0)
        def _():
            for side in range(2):
                arrived(k, source, side)

        rows = xin[source].reshape(pair_rows, xin.shape[3])
        grads = g_ref[source].reshape(pair_rows, xin.shape[3])
        probs = router_softmax(rows, small_ref[...], experts)
        lanes = lax.broadcasted_iota(jnp.int32, probs.shape, 1)
        gate = jnp.sum(jnp.where(lanes == here, probs, 0.0), axis=1, keepdims=True)
        gated = (gate * grads.astype(single)).astype(low)
        span = pl.ds(pl.multiple_of(source * pair_rows, pair_rows), pair_rows)
        gg[span, :] = gated
        pre = nn(rows, w_in[...])
        grad_hidden = nt(gated, w_out[...])
        square = pre * pre
        wave = jnp.tanh(0.7978845608028654 * pre * (1.0 + 0.044715 * square))
        left = 0.5 + 0.5 * wave
        active = (pre * left).astype(low)
        slope = left + (0.5 * pre) * (1.0 - wave * wave) * (0.7978845608028654 + 0.10703222440890037 * square)
        grad_pre = (grad_hidden * slope).astype(low)
        hid[span, :] = active
        gpre[span, :] = grad_pre
        out = nn(active, w_out[...]).astype(low)
        out_ref[source] = out.reshape(out_ref.shape[1:])
        pltpu.make_async_copy(out_ref.at[source], out_hbm.at[source], os_result.at[k]).start()
        grad_gate = jnp.sum(grads.astype(single) * out.astype(single), axis=1, keepdims=True)
        chosen = jnp.where(lanes == here, 1.0, 0.0)
        grad_logits = jnp.where(lanes < experts, gate * grad_gate * (chosen - probs), 0.0)
        logit_grads[span, :] = grad_logits
        router = small_ref[...]
        total = nt(grad_pre, w_in[...]) + sum(nt(part, router) for part in thirds_of(grad_logits))
        gm[source] = total.astype(low).reshape(gm.shape[1:])

        def reply(side, slot):
            return send(
                gm.at[source, side], back_ref.at[chip, core], (ms.at[k, slot], mr.at[k, core]), (rep, source * 2 + side)
            )

        @pl.when(k == 0)
        def _():
            for copy in sent[5:]:
                copy.start()
            reply(1 - core, 0).start()
            pltpu.make_async_copy(gm.at[chip, core], back_ref.at[chip, core], ls).start()

        @pl.when(k > 0)
        def _():
            for side in range(2):
                reply(side, side).start()

    every = xin[...].reshape(gg.shape)
    x_t[...] = every.T

    def strip_writes(part):
        rows = pl.ds(pl.multiple_of(part * lines, lines), lines)
        tail = pl.ds(4 * lines, 4 * lines)
        if gw_out.shape[1] == 1:
            second = (gw_out.at[part, 0], ge_hbm.at[part // fasts, part % fasts, tail])
        else:
            second = (gw_out.at[part], ge_hbm.at[part, :, tail])
        return [
            pltpu.make_async_copy(gw_in.at[part], ge_hbm.at[:, :, rows], os_in.at[part]),
            pltpu.make_async_copy(*second, os_out.at[part]),
        ]

    grads_out = [
        send(gw_in.at[0, :, (fast + j + 1) % fasts], rx_hbm.at[j], (ex_s.at[j], ex_r.at[j]), device)
        for j, device in enumerate(beside)
    ], [
        send(gw_in.at[1, (slow + j + 1) % slows], ry_hbm.at[j], (ey_s.at[j], ey_r.at[j]), device)
        for j, device in enumerate(beyond)
    ]

    @pl.loop(0, hidden // width)
    def strip(part):
        cols = pl.ds(pl.multiple_of(part * width, width), width)
        gw_in[part] = nn(x_t[...], gpre[:, cols]).astype(low).reshape(gw_in.shape[1:])
        strip_writes(part)[0].start()
        for turn in range(2):

            @pl.when(part == turn)
            def _():
                for copy in grads_out[turn]:
                    copy.start()

    @pl.loop(0, hidden // width)
    def second_strip(part):
        cols = pl.ds(pl.multiple_of(part * width, width), width)
        gw_out[part] = tn(hid[:, cols], gg[...]).astype(low).reshape(gw_out.shape[1:])
        strip_writes(part)[1].start()

    rg_ref[...] = sum(nn(x_t[...], part) for part in thirds_of(logit_grads[...]))
    pltpu.make_async_copy(gm.at[chip, core], back_ref.at[chip, core], ls).wait()

    def replied(k, source, side):
        piece = back_ref.at[source, side]
        send(piece, piece, (ms.at[0, 0], mr.at[k, side]), twin).wait_recv()

    replied(0, chip, 1 - core)
    for k in range(1, chips):
        for side in range(2):
            replied(k, chip_across(chip, k), side)
    for copy in sent:
        copy.wait_send()
    for part in range(hidden // width):
        for copy in strip_writes(part):
            copy.wait()
    for k in range(chips):
        source = chip_across(chip, k)
        pltpu.make_async_copy(out_ref.at[source], out_hbm.at[source], os_result.at[k]).wait()
    for copy in grads_out[0] + grads_out[1]:
        copy.wait()
    send(gm.at[chip, 0], back_ref.at[chip, core], (ms.at[0, 0], mr.at[0, 0]), twin).wait_send()
    for k in range(1, chips):
        for side in range(2):
            send(gm.at[chip, 0], back_ref.at[chip, core], (ms.at[k, side], mr.at[0, 0]), twin).wait_send()


def moe(rows_out, grad_in, small, w_in, w_out):
    chips, _, cap, width = rows_out.shape
    slots = chips * 2 * cap
    hidden = w_in.shape[1]
    shape = jax.ShapeDtypeStruct
    pairs = pltpu.SemaphoreType.DMA
    strips = hidden // width
    slows, fasts = rep_places()[3:]
    lines = width // (slows * fasts)
    return pl.pallas_call(
        moe_kernel,
        out_shape=(
            shape(rows_out.shape, low), shape(rows_out.shape, low), shape((slows, fasts, 8 * lines, width), low),
            shape((fasts - 1, slows, lines, width), low), shape((slows - 1, fasts, lines, width), low),
            shape((width, TILE), single),
        ),
        in_specs=[in_vmem] + [anywhere] * 4,
        out_specs=(anywhere,) * 5 + (in_vmem,),
        scratch_shapes=[
            pltpu.VMEM((width, hidden), low), pltpu.VMEM((hidden, width), low),
            pltpu.VMEM(rows_out.shape, low), pltpu.VMEM(rows_out.shape, low), pltpu.VMEM((slots, width), low),
            pltpu.VMEM((slots, hidden), low), pltpu.VMEM((slots, hidden), low),
            pltpu.VMEM((slots, TILE), single), pltpu.VMEM((width, slots), low),
            pltpu.VMEM((strips, slows, fasts, lines, width), low),
            pltpu.VMEM((strips, width // (4 * lines), 4 * lines, width), low),
            pltpu.VMEM(rows_out.shape, low), pltpu.VMEM(rows_out.shape, low),
            pairs((chips, 2)), pairs((chips, 2)), pairs((chips, 2)), pairs((chips, 2)), pairs((2,)), pairs,
            pairs((strips,)), pairs((strips,)), pairs((fasts - 1,)), pairs((fasts - 1,)), pairs((slows - 1,)),
            pairs((slows - 1,)), pairs((2,)), pairs((chips,)),
        ],
        compiler_params=pltpu.CompilerParams(collective_id=3, has_side_effects=True, vmem_limit_bytes=vmem_cap),
        cost_estimate=pl.CostEstimate(flops=40_000_000_000, bytes_accessed=40_000_000, transcendentals=3_000_000),
        name="moe",
    )(small, rows_out, grad_in, w_in, w_out)


def back_kernel(
    col_ref, gain_ref, lse_ref, rev_ref, bucket_ref, rg_ref, back_hbm, mid_hbm, cot_hbm, q_hbm, k_hbm, v_hbm, o_hbm,
    every_hbm, w_hbm, n_hbm, ge_hbm, rx_hbm, ry_hbm, out_hbm,
    z_ref, kx_ref, ky_ref, dense_hbm, p_hbm, e_hbm, own_hbm, gres_hbm, ra_hbm, rb_hbm, ret_hbm, lx_hbm, ly_hbm,
    tiles, sums, diag, kt, dqt, far_sums, g_ref, dq_ref, dk_ref, dv_ref, attn_gain,
    every_ref, w_ref, n_ref, back_ref, mid_ref, cot_ref, q_ref, k_ref, v_ref, o_ref,
    dense_ref, own_ref, gres_ref,
    x_own, x_in, x_sum, y_own, y_in, y_sum, o_grad, o_half, o_sum, o_in, h_grad, h_half, h_sum, h_in,
    loc, out, lx_s, lx_r, ly_s, ly_r, xs, xr, as_, ar, bs, br, os_, or_, oz_s, oz_r, hs_, hr_, hz_s, hz_r,
):
    shard_id = lax.axis_index("shard")
    shards = lax.axis_size("shard")
    rows, width = mid_ref.shape
    blocks = k_ref.shape[0] // TILE - 4
    half = TILE // 2
    experts = shards
    heads_held = rev_ref.shape[0]
    rep, slow, fast, slows, fasts = rep_places()
    _, chip, core, chips, _ = places()
    along, _, twin = peer_lists()
    lines = x_own.shape[1]
    loads = [
        pltpu.make_async_copy(source, target, loc.at[i])
        for i, (source, target) in enumerate((
            (back_hbm, back_ref), (mid_hbm, mid_ref), (cot_hbm, cot_ref), (w_hbm.at[3], w_ref.at[3]), (o_hbm, o_ref),
            (q_hbm, q_ref), (k_hbm, k_ref), (v_hbm, v_ref), (n_hbm, n_ref), (w_hbm.at[pl.ds(0, 3)], w_ref.at[pl.ds(0, 3)]),
            (every_hbm, every_ref), (out_hbm.at[chip, core], ret_hbm.at[chip, core]),
            (ge_hbm.at[:, fast, pl.ds(0, lines)], x_own), (rx_hbm, x_in),
            (ge_hbm.at[slow, :, pl.ds(lines, lines)], y_own), (ry_hbm, y_in),
        ))
    ]
    for copy in loads:
        copy.start()
    writes = []

    def write(source, target):
        writes.append(pltpu.make_async_copy(source, target, out.at[len(writes)]))
        writes[-1].start()

    beside = [(slow * fasts + (fast + j) % fasts, shard_id) for j in range(1, fasts)]
    beyond = [((slow + j) % slows * fasts + fast, shard_id) for j in range(1, slows)]
    nearby = result_peers(rep, chip, core, range(NEAR))
    far_twins = [(rep, (chip + k) % chips * 2 + 1 - core) for k in range(1, chips)]
    greet([twin] + along + far_twins + beside + beyond)
    sent = [
        send(ge_hbm.at[:, (fast + j + 1) % fasts, pl.ds(2 * lines, 3 * lines)], ra_hbm.at[j], (as_.at[j], ar.at[j]), device)
        for j, device in enumerate(beside)
    ] + [
        send(ge_hbm.at[(slow + j + 1) % slows, :, pl.ds(5 * lines, 3 * lines)], rb_hbm.at[j], (bs.at[j], br.at[j]), device)
        for j, device in enumerate(beyond)
    ] + [
        send(out_hbm.at[chip_across(chip, k), side if k else 1 - core], ret_hbm.at[chip, core], (xs.at[k, side], xr.at[k, core]), device)
        for k, side, device in nearby
    ]
    for copy in sent:
        copy.start()
    for copy in loads[12:]:
        copy.wait()
    for held, came, total in ((x_own, x_in, x_sum), (y_own, y_in, y_sum)):
        value = held[...].astype(single)
        for j in range(came.shape[0]):
            value = value + came[j].astype(single)
        total[...] = value.astype(low)
    second = [
        send(x_sum.at[(slow + j + 1) % slows], lx_hbm.at[j], (lx_s.at[j], lx_r.at[j]), device)
        for j, device in enumerate(beyond)
    ] + [
        send(y_sum.at[(fast + j + 1) % fasts], ly_hbm.at[j], (ly_s.at[j], ly_r.at[j]), device)
        for j, device in enumerate(beside)
    ]
    for copy in second:
        copy.start()
    kx_ref[...] = x_sum[slow]
    ky_ref[...] = y_sum[fast]
    diag[...] = jnp.zeros_like(diag)
    far_sums[...] = jnp.zeros_like(far_sums)
    tile_rows = lax.broadcasted_iota(jnp.int32, (TILE, TILE), 0)
    tile_cols = lax.broadcasted_iota(jnp.int32, (TILE, TILE), 1)
    flip = (tile_rows + tile_cols == TILE - 1).astype(single)

    for copy in loads[:5]:
        copy.wait()
    slots = lax.broadcasted_iota(jnp.int32, (rows, back_ref.shape[0]), 1)
    grad_mid = nn((slots == col_ref[:, 0:1]).astype(low), back_ref[...])
    resid_mid = mid_ref[...]
    grad_gain_moe = jnp.sum(grad_mid * resid_mid * inverse_rms(resid_mid), axis=0, keepdims=True)
    grad_resid = cot_ref[...].astype(single) + norm_pull(grad_mid, resid_mid, gain_ref[1:2, :])
    gres_ref[...] = grad_resid
    write(gres_ref, gres_hbm)
    grad_attn = grad_resid.astype(low)
    g_ref[...] = nt(grad_attn, w_ref[3]).astype(low)
    o_grad[...] = nn(o_ref[...].astype(low), grad_attn).reshape(o_grad.shape).astype(low)
    o_halves = [send(o_grad.at[2 * k + 1 - core], o_half.at[k], (os_.at[k], or_.at[k]), twin) for k in range(chips)]
    o_sends = [
        send(o_sum.at[(chip + k + 1) % chips], o_in.at[k], (oz_s.at[k], oz_r.at[k]), device)
        for k, device in enumerate(along)
    ]
    for copy in o_halves:
        copy.start()
    h_halves = [send(h_grad.at[2 * k + 1 - core], h_half.at[k], (hs_.at[k], hr_.at[k]), twin) for k in range(chips)]
    h_sends = [
        send(h_sum.at[(chip + k + 1) % chips], h_in.at[k], (hz_s.at[k], hz_r.at[k]), device)
        for k, device in enumerate(along)
    ]
    for copy in loads[5:12]:
        copy.wait()
    own = pl.ds(pl.multiple_of(shard_id * TILE, TILE), TILE)
    tail = slice((blocks + 2) * TILE, (blocks + 4) * TILE)
    early = width // 2

    @pl.loop(0, width // TILE)
    def pair_loop(pair):
        cols = pl.ds(pl.multiple_of(pair * TILE, TILE), TILE)
        kt[...] = k_ref[:, cols].T
        g_pair = g_ref[:, cols]
        q_both, g_both = both_heads(q_ref[:, cols]), both_heads(g_pair)
        delta_t = g_pair.astype(single).T * o_ref[cols, :]
        delta = jnp.concatenate(
            [jnp.sum(delta_t[:half], axis=0, keepdims=True), jnp.sum(delta_t[half:], axis=0, keepdims=True)], axis=1
        )
        log_total = jnp.concatenate([lse_ref[pl.ds(pair * 2, 1), :], lse_ref[pl.ds(pair * 2 + 1, 1), :]], axis=1)
        for side in range(2):
            rev_row = rev_ref[pl.ds(pair * 2 + side, 1), :]
            fill_tiles(tiles.at[side], rev_row, rev_row[:, SPAN - 1 : SPAN], rev_row[:, SPAN : SPAN + 1])
        sums[...] = jnp.zeros_like(sums)

        def block_grads(part, q_rows, g_rows, shift, scale, grid):
            keys = slice(part * SPAN, (part + 1) * SPAN)
            count = q_rows.shape[0] // 2
            scores = with_bias(nt(k_ref[keys, cols], q_rows), tiles, grid)
            weights = jnp.exp(scores - shift)
            grad_scores = weights * (nt(v_ref[keys, cols], g_rows) - scale)
            for i, row in enumerate(grid):
                for j, (side, kind) in enumerate(row):
                    sums[side, kind] += tile_of(grad_scores, i, j)
            raw = grad_scores.astype(low)
            dk_ref[keys, cols] = nn(raw, q_rows).astype(low)
            dv_ref[keys, cols] = nn(weights.astype(low), g_rows).astype(low)
            return [nn(kt[:half, keys], raw[:, :count]), nn(kt[half:, keys], raw[:, count:])]

        grads = [jnp.zeros((half, rows), single)] * 2
        for part in range(blocks // 2):
            more = block_grads(part, q_both, g_both, log_total, delta, prompt_grid(part, shard_id, blocks))
            grads = [old + new for old, new in zip(grads, more)]
        local = [old[:, PR_DEV:] for old in grads]
        held = (continuation(q_both, 0), continuation(g_both, 0), continuation(log_total, 1), continuation(delta, 1))
        for part in range(2):
            more = block_grads(blocks // 2 + part, *held, local_grid(part, shard_id))
            local = [old + new for old, new in zip(local, more)]
        for side in range(2):
            head = pair * 2 + side
            dqt[side * half : (side + 1) * half, :] = jnp.concatenate([grads[side][:, :PR_DEV], local[side]], axis=1)
            near = jnp.concatenate(
                [
                    sums[side, 1] + sums[side, causal_tile], sums[side, 0], jnp.zeros((TILE, TILE), single),
                    sums[side, 2],
                ],
                axis=1,
            )
            flipped = jnp.dot(flip, near, precision=lax.Precision.HIGHEST, preferred_element_type=single)
            rolled = pltpu.roll(flipped, 3 * TILE + 1, 1, stride=1, stride_axis=0)
            diag[pl.ds(head, 1), :] = jnp.sum(rolled, axis=0, keepdims=True)
            far_sums[pl.ds(head, 1), :] = jnp.concatenate(
                [
                    jnp.sum(sums[side, far_before], axis=0, keepdims=True),
                    jnp.sum(sums[side, far_after], axis=0, keepdims=True),
                ],
                axis=1,
            )
        dq_ref[:, cols] = (dqt[...].T * 0.125).astype(low)

        @pl.when(pair == 0)
        def _():
            for k in range(chips):
                o_halves[k].wait_recv()
                o_sum[k] = (o_grad[2 * k + core].astype(single) + o_half[k].astype(single)).astype(low)
            for copy in o_sends:
                copy.start()

        @pl.when(pair == width // SPAN - 1)
        def _():
            normed = jnp.concatenate([n_ref[:, own], n_ref[:, tail]], axis=1)
            for i, (left, right) in enumerate(((normed, dq_ref), (n_ref[...], dk_ref), (n_ref[...], dv_ref))):
                part = nn(left, right[:, :early]).reshape(shards, h_grad.shape[1], early)
                h_grad[:, :, i * early : (i + 1) * early] = part.astype(low)
            for copy in h_halves:
                copy.start()

        @pl.when(pair == width // SPAN)
        def _():
            for k in range(chips):
                h_halves[k].wait_recv()
                h_sum[k] = (h_grad[2 * k + core].astype(single) + h_half[k].astype(single)).astype(low)
            for copy in h_sends:
                copy.start()

    lanes = lax.broadcasted_iota(jnp.int32, (heads_held, 4 * TILE), 1)
    before = jnp.sum(far_sums[:, :TILE], axis=1, keepdims=True)
    after = jnp.sum(far_sums[:, TILE:], axis=1, keepdims=True)
    by_gap = diag[...] + jnp.where(lanes == SPAN - 1, before, 0.0) + jnp.where(lanes == SPAN, after, 0.0)
    shard_rows = width // shards
    table_rows = 2 * TILE // 8 // shards
    owner = lax.broadcasted_iota(jnp.int32, (shards, shard_rows, 4 * TILE), 0)
    offset = lax.broadcasted_iota(jnp.int32, (shards, shard_rows, 4 * TILE), 1)
    held = jnp.where(offset < table_rows, owner * table_rows + offset, -1).reshape(width, 4 * TILE)
    hot = (held == bucket_ref[0:1, :]).astype(low)
    grad_table = sum(nt(part, hot) for part in thirds_of(by_gap))

    attn_gain[...] = jnp.zeros_like(attn_gain)
    normed = jnp.concatenate([n_ref[:, own], n_ref[:, tail]], axis=1)
    dense_ref[:, :early] = nn(normed, dq_ref[:, early:]).astype(low)
    grad_own = nt(dq_ref[...], w_ref[0])
    values = jnp.concatenate([every_ref[own, :], every_ref[tail, :]], axis=0).astype(single)
    attn_gain[...] += jnp.sum(fold8(grad_own * (values * inverse_rms(values))), axis=0)
    own_ref[...] = grad_own

    def pull_rows(part):
        span = pl.ds(pl.multiple_of(part * SPAN, SPAN), SPAN)
        values = every_ref[span, :].astype(single)
        grads = nt(dk_ref[span, :], w_ref[1]) + nt(dv_ref[span, :], w_ref[2])
        attn_gain[...] += jnp.sum(fold8(grads * (values * inverse_rms(values))), axis=0)
        return grads

    @pl.loop(0, blocks // 2)
    def pull_prompt(part):
        k_ref[pl.ds(pl.multiple_of(part * SPAN, SPAN), SPAN), :] = pull_rows(part).astype(low)

    write(k_ref.at[pl.ds(0, blocks * TILE)], p_hbm)
    k_ref[blocks * TILE : (blocks + 2) * TILE, :] = pull_rows(blocks // 2).astype(low)
    write(k_ref.at[pl.ds(blocks * TILE, SPAN)], e_hbm)
    own_ref[PR_DEV:, :] += pull_rows(blocks // 2 + 1)
    write(own_ref, own_hbm)

    dense_ref[:, early : 2 * early] = nn(n_ref[...], dk_ref[:, early:]).astype(low)
    dense_ref[:, 2 * early : 3 * early] = nn(n_ref[...], dv_ref[:, early:]).astype(low)

    small_t = jnp.concatenate(
        [
            jnp.zeros((experts, width), single), jnp.sum(attn_gain[...], axis=0, keepdims=True), grad_gain_moe,
            grad_table, jnp.zeros((TILE - experts - 2 - heads_held, width), single),
        ],
        axis=0,
    )
    dense_ref[:, 3 * early :] = (small_t.T + rg_ref[...]).astype(low)
    write(dense_ref, dense_hbm)
    o_total = o_sum[chip].astype(single)
    for k in range(chips - 1):
        o_sends[k].wait_recv()
        o_total = o_total + o_in[k].astype(single)
    z_ref[:, :width] = o_total.astype(low)
    h_total = h_sum[chip].astype(single)
    for k in range(chips - 1):
        h_sends[k].wait_recv()
        h_total = h_total + h_in[k].astype(single)
    z_ref[:, width:] = h_total.astype(low)
    for copy in o_halves + o_sends + h_halves + h_sends:
        copy.wait_send()
    for copy in writes:
        copy.wait()
    for k, side in result_slots(core, range(NEAR)):
        piece = ret_hbm.at[chip_across(chip, k), side]
        send(piece, piece, (xs.at[0, 0], xr.at[k, side]), twin).wait_recv()
    for j in range(fasts - 1):
        send(ra_hbm.at[j], ra_hbm.at[j], (as_.at[j], ar.at[j]), twin).wait_recv()
    for j in range(slows - 1):
        send(rb_hbm.at[j], rb_hbm.at[j], (bs.at[j], br.at[j]), twin).wait_recv()
    for copy in second:
        copy.wait()
    for copy in sent:
        copy.wait_send()


def back(
    returned, col_slots, mid, cotangent, gains, every_tok, weights, kept, bucket_row, router_grads, grads, rx, ry, result
):
    rows, width = mid.shape
    normed, queries, keys, values, attended, lse, rev = kept
    count = keys.shape[0]
    shards = lax.axis_size("shard")
    slows, fasts, eighths = grads.shape[:3]
    m = eighths // 8
    chips, lines, early = shards // 2, width // shards, width // 2
    vm = pltpu.VMEM
    shape = jax.ShapeDtypeStruct
    pairs = pltpu.SemaphoreType.DMA
    args = (
        col_slots, gains, lse, rev, bucket_row, router_grads, returned, mid, cotangent, queries, keys, values, attended,
        every_tok, weights, normed, grads, rx, ry, result,
    )
    return pl.pallas_call(
        back_kernel,
        out_shape=(
            shape((lines, width + 3 * early), low), shape((m, width), low), shape((m, width), low),
            shape((width, 3 * early + TILE), low),
            shape((count - 2 * SPAN, width), low), shape((SPAN, width), low),
            shape((rows, width), single), shape((rows, width), single),
            shape((fasts - 1, slows, 3 * m, width), low), shape((slows - 1, fasts, 3 * m, width), low),
            shape(result.shape, low), shape((slows - 1, m, width), low), shape((fasts - 1, m, width), low),
        ),
        in_specs=[in_vmem] * 6 + [anywhere] * 14,
        out_specs=(in_vmem,) * 3 + (anywhere,) * 10,
        scratch_shapes=[
            pltpu.VMEM((2, tile_kinds, TILE, TILE), single), pltpu.VMEM((2, tile_kinds, TILE, TILE), single),
            pltpu.VMEM((16, 4 * TILE), single), pltpu.VMEM((TILE, count), low), pltpu.VMEM((TILE, rows), single),
            pltpu.VMEM((16, 2 * TILE), single),
            pltpu.VMEM((rows, width), low), pltpu.VMEM((rows, width), low), pltpu.VMEM((count, width), low),
            pltpu.VMEM((count, width), low), pltpu.VMEM((8, width), single),
            pltpu.VMEM(every_tok.shape, low), pltpu.VMEM(weights.shape, low), pltpu.VMEM(normed.shape, low),
            vm(returned.shape, low), vm((rows, width), single), vm((rows, width), low), vm((rows, width), low),
            vm(keys.shape, low), vm(keys.shape, low), vm(attended.shape, single),
            vm((width, 3 * early + TILE), low),
            vm((rows, width), single), vm((rows, width), single),
            vm((slows, m, width), low), vm((fasts - 1, slows, m, width), low), vm((slows, m, width), low),
            vm((fasts, m, width), low), vm((slows - 1, fasts, m, width), low), vm((fasts, m, width), low),
            vm((shards, lines, width), low), vm((chips, lines, width), low),
            vm((chips, lines, width), low), vm((chips - 1, lines, width), low),
            vm((shards, lines, 3 * early), low), vm((chips, lines, 3 * early), low),
            vm((chips, lines, 3 * early), low), vm((chips - 1, lines, 3 * early), low),
            pairs((16,)), pairs((6,)), pairs((slows - 1,)), pairs((slows - 1,)), pairs((fasts - 1,)), pairs((fasts - 1,)),
            pairs((NEAR, 2)), pairs((NEAR, 2)), pairs((fasts - 1,)), pairs((fasts - 1,)),
            pairs((slows - 1,)), pairs((slows - 1,)), pairs((chips,)), pairs((chips,)), pairs((chips - 1,)),
            pairs((chips - 1,)), pairs((chips,)), pairs((chips,)), pairs((chips - 1,)), pairs((chips - 1,)),
        ],
        compiler_params=pltpu.CompilerParams(collective_id=4, has_side_effects=True, vmem_limit_bytes=vmem_cap),
        cost_estimate=pl.CostEstimate(flops=60_000_000_000, bytes_accessed=40_000_000, transcendentals=8_000_000),
        name="back",
    )(*args)


def places():
    rep, shard = lax.axis_index("rep"), lax.axis_index("shard")
    return rep, shard // 2, shard % 2, lax.axis_size("shard") // 2, rep % QUARTERS


def peer_lists():
    rep, chip, core, chips, quarter = places()
    along = [(rep, (chip + k) % chips * 2 + core) for k in range(1, chips)]
    across = [(rep - quarter + (quarter + j) % QUARTERS, chip * 2 + core) for j in range(1, QUARTERS)]
    twin = (rep, chip * 2 + 1 - core)
    return along, across, twin


def chip_across(chip, k):
    partner, bit = 0, 1
    while bit < lax.axis_size("shard") // 2:
        partner = partner + bit * ((chip // bit + k // bit) % 2)
        bit = bit * 2
    return partner


def result_peers(rep, chip, core, chosen):
    return [
        (k, side, (rep, chip_across(chip, k) * 2 + (side if k else 1 - core)))
        for k in chosen for side in range(2 if k else 1)
    ]


def result_slots(core, chosen):
    return [(k, side if k else 1 - core) for k in chosen for side in range(2 if k else 1)]


def greet(devices):
    barrier = pltpu.get_barrier_semaphore()
    for device in devices:
        pl.semaphore_signal(barrier, inc=1, device_id=device, device_id_type=mesh_ids)
    pl.semaphore_wait(barrier, len(devices))


def send(source, target, sems, device):
    return pltpu.make_async_remote_copy(
        src_ref=source, dst_ref=target, send_sem=sems[0], recv_sem=sems[1],
        device_id=device, device_id_type=mesh_ids,
    )


def rep_places():
    rep, reps = lax.axis_index("rep"), lax.axis_size("rep")
    fasts = QUARTERS if reps % (QUARTERS * QUARTERS) == 0 else 2
    return rep, rep // fasts, rep % fasts, reps // fasts, fasts


def reduce_kernel(
    gain_ref, col_ref, d_hbm, p_hbm, e_hbm, own_hbm, gres_hbm, tok_hbm, mid_hbm, gate_hbm, out_hbm, ret_hbm,
    ge_hbm, ra_hbm, rb_hbm, z_hbm,
    early_ref, late_ref, gt_hbm, mix_hbm, ka_hbm, la_hbm, kb_hbm, lb_hbm,
    d_own, half, hr, tr, mr, cr, zs, tz, z_last, z_above, z_all, last, above_in, gathered,
    p_own, p_half, p_sum, p_in, e_in, own, gres, tok, mid, gate, ret,
    a_own, a_in, a_sum, b_own, b_in, b_sum, gt_ref, mix_ref, out,
    loc, ps_s, ps_r, ds_s, ds_r, pz_s, pz_r, rr_s, rr_r, rz_s, rz_r, zr_s, zr_r, zh_s, zh_r, za_s, za_r,
    dh_s, dh_r, da_s, da_r, ea_s, ea_r, eb_s, eb_r, xs, xr,
):
    rep, chip, core, chips, quarter = places()
    along, across, twin = peer_lists()
    _, slow, fast, slows, fasts = rep_places()
    classes = lax.axis_size("rep") // QUARTERS
    here = chip * 2 + core
    beside = [(slow * fasts + (fast + j) % fasts, here) for j in range(1, fasts)]
    beyond = [((slow + j) % slows * fasts + fast, here) for j in range(1, slows)]
    above = [((rep // QUARTERS + k) % classes * QUARTERS + quarter, here) for k in range(1, classes)]
    wide = lambda held: held.astype(single)
    lines = ge_hbm.shape[2] // 8
    pending = []

    def load(source, target, index, sems=loc):
        copy = pltpu.make_async_copy(source, target, sems.at[index])
        copy.start()
        return copy

    def go(source, target, sems, device):
        copy = send(source, target, sems, device)
        copy.start()
        pending.append(copy)

    def landed(piece, sems):
        send(piece, piece, sems, twin).wait_recv()

    early_in = load(z_hbm, zs, 12)
    a_loads = [load(ge_hbm.at[:, fast, pl.ds(2 * lines, 3 * lines)], a_own, 0), load(ra_hbm, a_in, 1)]
    halves = [load(d_hbm.at[:, core], d_own, 5), load(p_hbm.at[:, core], p_own, 4)]
    b_loads = [load(ge_hbm.at[slow, :, pl.ds(5 * lines, 3 * lines)], b_own, 2), load(rb_hbm, b_in, 3)]
    rest = [
        load(ret_hbm.at[chip_across(chip, k)], ret.at[chip_across(chip, k)], 13 + k) for k in range(NEAR)
    ] + [
        load(mid_hbm, mid, 7), load(gate_hbm, gate, 8), load(own_hbm, own, 9),
        load(gres_hbm, gres, 10), load(tok_hbm, tok, 11),
    ]
    others = [(rep, (here + k) % (2 * chips)) for k in range(1, 2 * chips)]
    greets = list(others)
    for device in across + beside + beyond + above:
        greets.append(device)
    greet(greets)
    for k in range(chips):
        go(d_hbm.at[k, 1 - core], half.at[k], (ds_s.at[k], ds_r.at[k]), twin)
    go(p_hbm.at[:, 1 - core], p_half, (ps_s.at[0], ps_r.at[0]), twin)
    go(e_hbm, e_in, (ps_s.at[1], ps_r.at[1]), twin)
    for k, side, device in result_peers(rep, chip, core, range(NEAR, chips)):
        go(out_hbm.at[chip_across(chip, k), side], ret.at[chip, core], (xs.at[k - NEAR, side], xr.at[k - NEAR, core]), device)
    early_in.wait()
    for j, device in enumerate(across):
        go(zs.at[(quarter + j + 1) % QUARTERS], tz.at[j], (zr_s.at[j], zr_r.at[j]), device)

    for copy in a_loads:
        copy.wait()
    for t in range(slows):
        total = wide(a_own[t])
        for j in range(fasts - 1):
            total = total + wide(a_in[j, t])
        a_sum[t] = total.astype(low)
    for copy in halves:
        copy.wait()
    for k in range(chips):
        landed(half.at[k], (ds_s.at[k], ds_r.at[k]))
        for t in range(QUARTERS):
            hr[t, k] = (wide(d_own[k, t]) + wide(half[k, t])).astype(low)
    for j, device in enumerate(across):
        go(hr.at[(quarter + j + 1) % QUARTERS], tr.at[j], (rr_s.at[j], rr_r.at[j]), device)
    landed(p_half, (ps_s.at[0], ps_r.at[0]))
    for k in range(chips):
        p_sum[k] = (wide(p_own[k]) + wide(p_half[k])).astype(low)
    for k, device in enumerate(along):
        go(p_sum.at[(chip + k + 1) % chips], p_in.at[k], (pz_s.at[k], pz_r.at[k]), device)
    for copy in b_loads:
        copy.wait()
    for t in range(fasts):
        total = wide(b_own[t])
        for j in range(slows - 1):
            total = total + wide(b_in[j, t])
        b_sum[t] = total.astype(low)
    def class_sum(held, came, s_sems, r_sems):
        total = wide(held[...])
        for j, device in enumerate(above):
            go(held, came.at[j], (s_sems.at[j], r_sems.at[j]), device)
        for j in range(classes - 1):
            landed(came.at[j], (s_sems.at[j], r_sems.at[j]))
            total = total + wide(came[j])
        return total.astype(low)

    def hand_out(pieces, s_sems, r_sems):
        for j, device in enumerate(across):
            go(pieces.at[quarter], pieces.at[quarter], (s_sems.at[j], r_sems.at[j]), device)

    def handed(pieces, s_sems, r_sems):
        for j in range(QUARTERS - 1):
            landed(pieces.at[(quarter + QUARTERS - j - 1) % QUARTERS], (s_sems.at[j], r_sems.at[j]))

    for j in range(QUARTERS - 1):
        landed(tz.at[j], (zr_s.at[j], zr_r.at[j]))
    total = wide(zs[quarter])
    for j in range(QUARTERS - 1):
        total = total + wide(tz[j])
    z_last[...] = total.astype(low)
    z_all[quarter] = class_sum(z_last, z_above, zh_s, zh_r) if classes > 1 else z_last[...]
    hand_out(z_all, za_s, za_r)

    for copy in rest:
        copy.wait()
    writes = [load(a_sum.at[slow], ka_hbm, 0, out), load(b_sum.at[fast], kb_hbm, 1, out)]

    for j in range(QUARTERS - 1):
        landed(tr.at[j], (rr_s.at[j], rr_r.at[j]))
    for j, device in enumerate(beyond):
        go(a_sum.at[(slow + j + 1) % slows], la_hbm.at[j], (ea_s.at[j], ea_r.at[j]), device)
    for j, device in enumerate(beside):
        go(b_sum.at[(fast + j + 1) % fasts], lb_hbm.at[j], (eb_s.at[j], eb_r.at[j]), device)

    for k in range(chips):
        total = wide(hr[quarter, k])
        for j in range(QUARTERS - 1):
            total = total + wide(tr[j, k])
        mr[k] = total.astype(low)
    for k, device in enumerate(along):
        go(mr.at[(chip + k + 1) % chips], cr.at[k], (rz_s.at[k], rz_r.at[k]), device)

    for k in range(chips - 1):
        landed(p_in.at[k], (pz_s.at[k], pz_r.at[k]))
    landed(e_in, (ps_s.at[1], ps_r.at[1]))
    total = wide(p_sum[chip])
    for k in range(chips - 1):
        total = total + wide(p_in[k])
    grads = own[...] + jnp.concatenate([total, wide(e_in[...])], axis=0)
    gt_ref[...] = gres[...] + norm_pull(grads, wide(tok[...]), gain_ref[0:1, :])
    writes.append(load(gt_ref, gt_hbm, 2, out))

    for k in range(chips - 1):
        landed(cr.at[k], (rz_s.at[k], rz_r.at[k]))
    total = wide(mr[chip])
    for k in range(chips - 1):
        total = total + wide(cr[k])
    last[...] = total.astype(low)
    gathered[quarter] = class_sum(last, above_in, dh_s, dh_r) if classes > 1 else last[...]
    hand_out(gathered, da_s, da_r)
    for k, side in result_slots(core, range(NEAR, chips)):
        landed(ret.at[chip_across(chip, k), side], (xs.at[k - NEAR, side], xr.at[k - NEAR, side]))
    slots = lax.broadcasted_iota(jnp.int32, (tok.shape[0], 2 * chips * ret.shape[2]), 1)
    chosen = nn((slots == col_ref[:, 0:1]).astype(low), ret[...].reshape(slots.shape[1], tok.shape[1]))
    mix_ref[...] = (mid[...] + gate[:, 0:1] * chosen).astype(low)
    writes.append(load(mix_ref, mix_hbm, 3, out))
    handed(z_all, za_s, za_r)
    early_ref[...] = z_all[...]
    handed(gathered, da_s, da_r)
    late_ref[...] = gathered[...]
    for j in range(slows - 1):
        landed(la_hbm.at[j], (ea_s.at[j], ea_r.at[j]))
    for j in range(fasts - 1):
        landed(lb_hbm.at[j], (eb_s.at[j], eb_r.at[j]))
    for copy in writes:
        copy.wait()
    for copy in pending:
        copy.wait_send()


def reduce_all(gains, col_slots, dense, prompt_part, near_part, own, gres, tokens, mid, gate, result, returned, grads, ra, rb, z):
    chips = lax.axis_size("shard") // 2
    classes = lax.axis_size("rep") // QUARTERS
    slows, fasts, eighths = grads.shape[:3]
    part = (3 * eighths // 8, mid.shape[1])
    rows, width = mid.shape
    lines, lanes = dense.shape[3:]
    wider = z.shape[2]
    shape = jax.ShapeDtypeStruct
    sem = pltpu.SemaphoreType.DMA
    vm = pltpu.VMEM
    count, others = chips - 1, QUARTERS - 1
    ours = prompt_part.shape[2:]
    extra = max(classes - 1, 1)
    args = (gains, col_slots, dense, prompt_part, near_part, own, gres, tokens, mid, gate, result, returned, grads, ra, rb, z)
    return pl.pallas_call(
        reduce_kernel,
        out_shape=(
            shape((QUARTERS, lines, wider), low), shape((QUARTERS, lines, lanes), low),
            shape((rows, width), single), shape((rows, width), low),
            shape(part, low), shape((slows - 1,) + part, low), shape(part, low), shape((fasts - 1,) + part, low),
        ),
        in_specs=[in_vmem] * 2 + [anywhere] * 14,
        out_specs=(in_vmem,) * 2 + (anywhere,) * 6,
        scratch_shapes=[
            vm((chips, QUARTERS, lines, lanes), low), vm((chips, QUARTERS, lines, lanes), low),
            vm((QUARTERS, chips, lines, lanes), low), vm((others, chips, lines, lanes), low),
            vm((chips, lines, lanes), low), vm((count, lines, lanes), low),
            vm((QUARTERS, lines, wider), low), vm((others, lines, wider), low), vm((lines, wider), low),
            vm((extra, lines, wider), low), vm((QUARTERS, lines, wider), low),
            vm((lines, lanes), low), vm((extra, lines, lanes), low), vm((QUARTERS, lines, lanes), low),
            vm((chips,) + ours, low), vm((chips,) + ours, low), vm((chips,) + ours, low), vm((count,) + ours, low),
            vm(near_part.shape, low), vm((rows, width), single), vm((rows, width), single), vm((rows, width), low),
            vm((rows, width), single), vm(gate.shape, single), vm(result.shape, low),
            vm((slows,) + part, low), vm(ra.shape, low), vm((slows,) + part, low),
            vm((fasts,) + part, low), vm(rb.shape, low), vm((fasts,) + part, low),
            vm((rows, width), single), vm((rows, width), low), sem((4,)),
            sem((13 + NEAR,)), sem((2,)), sem((2,)), sem((chips,)), sem((chips,)), sem((count,)), sem((count,)),
            sem((others,)), sem((others,)), sem((count,)), sem((count,)),
            sem((others,)), sem((others,)), sem((extra,)), sem((extra,)), sem((others,)), sem((others,)),
            sem((extra,)), sem((extra,)), sem((others,)), sem((others,)),
            sem((slows - 1,)), sem((slows - 1,)), sem((fasts - 1,)), sem((fasts - 1,)),
            sem((chips - NEAR, 2)), sem((chips - NEAR, 2)),
        ],
        compiler_params=pltpu.CompilerParams(collective_id=1, has_side_effects=True, vmem_limit_bytes=vmem_cap),
        cost_estimate=pl.CostEstimate(flops=0, bytes_accessed=200_000_000, transcendentals=0),
        name="reduce_all",
    )(*args)


def finish_kernel(
    kx_ref, lx_ref, ky_ref, ly_ref, ka_ref, la_ref, kc_ref, lc_ref, kb_ref, lb_ref, early_ref, late_ref, small_ref, gt_ref, mix_ref, *outs
):
    ea_ref, eb_ref, q_ref, k_ref, v_ref, o_ref, router_ref, attn_ref, moe_ref, table_ref, gt_out, mix_out = outs
    gt_out[...] = gt_ref[...]
    mix_out[...] = mix_ref[...]
    width = q_ref.shape[2]
    experts = router_ref.shape[0]
    step = pl.program_id(0)

    def total(held, came):
        value = held[...].reshape(ea_ref.shape).astype(single)
        for j in range(came.shape[0]):
            value = value + came[j].reshape(ea_ref.shape).astype(single)
        return value

    for target, first, last, sources in (
        (ea_ref, 0, 0, (kx_ref, lx_ref)), (ea_ref, 1, 1, (ky_ref, ly_ref)), (ea_ref, 2, 3, (ka_ref, la_ref)),
        (eb_ref, 0, 0, (kc_ref, lc_ref)), (eb_ref, 1, 3, (kb_ref, lb_ref)),
    ):

        @pl.when((step >= first) & (step <= last))
        def _():
            target[...] = total(*sources)

    half = width // 2
    o_ref[...] = early_ref[:, :, :width].astype(single)
    for i, ref in enumerate((q_ref, k_ref, v_ref)):
        ref[:, :, :half] = early_ref[:, :, width + i * half : width + (i + 1) * half].astype(single)
        ref[:, :, half:] = late_ref[:, :, i * half : (i + 1) * half].astype(single)

    @pl.when(pl.program_id(0) == 0)
    def _():
        small = small_ref[...].astype(single).reshape(router_ref.shape[1], TILE)
        turned = small.T
        router_ref[...] = turned[:experts]
        attn_ref[...] = turned[experts : experts + 1]
        moe_ref[...] = turned[experts + 1 : experts + 2]
        table_ref[...] = small[: table_ref.shape[0], experts + 2 : experts + 2 + table_ref.shape[1]]


def finish(kx, lx, ky, ly, ka, la, kb, lb, early, late, grad_tokens, mixed, experts, table_rows, heads):
    shape = jax.ShapeDtypeStruct
    _, lines, wider = early.shape
    lanes = late.shape[2]
    width = kb.shape[1]
    rows = QUARTERS * lines
    steps = QUARTERS
    m = kx.shape[0]
    ka, kb = (part.reshape(3, m, width) for part in (ka, kb))
    la, lb = (part.reshape(-1, 3, m, width) for part in (la, lb))
    block = lambda pick: pl.BlockSpec((1, m, width), lambda i: (pick(i), 0, 0))
    blocks = lambda array, pick: pl.BlockSpec((array.shape[0], 1, m, width), lambda i: (0, pick(i), 0, 0))
    strip, rest = (lambda i: jnp.maximum(i - 2, 0)), (lambda i: jnp.maximum(i - 1, 0))
    part = pl.BlockSpec((1, lines, width), lambda i: (i, 0, 0))
    once = lambda *dims: pl.BlockSpec(dims, lambda i: (0,) * len(dims))
    some = pl.BlockSpec((mixed.shape[0] // steps, width), lambda i: (i, 0))
    return pl.pallas_call(
        finish_kernel,
        grid=(steps,),
        out_shape=(
            shape((m, steps * width), single), shape((steps * m, width), single), *(shape((QUARTERS, lines, width), single),) * 4,
            shape((experts, rows), single), shape((1, rows), single), shape((1, rows), single),
            shape((table_rows, heads), single), shape(grad_tokens.shape, single), shape(mixed.shape, low),
        ),
        in_specs=[
            once(*kx.shape), once(*lx.shape), once(*ky.shape), once(*ly.shape),
            block(strip), blocks(la, strip), block(lambda i: 2), blocks(la, lambda i: 2), block(rest), blocks(lb, rest),
            pl.BlockSpec((1, lines, wider), lambda i: (i, 0, 0)), pl.BlockSpec((1, lines, lanes), lambda i: (i, 0, 0)),
            pl.BlockSpec((QUARTERS, lines, TILE), lambda i: (0, 0, lanes // TILE - 1)), some, some,
        ],
        out_specs=(
            pl.BlockSpec((m, width), lambda i: (0, i)), pl.BlockSpec((m, width), lambda i: (i, 0)),
            part, part, part, part, once(experts, rows), once(1, rows), once(1, rows), once(table_rows, heads),
            some, some,
        ),
        compiler_params=pltpu.CompilerParams(vmem_limit_bytes=vmem_cap),
        cost_estimate=pl.CostEstimate(flops=0, bytes_accessed=12_000_000, transcendentals=0),
        name="finish",
    )(kx, lx, ky, ly, ka, la, ka, la, kb, lb, early, late, late, grad_tokens, mixed)


def local(
    tokens,
    routes,
    slot_ids,
    w_query,
    w_key,
    w_value,
    w_output,
    w_router,
    norm_attn,
    norm_moe,
    rel_table,
    w_in,
    w_out,
    cotangent,
):
    shard_count = lax.axis_size("shard")
    token_rows, model_width = tokens.shape
    prompt_len = PR_DEV * shard_count
    weight_rows, expert_count = w_router.shape
    table_rows, head_count = rel_table.shape
    capacity = 2 * token_rows // expert_count
    slot_count = expert_count * capacity

    small = jnp.concatenate(
        [w_router.T, norm_attn[None], norm_moe[None], jnp.pad(rel_table.T, ((0, 0), (0, weight_rows - table_rows)))]
    )
    small = jnp.pad(small, ((0, TILE - small.shape[0]), (0, TILE - weight_rows)))
    ints = jnp.stack([routes, slot_ids])
    bucket_row = jnp.asarray(np.tile(distance_buckets(table_rows * shard_count), (8, 1)), jnp.int32)
    (
        lse, rev, gate, col_slots, gains, slots_out, grad_in, weights, every_tok, small, normed, queries, keys, values,
        attended, mid,
    ) = front(ints, bucket_row, cotangent, (w_query, w_key, w_value, w_output), tokens, small, slot_count)
    by_chip = (shard_count // 2, 2, capacity, model_width)
    grad_back, result, grads, rx, ry, router_grads = moe(
        slots_out.reshape(by_chip), grad_in.reshape(by_chip), small, w_in[0], w_out[0]
    )
    early_part, kx, ky, dense, prompt_part, near_part, grad_own, grad_resid, ra, rb, returned, lx, ly = back(
        grad_back.reshape(slot_count, model_width), col_slots, mid, cotangent, gains, every_tok, weights,
        (normed, queries, keys, values, attended, lse, rev), bucket_row, router_grads, grads, rx, ry, result,
    )
    chips = shard_count // 2
    lines = weight_rows // QUARTERS
    early, late, grad_tokens, mixed, ka, la, kb, lb = reduce_all(
        gains, col_slots, dense.reshape(chips, 2, QUARTERS, lines, -1),
        prompt_part.reshape(chips, 2, PR_DEV, model_width), near_part, grad_own, grad_resid, tokens, mid, gate,
        result, returned, grads, ra, rb,
        early_part.reshape(QUARTERS, lines, -1),
    )
    in_grad, out_grad, gq, gk, gv, go, router, gain_attn, gain_moe, table, grad_tokens, mixed = finish(
        kx, lx, ky, ly, ka, la, kb, lb, early, late, grad_tokens, mixed, expert_count, table_rows, head_count
    )
    return (
        mixed,
        grad_tokens,
        *(part.reshape(weight_rows, model_width) for part in (gq, gk, gv, go)),
        router.T,
        gain_attn[0],
        gain_moe[0],
        table,
        in_grad[None],
        out_grad[None],
    )


def solution(mesh):
    return jax.shard_map(
        local,
        mesh=mesh,
        in_specs=(
            P(("rep", "shard"), None),
            P(("rep", "shard")),
            P(("rep", "shard")),
            P("shard", None),
            P("shard", None),
            P("shard", None),
            P("shard", None),
            P("shard", None),
            P("shard"),
            P("shard"),
            P("shard", None),
            P("shard", None, None),
            P("shard", None, None),
            P(("rep", "shard"), None),
        ),
        out_specs=(
            P(("rep", "shard"), None),
            P(("rep", "shard"), None),
            P("shard", None),
            P("shard", None),
            P("shard", None),
            P("shard", None),
            P("shard", None),
            P("shard"),
            P("shard"),
            P("shard", None),
            P("shard", "rep", None),
            P("shard", "rep", None),
        ),
        check_vma=False,
    )
```

```python
import jax
import jax.numpy as jnp
import numpy as np
from jax import lax
from jax.experimental import pallas as pl
from jax.experimental.pallas import tpu as pltpu
from jax.sharding import PartitionSpec as P

PR_DEV = 128
TILE = 128
SPAN = 2 * TILE
NEAR = 3
QUARTERS = 4
far_before, far_after, causal_tile, hidden_tile, tile_kinds = 3, 4, 5, 6, 7
vmem_cap = 60 * 1024 * 1024
mesh_ids = pl.DeviceIdType.MESH
bucket_edges = (12, 16, 23, 32, 46, 64, 91)
norm_epsilon = 1e-06
masked_score = -1e30
low, single = jnp.bfloat16, jnp.float32
in_vmem = pl.BlockSpec(memory_space=pltpu.VMEM)
anywhere = pl.BlockSpec(memory_space=pl.ANY)


def inverse_rms(values):
    return lax.rsqrt(jnp.mean(values * values, axis=-1, keepdims=True) + norm_epsilon)


def norm_pull(grad, values, gain):
    scale = inverse_rms(values)
    pulled = grad * gain
    mean = jnp.mean(pulled * values, axis=-1, keepdims=True)
    return scale * pulled - values * (scale * scale * scale * mean)


def nt(left, right):
    return lax.dot_general(left, right, (((1,), (1,)), ((), ())), preferred_element_type=single)


def tn(left, right):
    return lax.dot_general(left, right, (((0,), (0,)), ((), ())), preferred_element_type=single)


def nn(left, right):
    return jnp.dot(left, right, preferred_element_type=single)


def thirds_of(values):
    first = values.astype(low)
    rest = values - first.astype(single)
    second = rest.astype(low)
    return first, second, (rest - second.astype(single)).astype(low)


def fill_tiles(tiles_ref, rev_row, low, high):
    spread = jnp.broadcast_to(rev_row, (TILE, 4 * TILE))
    rolled = pltpu.roll(spread, 0, 1, stride=1, stride_axis=0)
    keys = lax.broadcasted_iota(jnp.int32, (TILE, TILE), 0)
    rows = lax.broadcasted_iota(jnp.int32, (TILE, TILE), 1)
    tiles_ref[0] = rolled[:, TILE : 2 * TILE]
    tiles_ref[1] = rolled[:, :TILE]
    tiles_ref[2] = rolled[:, 3 * TILE :]
    tiles_ref[far_before] = jnp.broadcast_to(low, (TILE, TILE))
    tiles_ref[far_after] = jnp.broadcast_to(high, (TILE, TILE))
    tiles_ref[causal_tile] = jnp.where(keys <= rows, rolled[:, :TILE], masked_score)
    tiles_ref[hidden_tile] = jnp.full((TILE, TILE), masked_score, jnp.float32)


def prompt_tile(block, chunk, shard_id, block_count):
    if chunk == 0:
        gap = block - shard_id
        far = jnp.where(gap < 0, far_before, far_after)
        return jnp.where(jnp.abs(gap) <= 1, gap + 1, far)
    if chunk == 1 and block == block_count - 1:
        return jnp.where(shard_id % 2 == 0, 0, far_before)
    return far_before


def local_tile(block, chunk, shard_id):
    if block >= 2:
        return ((causal_tile, 0), (hidden_tile, causal_tile))[block - 2][chunk]
    kind = 0 if (block, chunk) == (1, 0) else far_before
    return jnp.where(shard_id % 2 == 1, kind, hidden_tile)


def prompt_grid(part, shard_id, block_count):
    return [
        [(side, prompt_tile(2 * part + half, chunk, shard_id, block_count)) for side in range(2) for chunk in range(3)]
        for half in range(2)
    ]


def local_grid(part, shard_id):
    return [
        [(side, local_tile(2 * part + half, chunk, shard_id)) for side in range(2) for chunk in range(2)]
        for half in range(2)
    ]


def tile_of(values, i, j):
    return values[i * TILE : (i + 1) * TILE, j * TILE : (j + 1) * TILE]


def with_bias(scores, tiles_ref, grid):
    lines = [
        jnp.concatenate(
            [tile_of(scores, i, j) + tiles_ref[side, kind] for j, (side, kind) in enumerate(row)], axis=1
        )
        for i, row in enumerate(grid)
    ]
    return jnp.concatenate(lines, axis=0)


def both_heads(values):
    first = head_mask(values.shape[0], 0)
    none = jnp.zeros_like(values)
    return jnp.concatenate([jnp.where(first, values, none), jnp.where(first, none, values)], axis=0)


def continuation(values, axis):
    rows = values.shape[axis] // 2
    pick = (lambda a, b: values[:, a:b]) if axis else (lambda a, b: values[a:b])
    return jnp.concatenate([pick(PR_DEV, rows), pick(rows + PR_DEV, 2 * rows)], axis=axis)


def fold8(values):
    return values.reshape(values.shape[0] // 8, 8, values.shape[1])


def head_mask(rows, side):
    lanes = lax.broadcasted_iota(jnp.int32, (rows, TILE), 1)
    return (lanes < TILE // 2) if side == 0 else (lanes >= TILE // 2)


def distance_buckets(bucket_count):
    steps = np.arange(4 * TILE)
    gap = -np.where(steps < 2 * TILE, steps, steps - 4 * TILE)
    size = np.abs(gap)
    far = sum((size >= edge).astype(np.int64) for edge in bucket_edges)
    exact = bucket_count // 4
    return np.where(gap > 0, bucket_count // 2, 0) + np.where(size < exact, size, exact + far)


def front_kernel(
    route_ref, slot_ref, bucket_ref, cot_ref, router_ref, first_ref, second_ref, table_ref, wq_hbm, wk_hbm, wv_hbm, wo_hbm, tok_hbm,
    lse_ref, rev_ref, gate_ref, col_ref, gain_ref, x_ref, gin_hbm, w_hbm, every_hbm, small_hbm,
    n_hbm, q_hbm, k_hbm, v_hbm, o_hbm, mid_hbm,
    tiles, vt, sp, sl, gbuf, w_ref, every_ref, small_ref, tok_ref, shard_w, little,
    n_ref, nt_ref, q_ref, k_ref, v_ref, ot_ref, mid_ref,
    gs, gr, loc, wz_s, wz_r, tz_s, tz_r, sz_s, sz_r, wr_s, wr_r, wt_s, wt_r, tt_s, tt_r, st_s, st_r, et_s, et_r,
):
    rep, chip, core, chips, quarter = places()
    along, across, twin = peer_lists()
    shards = chips * 2
    shard_id = chip * 2 + core
    rows, width = tok_ref.shape
    experts = shards
    blocks = every_ref.shape[0] // TILE - 4
    half = TILE // 2
    heads_held = rev_ref.shape[0]
    lines = shard_w.shape[1]
    rest_rows = rows - PR_DEV
    prompt_len = blocks * TILE
    others = [(rep, (shard_id + k) % shards) for k in range(1, shards)]

    def w_rows(source, side):
        return pl.ds(pl.multiple_of((source * 2 + side) * lines, lines), lines)

    def t_rows(source, side):
        return every_ref.at[pl.ds(pl.multiple_of((source * 2 + side) * PR_DEV, PR_DEV), PR_DEV)]

    loads = [
        pltpu.make_async_copy(source, shard_w.at[i], loc.at[i])
        for i, source in enumerate((wq_hbm, wk_hbm, wv_hbm, wo_hbm))
    ] + [pltpu.make_async_copy(tok_hbm, tok_ref, loc.at[4])]
    for copy in loads:
        copy.start()
    gains = [ref[...].astype(single).reshape(1, lines) for ref in (first_ref, second_ref)]
    short = jnp.zeros((2 * TILE // 8 - 2 - experts, lines), single)
    turned = jnp.concatenate([router_ref[...].astype(single), *gains, short], axis=0).astype(low)
    lane = lambda count: lax.broadcasted_iota(jnp.int32, (count, TILE), 1)
    line = lambda count: lax.broadcasted_iota(jnp.int32, (count, TILE), 0)
    left = tn(turned, (line(turned.shape[0]) == lane(turned.shape[0])).astype(low))
    heads = table_ref.shape[1]
    table = nn(table_ref[...], (line(heads) + experts + 2 == lane(heads)).astype(low))
    below = jnp.zeros((lines - table.shape[0], TILE), single)
    little[...] = (left + jnp.concatenate([table, below], axis=0)).astype(low)
    greeted = [twin] + along
    for device in across + [(rep, (chip + k) % chips * 2 + 1 - core) for k in range(1, chips)]:
        greeted.append(device)
    greet(greeted)
    started = []

    def go(source, target, sems, device):
        copy = send(source, target, sems, device)
        copy.start()
        started.append(copy)

    def landed(piece, sems):
        send(piece, piece, sems, twin).wait_recv()

    for copy in loads:
        copy.wait()
    mine = w_rows(chip, core)
    prompt, rest = tok_ref.at[pl.ds(0, PR_DEV)], tok_ref.at[pl.ds(PR_DEV, rest_rows)]
    for k, device in enumerate(along):
        go(shard_w.at[quarter], w_ref.at[quarter, mine], (wz_s.at[k], wz_r.at[k]), device)
        go(little, small_ref.at[mine], (sz_s.at[k], sz_r.at[k]), device)
    go(little, small_ref.at[mine], (st_s.at[0], st_r.at[0]), twin)
    go(rest, every_ref.at[pl.ds(prompt_len, rest_rows)], (et_s.at[0], et_r.at[0]), twin)
    go(prompt, t_rows(chip, core), (tt_s.at[0], tt_r.at[0]), twin)
    go(shard_w, w_ref.at[:, mine], (wt_s.at[0], wt_r.at[0]), twin)
    w_ref[:, mine, :] = shard_w[...]
    small_ref[mine, :] = little[...]
    every_ref[pl.ds(pl.multiple_of(shard_id * PR_DEV, PR_DEV), PR_DEV), :] = tok_ref[:PR_DEV, :]
    every_ref[prompt_len + rest_rows :, :] = tok_ref[PR_DEV:, :]
    routes = route_ref[...].reshape(1, rows)
    dispatch = routes * (x_ref.shape[0] // experts) + slot_ref[...].reshape(1, rows)
    ints = jnp.concatenate([routes, dispatch, jnp.zeros((6, rows), jnp.int32)], axis=0).astype(single).T
    route_col = ints[:, 0:1].astype(jnp.int32)
    col_ref[...] = jnp.broadcast_to(ints[:, 1:2].astype(jnp.int32), col_ref.shape)
    slots = lax.broadcasted_iota(jnp.int32, (x_ref.shape[0], rows), 0)
    place = (slots == dispatch).astype(low)
    gbuf[...] = nn(place, cot_ref[...]).astype(low).reshape(gbuf.shape)
    own_g = pltpu.make_async_copy(gbuf.at[shard_id], gin_hbm.at[shard_id], loc.at[6])
    own_g.start()

    for k in range(1, chips):
        source = (chip + chips - k) % chips
        piece = w_ref.at[quarter, w_rows(source, core)]
        landed(piece, (wz_s.at[k - 1], wz_r.at[k - 1]))
        for j, device in enumerate(across):
            go(piece, piece, (wr_s.at[k - 1, j], wr_r.at[k - 1, j]), device)
        go(prompt, t_rows(chip, core), (tz_s.at[k - 1], tz_r.at[k - 1]), along[k - 1])
    for k in range(1, chips):
        source = (chip + chips - k) % chips
        piece = small_ref.at[w_rows(source, core)]
        landed(piece, (sz_s.at[k - 1], sz_r.at[k - 1]))
        go(piece, piece, (st_s.at[k], st_r.at[k]), twin)
    for k in range(1, chips):
        source = (chip + chips - k) % chips
        piece = t_rows(source, core)
        landed(piece, (tz_s.at[k - 1], tz_r.at[k - 1]))
        go(piece, piece, (tt_s.at[k], tt_r.at[k]), twin)
    for k, device in enumerate(others):
        go(gbuf.at[device[1]], gin_hbm.at[shard_id], (gs.at[k], gr.at[k]), device)
    for k in range(chips):
        source = (chip + chips - k) % chips
        landed(small_ref.at[w_rows(source, 1 - core)], (st_s.at[k], st_r.at[k]))
    writes = []

    def write(source, target):
        writes.append(pltpu.make_async_copy(source, target, loc.at[7 + len(writes)]))
        writes[-1].start()

    write(small_ref, small_hbm)

    small_t = small_ref[...].astype(single).T
    gain_attn = small_t[experts : experts + 1]
    gain_moe = small_t[experts + 1 : experts + 2]
    gain_ref[...] = jnp.concatenate([gain_attn, gain_moe, jnp.zeros((6, width), single)], axis=0)
    shard_rows = width // shards
    table_rows = 2 * TILE // 8 // shards
    owner = lax.broadcasted_iota(jnp.int32, (shards, shard_rows, 4 * TILE), 0)
    offset = lax.broadcasted_iota(jnp.int32, (shards, shard_rows, 4 * TILE), 1)
    held = jnp.where(offset < table_rows, owner * table_rows + offset, -1).reshape(width, 4 * TILE)
    hot = (held == bucket_ref[0:1, :]).astype(low)
    table_t = small_t[experts + 2 : experts + 2 + heads_held].astype(low)
    rev_ref[...] = nn(table_t, hot)

    for k in range(chips):
        source = (chip + chips - k) % chips
        landed(t_rows(source, 1 - core), (tt_s.at[k], tt_r.at[k]))
    landed(every_ref.at[pl.ds(prompt_len, rest_rows)], (et_s.at[0], et_r.at[0]))
    write(every_ref, every_hbm)

    @pl.loop(0, every_ref.shape[0] // SPAN)
    def scale(part):
        span = pl.ds(pl.multiple_of(part * SPAN, SPAN), SPAN)
        values = every_ref[span, :].astype(single)
        normed = values * inverse_rms(values) * gain_attn
        n_ref[span, :] = normed.astype(low)
        nt_ref[:, span] = normed.T.astype(low)

    write(nt_ref, n_hbm)
    for k in range(1, chips):
        source = (chip + chips - k) % chips
        for j in range(1, QUARTERS):
            piece = w_ref.at[(quarter + QUARTERS - j) % QUARTERS, w_rows(source, core)]
            landed(piece, (wr_s.at[k - 1, j - 1], wr_r.at[k - 1, j - 1]))
        piece = w_ref.at[:, w_rows(source, core)]
        go(piece, piece, (wt_s.at[k], wt_r.at[k]), twin)
    for k in range(chips):
        source = (chip + chips - k) % chips
        landed(w_ref.at[:, w_rows(source, 1 - core)], (wt_s.at[k], wt_r.at[k]))
    write(w_ref, w_hbm)

    k_ref[...] = nn(n_ref[...], w_ref[1]).astype(low)
    v_ref[...] = nn(n_ref[...], w_ref[2]).astype(low)

    own = pl.ds(pl.multiple_of(shard_id * TILE, TILE), TILE)
    normed = jnp.concatenate([n_ref[own, :], n_ref[(blocks + 2) * TILE :, :]], axis=0)
    q_ref[...] = (nn(normed, w_ref[0]).astype(low) * jnp.asarray(0.125, low)).astype(low)
    write(k_ref, k_hbm)
    write(v_ref, v_hbm)
    write(q_ref, q_hbm)

    @pl.loop(0, width // TILE)
    def pair_loop(pair):
        cols = pl.ds(pl.multiple_of(pair * TILE, TILE), TILE)
        vt[...] = v_ref[:, cols].T
        q_both = both_heads(q_ref[:, cols])
        q_local = continuation(q_both, 0)
        for side in range(2):
            rev_row = rev_ref[pl.ds(pair * 2 + side, 1), :]
            fill_tiles(tiles.at[side], rev_row, rev_row[:, SPAN - 1 : SPAN], rev_row[:, SPAN : SPAN + 1])
        top = jnp.full((8, 2 * rows), masked_score, single)
        for part in range(blocks // 2):
            keys = slice(part * SPAN, (part + 1) * SPAN)
            scores = with_bias(nt(k_ref[keys, cols], q_both), tiles, prompt_grid(part, shard_id, blocks))
            sp[keys, :] = scores
            top = jnp.maximum(top, jnp.max(fold8(scores), axis=0))
        local = continuation(top, 1)
        for part in range(2):
            keys = slice(part * SPAN, (part + 1) * SPAN)
            held = slice((blocks // 2 + part) * SPAN, (blocks // 2 + part + 1) * SPAN)
            scores = with_bias(nt(k_ref[held, cols], q_local), tiles, local_grid(part, shard_id))
            sl[keys, :] = scores
            local = jnp.maximum(local, jnp.max(fold8(scores), axis=0))
        rest = rows - PR_DEV
        top = jnp.concatenate(
            [top[:, :PR_DEV], local[:, :rest], top[:, rows : rows + PR_DEV], local[:, rest:]], axis=1
        )
        top = jnp.max(top, axis=0, keepdims=True)
        total = jnp.zeros((8, 2 * rows), single)
        summed = [jnp.zeros((half, rows), single)] * 2
        for part in range(blocks // 2):
            keys = slice(part * SPAN, (part + 1) * SPAN)
            weights = jnp.exp(sp[keys, :] - top)
            total = total + jnp.sum(fold8(weights), axis=0)
            weights = weights.astype(low)
            for side in range(2):
                heads = slice(side * half, (side + 1) * half)
                summed[side] = summed[side] + nn(vt[heads, keys], weights[:, side * rows : (side + 1) * rows])
        top_local, total_local = continuation(top, 1), continuation(total, 1)
        summed_local = [part_sum[:, PR_DEV:] for part_sum in summed]
        for part in range(2):
            keys = slice(part * SPAN, (part + 1) * SPAN)
            held = slice((blocks // 2 + part) * SPAN, (blocks // 2 + part + 1) * SPAN)
            weights = jnp.exp(sl[keys, :] - top_local)
            total_local = total_local + jnp.sum(fold8(weights), axis=0)
            weights = weights.astype(low)
            for side in range(2):
                heads = slice(side * half, (side + 1) * half)
                summed_local[side] = summed_local[side] + nn(
                    vt[heads, held], weights[:, side * rest : (side + 1) * rest]
                )
        for side in range(2):
            head = pair * 2 + side
            ours = slice(side * rows, (side + 1) * rows)
            sums = jnp.concatenate(
                [total[:, side * rows : side * rows + PR_DEV], total_local[:, side * rest : (side + 1) * rest]], axis=1
            )
            sums = jnp.sum(sums, axis=0, keepdims=True)
            mixed = jnp.concatenate([summed[side][:, :PR_DEV], summed_local[side]], axis=1)
            ot_ref[pl.ds(pl.multiple_of(head * half, half), half), :] = mixed / sums
            lse_ref[pl.ds(head, 1), :] = top[:, ours] + jnp.log(sums)

    resid_mid = tok_ref[...].astype(single) + nn(ot_ref[...].T.astype(low), w_ref[3])
    mid_ref[...] = resid_mid
    write(ot_ref, o_hbm)
    write(mid_ref, mid_hbm)
    mid_low = (resid_mid * inverse_rms(resid_mid) * gain_moe).astype(low)
    probs = router_softmax(mid_low, small_ref[...], experts)
    lanes = lax.broadcasted_iota(jnp.int32, probs.shape, 1)
    gate = jnp.sum(jnp.where(lanes == route_col, probs, 0.0), axis=1, keepdims=True)
    gate_ref[...] = jnp.broadcast_to(gate, gate_ref.shape)
    x_ref[...] = nn(place, mid_low).astype(low)
    own_g.wait()
    for k in range(shards - 1):
        landed(gin_hbm.at[(shard_id + shards - k - 1) % shards], (gs.at[k], gr.at[k]))
    for copy in writes:
        copy.wait()
    for copy in started:
        copy.wait_send()


def router_softmax(rows_low, small, experts):
    logits = nn(rows_low, small)
    lanes = lax.broadcasted_iota(jnp.int32, logits.shape, 1)
    logits = jnp.where(lanes < experts, logits, masked_score)
    powers = jnp.exp(logits - jnp.max(logits, axis=1, keepdims=True))
    return powers / jnp.sum(powers, axis=1, keepdims=True)


def front(routes, slot_ids, bucket_row, cotangent, weights, tokens, rows_small, slot_count):
    rows, width = tokens.shape
    shards = lax.axis_size("shard")
    chips, count = shards // 2, shards // 2 - 1
    keys = shards * PR_DEV + 2 * (rows - PR_DEV)
    lines = width // shards
    shape = jax.ShapeDtypeStruct
    sem = pltpu.SemaphoreType.DMA
    vm = pltpu.VMEM
    return pl.pallas_call(
        front_kernel,
        out_shape=(
            shape((16, rows), single), shape((16, 4 * TILE), single), shape((rows, TILE), single),
            shape((rows, TILE), jnp.int32), shape((8, width), single), shape((slot_count, width), low),
            shape((shards, slot_count // shards, width), low), shape((4, width, width), low),
            shape((keys, width), low), shape((width, TILE), low),
            shape((width, keys), low), shape((rows, width), low), shape((keys, width), low),
            shape((keys, width), low), shape((width, rows), single), shape((rows, width), single),
        ),
        in_specs=[in_vmem] * 8 + [anywhere] * 5,
        out_specs=(in_vmem,) * 6 + (anywhere,) * 10,
        scratch_shapes=[
            vm((2, tile_kinds, TILE, TILE), single), vm((TILE, keys), low), vm((keys - 2 * SPAN, 2 * rows), single),
            vm((2 * SPAN, 2 * (rows - TILE)), single),
            vm((shards, slot_count // shards, width), low), vm((4, width, width), low), vm((keys, width), low),
            vm((width, TILE), low), vm((rows, width), low), vm((4, lines, width), low), vm((lines, TILE), low),
            vm((keys, width), low), vm((width, keys), low), vm((rows, width), low), vm((keys, width), low),
            vm((keys, width), low), vm((width, rows), single), vm((rows, width), single),
            sem((shards - 1,)), sem((shards - 1,)), sem((16,)), sem((count,)), sem((count,)), sem((count,)),
            sem((count,)), sem((count,)), sem((count,)), sem((count, 3)), sem((count, 3)), sem((chips,)), sem((chips,)),
            sem((chips,)), sem((chips,)), sem((chips,)), sem((chips,)), sem((1,)), sem((1,)),
        ],
        compiler_params=pltpu.CompilerParams(collective_id=2, has_side_effects=True, vmem_limit_bytes=vmem_cap),
        cost_estimate=pl.CostEstimate(flops=30_000_000_000, bytes_accessed=20_000_000, transcendentals=8_000_000),
        name="front",
    )(routes, slot_ids, bucket_row, cotangent, *rows_small, *weights, tokens)


def moe_kernel(
    small_ref, x_ref, g_hbm, w_in_ref, w_out_ref,
    back_ref, out_hbm, ge_hbm, rx_hbm, ry_hbm, rg_ref,
    w_in, w_out, xin, gm, gg, hid, gpre, logit_grads, x_t, gw_in, gw_out, g_ref, out_ref,
    xs, xr, ms, mr, ws, ls, os_in, os_out, ex_s, ex_r, ey_s, ey_r, own, os_result,
):
    rep, chip, core, chips, quarter = places()
    experts = chips * 2
    here = chip * 2 + core
    pair_rows = 2 * xin.shape[2]
    hidden = w_in_ref.shape[1]
    width = w_in_ref.shape[0]
    _, slow, fast, slows, fasts = rep_places()
    lines = gw_in.shape[3]
    beside = [(slow * fasts + (fast + j) % fasts, here) for j in range(1, fasts)]
    beyond = [((slow + j) % slows * fasts + fast, here) for j in range(1, slows)]
    loads = [
        pltpu.make_async_copy(w_in_ref, w_in, ws.at[0]),
        pltpu.make_async_copy(w_out_ref, w_out, ws.at[1]),
    ]
    held = [
        pltpu.make_async_copy(x_ref.at[chip, core], xin.at[chip, core], own.at[0]),
        pltpu.make_async_copy(g_hbm, g_ref, own.at[1]),
    ]
    for copy in held + loads:
        copy.start()
    twin = (rep, chip * 2 + 1 - core)
    targets = [
        (k, side, (rep, chip_across(chip, k) * 2 + side)) for k in range(1, chips) for side in range(2)
    ]
    greet([twin] + [device for _, _, device in targets] + beside + beyond)
    sent = [send(x_ref.at[chip, 1 - core], xin.at[chip, core], (xs.at[0, 0], xr.at[0, core]), twin)]
    for k, side, device in targets:
        sent.append(
            send(x_ref.at[chip_across(chip, k), side], xin.at[chip, core], (xs.at[k, side], xr.at[k, core]), device)
        )
    for copy in sent[:5]:
        copy.start()
    for copy in held + loads[:1]:
        copy.wait()

    def arrived(k, source, side):
        piece = xin.at[source, side]
        send(piece, piece, (xs.at[0, 0], xr.at[k, side]), twin).wait_recv()

    @pl.loop(0, chips)
    def chunk(k):
        source = chip_across(chip, k)

        @pl.when(k == 0)
        def _():
            arrived(0, chip, 1 - core)

        @pl.when(k > 0)
        def _():
            for side in range(2):
                arrived(k, source, side)

        rows = xin[source].reshape(pair_rows, xin.shape[3])
        grads = g_ref[source].reshape(pair_rows, xin.shape[3])
        probs = router_softmax(rows, small_ref[...], experts)
        lanes = lax.broadcasted_iota(jnp.int32, probs.shape, 1)
        gate = jnp.sum(jnp.where(lanes == here, probs, 0.0), axis=1, keepdims=True)
        gated = (gate * grads.astype(single)).astype(low)
        span = pl.ds(pl.multiple_of(source * pair_rows, pair_rows), pair_rows)
        gg[span, :] = gated
        pre = nn(rows, w_in[...])

        @pl.when(k == 0)
        def _():
            loads[1].wait()

        grad_hidden = nt(gated, w_out[...])
        square = pre * pre
        wave = jnp.tanh(0.7978845608028654 * pre * (1.0 + 0.044715 * square))
        left = 0.5 + 0.5 * wave
        active = (pre * left).astype(low)
        slope = left + (0.5 * pre) * (1.0 - wave * wave) * (0.7978845608028654 + 0.10703222440890037 * square)
        grad_pre = (grad_hidden * slope).astype(low)
        hid[span, :] = active
        gpre[span, :] = grad_pre
        out = nn(active, w_out[...]).astype(low)
        out_ref[source] = out.reshape(out_ref.shape[1:])
        pltpu.make_async_copy(out_ref.at[source], out_hbm.at[source], os_result.at[k]).start()
        grad_gate = jnp.sum(grads.astype(single) * out.astype(single), axis=1, keepdims=True)
        chosen = jnp.where(lanes == here, 1.0, 0.0)
        grad_logits = jnp.where(lanes < experts, gate * grad_gate * (chosen - probs), 0.0)
        logit_grads[span, :] = grad_logits
        router = small_ref[...]
        total = nt(grad_pre, w_in[...]) + sum(nt(part, router) for part in thirds_of(grad_logits))
        gm[source] = total.astype(low).reshape(gm.shape[1:])

        def reply(side, slot):
            return send(
                gm.at[source, side], back_ref.at[chip, core], (ms.at[k, slot], mr.at[k, core]), (rep, source * 2 + side)
            )

        @pl.when(k == 0)
        def _():
            for copy in sent[5:]:
                copy.start()
            reply(1 - core, 0).start()
            pltpu.make_async_copy(gm.at[chip, core], back_ref.at[chip, core], ls).start()

        @pl.when(k > 0)
        def _():
            for side in range(2):
                reply(side, side).start()

    every = xin[...].reshape(gg.shape)
    x_t[...] = every.T

    def strip_writes(part):
        rows = pl.ds(pl.multiple_of(part * lines, lines), lines)
        tail = pl.ds(4 * lines, 4 * lines)
        if gw_out.shape[1] == 1:
            second = (gw_out.at[part, 0], ge_hbm.at[part // fasts, part % fasts, tail])
        else:
            second = (gw_out.at[part], ge_hbm.at[part, :, tail])
        return [
            pltpu.make_async_copy(gw_in.at[part], ge_hbm.at[:, :, rows], os_in.at[part]),
            pltpu.make_async_copy(*second, os_out.at[part]),
        ]

    grads_out = [
        send(gw_in.at[0, :, (fast + j + 1) % fasts], rx_hbm.at[j], (ex_s.at[j], ex_r.at[j]), device)
        for j, device in enumerate(beside)
    ], [
        send(gw_in.at[1, (slow + j + 1) % slows], ry_hbm.at[j], (ey_s.at[j], ey_r.at[j]), device)
        for j, device in enumerate(beyond)
    ]

    @pl.loop(0, hidden // width)
    def strip(part):
        cols = pl.ds(pl.multiple_of(part * width, width), width)
        gw_in[part] = nn(x_t[...], gpre[:, cols]).astype(low).reshape(gw_in.shape[1:])
        strip_writes(part)[0].start()
        for turn in range(2):

            @pl.when(part == turn)
            def _():
                for copy in grads_out[turn]:
                    copy.start()

    @pl.loop(0, hidden // width)
    def second_strip(part):
        cols = pl.ds(pl.multiple_of(part * width, width), width)
        gw_out[part] = tn(hid[:, cols], gg[...]).astype(low).reshape(gw_out.shape[1:])
        strip_writes(part)[1].start()

    rg_ref[...] = sum(nn(x_t[...], part) for part in thirds_of(logit_grads[...]))
    pltpu.make_async_copy(gm.at[chip, core], back_ref.at[chip, core], ls).wait()

    def replied(k, source, side):
        piece = back_ref.at[source, side]
        send(piece, piece, (ms.at[0, 0], mr.at[k, side]), twin).wait_recv()

    replied(0, chip, 1 - core)
    for k in range(1, chips):
        for side in range(2):
            replied(k, chip_across(chip, k), side)
    for copy in sent:
        copy.wait_send()
    for part in range(hidden // width):
        for copy in strip_writes(part):
            copy.wait()
    for k in range(chips):
        source = chip_across(chip, k)
        pltpu.make_async_copy(out_ref.at[source], out_hbm.at[source], os_result.at[k]).wait()
    for copy in grads_out[0] + grads_out[1]:
        copy.wait()
    send(gm.at[chip, 0], back_ref.at[chip, core], (ms.at[0, 0], mr.at[0, 0]), twin).wait_send()
    for k in range(1, chips):
        for side in range(2):
            send(gm.at[chip, 0], back_ref.at[chip, core], (ms.at[k, side], mr.at[0, 0]), twin).wait_send()


def moe(rows_out, grad_in, small, w_in, w_out):
    chips, _, cap, width = rows_out.shape
    slots = chips * 2 * cap
    hidden = w_in.shape[1]
    shape = jax.ShapeDtypeStruct
    pairs = pltpu.SemaphoreType.DMA
    strips = hidden // width
    slows, fasts = rep_places()[3:]
    lines = width // (slows * fasts)
    return pl.pallas_call(
        moe_kernel,
        out_shape=(
            shape(rows_out.shape, low), shape(rows_out.shape, low), shape((slows, fasts, 8 * lines, width), low),
            shape((fasts - 1, slows, lines, width), low), shape((slows - 1, fasts, lines, width), low),
            shape((width, TILE), single),
        ),
        in_specs=[in_vmem] + [anywhere] * 4,
        out_specs=(anywhere,) * 5 + (in_vmem,),
        scratch_shapes=[
            pltpu.VMEM((width, hidden), low), pltpu.VMEM((hidden, width), low),
            pltpu.VMEM(rows_out.shape, low), pltpu.VMEM(rows_out.shape, low), pltpu.VMEM((slots, width), low),
            pltpu.VMEM((slots, hidden), low), pltpu.VMEM((slots, hidden), low),
            pltpu.VMEM((slots, TILE), single), pltpu.VMEM((width, slots), low),
            pltpu.VMEM((strips, slows, fasts, lines, width), low),
            pltpu.VMEM((strips, width // (4 * lines), 4 * lines, width), low),
            pltpu.VMEM(rows_out.shape, low), pltpu.VMEM(rows_out.shape, low),
            pairs((chips, 2)), pairs((chips, 2)), pairs((chips, 2)), pairs((chips, 2)), pairs((2,)), pairs,
            pairs((strips,)), pairs((strips,)), pairs((fasts - 1,)), pairs((fasts - 1,)), pairs((slows - 1,)),
            pairs((slows - 1,)), pairs((2,)), pairs((chips,)),
        ],
        compiler_params=pltpu.CompilerParams(collective_id=3, has_side_effects=True, vmem_limit_bytes=vmem_cap),
        cost_estimate=pl.CostEstimate(flops=40_000_000_000, bytes_accessed=40_000_000, transcendentals=3_000_000),
        name="moe",
    )(small, rows_out, grad_in, w_in, w_out)


def back_kernel(
    col_ref, gain_ref, lse_ref, rev_ref, bucket_ref, rg_ref, back_hbm, mid_hbm, cot_hbm, q_hbm, k_hbm, v_hbm, o_hbm,
    every_hbm, w_hbm, n_hbm, ge_hbm, rx_hbm, ry_hbm, out_hbm,
    z_ref, kx_ref, ky_ref, dense_hbm, p_hbm, e_hbm, own_hbm, gres_hbm, ra_hbm, rb_hbm, ret_hbm, lx_hbm, ly_hbm,
    tiles, sums, diag, kt, dqt, far_sums, g_ref, dq_ref, dk_ref, dv_ref, attn_gain,
    every_ref, w_ref, n_ref, back_ref, mid_ref, cot_ref, q_ref, k_ref, v_ref, o_ref,
    dense_ref, own_ref, gres_ref,
    x_own, x_in, x_sum, y_own, y_in, y_sum, o_grad, o_half, o_sum, o_in, h_grad, h_half, h_sum, h_in,
    loc, out, lx_s, lx_r, ly_s, ly_r, xs, xr, as_, ar, bs, br, os_, or_, oz_s, oz_r, hs_, hr_, hz_s, hz_r,
):
    shard_id = lax.axis_index("shard")
    shards = lax.axis_size("shard")
    rows, width = mid_ref.shape
    blocks = k_ref.shape[0] // TILE - 4
    half = TILE // 2
    experts = shards
    heads_held = rev_ref.shape[0]
    rep, slow, fast, slows, fasts = rep_places()
    _, chip, core, chips, _ = places()
    along, _, twin = peer_lists()
    lines = x_own.shape[1]
    loads = [
        pltpu.make_async_copy(source, target, loc.at[i])
        for i, (source, target) in enumerate((
            (back_hbm, back_ref), (mid_hbm, mid_ref), (cot_hbm, cot_ref), (w_hbm.at[3], w_ref.at[3]), (o_hbm, o_ref),
            (q_hbm, q_ref), (k_hbm, k_ref), (v_hbm, v_ref), (n_hbm, n_ref), (w_hbm.at[pl.ds(0, 3)], w_ref.at[pl.ds(0, 3)]),
            (every_hbm, every_ref), (out_hbm.at[chip, core], ret_hbm.at[chip, core]),
            (ge_hbm.at[:, fast, pl.ds(0, lines)], x_own), (rx_hbm, x_in),
            (ge_hbm.at[slow, :, pl.ds(lines, lines)], y_own), (ry_hbm, y_in),
        ))
    ]
    for copy in loads:
        copy.start()
    writes = []

    def write(source, target):
        writes.append(pltpu.make_async_copy(source, target, out.at[len(writes)]))
        writes[-1].start()

    beside = [(slow * fasts + (fast + j) % fasts, shard_id) for j in range(1, fasts)]
    beyond = [((slow + j) % slows * fasts + fast, shard_id) for j in range(1, slows)]
    nearby = result_peers(rep, chip, core, range(NEAR))
    far_twins = [(rep, (chip + k) % chips * 2 + 1 - core) for k in range(1, chips)]
    greet([twin] + along + far_twins + beside + beyond)
    sent = [
        send(ge_hbm.at[:, (fast + j + 1) % fasts, pl.ds(2 * lines, 3 * lines)], ra_hbm.at[j], (as_.at[j], ar.at[j]), device)
        for j, device in enumerate(beside)
    ] + [
        send(ge_hbm.at[(slow + j + 1) % slows, :, pl.ds(5 * lines, 3 * lines)], rb_hbm.at[j], (bs.at[j], br.at[j]), device)
        for j, device in enumerate(beyond)
    ] + [
        send(out_hbm.at[chip_across(chip, k), side if k else 1 - core], ret_hbm.at[chip, core], (xs.at[k, side], xr.at[k, core]), device)
        for k, side, device in nearby
    ]
    for copy in sent:
        copy.start()
    for copy in loads[12:]:
        copy.wait()
    for held, came, total in ((x_own, x_in, x_sum), (y_own, y_in, y_sum)):
        value = held[...].astype(single)
        for j in range(came.shape[0]):
            value = value + came[j].astype(single)
        total[...] = value.astype(low)
    second = [
        send(x_sum.at[(slow + j + 1) % slows], lx_hbm.at[j], (lx_s.at[j], lx_r.at[j]), device)
        for j, device in enumerate(beyond)
    ] + [
        send(y_sum.at[(fast + j + 1) % fasts], ly_hbm.at[j], (ly_s.at[j], ly_r.at[j]), device)
        for j, device in enumerate(beside)
    ]
    for copy in second:
        copy.start()
    kx_ref[...] = x_sum[slow]
    ky_ref[...] = y_sum[fast]
    diag[...] = jnp.zeros_like(diag)
    far_sums[...] = jnp.zeros_like(far_sums)
    tile_rows = lax.broadcasted_iota(jnp.int32, (TILE, TILE), 0)
    tile_cols = lax.broadcasted_iota(jnp.int32, (TILE, TILE), 1)
    flip = (tile_rows + tile_cols == TILE - 1).astype(single)

    for copy in loads[:5]:
        copy.wait()
    slots = lax.broadcasted_iota(jnp.int32, (rows, back_ref.shape[0]), 1)
    grad_mid = nn((slots == col_ref[:, 0:1]).astype(low), back_ref[...])
    resid_mid = mid_ref[...]
    grad_gain_moe = jnp.sum(grad_mid * resid_mid * inverse_rms(resid_mid), axis=0, keepdims=True)
    grad_resid = cot_ref[...].astype(single) + norm_pull(grad_mid, resid_mid, gain_ref[1:2, :])
    gres_ref[...] = grad_resid
    write(gres_ref, gres_hbm)
    grad_attn = grad_resid.astype(low)
    g_ref[...] = nt(grad_attn, w_ref[3]).astype(low)
    o_grad[...] = nn(o_ref[...].astype(low), grad_attn).reshape(o_grad.shape).astype(low)
    o_halves = [send(o_grad.at[2 * k + 1 - core], o_half.at[k], (os_.at[k], or_.at[k]), twin) for k in range(chips)]
    o_sends = [
        send(o_sum.at[(chip + k + 1) % chips], o_in.at[k], (oz_s.at[k], oz_r.at[k]), device)
        for k, device in enumerate(along)
    ]
    for copy in o_halves:
        copy.start()
    h_halves = [send(h_grad.at[2 * k + 1 - core], h_half.at[k], (hs_.at[k], hr_.at[k]), twin) for k in range(chips)]
    h_sends = [
        send(h_sum.at[(chip + k + 1) % chips], h_in.at[k], (hz_s.at[k], hz_r.at[k]), device)
        for k, device in enumerate(along)
    ]
    for copy in loads[5:12]:
        copy.wait()
    own = pl.ds(pl.multiple_of(shard_id * TILE, TILE), TILE)
    tail = slice((blocks + 2) * TILE, (blocks + 4) * TILE)
    early = width // 2

    @pl.loop(0, width // TILE)
    def pair_loop(pair):
        cols = pl.ds(pl.multiple_of(pair * TILE, TILE), TILE)
        kt[...] = k_ref[:, cols].T
        g_pair = g_ref[:, cols]
        q_both, g_both = both_heads(q_ref[:, cols]), both_heads(g_pair)
        delta_t = g_pair.astype(single).T * o_ref[cols, :]
        delta = jnp.concatenate(
            [jnp.sum(delta_t[:half], axis=0, keepdims=True), jnp.sum(delta_t[half:], axis=0, keepdims=True)], axis=1
        )
        log_total = jnp.concatenate([lse_ref[pl.ds(pair * 2, 1), :], lse_ref[pl.ds(pair * 2 + 1, 1), :]], axis=1)
        for side in range(2):
            rev_row = rev_ref[pl.ds(pair * 2 + side, 1), :]
            fill_tiles(tiles.at[side], rev_row, rev_row[:, SPAN - 1 : SPAN], rev_row[:, SPAN : SPAN + 1])
        sums[...] = jnp.zeros_like(sums)

        def block_grads(part, q_rows, g_rows, shift, scale, grid):
            keys = slice(part * SPAN, (part + 1) * SPAN)
            count = q_rows.shape[0] // 2
            scores = with_bias(nt(k_ref[keys, cols], q_rows), tiles, grid)
            weights = jnp.exp(scores - shift)
            grad_scores = weights * (nt(v_ref[keys, cols], g_rows) - scale)
            for i, row in enumerate(grid):
                for j, (side, kind) in enumerate(row):
                    sums[side, kind] += tile_of(grad_scores, i, j)
            raw = grad_scores.astype(low)
            dk_ref[keys, cols] = nn(raw, q_rows).astype(low)
            dv_ref[keys, cols] = nn(weights.astype(low), g_rows).astype(low)
            return [nn(kt[:half, keys], raw[:, :count]), nn(kt[half:, keys], raw[:, count:])]

        grads = [jnp.zeros((half, rows), single)] * 2
        for part in range(blocks // 2):
            more = block_grads(part, q_both, g_both, log_total, delta, prompt_grid(part, shard_id, blocks))
            grads = [old + new for old, new in zip(grads, more)]
        local = [old[:, PR_DEV:] for old in grads]
        held = (continuation(q_both, 0), continuation(g_both, 0), continuation(log_total, 1), continuation(delta, 1))
        for part in range(2):
            more = block_grads(blocks // 2 + part, *held, local_grid(part, shard_id))
            local = [old + new for old, new in zip(local, more)]
        for side in range(2):
            head = pair * 2 + side
            dqt[side * half : (side + 1) * half, :] = jnp.concatenate([grads[side][:, :PR_DEV], local[side]], axis=1)
            near = jnp.concatenate(
                [
                    sums[side, 1] + sums[side, causal_tile], sums[side, 0], jnp.zeros((TILE, TILE), single),
                    sums[side, 2],
                ],
                axis=1,
            )
            flipped = jnp.dot(flip, near, precision=lax.Precision.HIGHEST, preferred_element_type=single)
            rolled = pltpu.roll(flipped, 3 * TILE + 1, 1, stride=1, stride_axis=0)
            diag[pl.ds(head, 1), :] = jnp.sum(rolled, axis=0, keepdims=True)
            far_sums[pl.ds(head, 1), :] = jnp.concatenate(
                [
                    jnp.sum(sums[side, far_before], axis=0, keepdims=True),
                    jnp.sum(sums[side, far_after], axis=0, keepdims=True),
                ],
                axis=1,
            )
        dq_ref[:, cols] = (dqt[...].T * 0.125).astype(low)

        @pl.when(pair == 0)
        def _():
            for k in range(chips):
                o_halves[k].wait_recv()
                o_sum[k] = (o_grad[2 * k + core].astype(single) + o_half[k].astype(single)).astype(low)
            for copy in o_sends:
                copy.start()

        @pl.when(pair == width // SPAN - 1)
        def _():
            normed = jnp.concatenate([n_ref[:, own], n_ref[:, tail]], axis=1)
            for i, (left, right) in enumerate(((normed, dq_ref), (n_ref[...], dk_ref), (n_ref[...], dv_ref))):
                part = nn(left, right[:, :early]).reshape(shards, h_grad.shape[1], early)
                h_grad[:, :, i * early : (i + 1) * early] = part.astype(low)
            for copy in h_halves:
                copy.start()

        @pl.when(pair == width // SPAN)
        def _():
            for k in range(chips):
                h_halves[k].wait_recv()
                h_sum[k] = (h_grad[2 * k + core].astype(single) + h_half[k].astype(single)).astype(low)
            for copy in h_sends:
                copy.start()

    lanes = lax.broadcasted_iota(jnp.int32, (heads_held, 4 * TILE), 1)
    before = jnp.sum(far_sums[:, :TILE], axis=1, keepdims=True)
    after = jnp.sum(far_sums[:, TILE:], axis=1, keepdims=True)
    by_gap = diag[...] + jnp.where(lanes == SPAN - 1, before, 0.0) + jnp.where(lanes == SPAN, after, 0.0)
    shard_rows = width // shards
    table_rows = 2 * TILE // 8 // shards
    owner = lax.broadcasted_iota(jnp.int32, (shards, shard_rows, 4 * TILE), 0)
    offset = lax.broadcasted_iota(jnp.int32, (shards, shard_rows, 4 * TILE), 1)
    held = jnp.where(offset < table_rows, owner * table_rows + offset, -1).reshape(width, 4 * TILE)
    hot = (held == bucket_ref[0:1, :]).astype(low)
    grad_table = sum(nt(part, hot) for part in thirds_of(by_gap))

    attn_gain[...] = jnp.zeros_like(attn_gain)
    normed = jnp.concatenate([n_ref[:, own], n_ref[:, tail]], axis=1)
    dense_ref[:, :early] = nn(normed, dq_ref[:, early:]).astype(low)
    grad_own = nt(dq_ref[...], w_ref[0])
    values = jnp.concatenate([every_ref[own, :], every_ref[tail, :]], axis=0).astype(single)
    attn_gain[...] += jnp.sum(fold8(grad_own * (values * inverse_rms(values))), axis=0)
    own_ref[...] = grad_own

    def pull_rows(part):
        span = pl.ds(pl.multiple_of(part * SPAN, SPAN), SPAN)
        values = every_ref[span, :].astype(single)
        grads = nt(dk_ref[span, :], w_ref[1]) + nt(dv_ref[span, :], w_ref[2])
        attn_gain[...] += jnp.sum(fold8(grads * (values * inverse_rms(values))), axis=0)
        return grads

    @pl.loop(0, blocks // 2)
    def pull_prompt(part):
        k_ref[pl.ds(pl.multiple_of(part * SPAN, SPAN), SPAN), :] = pull_rows(part).astype(low)

    write(k_ref.at[pl.ds(0, blocks * TILE)], p_hbm)
    k_ref[blocks * TILE : (blocks + 2) * TILE, :] = pull_rows(blocks // 2).astype(low)
    write(k_ref.at[pl.ds(blocks * TILE, SPAN)], e_hbm)
    own_ref[PR_DEV:, :] += pull_rows(blocks // 2 + 1)
    write(own_ref, own_hbm)

    dense_ref[:, early : 2 * early] = nn(n_ref[...], dk_ref[:, early:]).astype(low)
    dense_ref[:, 2 * early : 3 * early] = nn(n_ref[...], dv_ref[:, early:]).astype(low)

    small_t = jnp.concatenate(
        [
            jnp.zeros((experts, width), single), jnp.sum(attn_gain[...], axis=0, keepdims=True), grad_gain_moe,
            grad_table, jnp.zeros((TILE - experts - 2 - heads_held, width), single),
        ],
        axis=0,
    )
    dense_ref[:, 3 * early :] = (small_t.T + rg_ref[...]).astype(low)
    write(dense_ref, dense_hbm)
    o_total = o_sum[chip].astype(single)
    for k in range(chips - 1):
        o_sends[k].wait_recv()
        o_total = o_total + o_in[k].astype(single)
    z_ref[:, :width] = o_total.astype(low)
    h_total = h_sum[chip].astype(single)
    for k in range(chips - 1):
        h_sends[k].wait_recv()
        h_total = h_total + h_in[k].astype(single)
    z_ref[:, width:] = h_total.astype(low)
    for copy in o_halves + o_sends + h_halves + h_sends:
        copy.wait_send()
    for copy in writes:
        copy.wait()
    for k, side in result_slots(core, range(NEAR)):
        piece = ret_hbm.at[chip_across(chip, k), side]
        send(piece, piece, (xs.at[0, 0], xr.at[k, side]), twin).wait_recv()
    for j in range(fasts - 1):
        send(ra_hbm.at[j], ra_hbm.at[j], (as_.at[j], ar.at[j]), twin).wait_recv()
    for j in range(slows - 1):
        send(rb_hbm.at[j], rb_hbm.at[j], (bs.at[j], br.at[j]), twin).wait_recv()
    for copy in second:
        copy.wait()
    for copy in sent:
        copy.wait_send()


def back(
    returned, col_slots, mid, cotangent, gains, every_tok, weights, kept, bucket_row, router_grads, grads, rx, ry, result
):
    rows, width = mid.shape
    normed, queries, keys, values, attended, lse, rev = kept
    count = keys.shape[0]
    shards = lax.axis_size("shard")
    slows, fasts, eighths = grads.shape[:3]
    m = eighths // 8
    chips, lines, early = shards // 2, width // shards, width // 2
    vm = pltpu.VMEM
    shape = jax.ShapeDtypeStruct
    pairs = pltpu.SemaphoreType.DMA
    args = (
        col_slots, gains, lse, rev, bucket_row, router_grads, returned, mid, cotangent, queries, keys, values, attended,
        every_tok, weights, normed, grads, rx, ry, result,
    )
    return pl.pallas_call(
        back_kernel,
        out_shape=(
            shape((lines, width + 3 * early), low), shape((m, width), low), shape((m, width), low),
            shape((width, 3 * early + TILE), low),
            shape((count - 2 * SPAN, width), low), shape((SPAN, width), low),
            shape((rows, width), single), shape((rows, width), single),
            shape((fasts - 1, slows, 3 * m, width), low), shape((slows - 1, fasts, 3 * m, width), low),
            shape(result.shape, low), shape((slows - 1, m, width), low), shape((fasts - 1, m, width), low),
        ),
        in_specs=[in_vmem] * 6 + [anywhere] * 14,
        out_specs=(in_vmem,) * 3 + (anywhere,) * 10,
        scratch_shapes=[
            pltpu.VMEM((2, tile_kinds, TILE, TILE), single), pltpu.VMEM((2, tile_kinds, TILE, TILE), single),
            pltpu.VMEM((16, 4 * TILE), single), pltpu.VMEM((TILE, count), low), pltpu.VMEM((TILE, rows), single),
            pltpu.VMEM((16, 2 * TILE), single),
            pltpu.VMEM((rows, width), low), pltpu.VMEM((rows, width), low), pltpu.VMEM((count, width), low),
            pltpu.VMEM((count, width), low), pltpu.VMEM((8, width), single),
            pltpu.VMEM(every_tok.shape, low), pltpu.VMEM(weights.shape, low), pltpu.VMEM(normed.shape, low),
            vm(returned.shape, low), vm((rows, width), single), vm((rows, width), low), vm((rows, width), low),
            vm(keys.shape, low), vm(keys.shape, low), vm(attended.shape, single),
            vm((width, 3 * early + TILE), low),
            vm((rows, width), single), vm((rows, width), single),
            vm((slows, m, width), low), vm((fasts - 1, slows, m, width), low), vm((slows, m, width), low),
            vm((fasts, m, width), low), vm((slows - 1, fasts, m, width), low), vm((fasts, m, width), low),
            vm((shards, lines, width), low), vm((chips, lines, width), low),
            vm((chips, lines, width), low), vm((chips - 1, lines, width), low),
            vm((shards, lines, 3 * early), low), vm((chips, lines, 3 * early), low),
            vm((chips, lines, 3 * early), low), vm((chips - 1, lines, 3 * early), low),
            pairs((16,)), pairs((6,)), pairs((slows - 1,)), pairs((slows - 1,)), pairs((fasts - 1,)), pairs((fasts - 1,)),
            pairs((NEAR, 2)), pairs((NEAR, 2)), pairs((fasts - 1,)), pairs((fasts - 1,)),
            pairs((slows - 1,)), pairs((slows - 1,)), pairs((chips,)), pairs((chips,)), pairs((chips - 1,)),
            pairs((chips - 1,)), pairs((chips,)), pairs((chips,)), pairs((chips - 1,)), pairs((chips - 1,)),
        ],
        compiler_params=pltpu.CompilerParams(collective_id=4, has_side_effects=True, vmem_limit_bytes=vmem_cap),
        cost_estimate=pl.CostEstimate(flops=60_000_000_000, bytes_accessed=40_000_000, transcendentals=8_000_000),
        name="back",
    )(*args)


def places():
    rep, shard = lax.axis_index("rep"), lax.axis_index("shard")
    return rep, shard // 2, shard % 2, lax.axis_size("shard") // 2, rep % QUARTERS


def peer_lists():
    rep, chip, core, chips, quarter = places()
    along = [(rep, (chip + k) % chips * 2 + core) for k in range(1, chips)]
    across = [(rep - quarter + (quarter + j) % QUARTERS, chip * 2 + core) for j in range(1, QUARTERS)]
    twin = (rep, chip * 2 + 1 - core)
    return along, across, twin


def chip_across(chip, k):
    partner, bit = 0, 1
    while bit < lax.axis_size("shard") // 2:
        partner = partner + bit * ((chip // bit + k // bit) % 2)
        bit = bit * 2
    return partner


def result_peers(rep, chip, core, chosen):
    return [
        (k, side, (rep, chip_across(chip, k) * 2 + (side if k else 1 - core)))
        for k in chosen for side in range(2 if k else 1)
    ]


def result_slots(core, chosen):
    return [(k, side if k else 1 - core) for k in chosen for side in range(2 if k else 1)]


def greet(devices):
    barrier = pltpu.get_barrier_semaphore()
    for device in devices:
        pl.semaphore_signal(barrier, inc=1, device_id=device, device_id_type=mesh_ids)
    pl.semaphore_wait(barrier, len(devices))


def send(source, target, sems, device):
    return pltpu.make_async_remote_copy(
        src_ref=source, dst_ref=target, send_sem=sems[0], recv_sem=sems[1],
        device_id=device, device_id_type=mesh_ids,
    )


def rep_places():
    rep, reps = lax.axis_index("rep"), lax.axis_size("rep")
    fasts = QUARTERS if reps % (QUARTERS * QUARTERS) == 0 else 2
    return rep, rep // fasts, rep % fasts, reps // fasts, fasts


def reduce_kernel(
    gain_ref, col_ref, d_hbm, p_hbm, e_hbm, own_hbm, gres_hbm, tok_hbm, mid_hbm, gate_hbm, out_hbm, ret_hbm,
    ge_hbm, ra_hbm, rb_hbm, z_hbm,
    early_ref, late_ref, gt_hbm, mix_hbm, ka_hbm, la_hbm, kb_hbm, lb_hbm,
    d_own, half, hr, tr, mr, cr, zs, tz, z_last, z_above, z_all, last, above_in, gathered,
    p_own, p_half, p_sum, p_in, e_in, own, gres, tok, mid, gate, ret,
    a_own, a_in, a_sum, b_own, b_in, b_sum, gt_ref, mix_ref, out,
    loc, ps_s, ps_r, ds_s, ds_r, pz_s, pz_r, rr_s, rr_r, rz_s, rz_r, zr_s, zr_r, zh_s, zh_r, za_s, za_r,
    dh_s, dh_r, da_s, da_r, ea_s, ea_r, eb_s, eb_r, xs, xr,
):
    rep, chip, core, chips, quarter = places()
    along, across, twin = peer_lists()
    _, slow, fast, slows, fasts = rep_places()
    classes = lax.axis_size("rep") // QUARTERS
    here = chip * 2 + core
    beside = [(slow * fasts + (fast + j) % fasts, here) for j in range(1, fasts)]
    beyond = [((slow + j) % slows * fasts + fast, here) for j in range(1, slows)]
    above = [((rep // QUARTERS + k) % classes * QUARTERS + quarter, here) for k in range(1, classes)]
    wide = lambda held: held.astype(single)
    lines = ge_hbm.shape[2] // 8
    pending = []

    def load(source, target, index, sems=loc):
        copy = pltpu.make_async_copy(source, target, sems.at[index])
        copy.start()
        return copy

    def go(source, target, sems, device):
        copy = send(source, target, sems, device)
        copy.start()
        pending.append(copy)

    def landed(piece, sems):
        send(piece, piece, sems, twin).wait_recv()

    early_in = load(z_hbm, zs, 12)
    a_loads = [load(ge_hbm.at[:, fast, pl.ds(2 * lines, 3 * lines)], a_own, 0), load(ra_hbm, a_in, 1)]
    halves = [load(d_hbm.at[:, core], d_own, 5), load(p_hbm.at[:, core], p_own, 4)]
    b_loads = [load(ge_hbm.at[slow, :, pl.ds(5 * lines, 3 * lines)], b_own, 2), load(rb_hbm, b_in, 3)]
    rest = [
        load(ret_hbm.at[chip_across(chip, k)], ret.at[chip_across(chip, k)], 13 + k) for k in range(NEAR)
    ] + [
        load(mid_hbm, mid, 7), load(gate_hbm, gate, 8), load(own_hbm, own, 9),
        load(gres_hbm, gres, 10), load(tok_hbm, tok, 11),
    ]
    others = [(rep, (here + k) % (2 * chips)) for k in range(1, 2 * chips)]
    greets = list(others)
    for device in across + beside + beyond + above:
        greets.append(device)
    greet(greets)
    for k in range(chips):
        go(d_hbm.at[k, 1 - core], half.at[k], (ds_s.at[k], ds_r.at[k]), twin)
    go(p_hbm.at[:, 1 - core], p_half, (ps_s.at[0], ps_r.at[0]), twin)
    go(e_hbm, e_in, (ps_s.at[1], ps_r.at[1]), twin)
    for k, side, device in result_peers(rep, chip, core, range(NEAR, chips)):
        go(out_hbm.at[chip_across(chip, k), side], ret.at[chip, core], (xs.at[k - NEAR, side], xr.at[k - NEAR, core]), device)
    early_in.wait()
    for j, device in enumerate(across):
        go(zs.at[(quarter + j + 1) % QUARTERS], tz.at[j], (zr_s.at[j], zr_r.at[j]), device)

    for copy in a_loads:
        copy.wait()
    for t in range(slows):
        total = wide(a_own[t])
        for j in range(fasts - 1):
            total = total + wide(a_in[j, t])
        a_sum[t] = total.astype(low)
    for copy in halves:
        copy.wait()
    for k in range(chips):
        landed(half.at[k], (ds_s.at[k], ds_r.at[k]))
        for t in range(QUARTERS):
            hr[t, k] = (wide(d_own[k, t]) + wide(half[k, t])).astype(low)
    for j, device in enumerate(across):
        go(hr.at[(quarter + j + 1) % QUARTERS], tr.at[j], (rr_s.at[j], rr_r.at[j]), device)
    landed(p_half, (ps_s.at[0], ps_r.at[0]))
    for k in range(chips):
        p_sum[k] = (wide(p_own[k]) + wide(p_half[k])).astype(low)
    for k, device in enumerate(along):
        go(p_sum.at[(chip + k + 1) % chips], p_in.at[k], (pz_s.at[k], pz_r.at[k]), device)
    for copy in b_loads:
        copy.wait()
    for t in range(fasts):
        total = wide(b_own[t])
        for j in range(slows - 1):
            total = total + wide(b_in[j, t])
        b_sum[t] = total.astype(low)
    def class_sum(held, came, s_sems, r_sems):
        total = wide(held[...])
        for j, device in enumerate(above):
            go(held, came.at[j], (s_sems.at[j], r_sems.at[j]), device)
        for j in range(classes - 1):
            landed(came.at[j], (s_sems.at[j], r_sems.at[j]))
            total = total + wide(came[j])
        return total.astype(low)

    def hand_out(pieces, s_sems, r_sems):
        for j, device in enumerate(across):
            go(pieces.at[quarter], pieces.at[quarter], (s_sems.at[j], r_sems.at[j]), device)

    def handed(pieces, s_sems, r_sems):
        for j in range(QUARTERS - 1):
            landed(pieces.at[(quarter + QUARTERS - j - 1) % QUARTERS], (s_sems.at[j], r_sems.at[j]))

    for j in range(QUARTERS - 1):
        landed(tz.at[j], (zr_s.at[j], zr_r.at[j]))
    total = wide(zs[quarter])
    for j in range(QUARTERS - 1):
        total = total + wide(tz[j])
    z_last[...] = total.astype(low)
    z_all[quarter] = class_sum(z_last, z_above, zh_s, zh_r) if classes > 1 else z_last[...]
    hand_out(z_all, za_s, za_r)

    for copy in rest:
        copy.wait()
    writes = [load(a_sum.at[slow], ka_hbm, 0, out), load(b_sum.at[fast], kb_hbm, 1, out)]

    for j in range(QUARTERS - 1):
        landed(tr.at[j], (rr_s.at[j], rr_r.at[j]))
    for j, device in enumerate(beyond):
        go(a_sum.at[(slow + j + 1) % slows], la_hbm.at[j], (ea_s.at[j], ea_r.at[j]), device)
    for j, device in enumerate(beside):
        go(b_sum.at[(fast + j + 1) % fasts], lb_hbm.at[j], (eb_s.at[j], eb_r.at[j]), device)

    for k in range(chips):
        total = wide(hr[quarter, k])
        for j in range(QUARTERS - 1):
            total = total + wide(tr[j, k])
        mr[k] = total.astype(low)
    for k, device in enumerate(along):
        go(mr.at[(chip + k + 1) % chips], cr.at[k], (rz_s.at[k], rz_r.at[k]), device)

    for k in range(chips - 1):
        landed(p_in.at[k], (pz_s.at[k], pz_r.at[k]))
    landed(e_in, (ps_s.at[1], ps_r.at[1]))
    total = wide(p_sum[chip])
    for k in range(chips - 1):
        total = total + wide(p_in[k])
    grads = own[...] + jnp.concatenate([total, wide(e_in[...])], axis=0)
    gt_ref[...] = gres[...] + norm_pull(grads, wide(tok[...]), gain_ref[0:1, :])
    writes.append(load(gt_ref, gt_hbm, 2, out))

    for k in range(chips - 1):
        landed(cr.at[k], (rz_s.at[k], rz_r.at[k]))
    total = wide(mr[chip])
    for k in range(chips - 1):
        total = total + wide(cr[k])
    last[...] = total.astype(low)
    gathered[quarter] = class_sum(last, above_in, dh_s, dh_r) if classes > 1 else last[...]
    hand_out(gathered, da_s, da_r)
    for k, side in result_slots(core, range(NEAR, chips)):
        landed(ret.at[chip_across(chip, k), side], (xs.at[k - NEAR, side], xr.at[k - NEAR, side]))
    slots = lax.broadcasted_iota(jnp.int32, (tok.shape[0], 2 * chips * ret.shape[2]), 1)
    chosen = nn((slots == col_ref[:, 0:1]).astype(low), ret[...].reshape(slots.shape[1], tok.shape[1]))
    mix_ref[...] = (mid[...] + gate[:, 0:1] * chosen).astype(low)
    writes.append(load(mix_ref, mix_hbm, 3, out))
    handed(z_all, za_s, za_r)
    early_ref[...] = z_all[...]
    handed(gathered, da_s, da_r)
    late_ref[...] = gathered[...]
    for j in range(slows - 1):
        landed(la_hbm.at[j], (ea_s.at[j], ea_r.at[j]))
    for j in range(fasts - 1):
        landed(lb_hbm.at[j], (eb_s.at[j], eb_r.at[j]))
    for copy in writes:
        copy.wait()
    for copy in pending:
        copy.wait_send()


def reduce_all(gains, col_slots, dense, prompt_part, near_part, own, gres, tokens, mid, gate, result, returned, grads, ra, rb, z):
    chips = lax.axis_size("shard") // 2
    classes = lax.axis_size("rep") // QUARTERS
    slows, fasts, eighths = grads.shape[:3]
    part = (3 * eighths // 8, mid.shape[1])
    rows, width = mid.shape
    lines, lanes = dense.shape[3:]
    wider = z.shape[2]
    shape = jax.ShapeDtypeStruct
    sem = pltpu.SemaphoreType.DMA
    vm = pltpu.VMEM
    count, others = chips - 1, QUARTERS - 1
    ours = prompt_part.shape[2:]
    extra = max(classes - 1, 1)
    args = (gains, col_slots, dense, prompt_part, near_part, own, gres, tokens, mid, gate, result, returned, grads, ra, rb, z)
    return pl.pallas_call(
        reduce_kernel,
        out_shape=(
            shape((QUARTERS, lines, wider), low), shape((QUARTERS, lines, lanes), low),
            shape((rows, width), single), shape((rows, width), low),
            shape(part, low), shape((slows - 1,) + part, low), shape(part, low), shape((fasts - 1,) + part, low),
        ),
        in_specs=[in_vmem] * 2 + [anywhere] * 14,
        out_specs=(in_vmem,) * 2 + (anywhere,) * 6,
        scratch_shapes=[
            vm((chips, QUARTERS, lines, lanes), low), vm((chips, QUARTERS, lines, lanes), low),
            vm((QUARTERS, chips, lines, lanes), low), vm((others, chips, lines, lanes), low),
            vm((chips, lines, lanes), low), vm((count, lines, lanes), low),
            vm((QUARTERS, lines, wider), low), vm((others, lines, wider), low), vm((lines, wider), low),
            vm((extra, lines, wider), low), vm((QUARTERS, lines, wider), low),
            vm((lines, lanes), low), vm((extra, lines, lanes), low), vm((QUARTERS, lines, lanes), low),
            vm((chips,) + ours, low), vm((chips,) + ours, low), vm((chips,) + ours, low), vm((count,) + ours, low),
            vm(near_part.shape, low), vm((rows, width), single), vm((rows, width), single), vm((rows, width), low),
            vm((rows, width), single), vm(gate.shape, single), vm(result.shape, low),
            vm((slows,) + part, low), vm(ra.shape, low), vm((slows,) + part, low),
            vm((fasts,) + part, low), vm(rb.shape, low), vm((fasts,) + part, low),
            vm((rows, width), single), vm((rows, width), low), sem((4,)),
            sem((13 + NEAR,)), sem((2,)), sem((2,)), sem((chips,)), sem((chips,)), sem((count,)), sem((count,)),
            sem((others,)), sem((others,)), sem((count,)), sem((count,)),
            sem((others,)), sem((others,)), sem((extra,)), sem((extra,)), sem((others,)), sem((others,)),
            sem((extra,)), sem((extra,)), sem((others,)), sem((others,)),
            sem((slows - 1,)), sem((slows - 1,)), sem((fasts - 1,)), sem((fasts - 1,)),
            sem((chips - NEAR, 2)), sem((chips - NEAR, 2)),
        ],
        compiler_params=pltpu.CompilerParams(collective_id=1, has_side_effects=True, vmem_limit_bytes=vmem_cap),
        cost_estimate=pl.CostEstimate(flops=0, bytes_accessed=200_000_000, transcendentals=0),
        name="reduce_all",
    )(*args)


def finish_kernel(
    kx_ref, lx_ref, ky_ref, ly_ref, ka_ref, la_ref, kc_ref, lc_ref, kb_ref, lb_ref, early_ref, late_ref, small_ref, gt_ref, mix_ref, *outs
):
    ea_ref, eb_ref, q_ref, k_ref, v_ref, o_ref, router_ref, attn_ref, moe_ref, table_ref, gt_out, mix_out = outs
    gt_out[...] = gt_ref[...]
    mix_out[...] = mix_ref[...]
    width = q_ref.shape[2]
    experts = router_ref.shape[0]
    step = pl.program_id(0)

    def total(held, came):
        value = held[...].reshape(ea_ref.shape).astype(single)
        for j in range(came.shape[0]):
            value = value + came[j].reshape(ea_ref.shape).astype(single)
        return value

    for target, first, last, sources in (
        (ea_ref, 0, 0, (kx_ref, lx_ref)), (ea_ref, 1, 1, (ky_ref, ly_ref)), (ea_ref, 2, 3, (ka_ref, la_ref)),
        (eb_ref, 0, 0, (kc_ref, lc_ref)), (eb_ref, 1, 3, (kb_ref, lb_ref)),
    ):

        @pl.when((step >= first) & (step <= last))
        def _():
            target[...] = total(*sources)

    half = width // 2
    o_ref[...] = early_ref[:, :, :width].astype(single)
    for i, ref in enumerate((q_ref, k_ref, v_ref)):
        ref[:, :, :half] = early_ref[:, :, width + i * half : width + (i + 1) * half].astype(single)
        ref[:, :, half:] = late_ref[:, :, i * half : (i + 1) * half].astype(single)

    @pl.when(pl.program_id(0) == 0)
    def _():
        small = small_ref[...].astype(single).reshape(router_ref.shape[1], TILE)
        turned = small.T
        router_ref[...] = turned[:experts]
        attn_ref[...] = turned[experts : experts + 1]
        moe_ref[...] = turned[experts + 1 : experts + 2]
        table_ref[...] = small[: table_ref.shape[0], experts + 2 : experts + 2 + table_ref.shape[1]]


def finish(kx, lx, ky, ly, ka, la, kb, lb, early, late, grad_tokens, mixed, experts, table_rows, heads):
    shape = jax.ShapeDtypeStruct
    _, lines, wider = early.shape
    lanes = late.shape[2]
    width = kb.shape[1]
    rows = QUARTERS * lines
    steps = QUARTERS
    m = kx.shape[0]
    ka, kb = (part.reshape(3, m, width) for part in (ka, kb))
    la, lb = (part.reshape(-1, 3, m, width) for part in (la, lb))
    block = lambda pick: pl.BlockSpec((1, m, width), lambda i: (pick(i), 0, 0))
    blocks = lambda array, pick: pl.BlockSpec((array.shape[0], 1, m, width), lambda i: (0, pick(i), 0, 0))
    strip, rest = (lambda i: jnp.maximum(i - 2, 0)), (lambda i: jnp.maximum(i - 1, 0))
    part = pl.BlockSpec((1, lines, width), lambda i: (i, 0, 0))
    once = lambda *dims: pl.BlockSpec(dims, lambda i: (0,) * len(dims))
    some = pl.BlockSpec((mixed.shape[0] // steps, width), lambda i: (i, 0))
    return pl.pallas_call(
        finish_kernel,
        grid=(steps,),
        out_shape=(
            shape((m, steps * width), single), shape((steps * m, width), single), *(shape((QUARTERS, lines, width), single),) * 4,
            shape((experts, rows), single), shape((1, rows), single), shape((1, rows), single),
            shape((table_rows, heads), single), shape(grad_tokens.shape, single), shape(mixed.shape, low),
        ),
        in_specs=[
            once(*kx.shape), once(*lx.shape), once(*ky.shape), once(*ly.shape),
            block(strip), blocks(la, strip), block(lambda i: 2), blocks(la, lambda i: 2), block(rest), blocks(lb, rest),
            pl.BlockSpec((1, lines, wider), lambda i: (i, 0, 0)), pl.BlockSpec((1, lines, lanes), lambda i: (i, 0, 0)),
            pl.BlockSpec((QUARTERS, lines, TILE), lambda i: (0, 0, lanes // TILE - 1)), some, some,
        ],
        out_specs=(
            pl.BlockSpec((m, width), lambda i: (0, i)), pl.BlockSpec((m, width), lambda i: (i, 0)),
            part, part, part, part, once(experts, rows), once(1, rows), once(1, rows), once(table_rows, heads),
            some, some,
        ),
        compiler_params=pltpu.CompilerParams(vmem_limit_bytes=vmem_cap),
        cost_estimate=pl.CostEstimate(flops=0, bytes_accessed=12_000_000, transcendentals=0),
        name="finish",
    )(kx, lx, ky, ly, ka, la, ka, la, kb, lb, early, late, late, grad_tokens, mixed)


def local(
    tokens,
    routes,
    slot_ids,
    w_query,
    w_key,
    w_value,
    w_output,
    w_router,
    norm_attn,
    norm_moe,
    rel_table,
    w_in,
    w_out,
    cotangent,
):
    shard_count = lax.axis_size("shard")
    token_rows, model_width = tokens.shape
    prompt_len = PR_DEV * shard_count
    weight_rows, expert_count = w_router.shape
    table_rows, head_count = rel_table.shape
    capacity = 2 * token_rows // expert_count
    slot_count = expert_count * capacity

    rows_small = (w_router.T, norm_attn, norm_moe, rel_table)
    bucket_row = jnp.asarray(np.tile(distance_buckets(table_rows * shard_count), (8, 1)), jnp.int32)
    (
        lse, rev, gate, col_slots, gains, slots_out, grad_in, weights, every_tok, small, normed, queries, keys, values,
        attended, mid,
    ) = front(routes, slot_ids, bucket_row, cotangent, (w_query, w_key, w_value, w_output), tokens, rows_small, slot_count)
    by_chip = (shard_count // 2, 2, capacity, model_width)
    grad_back, result, grads, rx, ry, router_grads = moe(
        slots_out.reshape(by_chip), grad_in.reshape(by_chip), small, w_in[0], w_out[0]
    )
    early_part, kx, ky, dense, prompt_part, near_part, grad_own, grad_resid, ra, rb, returned, lx, ly = back(
        grad_back.reshape(slot_count, model_width), col_slots, mid, cotangent, gains, every_tok, weights,
        (normed, queries, keys, values, attended, lse, rev), bucket_row, router_grads, grads, rx, ry, result,
    )
    chips = shard_count // 2
    lines = weight_rows // QUARTERS
    early, late, grad_tokens, mixed, ka, la, kb, lb = reduce_all(
        gains, col_slots, dense.reshape(chips, 2, QUARTERS, lines, -1),
        prompt_part.reshape(chips, 2, PR_DEV, model_width), near_part, grad_own, grad_resid, tokens, mid, gate,
        result, returned, grads, ra, rb,
        early_part.reshape(QUARTERS, lines, -1),
    )
    in_grad, out_grad, gq, gk, gv, go, router, gain_attn, gain_moe, table, grad_tokens, mixed = finish(
        kx, lx, ky, ly, ka, la, kb, lb, early, late, grad_tokens, mixed, expert_count, table_rows, head_count
    )
    return (
        mixed,
        grad_tokens,
        *(part.reshape(weight_rows, model_width) for part in (gq, gk, gv, go)),
        router.T,
        gain_attn[0],
        gain_moe[0],
        table,
        in_grad[None],
        out_grad[None],
    )


def solution(mesh):
    return jax.shard_map(
        local,
        mesh=mesh,
        in_specs=(
            P(("rep", "shard"), None),
            P(("rep", "shard")),
            P(("rep", "shard")),
            P("shard", None),
            P("shard", None),
            P("shard", None),
            P("shard", None),
            P("shard", None),
            P("shard"),
            P("shard"),
            P("shard", None),
            P("shard", None, None),
            P("shard", None, None),
            P(("rep", "shard"), None),
        ),
        out_specs=(
            P(("rep", "shard"), None),
            P(("rep", "shard"), None),
            P("shard", None),
            P("shard", None),
            P("shard", None),
            P("shard", None),
            P("shard", None),
            P("shard"),
            P("shard"),
            P("shard", None),
            P("shard", "rep", None),
            P("shard", "rep", None),
        ),
        check_vma=False,
    )
```

```python
import jax
import jax.numpy as jnp
import numpy as np
from jax import lax
from jax.experimental import pallas as pl
from jax.experimental.pallas import tpu as pltpu
from jax.sharding import PartitionSpec as P

PR_DEV = 128
TILE = 128
SPAN = 2 * TILE
NEAR = 3
QUARTERS = 4
far_before, far_after, causal_tile, hidden_tile, tile_kinds = 3, 4, 5, 6, 7
vmem_cap = 60 * 1024 * 1024
mesh_ids = pl.DeviceIdType.MESH
bucket_edges = (12, 16, 23, 32, 46, 64, 91)
norm_epsilon = 1e-06
masked_score = -1e30
low, single = jnp.bfloat16, jnp.float32
in_vmem = pl.BlockSpec(memory_space=pltpu.VMEM)
anywhere = pl.BlockSpec(memory_space=pl.ANY)


def inverse_rms(values):
    return lax.rsqrt(jnp.mean(values * values, axis=-1, keepdims=True) + norm_epsilon)


def norm_pull(grad, values, gain):
    scale = inverse_rms(values)
    pulled = grad * gain
    mean = jnp.mean(pulled * values, axis=-1, keepdims=True)
    return scale * pulled - values * (scale * scale * scale * mean)


def nt(left, right):
    return lax.dot_general(left, right, (((1,), (1,)), ((), ())), preferred_element_type=single)


def tn(left, right):
    return lax.dot_general(left, right, (((0,), (0,)), ((), ())), preferred_element_type=single)


def nn(left, right):
    return jnp.dot(left, right, preferred_element_type=single)


def thirds_of(values):
    first = values.astype(low)
    rest = values - first.astype(single)
    second = rest.astype(low)
    return first, second, (rest - second.astype(single)).astype(low)


def fill_tiles(tiles_ref, rev_row, low, high):
    spread = jnp.broadcast_to(rev_row, (TILE, 4 * TILE))
    rolled = pltpu.roll(spread, 0, 1, stride=1, stride_axis=0)
    keys = lax.broadcasted_iota(jnp.int32, (TILE, TILE), 0)
    rows = lax.broadcasted_iota(jnp.int32, (TILE, TILE), 1)
    tiles_ref[0] = rolled[:, TILE : 2 * TILE]
    tiles_ref[1] = rolled[:, :TILE]
    tiles_ref[2] = rolled[:, 3 * TILE :]
    tiles_ref[far_before] = jnp.broadcast_to(low, (TILE, TILE))
    tiles_ref[far_after] = jnp.broadcast_to(high, (TILE, TILE))
    tiles_ref[causal_tile] = jnp.where(keys <= rows, rolled[:, :TILE], masked_score)
    tiles_ref[hidden_tile] = jnp.full((TILE, TILE), masked_score, jnp.float32)


def prompt_tile(block, chunk, shard_id, block_count):
    if chunk == 0:
        gap = block - shard_id
        far = jnp.where(gap < 0, far_before, far_after)
        return jnp.where(jnp.abs(gap) <= 1, gap + 1, far)
    if chunk == 1 and block == block_count - 1:
        return jnp.where(shard_id % 2 == 0, 0, far_before)
    return far_before


def local_tile(block, chunk, shard_id):
    if block >= 2:
        return ((causal_tile, 0), (hidden_tile, causal_tile))[block - 2][chunk]
    kind = 0 if (block, chunk) == (1, 0) else far_before
    return jnp.where(shard_id % 2 == 1, kind, hidden_tile)


def prompt_grid(part, shard_id, block_count):
    return [
        [(side, prompt_tile(2 * part + half, chunk, shard_id, block_count)) for side in range(2) for chunk in range(3)]
        for half in range(2)
    ]


def local_grid(part, shard_id):
    return [
        [(side, local_tile(2 * part + half, chunk, shard_id)) for side in range(2) for chunk in range(2)]
        for half in range(2)
    ]


def tile_of(values, i, j):
    return values[i * TILE : (i + 1) * TILE, j * TILE : (j + 1) * TILE]


def with_bias(scores, tiles_ref, grid):
    lines = [
        jnp.concatenate(
            [tile_of(scores, i, j) + tiles_ref[side, kind] for j, (side, kind) in enumerate(row)], axis=1
        )
        for i, row in enumerate(grid)
    ]
    return jnp.concatenate(lines, axis=0)


def both_heads(values):
    first = head_mask(values.shape[0], 0)
    none = jnp.zeros_like(values)
    return jnp.concatenate([jnp.where(first, values, none), jnp.where(first, none, values)], axis=0)


def continuation(values, axis):
    rows = values.shape[axis] // 2
    pick = (lambda a, b: values[:, a:b]) if axis else (lambda a, b: values[a:b])
    return jnp.concatenate([pick(PR_DEV, rows), pick(rows + PR_DEV, 2 * rows)], axis=axis)


def fold8(values):
    return values.reshape(values.shape[0] // 8, 8, values.shape[1])


def head_mask(rows, side):
    lanes = lax.broadcasted_iota(jnp.int32, (rows, TILE), 1)
    return (lanes < TILE // 2) if side == 0 else (lanes >= TILE // 2)


def distance_buckets(bucket_count):
    steps = np.arange(4 * TILE)
    gap = -np.where(steps < 2 * TILE, steps, steps - 4 * TILE)
    size = np.abs(gap)
    far = sum((size >= edge).astype(np.int64) for edge in bucket_edges)
    exact = bucket_count // 4
    return np.where(gap > 0, bucket_count // 2, 0) + np.where(size < exact, size, exact + far)


def front_kernel(
    route_ref, slot_ref, bucket_ref, cot_ref, router_ref, first_ref, second_ref, table_ref, wq_hbm, wk_hbm, wv_hbm, wo_hbm, tok_hbm,
    lse_ref, rev_ref, gate_ref, col_ref, gain_ref, x_ref, gin_hbm, w_hbm, every_hbm, small_hbm,
    n_hbm, q_hbm, k_hbm, v_hbm, o_hbm, mid_hbm,
    tiles, vt, sp, sl, gbuf, w_ref, every_ref, small_ref, tok_ref, shard_w, little,
    n_ref, nt_ref, q_ref, k_ref, v_ref, ot_ref, mid_ref,
    gs, gr, loc, wz_s, wz_r, tz_s, tz_r, sz_s, sz_r, wr_s, wr_r, wt_s, wt_r, tt_s, tt_r, st_s, st_r, et_s, et_r,
):
    rep, chip, core, chips, quarter = places()
    along, across, twin = peer_lists()
    shards = chips * 2
    shard_id = chip * 2 + core
    rows, width = tok_ref.shape
    experts = shards
    blocks = every_ref.shape[0] // TILE - 4
    half = TILE // 2
    heads_held = rev_ref.shape[0]
    lines = shard_w.shape[1]
    rest_rows = rows - PR_DEV
    prompt_len = blocks * TILE
    others = [(rep, (shard_id + k) % shards) for k in range(1, shards)]

    def w_rows(source, side):
        return pl.ds(pl.multiple_of((source * 2 + side) * lines, lines), lines)

    def t_rows(source, side):
        return every_ref.at[pl.ds(pl.multiple_of((source * 2 + side) * PR_DEV, PR_DEV), PR_DEV)]

    loads = [
        pltpu.make_async_copy(source, shard_w.at[i], loc.at[i])
        for i, source in enumerate((wq_hbm, wk_hbm, wv_hbm, wo_hbm))
    ] + [pltpu.make_async_copy(tok_hbm, tok_ref, loc.at[4])]
    for copy in loads:
        copy.start()
    gains = [ref[...].astype(single).reshape(1, lines) for ref in (first_ref, second_ref)]
    short = jnp.zeros((2 * TILE // 8 - 2 - experts, lines), single)
    turned = jnp.concatenate([router_ref[...].astype(single), *gains, short], axis=0).astype(low)
    lane = lambda count: lax.broadcasted_iota(jnp.int32, (count, TILE), 1)
    line = lambda count: lax.broadcasted_iota(jnp.int32, (count, TILE), 0)
    left = tn(turned, (line(turned.shape[0]) == lane(turned.shape[0])).astype(low))
    heads = table_ref.shape[1]
    table = nn(table_ref[...], (line(heads) + experts + 2 == lane(heads)).astype(low))
    below = jnp.zeros((lines - table.shape[0], TILE), single)
    little[...] = (left + jnp.concatenate([table, below], axis=0)).astype(low)
    greeted = [twin] + along
    for device in across + [(rep, (chip + k) % chips * 2 + 1 - core) for k in range(1, chips)]:
        greeted.append(device)
    greet(greeted)
    started = []

    def go(source, target, sems, device):
        copy = send(source, target, sems, device)
        copy.start()
        started.append(copy)

    def landed(piece, sems):
        send(piece, piece, sems, twin).wait_recv()

    for copy in loads[:4]:
        copy.wait()
    mine = w_rows(chip, core)
    prompt, rest = tok_ref.at[pl.ds(0, PR_DEV)], tok_ref.at[pl.ds(PR_DEV, rest_rows)]
    for k, device in enumerate(along):
        go(shard_w.at[quarter], w_ref.at[quarter, mine], (wz_s.at[k], wz_r.at[k]), device)
        go(little, small_ref.at[mine], (sz_s.at[k], sz_r.at[k]), device)
    go(little, small_ref.at[mine], (st_s.at[0], st_r.at[0]), twin)
    loads[4].wait()
    go(rest, every_ref.at[pl.ds(prompt_len, rest_rows)], (et_s.at[0], et_r.at[0]), twin)
    go(prompt, t_rows(chip, core), (tt_s.at[0], tt_r.at[0]), twin)
    go(shard_w, w_ref.at[:, mine], (wt_s.at[0], wt_r.at[0]), twin)
    w_ref[:, mine, :] = shard_w[...]
    small_ref[mine, :] = little[...]
    every_ref[pl.ds(pl.multiple_of(shard_id * PR_DEV, PR_DEV), PR_DEV), :] = tok_ref[:PR_DEV, :]
    every_ref[prompt_len + rest_rows :, :] = tok_ref[PR_DEV:, :]
    routes = route_ref[...].reshape(1, rows)
    dispatch = routes * (x_ref.shape[0] // experts) + slot_ref[...].reshape(1, rows)
    ints = jnp.concatenate([routes, dispatch, jnp.zeros((6, rows), jnp.int32)], axis=0).astype(single).T
    route_col = ints[:, 0:1].astype(jnp.int32)
    col_ref[...] = jnp.broadcast_to(ints[:, 1:2].astype(jnp.int32), col_ref.shape)
    slots = lax.broadcasted_iota(jnp.int32, (x_ref.shape[0], rows), 0)
    place = (slots == dispatch).astype(low)
    gbuf[...] = nn(place, cot_ref[...]).astype(low).reshape(gbuf.shape)
    own_g = pltpu.make_async_copy(gbuf.at[shard_id], gin_hbm.at[shard_id], loc.at[6])
    own_g.start()

    for k in range(1, chips):
        source = (chip + chips - k) % chips
        piece = w_ref.at[quarter, w_rows(source, core)]
        landed(piece, (wz_s.at[k - 1], wz_r.at[k - 1]))
        for j, device in enumerate(across):
            go(piece, piece, (wr_s.at[k - 1, j], wr_r.at[k - 1, j]), device)
        go(prompt, t_rows(chip, core), (tz_s.at[k - 1], tz_r.at[k - 1]), along[k - 1])
    for k in range(1, chips):
        source = (chip + chips - k) % chips
        piece = small_ref.at[w_rows(source, core)]
        landed(piece, (sz_s.at[k - 1], sz_r.at[k - 1]))
        go(piece, piece, (st_s.at[k], st_r.at[k]), twin)
    for k in range(1, chips):
        source = (chip + chips - k) % chips
        piece = t_rows(source, core)
        landed(piece, (tz_s.at[k - 1], tz_r.at[k - 1]))
        go(piece, piece, (tt_s.at[k], tt_r.at[k]), twin)
    for k, device in enumerate(others):
        go(gbuf.at[device[1]], gin_hbm.at[shard_id], (gs.at[k], gr.at[k]), device)
    for k in range(chips):
        source = (chip + chips - k) % chips
        landed(small_ref.at[w_rows(source, 1 - core)], (st_s.at[k], st_r.at[k]))
    writes = []

    def write(source, target):
        writes.append(pltpu.make_async_copy(source, target, loc.at[7 + len(writes)]))
        writes[-1].start()

    write(small_ref, small_hbm)

    small_t = small_ref[...].astype(single).T
    gain_attn = small_t[experts : experts + 1]
    gain_moe = small_t[experts + 1 : experts + 2]
    gain_ref[...] = jnp.concatenate([gain_attn, gain_moe, jnp.zeros((6, width), single)], axis=0)
    shard_rows = width // shards
    table_rows = 2 * TILE // 8 // shards
    owner = lax.broadcasted_iota(jnp.int32, (shards, shard_rows, 4 * TILE), 0)
    offset = lax.broadcasted_iota(jnp.int32, (shards, shard_rows, 4 * TILE), 1)
    held = jnp.where(offset < table_rows, owner * table_rows + offset, -1).reshape(width, 4 * TILE)
    hot = (held == bucket_ref[0:1, :]).astype(low)
    table_t = small_t[experts + 2 : experts + 2 + heads_held].astype(low)
    rev_ref[...] = nn(table_t, hot)

    for k in range(chips):
        source = (chip + chips - k) % chips
        landed(t_rows(source, 1 - core), (tt_s.at[k], tt_r.at[k]))
    landed(every_ref.at[pl.ds(prompt_len, rest_rows)], (et_s.at[0], et_r.at[0]))
    write(every_ref, every_hbm)

    @pl.loop(0, every_ref.shape[0] // SPAN)
    def scale(part):
        span = pl.ds(pl.multiple_of(part * SPAN, SPAN), SPAN)
        values = every_ref[span, :].astype(single)
        normed = values * inverse_rms(values) * gain_attn
        n_ref[span, :] = normed.astype(low)
        nt_ref[:, span] = normed.T.astype(low)

    write(nt_ref, n_hbm)
    for k in range(1, chips):
        source = (chip + chips - k) % chips
        for j in range(1, QUARTERS):
            piece = w_ref.at[(quarter + QUARTERS - j) % QUARTERS, w_rows(source, core)]
            landed(piece, (wr_s.at[k - 1, j - 1], wr_r.at[k - 1, j - 1]))
        piece = w_ref.at[:, w_rows(source, core)]
        go(piece, piece, (wt_s.at[k], wt_r.at[k]), twin)
    for k in range(chips):
        source = (chip + chips - k) % chips
        landed(w_ref.at[:, w_rows(source, 1 - core)], (wt_s.at[k], wt_r.at[k]))
    write(w_ref, w_hbm)

    k_ref[...] = nn(n_ref[...], w_ref[1]).astype(low)
    v_ref[...] = nn(n_ref[...], w_ref[2]).astype(low)

    own = pl.ds(pl.multiple_of(shard_id * TILE, TILE), TILE)
    normed = jnp.concatenate([n_ref[own, :], n_ref[(blocks + 2) * TILE :, :]], axis=0)
    q_ref[...] = (nn(normed, w_ref[0]).astype(low) * jnp.asarray(0.125, low)).astype(low)
    write(k_ref, k_hbm)
    write(v_ref, v_hbm)
    write(q_ref, q_hbm)

    @pl.loop(0, width // TILE)
    def pair_loop(pair):
        cols = pl.ds(pl.multiple_of(pair * TILE, TILE), TILE)
        vt[...] = v_ref[:, cols].T
        q_both = both_heads(q_ref[:, cols])
        q_local = continuation(q_both, 0)
        for side in range(2):
            rev_row = rev_ref[pl.ds(pair * 2 + side, 1), :]
            fill_tiles(tiles.at[side], rev_row, rev_row[:, SPAN - 1 : SPAN], rev_row[:, SPAN : SPAN + 1])
        top = jnp.full((8, 2 * rows), masked_score, single)
        for part in range(blocks // 2):
            keys = slice(part * SPAN, (part + 1) * SPAN)
            scores = with_bias(nt(k_ref[keys, cols], q_both), tiles, prompt_grid(part, shard_id, blocks))
            sp[keys, :] = scores
            top = jnp.maximum(top, jnp.max(fold8(scores), axis=0))
        local = continuation(top, 1)
        for part in range(2):
            keys = slice(part * SPAN, (part + 1) * SPAN)
            held = slice((blocks // 2 + part) * SPAN, (blocks // 2 + part + 1) * SPAN)
            scores = with_bias(nt(k_ref[held, cols], q_local), tiles, local_grid(part, shard_id))
            sl[keys, :] = scores
            local = jnp.maximum(local, jnp.max(fold8(scores), axis=0))
        rest = rows - PR_DEV
        top = jnp.concatenate(
            [top[:, :PR_DEV], local[:, :rest], top[:, rows : rows + PR_DEV], local[:, rest:]], axis=1
        )
        top = jnp.max(top, axis=0, keepdims=True)
        total = jnp.zeros((8, 2 * rows), single)
        summed = [jnp.zeros((half, rows), single)] * 2
        for part in range(blocks // 2):
            keys = slice(part * SPAN, (part + 1) * SPAN)
            weights = jnp.exp(sp[keys, :] - top)
            total = total + jnp.sum(fold8(weights), axis=0)
            weights = weights.astype(low)
            for side in range(2):
                heads = slice(side * half, (side + 1) * half)
                summed[side] = summed[side] + nn(vt[heads, keys], weights[:, side * rows : (side + 1) * rows])
        top_local, total_local = continuation(top, 1), continuation(total, 1)
        summed_local = [part_sum[:, PR_DEV:] for part_sum in summed]
        for part in range(2):
            keys = slice(part * SPAN, (part + 1) * SPAN)
            held = slice((blocks // 2 + part) * SPAN, (blocks // 2 + part + 1) * SPAN)
            weights = jnp.exp(sl[keys, :] - top_local)
            total_local = total_local + jnp.sum(fold8(weights), axis=0)
            weights = weights.astype(low)
            for side in range(2):
                heads = slice(side * half, (side + 1) * half)
                summed_local[side] = summed_local[side] + nn(
                    vt[heads, held], weights[:, side * rest : (side + 1) * rest]
                )
        for side in range(2):
            head = pair * 2 + side
            ours = slice(side * rows, (side + 1) * rows)
            sums = jnp.concatenate(
                [total[:, side * rows : side * rows + PR_DEV], total_local[:, side * rest : (side + 1) * rest]], axis=1
            )
            sums = jnp.sum(sums, axis=0, keepdims=True)
            mixed = jnp.concatenate([summed[side][:, :PR_DEV], summed_local[side]], axis=1)
            ot_ref[pl.ds(pl.multiple_of(head * half, half), half), :] = mixed / sums
            lse_ref[pl.ds(head, 1), :] = top[:, ours] + jnp.log(sums)

    resid_mid = tok_ref[...].astype(single) + nn(ot_ref[...].T.astype(low), w_ref[3])
    mid_ref[...] = resid_mid
    write(ot_ref, o_hbm)
    write(mid_ref, mid_hbm)
    mid_low = (resid_mid * inverse_rms(resid_mid) * gain_moe).astype(low)
    probs = router_softmax(mid_low, small_ref[...], experts)
    lanes = lax.broadcasted_iota(jnp.int32, probs.shape, 1)
    gate = jnp.sum(jnp.where(lanes == route_col, probs, 0.0), axis=1, keepdims=True)
    gate_ref[...] = jnp.broadcast_to(gate, gate_ref.shape)
    x_ref[...] = nn(place, mid_low).astype(low)
    own_g.wait()
    for k in range(shards - 1):
        landed(gin_hbm.at[(shard_id + shards - k - 1) % shards], (gs.at[k], gr.at[k]))
    for copy in writes:
        copy.wait()
    for copy in started:
        copy.wait_send()


def router_softmax(rows_low, small, experts):
    logits = nn(rows_low, small)
    lanes = lax.broadcasted_iota(jnp.int32, logits.shape, 1)
    logits = jnp.where(lanes < experts, logits, masked_score)
    powers = jnp.exp(logits - jnp.max(logits, axis=1, keepdims=True))
    return powers / jnp.sum(powers, axis=1, keepdims=True)


def front(routes, slot_ids, bucket_row, cotangent, weights, tokens, rows_small, slot_count):
    rows, width = tokens.shape
    shards = lax.axis_size("shard")
    chips, count = shards // 2, shards // 2 - 1
    keys = shards * PR_DEV + 2 * (rows - PR_DEV)
    lines = width // shards
    shape = jax.ShapeDtypeStruct
    sem = pltpu.SemaphoreType.DMA
    vm = pltpu.VMEM
    return pl.pallas_call(
        front_kernel,
        out_shape=(
            shape((16, rows), single), shape((16, 4 * TILE), single), shape((rows, TILE), single),
            shape((rows, TILE), jnp.int32), shape((8, width), single), shape((slot_count, width), low),
            shape((shards, slot_count // shards, width), low), shape((4, width, width), low),
            shape((keys, width), low), shape((width, TILE), low),
            shape((width, keys), low), shape((rows, width), low), shape((keys, width), low),
            shape((keys, width), low), shape((width, rows), single), shape((rows, width), single),
        ),
        in_specs=[in_vmem] * 8 + [anywhere] * 5,
        out_specs=(in_vmem,) * 6 + (anywhere,) * 10,
        scratch_shapes=[
            vm((2, tile_kinds, TILE, TILE), single), vm((TILE, keys), low), vm((keys - 2 * SPAN, 2 * rows), single),
            vm((2 * SPAN, 2 * (rows - TILE)), single),
            vm((shards, slot_count // shards, width), low), vm((4, width, width), low), vm((keys, width), low),
            vm((width, TILE), low), vm((rows, width), low), vm((4, lines, width), low), vm((lines, TILE), low),
            vm((keys, width), low), vm((width, keys), low), vm((rows, width), low), vm((keys, width), low),
            vm((keys, width), low), vm((width, rows), single), vm((rows, width), single),
            sem((shards - 1,)), sem((shards - 1,)), sem((16,)), sem((count,)), sem((count,)), sem((count,)),
            sem((count,)), sem((count,)), sem((count,)), sem((count, 3)), sem((count, 3)), sem((chips,)), sem((chips,)),
            sem((chips,)), sem((chips,)), sem((chips,)), sem((chips,)), sem((1,)), sem((1,)),
        ],
        compiler_params=pltpu.CompilerParams(collective_id=2, has_side_effects=True, vmem_limit_bytes=vmem_cap),
        cost_estimate=pl.CostEstimate(flops=30_000_000_000, bytes_accessed=20_000_000, transcendentals=8_000_000),
        name="front",
    )(routes, slot_ids, bucket_row, cotangent, *rows_small, *weights, tokens)


def moe_kernel(
    small_ref, x_ref, g_hbm, w_in_ref, w_out_ref,
    back_ref, out_hbm, ge_hbm, rx_hbm, ry_hbm, rg_ref,
    w_in, w_out, xin, gm, gg, hid, gpre, logit_grads, x_t, gw_in, gw_out, g_ref, out_ref,
    xs, xr, ms, mr, ws, ls, os_in, os_out, ex_s, ex_r, ey_s, ey_r, own, os_result,
):
    rep, chip, core, chips, quarter = places()
    experts = chips * 2
    here = chip * 2 + core
    pair_rows = 2 * xin.shape[2]
    hidden = w_in_ref.shape[1]
    width = w_in_ref.shape[0]
    _, slow, fast, slows, fasts = rep_places()
    lines = gw_in.shape[3]
    beside = [(slow * fasts + (fast + j) % fasts, here) for j in range(1, fasts)]
    beyond = [((slow + j) % slows * fasts + fast, here) for j in range(1, slows)]
    loads = [
        pltpu.make_async_copy(w_in_ref, w_in, ws.at[0]),
        pltpu.make_async_copy(w_out_ref, w_out, ws.at[1]),
    ]
    held = [
        pltpu.make_async_copy(x_ref.at[chip, core], xin.at[chip, core], own.at[0]),
        pltpu.make_async_copy(g_hbm, g_ref, own.at[1]),
    ]
    for copy in held + loads:
        copy.start()
    twin = (rep, chip * 2 + 1 - core)
    targets = [
        (k, side, (rep, chip_across(chip, k) * 2 + side)) for k in range(1, chips) for side in range(2)
    ]
    greet([twin] + [device for _, _, device in targets] + beside + beyond)
    sent = [send(x_ref.at[chip, 1 - core], xin.at[chip, core], (xs.at[0, 0], xr.at[0, core]), twin)]
    for k, side, device in targets:
        sent.append(
            send(x_ref.at[chip_across(chip, k), side], xin.at[chip, core], (xs.at[k, side], xr.at[k, core]), device)
        )
    for copy in sent[:5]:
        copy.start()
    for copy in held + loads[:1]:
        copy.wait()

    def arrived(k, source, side):
        piece = xin.at[source, side]
        send(piece, piece, (xs.at[0, 0], xr.at[k, side]), twin).wait_recv()

    @pl.loop(0, chips)
    def chunk(k):
        source = chip_across(chip, k)

        @pl.when(k == 0)
        def _():
            arrived(0, chip, 1 - core)

        @pl.when(k > 0)
        def _():
            for side in range(2):
                arrived(k, source, side)

        rows = xin[source].reshape(pair_rows, xin.shape[3])
        grads = g_ref[source].reshape(pair_rows, xin.shape[3])
        probs = router_softmax(rows, small_ref[...], experts)
        lanes = lax.broadcasted_iota(jnp.int32, probs.shape, 1)
        gate = jnp.sum(jnp.where(lanes == here, probs, 0.0), axis=1, keepdims=True)
        gated = (gate * grads.astype(single)).astype(low)
        span = pl.ds(pl.multiple_of(source * pair_rows, pair_rows), pair_rows)
        gg[span, :] = gated
        pre = nn(rows, w_in[...])

        @pl.when(k == 0)
        def _():
            loads[1].wait()

        grad_hidden = nt(gated, w_out[...])
        square = pre * pre
        wave = jnp.tanh(0.7978845608028654 * pre * (1.0 + 0.044715 * square))
        left = 0.5 + 0.5 * wave
        active = (pre * left).astype(low)
        slope = left + (0.5 * pre) * (1.0 - wave * wave) * (0.7978845608028654 + 0.10703222440890037 * square)
        grad_pre = (grad_hidden * slope).astype(low)
        hid[span, :] = active
        gpre[span, :] = grad_pre
        out = nn(active, w_out[...]).astype(low)
        out_ref[source] = out.reshape(out_ref.shape[1:])
        pltpu.make_async_copy(out_ref.at[source], out_hbm.at[source], os_result.at[k]).start()
        grad_gate = jnp.sum(grads.astype(single) * out.astype(single), axis=1, keepdims=True)
        chosen = jnp.where(lanes == here, 1.0, 0.0)
        grad_logits = jnp.where(lanes < experts, gate * grad_gate * (chosen - probs), 0.0)
        logit_grads[span, :] = grad_logits
        router = small_ref[...]
        total = nt(grad_pre, w_in[...]) + sum(nt(part, router) for part in thirds_of(grad_logits))
        gm[source] = total.astype(low).reshape(gm.shape[1:])

        def reply(side, slot):
            return send(
                gm.at[source, side], back_ref.at[chip, core], (ms.at[k, slot], mr.at[k, core]), (rep, source * 2 + side)
            )

        @pl.when(k == 0)
        def _():
            for copy in sent[5:]:
                copy.start()
            reply(1 - core, 0).start()
            pltpu.make_async_copy(gm.at[chip, core], back_ref.at[chip, core], ls).start()

        @pl.when(k > 0)
        def _():
            for side in range(2):
                reply(side, side).start()

    every = xin[...].reshape(gg.shape)
    x_t[...] = every.T

    def strip_writes(part):
        rows = pl.ds(pl.multiple_of(part * lines, lines), lines)
        tail = pl.ds(4 * lines, 4 * lines)
        if gw_out.shape[1] == 1:
            second = (gw_out.at[part, 0], ge_hbm.at[part // fasts, part % fasts, tail])
        else:
            second = (gw_out.at[part], ge_hbm.at[part, :, tail])
        return [
            pltpu.make_async_copy(gw_in.at[part], ge_hbm.at[:, :, rows], os_in.at[part]),
            pltpu.make_async_copy(*second, os_out.at[part]),
        ]

    grads_out = [
        send(gw_in.at[0, :, (fast + j + 1) % fasts], rx_hbm.at[j], (ex_s.at[j], ex_r.at[j]), device)
        for j, device in enumerate(beside)
    ], [
        send(gw_in.at[1, (slow + j + 1) % slows], ry_hbm.at[j], (ey_s.at[j], ey_r.at[j]), device)
        for j, device in enumerate(beyond)
    ]

    @pl.loop(0, hidden // width)
    def strip(part):
        cols = pl.ds(pl.multiple_of(part * width, width), width)
        gw_in[part] = nn(x_t[...], gpre[:, cols]).astype(low).reshape(gw_in.shape[1:])
        strip_writes(part)[0].start()
        for turn in range(2):

            @pl.when(part == turn)
            def _():
                for copy in grads_out[turn]:
                    copy.start()

    @pl.loop(0, hidden // width)
    def second_strip(part):
        cols = pl.ds(pl.multiple_of(part * width, width), width)
        gw_out[part] = tn(hid[:, cols], gg[...]).astype(low).reshape(gw_out.shape[1:])
        strip_writes(part)[1].start()

    rg_ref[...] = sum(nn(x_t[...], part) for part in thirds_of(logit_grads[...]))
    pltpu.make_async_copy(gm.at[chip, core], back_ref.at[chip, core], ls).wait()

    def replied(k, source, side):
        piece = back_ref.at[source, side]
        send(piece, piece, (ms.at[0, 0], mr.at[k, side]), twin).wait_recv()

    replied(0, chip, 1 - core)
    for k in range(1, chips):
        for side in range(2):
            replied(k, chip_across(chip, k), side)
    for copy in sent:
        copy.wait_send()
    for part in range(hidden // width):
        for copy in strip_writes(part):
            copy.wait()
    for k in range(chips):
        source = chip_across(chip, k)
        pltpu.make_async_copy(out_ref.at[source], out_hbm.at[source], os_result.at[k]).wait()
    for copy in grads_out[0] + grads_out[1]:
        copy.wait()
    send(gm.at[chip, 0], back_ref.at[chip, core], (ms.at[0, 0], mr.at[0, 0]), twin).wait_send()
    for k in range(1, chips):
        for side in range(2):
            send(gm.at[chip, 0], back_ref.at[chip, core], (ms.at[k, side], mr.at[0, 0]), twin).wait_send()


def moe(rows_out, grad_in, small, w_in, w_out):
    chips, _, cap, width = rows_out.shape
    slots = chips * 2 * cap
    hidden = w_in.shape[1]
    shape = jax.ShapeDtypeStruct
    pairs = pltpu.SemaphoreType.DMA
    strips = hidden // width
    slows, fasts = rep_places()[3:]
    lines = width // (slows * fasts)
    return pl.pallas_call(
        moe_kernel,
        out_shape=(
            shape(rows_out.shape, low), shape(rows_out.shape, low), shape((slows, fasts, 8 * lines, width), low),
            shape((fasts - 1, slows, lines, width), low), shape((slows - 1, fasts, lines, width), low),
            shape((width, TILE), single),
        ),
        in_specs=[in_vmem] + [anywhere] * 4,
        out_specs=(anywhere,) * 5 + (in_vmem,),
        scratch_shapes=[
            pltpu.VMEM((width, hidden), low), pltpu.VMEM((hidden, width), low),
            pltpu.VMEM(rows_out.shape, low), pltpu.VMEM(rows_out.shape, low), pltpu.VMEM((slots, width), low),
            pltpu.VMEM((slots, hidden), low), pltpu.VMEM((slots, hidden), low),
            pltpu.VMEM((slots, TILE), single), pltpu.VMEM((width, slots), low),
            pltpu.VMEM((strips, slows, fasts, lines, width), low),
            pltpu.VMEM((strips, width // (4 * lines), 4 * lines, width), low),
            pltpu.VMEM(rows_out.shape, low), pltpu.VMEM(rows_out.shape, low),
            pairs((chips, 2)), pairs((chips, 2)), pairs((chips, 2)), pairs((chips, 2)), pairs((2,)), pairs,
            pairs((strips,)), pairs((strips,)), pairs((fasts - 1,)), pairs((fasts - 1,)), pairs((slows - 1,)),
            pairs((slows - 1,)), pairs((2,)), pairs((chips,)),
        ],
        compiler_params=pltpu.CompilerParams(collective_id=3, has_side_effects=True, vmem_limit_bytes=vmem_cap),
        cost_estimate=pl.CostEstimate(flops=40_000_000_000, bytes_accessed=40_000_000, transcendentals=3_000_000),
        name="moe",
    )(small, rows_out, grad_in, w_in, w_out)


def back_kernel(
    col_ref, gain_ref, lse_ref, rev_ref, bucket_ref, rg_ref, back_hbm, mid_hbm, cot_hbm, q_hbm, k_hbm, v_hbm, o_hbm,
    every_hbm, w_hbm, n_hbm, ge_hbm, rx_hbm, ry_hbm, out_hbm,
    z_ref, kx_ref, ky_ref, dense_hbm, p_hbm, e_hbm, own_hbm, gres_hbm, ra_hbm, rb_hbm, ret_hbm, lx_hbm, ly_hbm,
    tiles, sums, diag, kt, dqt, far_sums, g_ref, dq_ref, dk_ref, dv_ref, attn_gain,
    every_ref, w_ref, n_ref, back_ref, mid_ref, cot_ref, q_ref, k_ref, v_ref, o_ref,
    dense_ref, own_ref, gres_ref,
    x_own, x_in, x_sum, y_own, y_in, y_sum, o_grad, o_half, o_sum, o_in, h_grad, h_half, h_sum, h_in,
    loc, out, lx_s, lx_r, ly_s, ly_r, xs, xr, as_, ar, bs, br, os_, or_, oz_s, oz_r, hs_, hr_, hz_s, hz_r,
):
    shard_id = lax.axis_index("shard")
    shards = lax.axis_size("shard")
    rows, width = mid_ref.shape
    blocks = k_ref.shape[0] // TILE - 4
    half = TILE // 2
    experts = shards
    heads_held = rev_ref.shape[0]
    rep, slow, fast, slows, fasts = rep_places()
    _, chip, core, chips, _ = places()
    along, _, twin = peer_lists()
    lines = x_own.shape[1]
    loads = [
        pltpu.make_async_copy(source, target, loc.at[i])
        for i, (source, target) in enumerate((
            (back_hbm, back_ref), (mid_hbm, mid_ref), (cot_hbm, cot_ref), (w_hbm.at[3], w_ref.at[3]), (o_hbm, o_ref),
            (q_hbm, q_ref), (k_hbm, k_ref), (v_hbm, v_ref), (n_hbm, n_ref), (w_hbm.at[pl.ds(0, 3)], w_ref.at[pl.ds(0, 3)]),
            (every_hbm, every_ref), (out_hbm.at[chip, core], ret_hbm.at[chip, core]),
            (ge_hbm.at[:, fast, pl.ds(0, lines)], x_own), (rx_hbm, x_in),
            (ge_hbm.at[slow, :, pl.ds(lines, lines)], y_own), (ry_hbm, y_in),
        ))
    ]
    for copy in loads:
        copy.start()
    writes = []

    def write(source, target):
        writes.append(pltpu.make_async_copy(source, target, out.at[len(writes)]))
        writes[-1].start()

    beside = [(slow * fasts + (fast + j) % fasts, shard_id) for j in range(1, fasts)]
    beyond = [((slow + j) % slows * fasts + fast, shard_id) for j in range(1, slows)]
    nearby = result_peers(rep, chip, core, range(NEAR))
    far_twins = [(rep, (chip + k) % chips * 2 + 1 - core) for k in range(1, chips)]
    greet([twin] + along + far_twins + beside + beyond)
    sent = [
        send(ge_hbm.at[:, (fast + j + 1) % fasts, pl.ds(2 * lines, 3 * lines)], ra_hbm.at[j], (as_.at[j], ar.at[j]), device)
        for j, device in enumerate(beside)
    ] + [
        send(ge_hbm.at[(slow + j + 1) % slows, :, pl.ds(5 * lines, 3 * lines)], rb_hbm.at[j], (bs.at[j], br.at[j]), device)
        for j, device in enumerate(beyond)
    ] + [
        send(out_hbm.at[chip_across(chip, k), side if k else 1 - core], ret_hbm.at[chip, core], (xs.at[k, side], xr.at[k, core]), device)
        for k, side, device in nearby
    ]
    for copy in sent:
        copy.start()
    for copy in loads[12:]:
        copy.wait()
    for held, came, total in ((x_own, x_in, x_sum), (y_own, y_in, y_sum)):
        value = held[...].astype(single)
        for j in range(came.shape[0]):
            value = value + came[j].astype(single)
        total[...] = value.astype(low)
    second = [
        send(x_sum.at[(slow + j + 1) % slows], lx_hbm.at[j], (lx_s.at[j], lx_r.at[j]), device)
        for j, device in enumerate(beyond)
    ] + [
        send(y_sum.at[(fast + j + 1) % fasts], ly_hbm.at[j], (ly_s.at[j], ly_r.at[j]), device)
        for j, device in enumerate(beside)
    ]
    for copy in second:
        copy.start()
    kx_ref[...] = x_sum[slow]
    ky_ref[...] = y_sum[fast]
    diag[...] = jnp.zeros_like(diag)
    far_sums[...] = jnp.zeros_like(far_sums)
    tile_rows = lax.broadcasted_iota(jnp.int32, (TILE, TILE), 0)
    tile_cols = lax.broadcasted_iota(jnp.int32, (TILE, TILE), 1)
    flip = (tile_rows + tile_cols == TILE - 1).astype(single)

    for copy in loads[:5]:
        copy.wait()
    slots = lax.broadcasted_iota(jnp.int32, (rows, back_ref.shape[0]), 1)
    grad_mid = nn((slots == col_ref[:, 0:1]).astype(low), back_ref[...])
    resid_mid = mid_ref[...]
    grad_gain_moe = jnp.sum(grad_mid * resid_mid * inverse_rms(resid_mid), axis=0, keepdims=True)
    grad_resid = cot_ref[...].astype(single) + norm_pull(grad_mid, resid_mid, gain_ref[1:2, :])
    gres_ref[...] = grad_resid
    write(gres_ref, gres_hbm)
    grad_attn = grad_resid.astype(low)
    g_ref[...] = nt(grad_attn, w_ref[3]).astype(low)
    o_grad[...] = nn(o_ref[...].astype(low), grad_attn).reshape(o_grad.shape).astype(low)
    o_halves = [send(o_grad.at[2 * k + 1 - core], o_half.at[k], (os_.at[k], or_.at[k]), twin) for k in range(chips)]
    o_sends = [
        send(o_sum.at[(chip + k + 1) % chips], o_in.at[k], (oz_s.at[k], oz_r.at[k]), device)
        for k, device in enumerate(along)
    ]
    for copy in o_halves:
        copy.start()
    h_halves = [send(h_grad.at[2 * k + 1 - core], h_half.at[k], (hs_.at[k], hr_.at[k]), twin) for k in range(chips)]
    h_sends = [
        send(h_sum.at[(chip + k + 1) % chips], h_in.at[k], (hz_s.at[k], hz_r.at[k]), device)
        for k, device in enumerate(along)
    ]
    for copy in loads[5:12]:
        copy.wait()
    own = pl.ds(pl.multiple_of(shard_id * TILE, TILE), TILE)
    tail = slice((blocks + 2) * TILE, (blocks + 4) * TILE)
    early = width // 2

    @pl.loop(0, width // TILE)
    def pair_loop(pair):
        cols = pl.ds(pl.multiple_of(pair * TILE, TILE), TILE)
        kt[...] = k_ref[:, cols].T
        g_pair = g_ref[:, cols]
        q_both, g_both = both_heads(q_ref[:, cols]), both_heads(g_pair)
        delta_t = g_pair.astype(single).T * o_ref[cols, :]
        delta = jnp.concatenate(
            [jnp.sum(delta_t[:half], axis=0, keepdims=True), jnp.sum(delta_t[half:], axis=0, keepdims=True)], axis=1
        )
        log_total = jnp.concatenate([lse_ref[pl.ds(pair * 2, 1), :], lse_ref[pl.ds(pair * 2 + 1, 1), :]], axis=1)
        for side in range(2):
            rev_row = rev_ref[pl.ds(pair * 2 + side, 1), :]
            fill_tiles(tiles.at[side], rev_row, rev_row[:, SPAN - 1 : SPAN], rev_row[:, SPAN : SPAN + 1])
        sums[...] = jnp.zeros_like(sums)

        def block_grads(part, q_rows, g_rows, shift, scale, grid):
            keys = slice(part * SPAN, (part + 1) * SPAN)
            count = q_rows.shape[0] // 2
            scores = with_bias(nt(k_ref[keys, cols], q_rows), tiles, grid)
            weights = jnp.exp(scores - shift)
            grad_scores = weights * (nt(v_ref[keys, cols], g_rows) - scale)
            for i, row in enumerate(grid):
                for j, (side, kind) in enumerate(row):
                    sums[side, kind] += tile_of(grad_scores, i, j)
            raw = grad_scores.astype(low)
            dk_ref[keys, cols] = nn(raw, q_rows).astype(low)
            dv_ref[keys, cols] = nn(weights.astype(low), g_rows).astype(low)
            return [nn(kt[:half, keys], raw[:, :count]), nn(kt[half:, keys], raw[:, count:])]

        grads = [jnp.zeros((half, rows), single)] * 2
        for part in range(blocks // 2):
            more = block_grads(part, q_both, g_both, log_total, delta, prompt_grid(part, shard_id, blocks))
            grads = [old + new for old, new in zip(grads, more)]
        local = [old[:, PR_DEV:] for old in grads]
        held = (continuation(q_both, 0), continuation(g_both, 0), continuation(log_total, 1), continuation(delta, 1))
        for part in range(2):
            more = block_grads(blocks // 2 + part, *held, local_grid(part, shard_id))
            local = [old + new for old, new in zip(local, more)]
        for side in range(2):
            head = pair * 2 + side
            dqt[side * half : (side + 1) * half, :] = jnp.concatenate([grads[side][:, :PR_DEV], local[side]], axis=1)
            near = jnp.concatenate(
                [
                    sums[side, 1] + sums[side, causal_tile], sums[side, 0], jnp.zeros((TILE, TILE), single),
                    sums[side, 2],
                ],
                axis=1,
            )
            flipped = jnp.dot(flip, near, precision=lax.Precision.HIGHEST, preferred_element_type=single)
            rolled = pltpu.roll(flipped, 3 * TILE + 1, 1, stride=1, stride_axis=0)
            diag[pl.ds(head, 1), :] = jnp.sum(rolled, axis=0, keepdims=True)
            far_sums[pl.ds(head, 1), :] = jnp.concatenate(
                [
                    jnp.sum(sums[side, far_before], axis=0, keepdims=True),
                    jnp.sum(sums[side, far_after], axis=0, keepdims=True),
                ],
                axis=1,
            )
        dq_ref[:, cols] = (dqt[...].T * 0.125).astype(low)

        @pl.when(pair == 0)
        def _():
            for k in range(chips):
                o_halves[k].wait_recv()
                o_sum[k] = (o_grad[2 * k + core].astype(single) + o_half[k].astype(single)).astype(low)
            for copy in o_sends:
                copy.start()

        @pl.when(pair == width // SPAN - 1)
        def _():
            normed = jnp.concatenate([n_ref[:, own], n_ref[:, tail]], axis=1)
            for i, (left, right) in enumerate(((normed, dq_ref), (n_ref[...], dk_ref), (n_ref[...], dv_ref))):
                part = nn(left, right[:, :early]).reshape(shards, h_grad.shape[1], early)
                h_grad[:, :, i * early : (i + 1) * early] = part.astype(low)
            for copy in h_halves:
                copy.start()

        @pl.when(pair == width // SPAN)
        def _():
            for k in range(chips):
                h_halves[k].wait_recv()
                h_sum[k] = (h_grad[2 * k + core].astype(single) + h_half[k].astype(single)).astype(low)
            for copy in h_sends:
                copy.start()

    lanes = lax.broadcasted_iota(jnp.int32, (heads_held, 4 * TILE), 1)
    before = jnp.sum(far_sums[:, :TILE], axis=1, keepdims=True)
    after = jnp.sum(far_sums[:, TILE:], axis=1, keepdims=True)
    by_gap = diag[...] + jnp.where(lanes == SPAN - 1, before, 0.0) + jnp.where(lanes == SPAN, after, 0.0)
    shard_rows = width // shards
    table_rows = 2 * TILE // 8 // shards
    owner = lax.broadcasted_iota(jnp.int32, (shards, shard_rows, 4 * TILE), 0)
    offset = lax.broadcasted_iota(jnp.int32, (shards, shard_rows, 4 * TILE), 1)
    held = jnp.where(offset < table_rows, owner * table_rows + offset, -1).reshape(width, 4 * TILE)
    hot = (held == bucket_ref[0:1, :]).astype(low)
    grad_table = sum(nt(part, hot) for part in thirds_of(by_gap))

    attn_gain[...] = jnp.zeros_like(attn_gain)
    normed = jnp.concatenate([n_ref[:, own], n_ref[:, tail]], axis=1)
    dense_ref[:, :early] = nn(normed, dq_ref[:, early:]).astype(low)
    grad_own = nt(dq_ref[...], w_ref[0])
    values = jnp.concatenate([every_ref[own, :], every_ref[tail, :]], axis=0).astype(single)
    attn_gain[...] += jnp.sum(fold8(grad_own * (values * inverse_rms(values))), axis=0)
    own_ref[...] = grad_own

    def pull_rows(part):
        span = pl.ds(pl.multiple_of(part * SPAN, SPAN), SPAN)
        values = every_ref[span, :].astype(single)
        grads = nt(dk_ref[span, :], w_ref[1]) + nt(dv_ref[span, :], w_ref[2])
        attn_gain[...] += jnp.sum(fold8(grads * (values * inverse_rms(values))), axis=0)
        return grads

    @pl.loop(0, blocks // 2)
    def pull_prompt(part):
        k_ref[pl.ds(pl.multiple_of(part * SPAN, SPAN), SPAN), :] = pull_rows(part).astype(low)

    write(k_ref.at[pl.ds(0, blocks * TILE)], p_hbm)
    k_ref[blocks * TILE : (blocks + 2) * TILE, :] = pull_rows(blocks // 2).astype(low)
    write(k_ref.at[pl.ds(blocks * TILE, SPAN)], e_hbm)
    own_ref[PR_DEV:, :] += pull_rows(blocks // 2 + 1)
    write(own_ref, own_hbm)

    dense_ref[:, early : 2 * early] = nn(n_ref[...], dk_ref[:, early:]).astype(low)
    dense_ref[:, 2 * early : 3 * early] = nn(n_ref[...], dv_ref[:, early:]).astype(low)

    small_t = jnp.concatenate(
        [
            jnp.zeros((experts, width), single), jnp.sum(attn_gain[...], axis=0, keepdims=True), grad_gain_moe,
            grad_table, jnp.zeros((TILE - experts - 2 - heads_held, width), single),
        ],
        axis=0,
    )
    dense_ref[:, 3 * early :] = (small_t.T + rg_ref[...]).astype(low)
    write(dense_ref, dense_hbm)
    o_total = o_sum[chip].astype(single)
    for k in range(chips - 1):
        o_sends[k].wait_recv()
        o_total = o_total + o_in[k].astype(single)
    z_ref[:, :width] = o_total.astype(low)
    h_total = h_sum[chip].astype(single)
    for k in range(chips - 1):
        h_sends[k].wait_recv()
        h_total = h_total + h_in[k].astype(single)
    z_ref[:, width:] = h_total.astype(low)
    for copy in o_halves + o_sends + h_halves + h_sends:
        copy.wait_send()
    for copy in writes:
        copy.wait()
    for k, side in result_slots(core, range(NEAR)):
        piece = ret_hbm.at[chip_across(chip, k), side]
        send(piece, piece, (xs.at[0, 0], xr.at[k, side]), twin).wait_recv()
    for j in range(fasts - 1):
        send(ra_hbm.at[j], ra_hbm.at[j], (as_.at[j], ar.at[j]), twin).wait_recv()
    for j in range(slows - 1):
        send(rb_hbm.at[j], rb_hbm.at[j], (bs.at[j], br.at[j]), twin).wait_recv()
    for copy in second:
        copy.wait()
    for copy in sent:
        copy.wait_send()


def back(
    returned, col_slots, mid, cotangent, gains, every_tok, weights, kept, bucket_row, router_grads, grads, rx, ry, result
):
    rows, width = mid.shape
    normed, queries, keys, values, attended, lse, rev = kept
    count = keys.shape[0]
    shards = lax.axis_size("shard")
    slows, fasts, eighths = grads.shape[:3]
    m = eighths // 8
    chips, lines, early = shards // 2, width // shards, width // 2
    vm = pltpu.VMEM
    shape = jax.ShapeDtypeStruct
    pairs = pltpu.SemaphoreType.DMA
    args = (
        col_slots, gains, lse, rev, bucket_row, router_grads, returned, mid, cotangent, queries, keys, values, attended,
        every_tok, weights, normed, grads, rx, ry, result,
    )
    return pl.pallas_call(
        back_kernel,
        out_shape=(
            shape((lines, width + 3 * early), low), shape((m, width), low), shape((m, width), low),
            shape((width, 3 * early + TILE), low),
            shape((count - 2 * SPAN, width), low), shape((SPAN, width), low),
            shape((rows, width), single), shape((rows, width), single),
            shape((fasts - 1, slows, 3 * m, width), low), shape((slows - 1, fasts, 3 * m, width), low),
            shape(result.shape, low), shape((slows - 1, m, width), low), shape((fasts - 1, m, width), low),
        ),
        in_specs=[in_vmem] * 6 + [anywhere] * 14,
        out_specs=(in_vmem,) * 3 + (anywhere,) * 10,
        scratch_shapes=[
            pltpu.VMEM((2, tile_kinds, TILE, TILE), single), pltpu.VMEM((2, tile_kinds, TILE, TILE), single),
            pltpu.VMEM((16, 4 * TILE), single), pltpu.VMEM((TILE, count), low), pltpu.VMEM((TILE, rows), single),
            pltpu.VMEM((16, 2 * TILE), single),
            pltpu.VMEM((rows, width), low), pltpu.VMEM((rows, width), low), pltpu.VMEM((count, width), low),
            pltpu.VMEM((count, width), low), pltpu.VMEM((8, width), single),
            pltpu.VMEM(every_tok.shape, low), pltpu.VMEM(weights.shape, low), pltpu.VMEM(normed.shape, low),
            vm(returned.shape, low), vm((rows, width), single), vm((rows, width), low), vm((rows, width), low),
            vm(keys.shape, low), vm(keys.shape, low), vm(attended.shape, single),
            vm((width, 3 * early + TILE), low),
            vm((rows, width), single), vm((rows, width), single),
            vm((slows, m, width), low), vm((fasts - 1, slows, m, width), low), vm((slows, m, width), low),
            vm((fasts, m, width), low), vm((slows - 1, fasts, m, width), low), vm((fasts, m, width), low),
            vm((shards, lines, width), low), vm((chips, lines, width), low),
            vm((chips, lines, width), low), vm((chips - 1, lines, width), low),
            vm((shards, lines, 3 * early), low), vm((chips, lines, 3 * early), low),
            vm((chips, lines, 3 * early), low), vm((chips - 1, lines, 3 * early), low),
            pairs((16,)), pairs((6,)), pairs((slows - 1,)), pairs((slows - 1,)), pairs((fasts - 1,)), pairs((fasts - 1,)),
            pairs((NEAR, 2)), pairs((NEAR, 2)), pairs((fasts - 1,)), pairs((fasts - 1,)),
            pairs((slows - 1,)), pairs((slows - 1,)), pairs((chips,)), pairs((chips,)), pairs((chips - 1,)),
            pairs((chips - 1,)), pairs((chips,)), pairs((chips,)), pairs((chips - 1,)), pairs((chips - 1,)),
        ],
        compiler_params=pltpu.CompilerParams(collective_id=4, has_side_effects=True, vmem_limit_bytes=vmem_cap),
        cost_estimate=pl.CostEstimate(flops=60_000_000_000, bytes_accessed=40_000_000, transcendentals=8_000_000),
        name="back",
    )(*args)


def places():
    rep, shard = lax.axis_index("rep"), lax.axis_index("shard")
    return rep, shard // 2, shard % 2, lax.axis_size("shard") // 2, rep % QUARTERS


def peer_lists():
    rep, chip, core, chips, quarter = places()
    along = [(rep, (chip + k) % chips * 2 + core) for k in range(1, chips)]
    across = [(rep - quarter + (quarter + j) % QUARTERS, chip * 2 + core) for j in range(1, QUARTERS)]
    twin = (rep, chip * 2 + 1 - core)
    return along, across, twin


def chip_across(chip, k):
    partner, bit = 0, 1
    while bit < lax.axis_size("shard") // 2:
        partner = partner + bit * ((chip // bit + k // bit) % 2)
        bit = bit * 2
    return partner


def result_peers(rep, chip, core, chosen):
    return [
        (k, side, (rep, chip_across(chip, k) * 2 + (side if k else 1 - core)))
        for k in chosen for side in range(2 if k else 1)
    ]


def result_slots(core, chosen):
    return [(k, side if k else 1 - core) for k in chosen for side in range(2 if k else 1)]


def greet(devices):
    barrier = pltpu.get_barrier_semaphore()
    for device in devices:
        pl.semaphore_signal(barrier, inc=1, device_id=device, device_id_type=mesh_ids)
    pl.semaphore_wait(barrier, len(devices))


def send(source, target, sems, device):
    return pltpu.make_async_remote_copy(
        src_ref=source, dst_ref=target, send_sem=sems[0], recv_sem=sems[1],
        device_id=device, device_id_type=mesh_ids,
    )


def rep_places():
    rep, reps = lax.axis_index("rep"), lax.axis_size("rep")
    fasts = QUARTERS if reps % (QUARTERS * QUARTERS) == 0 else 2
    return rep, rep // fasts, rep % fasts, reps // fasts, fasts


def reduce_kernel(
    gain_ref, col_ref, d_hbm, p_hbm, e_hbm, own_hbm, gres_hbm, tok_hbm, mid_hbm, gate_hbm, out_hbm, ret_hbm,
    ge_hbm, ra_hbm, rb_hbm, z_hbm,
    early_ref, late_ref, gt_hbm, mix_hbm, ka_hbm, la_hbm, kb_hbm, lb_hbm,
    d_own, half, hr, tr, mr, cr, zs, tz, z_last, z_above, z_all, last, above_in, gathered,
    p_own, p_half, p_sum, p_in, e_in, own, gres, tok, mid, gate, ret,
    a_own, a_in, a_sum, b_own, b_in, b_sum, gt_ref, mix_ref, out,
    loc, ps_s, ps_r, ds_s, ds_r, pz_s, pz_r, rr_s, rr_r, rz_s, rz_r, zr_s, zr_r, zh_s, zh_r, za_s, za_r,
    dh_s, dh_r, da_s, da_r, ea_s, ea_r, eb_s, eb_r, xs, xr,
):
    rep, chip, core, chips, quarter = places()
    along, across, twin = peer_lists()
    _, slow, fast, slows, fasts = rep_places()
    classes = lax.axis_size("rep") // QUARTERS
    here = chip * 2 + core
    beside = [(slow * fasts + (fast + j) % fasts, here) for j in range(1, fasts)]
    beyond = [((slow + j) % slows * fasts + fast, here) for j in range(1, slows)]
    above = [((rep // QUARTERS + k) % classes * QUARTERS + quarter, here) for k in range(1, classes)]
    wide = lambda held: held.astype(single)
    lines = ge_hbm.shape[2] // 8
    pending = []

    def load(source, target, index, sems=loc):
        copy = pltpu.make_async_copy(source, target, sems.at[index])
        copy.start()
        return copy

    def go(source, target, sems, device):
        copy = send(source, target, sems, device)
        copy.start()
        pending.append(copy)

    def landed(piece, sems):
        send(piece, piece, sems, twin).wait_recv()

    early_in = load(z_hbm, zs, 12)
    a_loads = [load(ge_hbm.at[:, fast, pl.ds(2 * lines, 3 * lines)], a_own, 0), load(ra_hbm, a_in, 1)]
    halves = [load(d_hbm.at[:, core], d_own, 5), load(p_hbm.at[:, core], p_own, 4)]
    b_loads = [load(ge_hbm.at[slow, :, pl.ds(5 * lines, 3 * lines)], b_own, 2), load(rb_hbm, b_in, 3)]
    rest = [
        load(ret_hbm.at[chip_across(chip, k)], ret.at[chip_across(chip, k)], 13 + k) for k in range(NEAR)
    ] + [
        load(mid_hbm, mid, 7), load(gate_hbm, gate, 8), load(own_hbm, own, 9),
        load(gres_hbm, gres, 10), load(tok_hbm, tok, 11),
    ]
    others = [(rep, (here + k) % (2 * chips)) for k in range(1, 2 * chips)]
    greets = list(others)
    for device in across + beside + beyond + above:
        greets.append(device)
    greet(greets)
    for k in range(chips):
        go(d_hbm.at[k, 1 - core], half.at[k], (ds_s.at[k], ds_r.at[k]), twin)
    go(p_hbm.at[:, 1 - core], p_half, (ps_s.at[0], ps_r.at[0]), twin)
    go(e_hbm, e_in, (ps_s.at[1], ps_r.at[1]), twin)
    for k, side, device in result_peers(rep, chip, core, range(NEAR, chips)):
        go(out_hbm.at[chip_across(chip, k), side], ret.at[chip, core], (xs.at[k - NEAR, side], xr.at[k - NEAR, core]), device)
    early_in.wait()
    for j, device in enumerate(across):
        go(zs.at[(quarter + j + 1) % QUARTERS], tz.at[j], (zr_s.at[j], zr_r.at[j]), device)

    for copy in a_loads:
        copy.wait()
    for t in range(slows):
        total = wide(a_own[t])
        for j in range(fasts - 1):
            total = total + wide(a_in[j, t])
        a_sum[t] = total.astype(low)
    for copy in halves:
        copy.wait()
    for k in range(chips):
        landed(half.at[k], (ds_s.at[k], ds_r.at[k]))
        for t in range(QUARTERS):
            hr[t, k] = (wide(d_own[k, t]) + wide(half[k, t])).astype(low)
    for j, device in enumerate(across):
        go(hr.at[(quarter + j + 1) % QUARTERS], tr.at[j], (rr_s.at[j], rr_r.at[j]), device)
    landed(p_half, (ps_s.at[0], ps_r.at[0]))
    for k in range(chips):
        p_sum[k] = (wide(p_own[k]) + wide(p_half[k])).astype(low)
    for k, device in enumerate(along):
        go(p_sum.at[(chip + k + 1) % chips], p_in.at[k], (pz_s.at[k], pz_r.at[k]), device)
    for copy in b_loads:
        copy.wait()
    for t in range(fasts):
        total = wide(b_own[t])
        for j in range(slows - 1):
            total = total + wide(b_in[j, t])
        b_sum[t] = total.astype(low)
    def class_sum(held, came, s_sems, r_sems):
        total = wide(held[...])
        for j, device in enumerate(above):
            go(held, came.at[j], (s_sems.at[j], r_sems.at[j]), device)
        for j in range(classes - 1):
            landed(came.at[j], (s_sems.at[j], r_sems.at[j]))
            total = total + wide(came[j])
        return total.astype(low)

    def hand_out(pieces, s_sems, r_sems):
        for j, device in enumerate(across):
            go(pieces.at[quarter], pieces.at[quarter], (s_sems.at[j], r_sems.at[j]), device)

    def handed(pieces, s_sems, r_sems):
        for j in range(QUARTERS - 1):
            landed(pieces.at[(quarter + QUARTERS - j - 1) % QUARTERS], (s_sems.at[j], r_sems.at[j]))

    for j in range(QUARTERS - 1):
        landed(tz.at[j], (zr_s.at[j], zr_r.at[j]))
    total = wide(zs[quarter])
    for j in range(QUARTERS - 1):
        total = total + wide(tz[j])
    z_last[...] = total.astype(low)
    z_all[quarter] = class_sum(z_last, z_above, zh_s, zh_r) if classes > 1 else z_last[...]
    hand_out(z_all, za_s, za_r)

    for copy in rest:
        copy.wait()
    writes = [load(a_sum.at[slow], ka_hbm, 0, out), load(b_sum.at[fast], kb_hbm, 1, out)]

    for j in range(QUARTERS - 1):
        landed(tr.at[j], (rr_s.at[j], rr_r.at[j]))
    for j, device in enumerate(beyond):
        go(a_sum.at[(slow + j + 1) % slows], la_hbm.at[j], (ea_s.at[j], ea_r.at[j]), device)
    for j, device in enumerate(beside):
        go(b_sum.at[(fast + j + 1) % fasts], lb_hbm.at[j], (eb_s.at[j], eb_r.at[j]), device)

    for k in range(chips):
        total = wide(hr[quarter, k])
        for j in range(QUARTERS - 1):
            total = total + wide(tr[j, k])
        mr[k] = total.astype(low)
    for k, device in enumerate(along):
        go(mr.at[(chip + k + 1) % chips], cr.at[k], (rz_s.at[k], rz_r.at[k]), device)

    for k in range(chips - 1):
        landed(p_in.at[k], (pz_s.at[k], pz_r.at[k]))
    landed(e_in, (ps_s.at[1], ps_r.at[1]))
    total = wide(p_sum[chip])
    for k in range(chips - 1):
        total = total + wide(p_in[k])
    grads = own[...] + jnp.concatenate([total, wide(e_in[...])], axis=0)
    gt_ref[...] = gres[...] + norm_pull(grads, wide(tok[...]), gain_ref[0:1, :])
    writes.append(load(gt_ref, gt_hbm, 2, out))

    for k in range(chips - 1):
        landed(cr.at[k], (rz_s.at[k], rz_r.at[k]))
    total = wide(mr[chip])
    for k in range(chips - 1):
        total = total + wide(cr[k])
    last[...] = total.astype(low)
    gathered[quarter] = class_sum(last, above_in, dh_s, dh_r) if classes > 1 else last[...]
    hand_out(gathered, da_s, da_r)
    for k, side in result_slots(core, range(NEAR, chips)):
        landed(ret.at[chip_across(chip, k), side], (xs.at[k - NEAR, side], xr.at[k - NEAR, side]))
    slots = lax.broadcasted_iota(jnp.int32, (tok.shape[0], 2 * chips * ret.shape[2]), 1)
    chosen = nn((slots == col_ref[:, 0:1]).astype(low), ret[...].reshape(slots.shape[1], tok.shape[1]))
    mix_ref[...] = (mid[...] + gate[:, 0:1] * chosen).astype(low)
    writes.append(load(mix_ref, mix_hbm, 3, out))
    handed(z_all, za_s, za_r)
    early_ref[...] = z_all[...]
    handed(gathered, da_s, da_r)
    late_ref[...] = gathered[...]
    for j in range(slows - 1):
        landed(la_hbm.at[j], (ea_s.at[j], ea_r.at[j]))
    for j in range(fasts - 1):
        landed(lb_hbm.at[j], (eb_s.at[j], eb_r.at[j]))
    for copy in writes:
        copy.wait()
    for copy in pending:
        copy.wait_send()


def reduce_all(gains, col_slots, dense, prompt_part, near_part, own, gres, tokens, mid, gate, result, returned, grads, ra, rb, z):
    chips = lax.axis_size("shard") // 2
    classes = lax.axis_size("rep") // QUARTERS
    slows, fasts, eighths = grads.shape[:3]
    part = (3 * eighths // 8, mid.shape[1])
    rows, width = mid.shape
    lines, lanes = dense.shape[3:]
    wider = z.shape[2]
    shape = jax.ShapeDtypeStruct
    sem = pltpu.SemaphoreType.DMA
    vm = pltpu.VMEM
    count, others = chips - 1, QUARTERS - 1
    ours = prompt_part.shape[2:]
    extra = max(classes - 1, 1)
    args = (gains, col_slots, dense, prompt_part, near_part, own, gres, tokens, mid, gate, result, returned, grads, ra, rb, z)
    return pl.pallas_call(
        reduce_kernel,
        out_shape=(
            shape((QUARTERS, lines, wider), low), shape((QUARTERS, lines, lanes), low),
            shape((rows, width), single), shape((rows, width), low),
            shape(part, low), shape((slows - 1,) + part, low), shape(part, low), shape((fasts - 1,) + part, low),
        ),
        in_specs=[in_vmem] * 2 + [anywhere] * 14,
        out_specs=(in_vmem,) * 2 + (anywhere,) * 6,
        scratch_shapes=[
            vm((chips, QUARTERS, lines, lanes), low), vm((chips, QUARTERS, lines, lanes), low),
            vm((QUARTERS, chips, lines, lanes), low), vm((others, chips, lines, lanes), low),
            vm((chips, lines, lanes), low), vm((count, lines, lanes), low),
            vm((QUARTERS, lines, wider), low), vm((others, lines, wider), low), vm((lines, wider), low),
            vm((extra, lines, wider), low), vm((QUARTERS, lines, wider), low),
            vm((lines, lanes), low), vm((extra, lines, lanes), low), vm((QUARTERS, lines, lanes), low),
            vm((chips,) + ours, low), vm((chips,) + ours, low), vm((chips,) + ours, low), vm((count,) + ours, low),
            vm(near_part.shape, low), vm((rows, width), single), vm((rows, width), single), vm((rows, width), low),
            vm((rows, width), single), vm(gate.shape, single), vm(result.shape, low),
            vm((slows,) + part, low), vm(ra.shape, low), vm((slows,) + part, low),
            vm((fasts,) + part, low), vm(rb.shape, low), vm((fasts,) + part, low),
            vm((rows, width), single), vm((rows, width), low), sem((4,)),
            sem((13 + NEAR,)), sem((2,)), sem((2,)), sem((chips,)), sem((chips,)), sem((count,)), sem((count,)),
            sem((others,)), sem((others,)), sem((count,)), sem((count,)),
            sem((others,)), sem((others,)), sem((extra,)), sem((extra,)), sem((others,)), sem((others,)),
            sem((extra,)), sem((extra,)), sem((others,)), sem((others,)),
            sem((slows - 1,)), sem((slows - 1,)), sem((fasts - 1,)), sem((fasts - 1,)),
            sem((chips - NEAR, 2)), sem((chips - NEAR, 2)),
        ],
        compiler_params=pltpu.CompilerParams(collective_id=1, has_side_effects=True, vmem_limit_bytes=vmem_cap),
        cost_estimate=pl.CostEstimate(flops=0, bytes_accessed=200_000_000, transcendentals=0),
        name="reduce_all",
    )(*args)


def finish_kernel(
    kx_ref, lx_ref, ky_ref, ly_ref, ka_ref, la_ref, kc_ref, lc_ref, kb_ref, lb_ref, early_ref, late_ref, small_ref, gt_ref, mix_ref, *outs
):
    ea_ref, eb_ref, q_ref, k_ref, v_ref, o_ref, router_ref, attn_ref, moe_ref, table_ref, gt_out, mix_out = outs
    gt_out[...] = gt_ref[...]
    mix_out[...] = mix_ref[...]
    width = q_ref.shape[2]
    experts = router_ref.shape[0]
    step = pl.program_id(0)

    def total(held, came):
        value = held[...].reshape(ea_ref.shape).astype(single)
        for j in range(came.shape[0]):
            value = value + came[j].reshape(ea_ref.shape).astype(single)
        return value

    for target, first, last, sources in (
        (ea_ref, 0, 0, (kx_ref, lx_ref)), (ea_ref, 1, 1, (ky_ref, ly_ref)), (ea_ref, 2, 3, (ka_ref, la_ref)),
        (eb_ref, 0, 0, (kc_ref, lc_ref)), (eb_ref, 1, 3, (kb_ref, lb_ref)),
    ):

        @pl.when((step >= first) & (step <= last))
        def _():
            target[...] = total(*sources)

    half = width // 2
    o_ref[...] = early_ref[:, :, :width].astype(single)
    for i, ref in enumerate((q_ref, k_ref, v_ref)):
        ref[:, :, :half] = early_ref[:, :, width + i * half : width + (i + 1) * half].astype(single)
        ref[:, :, half:] = late_ref[:, :, i * half : (i + 1) * half].astype(single)

    @pl.when(pl.program_id(0) == 0)
    def _():
        small = small_ref[...].astype(single).reshape(router_ref.shape[1], TILE)
        turned = small.T
        router_ref[...] = turned[:experts]
        attn_ref[...] = turned[experts : experts + 1]
        moe_ref[...] = turned[experts + 1 : experts + 2]
        table_ref[...] = small[: table_ref.shape[0], experts + 2 : experts + 2 + table_ref.shape[1]]


def finish(kx, lx, ky, ly, ka, la, kb, lb, early, late, grad_tokens, mixed, experts, table_rows, heads):
    shape = jax.ShapeDtypeStruct
    _, lines, wider = early.shape
    lanes = late.shape[2]
    width = kb.shape[1]
    rows = QUARTERS * lines
    steps = QUARTERS
    m = kx.shape[0]
    ka, kb = (part.reshape(3, m, width) for part in (ka, kb))
    la, lb = (part.reshape(-1, 3, m, width) for part in (la, lb))
    block = lambda pick: pl.BlockSpec((1, m, width), lambda i: (pick(i), 0, 0))
    blocks = lambda array, pick: pl.BlockSpec((array.shape[0], 1, m, width), lambda i: (0, pick(i), 0, 0))
    strip, rest = (lambda i: jnp.maximum(i - 2, 0)), (lambda i: jnp.maximum(i - 1, 0))
    part = pl.BlockSpec((1, lines, width), lambda i: (i, 0, 0))
    once = lambda *dims: pl.BlockSpec(dims, lambda i: (0,) * len(dims))
    some = pl.BlockSpec((mixed.shape[0] // steps, width), lambda i: (i, 0))
    return pl.pallas_call(
        finish_kernel,
        grid=(steps,),
        out_shape=(
            shape((m, steps * width), single), shape((steps * m, width), single), *(shape((QUARTERS, lines, width), single),) * 4,
            shape((experts, rows), single), shape((1, rows), single), shape((1, rows), single),
            shape((table_rows, heads), single), shape(grad_tokens.shape, single), shape(mixed.shape, low),
        ),
        in_specs=[
            once(*kx.shape), once(*lx.shape), once(*ky.shape), once(*ly.shape),
            block(strip), blocks(la, strip), block(lambda i: 2), blocks(la, lambda i: 2), block(rest), blocks(lb, rest),
            pl.BlockSpec((1, lines, wider), lambda i: (i, 0, 0)), pl.BlockSpec((1, lines, lanes), lambda i: (i, 0, 0)),
            pl.BlockSpec((QUARTERS, lines, TILE), lambda i: (0, 0, lanes // TILE - 1)), some, some,
        ],
        out_specs=(
            pl.BlockSpec((m, width), lambda i: (0, i)), pl.BlockSpec((m, width), lambda i: (i, 0)),
            part, part, part, part, once(experts, rows), once(1, rows), once(1, rows), once(table_rows, heads),
            some, some,
        ),
        compiler_params=pltpu.CompilerParams(vmem_limit_bytes=vmem_cap),
        cost_estimate=pl.CostEstimate(flops=0, bytes_accessed=12_000_000, transcendentals=0),
        name="finish",
    )(kx, lx, ky, ly, ka, la, ka, la, kb, lb, early, late, late, grad_tokens, mixed)


def local(
    tokens,
    routes,
    slot_ids,
    w_query,
    w_key,
    w_value,
    w_output,
    w_router,
    norm_attn,
    norm_moe,
    rel_table,
    w_in,
    w_out,
    cotangent,
):
    shard_count = lax.axis_size("shard")
    token_rows, model_width = tokens.shape
    prompt_len = PR_DEV * shard_count
    weight_rows, expert_count = w_router.shape
    table_rows, head_count = rel_table.shape
    capacity = 2 * token_rows // expert_count
    slot_count = expert_count * capacity

    rows_small = (w_router.T, norm_attn, norm_moe, rel_table)
    bucket_row = jnp.asarray(np.tile(distance_buckets(table_rows * shard_count), (8, 1)), jnp.int32)
    (
        lse, rev, gate, col_slots, gains, slots_out, grad_in, weights, every_tok, small, normed, queries, keys, values,
        attended, mid,
    ) = front(routes, slot_ids, bucket_row, cotangent, (w_query, w_key, w_value, w_output), tokens, rows_small, slot_count)
    by_chip = (shard_count // 2, 2, capacity, model_width)
    grad_back, result, grads, rx, ry, router_grads = moe(
        slots_out.reshape(by_chip), grad_in.reshape(by_chip), small, w_in[0], w_out[0]
    )
    early_part, kx, ky, dense, prompt_part, near_part, grad_own, grad_resid, ra, rb, returned, lx, ly = back(
        grad_back.reshape(slot_count, model_width), col_slots, mid, cotangent, gains, every_tok, weights,
        (normed, queries, keys, values, attended, lse, rev), bucket_row, router_grads, grads, rx, ry, result,
    )
    chips = shard_count // 2
    lines = weight_rows // QUARTERS
    early, late, grad_tokens, mixed, ka, la, kb, lb = reduce_all(
        gains, col_slots, dense.reshape(chips, 2, QUARTERS, lines, -1),
        prompt_part.reshape(chips, 2, PR_DEV, model_width), near_part, grad_own, grad_resid, tokens, mid, gate,
        result, returned, grads, ra, rb,
        early_part.reshape(QUARTERS, lines, -1),
    )
    in_grad, out_grad, gq, gk, gv, go, router, gain_attn, gain_moe, table, grad_tokens, mixed = finish(
        kx, lx, ky, ly, ka, la, kb, lb, early, late, grad_tokens, mixed, expert_count, table_rows, head_count
    )
    return (
        mixed,
        grad_tokens,
        *(part.reshape(weight_rows, model_width) for part in (gq, gk, gv, go)),
        router.T,
        gain_attn[0],
        gain_moe[0],
        table,
        in_grad[None],
        out_grad[None],
    )


def solution(mesh):
    return jax.shard_map(
        local,
        mesh=mesh,
        in_specs=(
            P(("rep", "shard"), None),
            P(("rep", "shard")),
            P(("rep", "shard")),
            P("shard", None),
            P("shard", None),
            P("shard", None),
            P("shard", None),
            P("shard", None),
            P("shard"),
            P("shard"),
            P("shard", None),
            P("shard", None, None),
            P("shard", None, None),
            P(("rep", "shard"), None),
        ),
        out_specs=(
            P(("rep", "shard"), None),
            P(("rep", "shard"), None),
            P("shard", None),
            P("shard", None),
            P("shard", None),
            P("shard", None),
            P("shard", None),
            P("shard"),
            P("shard"),
            P("shard", None),
            P("shard", "rep", None),
            P("shard", "rep", None),
        ),
        check_vma=False,
    )
```
